32 devices in a mesh: head: 4 (over x, core), seq: 8 (over z, y).
Axes of the slice: x: 2, y: 2, z: 4, core: 2. Of those that a mesh axis runs over, the one named last changes fastest.
Arguments:
- layer_input: bfloat16 [2, 8, 256, 768], P(None, 'seq', 'head'), may hold values from -6 to 6
- grad_out: bfloat16 [2, 8, 256, 768], P(None, 'seq', 'head'), may hold values from -6 to 6
- lengths: int32 [2], replicated, may hold values from 512 to 2048, as said below
- w_qkv: bfloat16 [768, 2304], P(('head', 'seq')), may hold values from -0.3125 to 0.3125
- w_out: bfloat16 [768, 768], P(('head', 'seq')), may hold values from -0.5 to 0.5
- w_fc: bfloat16 [768, 3072], P(('head', 'seq')), may hold values from -0.21875 to 0.21875
- w_proj: bfloat16 [3072, 768], P(('head', 'seq')), may hold values from -0.109375 to 0.109375
- b_fc: bfloat16 [3072], P(('head', 'seq')), may hold values from -0.8984375 to 0.8984375
- norm_gains: bfloat16 [2, 768], P(None, ('head', 'seq')), may hold values from 0.25 to 1.75
- biases: bfloat16 [6, 768], P(None, ('head', 'seq')), may hold values from -0.8984375 to 0.8984375
Outputs:
- layer_output: bfloat16 [2, 8, 256, 768], P(None, 'seq', 'head')
- grad_input: float32 [2, 8, 256, 768], P(None, 'seq', 'head')
- grad_w_qkv: float32 [768, 2304], P(('head', 'seq'))
- grad_w_out: float32 [768, 768], P(('head', 'seq'))
- grad_w_fc: float32 [768, 3072], P(('head', 'seq'))
- grad_w_proj: float32 [3072, 768], P(('head', 'seq'))
- grad_b_fc: float32 [3072], P(('head', 'seq'))
- grad_norm_gains: float32 [2, 768], P(None, ('head', 'seq'))
- grad_biases: float32 [6, 768], P(None, ('head', 'seq'))
- root_means: float32 [4], replicated
The draws below stay inside these ranges and needn't reach their ends.
Inputs may be any that keep to these rules, and one draw needn't show every extreme that they name: Sequence s has its valid tokens in its first lengths[s] slots of 2048; in every draw some sequence fills all 2048 slots and some other is shorter than 1536.
All inputs are finite; a program needn't handle non-finite values.
Results may differ from the reference program's by a relative error of at most 0.012.
The reference program's roundings to bfloat16 on the way count: a program that leaves them out, or rounds other values in their place, can miss the bound.
Values may be sent and summed in bfloat16 or wider, within the bound.
A program may use at most 192 MiB of HBM per device.

```python
import jax
import jax.numpy as jnp
from jax import lax

D = 768
FF = 3072
HEADS = 12
HEAD_DIM = 64
SEQS = 2
GROUP = 256
SEQ_BLOCKS = 8
SLOT_LEN = 2048


def draw_lengths(key, part):
    keys_all = jax.random.split(key, 3)
    shortest = SLOT_LEN // 4
    upper = 3 * SLOT_LEN // 4
    drawn = jax.random.randint(keys_all[0], (SEQS,), shortest, SLOT_LEN + 1, dtype=jnp.int32)
    short_one = jax.random.randint(keys_all[1], (SEQS,), shortest, upper, dtype=jnp.int32)
    order = jax.random.permutation(keys_all[2], jnp.arange(SEQS, dtype=jnp.int32))
    mixed_len = jnp.where(order == 1, short_one, drawn)
    return jnp.where(order == 0, SLOT_LEN, mixed_len).astype(jnp.int32)


def block_levels(stream_key, dims, cuts, low, top_value):
    def one(position, parts):
        steps = jax.random.uniform(jax.random.fold_in(jax.random.fold_in(stream_key, 6), position), (parts,), jnp.float32, low / len(cuts), top_value / len(cuts))
        return jnp.repeat(jnp.exp(steps), dims[position] // parts).reshape((-1,) + (1,) * (len(dims) - position - 1))

    level = one(*cuts[0])
    for cut in cuts[1:]:
        level = level * one(*cut)
    return level


def scatter_about(own_key, shape, width, most, pieces=(), held_as=jnp.bfloat16):
    entries = width * jax.random.normal(own_key, shape, jnp.float32)
    if pieces:
        entries = entries * block_levels(own_key, shape, pieces, -0.22, 0.18)
    return jnp.clip(entries, -most, most).astype(held_as)


def setup_inputs(seed: int = 0) -> dict:
    keys = jax.random.split(jax.random.key(seed), 11)
    layer_input = scatter_about(keys[0], (SEQS, SEQ_BLOCKS, GROUP, D), 1.0, 6.0, ((1, 8), (2, 4)))
    grad_out = scatter_about(keys[1], (SEQS, SEQ_BLOCKS, GROUP, D), 1.0, 6.0, ((1, 8), (2, 4)))
    lengths = draw_lengths(jax.random.fold_in(keys[10], 71), 0)
    w_qkv = scatter_about(keys[3], (D, 3 * D), (D // 2) ** -0.5, 0.3125, ((0, 32),))
    w_out = scatter_about(keys[4], (D, D), (max(1, D * 320 // SLOT_LEN)) ** -0.5, 0.5, ((0, 32),))
    w_fc = scatter_about(keys[5], (D, FF), D ** -0.5, 0.21875, ((0, 32),))
    w_proj = scatter_about(keys[6], (FF, D), FF ** -0.5, 0.109375, ((0, 32),))
    b_fc = scatter_about(keys[7], (FF,), 0.15, 0.8984375, ((0, 32),))
    norm_gains = jnp.clip(1.0 + 0.15 * jax.random.normal(keys[8], (2, D), jnp.float32), 0.25, 1.75).astype(jnp.bfloat16)
    biases = scatter_about(keys[9], (6, D), 0.15, 0.8984375, ((1, 32),))
    return dict(layer_input=layer_input, grad_out=grad_out, lengths=lengths, w_qkv=w_qkv, w_out=w_out, w_fc=w_fc, w_proj=w_proj, b_fc=b_fc, norm_gains=norm_gains, biases=biases)


@jax.custom_vjp
def low(v):
    return lax.optimization_barrier(v.astype(jnp.bfloat16)).astype(jnp.float32)

@jax.custom_vjp
def low_back(v):
    return v

def low_keep(v):
    return (low(v), None)

def low_pass(kept, grad):
    return (grad,)

def back_keep(v):
    return (v, None)

def back_low(kept, grad):
    return (low(grad),)
low.defvjp(low_keep, low_pass)
low_back.defvjp(back_keep, back_low)

def layer_norm(inputs, scales, shifts):
    centre = inputs - lax.optimization_barrier(jnp.mean(inputs, axis=-1, keepdims=True))
    return centre * lax.rsqrt(lax.optimization_barrier(jnp.mean(centre * centre, axis=-1, keepdims=True)) + 1e-05) * scales + shifts

def product(left_side, right_side):
    return jnp.dot(left_side, right_side, precision=lax.Precision.HIGHEST, preferred_element_type=jnp.float32)

def reference(layer_input, grad_out, lengths, w_qkv, w_out, w_fc, w_proj, b_fc, norm_gains, biases):
    total_rows = SEQS * SLOT_LEN
    query_rows = min(128, SLOT_LEN)
    allowed = jnp.arange(SLOT_LEN, dtype=jnp.int32)[None, :] < lengths[:, None]
    keep_rows = allowed.astype(jnp.float32).reshape(total_rows, 1)

    def attend(query_part, key_heads, value_heads):
        scores = jnp.einsum('sqhd,skhd->shqk', query_part, key_heads, precision=lax.Precision.HIGHEST)
        scores = low_back(scores)
        scores = jnp.where(allowed[:, None, None, :], scores, -1e+30)
        probabilities = jax.nn.softmax(scores, axis=-1)
        return jnp.einsum('shqk,skhd->sqhd', low(probabilities), value_heads, precision=lax.Precision.HIGHEST)
    guarded = jax.checkpoint(attend)

    def forward(inputs, weight_qkv, weight_out, weight_fc, weight_proj, bias_fc, gain_rows, bias_rows):
        first_in = low(layer_norm(inputs, gain_rows[0], bias_rows[0]))
        projected = product(first_in, weight_qkv)
        queries = low_back(low((projected[:, :D] + bias_rows[1]) * HEAD_DIM ** (-0.5)))
        keys_all = low_back(low(projected[:, D:2 * D]))
        values_all = low_back(low(projected[:, 2 * D:] + bias_rows[2]))
        key_heads = keys_all.reshape(SEQS, SLOT_LEN, HEADS, HEAD_DIM)
        value_heads = values_all.reshape(SEQS, SLOT_LEN, HEADS, HEAD_DIM)
        query_blocks = queries.reshape(SEQS, SLOT_LEN // query_rows, query_rows, HEADS, HEAD_DIM).transpose(1, 0, 2, 3, 4)

        def one_block(query_part):
            return guarded(query_part, key_heads, value_heads)
        outputs = lax.map(one_block, query_blocks)
        mixed_rows = outputs.transpose(1, 0, 2, 3, 4).reshape(total_rows, D)
        mixed_rows = low_back(low(mixed_rows))
        branch = low_back(product(mixed_rows, weight_out) + bias_rows[3])
        middle = inputs + branch
        second_in = low(layer_norm(middle, gain_rows[1], bias_rows[4]))
        hidden = low_back(product(second_in, weight_fc) + bias_fc)
        activated = low(hidden * jax.nn.sigmoid(1.702 * hidden))
        feed_out = low_back(product(activated, weight_proj) + bias_rows[5])
        final_rows = middle + feed_out
        return (final_rows * keep_rows, (branch, feed_out, final_rows))
    primals = (layer_input.reshape(total_rows, D).astype(jnp.float32), w_qkv.astype(jnp.float32), w_out.astype(jnp.float32), w_fc.astype(jnp.float32), w_proj.astype(jnp.float32), b_fc.astype(jnp.float32), norm_gains.astype(jnp.float32), biases.astype(jnp.float32))
    output, pullback, extras = jax.vjp(forward, *primals, has_aux=True)
    gradients = pullback(grad_out.reshape(total_rows, D).astype(jnp.float32))
    valid_count = jnp.sum(lengths).astype(jnp.float32) * D
    watched = (primals[0],) + tuple(extras)
    root_means = jnp.stack([jnp.sqrt(jnp.sum(keep_rows * watched_entry * watched_entry) / valid_count) for watched_entry in watched])
    return (output.reshape(layer_input.shape).astype(jnp.bfloat16), gradients[0].reshape(layer_input.shape), gradients[1], gradients[2], gradients[3], gradients[4], gradients[5], gradients[6], gradients[7], root_means)
```

```python
import functools

import jax
import jax.numpy as jnp
from jax import lax
from jax.sharding import PartitionSpec as P
from jax.experimental import pallas as pl
from jax.experimental.pallas import tpu as pltpu

HEAD_DIM = 64


masked_score = -1e30
block_keys = 512
quick_slope = 1.702
epsilon = 1e-05


def layer_norm_parts(inputs):
    centre = inputs - jnp.mean(inputs, axis=-1, keepdims=True)
    inverse = lax.rsqrt(jnp.mean(centre * centre, axis=-1, keepdims=True) + epsilon)
    return (centre * inverse, inverse)


def norm_backward(grad_normed, normed, inverse):
    return inverse * (
        grad_normed
        - jnp.mean(grad_normed, axis=-1, keepdims=True)
        - normed * jnp.mean(grad_normed * normed, axis=-1, keepdims=True)
    )


def split_heads(piece_block):
    return piece_block.reshape(
        piece_block.shape[0], piece_block.shape[1], piece_block.shape[2] // HEAD_DIM, HEAD_DIM
    )


def head_scores(left_side, right_side):
    return jnp.einsum("sqhd,skhd->shqk", left_side, right_side, preferred_element_type=jnp.float32)


def weighted(probabilities, right_side):
    return jnp.einsum(
        "shqk,skhd->sqhd", probabilities, right_side, preferred_element_type=jnp.float32
    )


def transposed(probabilities, right_side):
    return jnp.einsum(
        "shqk,sqhd->skhd", probabilities, right_side, preferred_element_type=jnp.float32
    )


def over_blocks(step_fn, running, pieces):
    extent = pieces[0].shape[1]
    number = extent // block_keys
    parted = tuple(
        (
            piece_part.reshape(
                (piece_part.shape[0], number, block_keys) + piece_part.shape[2:]
            ).swapaxes(0, 1)
            for piece_part in pieces
        )
    )

    def advance(inner_run, element):
        position, blocks = element
        return (step_fn(inner_run, blocks, position * block_keys), None)

    return lax.scan(advance, running, (jnp.arange(number, dtype=jnp.int32), parted))[0]


def spread_layer(layer_input, grad_out, lengths, w_qkv, w_out, w_fc, w_proj, b_fc, norm_gains, biases):
    sequences = layer_input.shape[0]
    slice_len = layer_input.shape[2]
    model_width = layer_input.shape[3]
    head_ways = lax.axis_size("head")
    group_len = slice_len * head_ways
    local_width = model_width // head_ways
    head_count = local_width // HEAD_DIM
    head_place = lax.axis_index("head")
    cycle_place = lax.axis_index("seq")
    flat_rows = sequences * slice_len
    full_qkv, full_out, full_fc, full_proj, full_bias_fc, full_gains, full_biases = (
        lax.all_gather(w_qkv, ("head", "seq"), axis=0, tiled=True),
        lax.all_gather(w_out, ("head", "seq"), axis=0, tiled=True),
        lax.all_gather(w_fc, ("head", "seq"), axis=0, tiled=True),
        lax.all_gather(w_proj, ("head", "seq"), axis=0, tiled=True),
        lax.all_gather(b_fc, ("head", "seq"), axis=0, tiled=True),
        lax.all_gather(norm_gains, ("head", "seq"), axis=1, tiled=True),
        lax.all_gather(biases, ("head", "seq"), axis=1, tiled=True),
    )
    gain_vals = full_gains.astype(jnp.float32)
    shift_vals = full_biases.astype(jnp.float32)
    bias_up = full_bias_fc.astype(jnp.float32)
    token_places = (
        cycle_place * group_len + head_place * slice_len + jnp.arange(slice_len, dtype=jnp.int32)
    )
    token_keep = (
        (token_places[None, :] < lengths[:, None]).astype(jnp.float32).reshape(flat_rows, 1)
    )
    own_places = cycle_place * group_len + jnp.arange(group_len, dtype=jnp.int32)
    own_allowed = (own_places[None, :] < lengths[:, None])[:, None, None, :]

    def allowed_at(offset, extent):
        places = offset + jnp.arange(extent, dtype=jnp.int32)
        return (places[None, :] < lengths[:, None])[:, None, None, :]

    inputs = layer_input.reshape(flat_rows, model_width).astype(jnp.float32)
    normed_one, inverse_one = layer_norm_parts(inputs)
    first_in = (normed_one * gain_vals[0] + shift_vals[0]).astype(jnp.bfloat16)
    projected = jnp.dot(first_in, full_qkv, preferred_element_type=jnp.float32)
    query_scale = HEAD_DIM ** (-0.5)
    queries = ((projected[:, :model_width] + shift_vals[1]) * query_scale).astype(jnp.bfloat16)
    keys_new = projected[:, model_width : 2 * model_width].astype(jnp.bfloat16)
    values_new = (projected[:, 2 * model_width :] + shift_vals[2]).astype(jnp.bfloat16)
    packed = jnp.stack([queries, keys_new, values_new], axis=1).reshape(
        sequences, slice_len, 3, head_ways, local_width
    )
    spread = lax.all_to_all(packed, "head", split_axis=3, concat_axis=1, tiled=True)
    query_block = spread[:, :, 0, 0]
    key_block = spread[:, :, 1, 0]
    value_block = spread[:, :, 2, 0]
    query_heads = split_heads(query_block)
    key_heads = split_heads(key_block)
    value_heads = split_heads(value_block)

    def maxima_step(running, pieces, offset):
        highest, denominator = running
        scores = head_scores(query_heads, split_heads(pieces[0]))
        allowed = allowed_at(offset, pieces[0].shape[1])
        scores = jnp.where(allowed, scores, masked_score)
        raised = jnp.maximum(highest, jnp.max(scores, axis=-1))
        weights = jnp.where(allowed, jnp.exp(scores - raised[..., None]), 0.0)
        denominator = denominator * jnp.exp(highest - raised) + jnp.sum(weights, axis=-1)
        return (raised, denominator)

    zero_rows = jnp.zeros((sequences, head_count, group_len), jnp.float32)
    highest, denominator = over_blocks(
        maxima_step,
        (zero_rows + masked_score, zero_rows),
        (lax.all_gather(key_block, "seq", axis=1, tiled=True),),
    )
    log_total = highest + jnp.log(denominator)

    def attention_weights(key_piece, offset):
        scores = head_scores(query_heads, key_piece)
        allowed = allowed_at(offset, key_piece.shape[1])
        return jnp.where(
            allowed, jnp.exp(jnp.where(allowed, scores, masked_score) - log_total[..., None]), 0.0
        )

    zero_heads = jnp.zeros((sequences, group_len, head_count, HEAD_DIM), jnp.float32)

    def output_step(running, pieces, offset):
        probabilities = attention_weights(split_heads(pieces[0]), offset)
        return running + weighted(probabilities.astype(jnp.bfloat16), split_heads(pieces[1]))

    attended = over_blocks(
        output_step,
        zero_heads,
        (
            lax.all_gather(key_block, "seq", axis=1, tiled=True),
            lax.all_gather(value_block, "seq", axis=1, tiled=True),
        ),
    )
    mixed_heads = attended.astype(jnp.bfloat16).reshape(
        sequences, head_ways, slice_len, local_width
    )
    gathered_out = lax.all_to_all(mixed_heads, "head", split_axis=1, concat_axis=3, tiled=True)
    mixed_rows = gathered_out.reshape(flat_rows, model_width)
    branch = jnp.dot(mixed_rows, full_out, preferred_element_type=jnp.float32) + shift_vals[3]
    middle = inputs + branch
    normed_two, inverse_two = layer_norm_parts(middle)
    second_in = (normed_two * gain_vals[1] + shift_vals[4]).astype(jnp.bfloat16)
    hidden = jnp.dot(second_in, full_fc, preferred_element_type=jnp.float32) + bias_up
    gate_sig = jax.nn.sigmoid(quick_slope * hidden)
    activated = (hidden * gate_sig).astype(jnp.bfloat16)
    feed_out = jnp.dot(activated, full_proj, preferred_element_type=jnp.float32) + shift_vals[5]
    final_rows = middle + feed_out
    result = (final_rows * token_keep).astype(jnp.bfloat16).reshape(layer_input.shape)
    local_squares = jnp.stack(
        [
            jnp.sum(token_keep * inputs * inputs),
            jnp.sum(token_keep * branch * branch),
            jnp.sum(token_keep * feed_out * feed_out),
            jnp.sum(token_keep * final_rows * final_rows),
        ]
    )
    squares = lax.psum(local_squares, ("head", "seq"))
    valid_count = jnp.sum(lengths).astype(jnp.float32) * model_width
    root_means = jnp.sqrt(squares / valid_count)
    grad_final = grad_out.reshape(flat_rows, model_width).astype(jnp.float32) * token_keep
    grad_feed = grad_final.astype(jnp.bfloat16)
    grad_proj = jnp.dot(activated.T, grad_feed, preferred_element_type=jnp.float32)
    grad_shift_proj = jnp.sum(grad_feed.astype(jnp.float32), axis=0)
    grad_act = jnp.dot(grad_feed, full_proj.T, preferred_element_type=jnp.float32)
    grad_hidden = (
        grad_act * (gate_sig + quick_slope * hidden * gate_sig * (1.0 - gate_sig))
    ).astype(jnp.bfloat16)
    grad_fc = jnp.dot(second_in.T, grad_hidden, preferred_element_type=jnp.float32)
    grad_bias_up = jnp.sum(grad_hidden.astype(jnp.float32), axis=0)
    grad_second = jnp.dot(grad_hidden, full_fc.T, preferred_element_type=jnp.float32)
    grad_gain_two = jnp.sum(grad_second * normed_two, axis=0)
    grad_shift_two = jnp.sum(grad_second, axis=0)
    grad_middle = grad_final + norm_backward(grad_second * gain_vals[1], normed_two, inverse_two)
    grad_branch = grad_middle.astype(jnp.bfloat16)
    grad_out_weight = jnp.dot(mixed_rows.T, grad_branch, preferred_element_type=jnp.float32)
    grad_shift_out = jnp.sum(grad_branch.astype(jnp.float32), axis=0)
    grad_mixed = jnp.dot(grad_branch, full_out.T, preferred_element_type=jnp.float32).astype(
        jnp.bfloat16
    )
    grad_spread = lax.all_to_all(
        grad_mixed.reshape(sequences, slice_len, head_ways, local_width),
        "head",
        split_axis=2,
        concat_axis=1,
        tiled=True,
    )
    grad_block = grad_spread[:, :, 0]
    grad_heads = split_heads(grad_block)

    def delta_step(running, pieces, offset):
        probabilities = attention_weights(split_heads(pieces[0]), offset)
        grad_probs = head_scores(grad_heads, split_heads(pieces[1]))
        return running + jnp.sum(probabilities * grad_probs, axis=-1)

    row_delta = over_blocks(
        delta_step,
        zero_rows,
        (
            lax.all_gather(key_block, "seq", axis=1, tiled=True),
            lax.all_gather(value_block, "seq", axis=1, tiled=True),
        ),
    )

    def query_step(running, pieces, offset):
        key_piece = split_heads(pieces[0])
        probabilities = attention_weights(key_piece, offset)
        grad_probs = head_scores(grad_heads, split_heads(pieces[1]))
        slopes = (probabilities * (grad_probs - row_delta[..., None])).astype(jnp.bfloat16)
        return running + weighted(slopes, key_piece)

    grad_query = over_blocks(
        query_step,
        zero_heads,
        (
            lax.all_gather(key_block, "seq", axis=1, tiled=True),
            lax.all_gather(value_block, "seq", axis=1, tiled=True),
        ),
    )
    all_logs, all_deltas = (
        lax.all_gather(log_total.transpose(0, 2, 1), "seq", axis=1, tiled=True),
        lax.all_gather(row_delta.transpose(0, 2, 1), "seq", axis=1, tiled=True),
    )

    def key_step(running, pieces, offset):
        query_piece = split_heads(pieces[0])
        grad_piece = split_heads(pieces[1])
        extent = pieces[0].shape[1]
        log_piece = lax.dynamic_slice_in_dim(all_logs, offset, extent, 1).transpose(0, 2, 1)
        delta_piece = lax.dynamic_slice_in_dim(all_deltas, offset, extent, 1).transpose(0, 2, 1)
        scores = head_scores(query_piece, key_heads)
        probabilities = jnp.where(
            own_allowed,
            jnp.exp(jnp.where(own_allowed, scores, masked_score) - log_piece[..., None]),
            0.0,
        )
        grad_value = running[1] + transposed(probabilities.astype(jnp.bfloat16), grad_piece)
        grad_probs = head_scores(grad_piece, value_heads)
        slopes = (probabilities * (grad_probs - delta_piece[..., None])).astype(jnp.bfloat16)
        grad_key = running[0] + transposed(slopes, query_piece)
        return (grad_key, grad_value)

    grad_key, grad_value = over_blocks(
        key_step,
        (zero_heads, zero_heads),
        (
            lax.all_gather(query_block, "seq", axis=1, tiled=True),
            lax.all_gather(grad_block, "seq", axis=1, tiled=True),
        ),
    )
    stacked = jnp.stack([grad_query, grad_key, grad_value], axis=2).astype(jnp.bfloat16)
    stacked = stacked.reshape(sequences, head_ways, slice_len, 3, local_width)
    returned = lax.all_to_all(stacked, "head", split_axis=1, concat_axis=4, tiled=True)
    column_scale = jnp.concatenate(
        [
            jnp.full((model_width,), query_scale, jnp.float32),
            jnp.ones((2 * model_width,), jnp.float32),
        ]
    )
    grad_projected = returned.reshape(flat_rows, 3 * model_width).astype(jnp.float32) * column_scale
    grad_shift_query = jnp.sum(grad_projected[:, :model_width], axis=0)
    grad_shift_value = jnp.sum(grad_projected[:, 2 * model_width :], axis=0)
    grad_projected_low = grad_projected.astype(jnp.bfloat16)
    grad_qkv = jnp.dot(first_in.T, grad_projected_low, preferred_element_type=jnp.float32)
    grad_first = jnp.dot(grad_projected_low, full_qkv.T, preferred_element_type=jnp.float32)
    grad_gain_one = jnp.sum(grad_first * normed_one, axis=0)
    grad_shift_one = jnp.sum(grad_first, axis=0)
    grad_inputs = grad_middle + norm_backward(grad_first * gain_vals[0], normed_one, inverse_one)
    grad_gain_rows = jnp.stack([grad_gain_one, grad_gain_two])
    grad_shift_rows = jnp.stack(
        [
            grad_shift_one,
            grad_shift_query,
            grad_shift_value,
            grad_shift_out,
            grad_shift_two,
            grad_shift_proj,
        ]
    )
    owned_grads = (
        lax.psum_scatter(grad_qkv, ("head", "seq"), scatter_dimension=0, tiled=True),
        lax.psum_scatter(grad_out_weight, ("head", "seq"), scatter_dimension=0, tiled=True),
        lax.psum_scatter(grad_fc, ("head", "seq"), scatter_dimension=0, tiled=True),
        lax.psum_scatter(grad_proj, ("head", "seq"), scatter_dimension=0, tiled=True),
        lax.psum_scatter(grad_bias_up, ("head", "seq"), scatter_dimension=0, tiled=True),
        lax.psum_scatter(grad_gain_rows, ("head", "seq"), scatter_dimension=1, tiled=True),
        lax.psum_scatter(grad_shift_rows, ("head", "seq"), scatter_dimension=1, tiled=True),
    )
    return (
        result,
        grad_inputs.reshape(layer_input.shape),
        owned_grads[0],
        owned_grads[1],
        owned_grads[2],
        owned_grads[3],
        owned_grads[4],
        owned_grads[5],
        owned_grads[6],
        root_means,
    )


f32 = jnp.float32
bf16 = jnp.bfloat16


def nn(left, right):
    return lax.dot_general(left, right, (((1,), (0,)), ((), ())), preferred_element_type=f32)


def nt(left, right):
    return lax.dot_general(left, right, (((1,), (1,)), ((), ())), preferred_element_type=f32)


def loop(low, high, step_fn):
    def advance(index, carry):
        step_fn(index)
        return carry

    lax.fori_loop(low, high, advance, 0)


def norm_parts(v):
    centre = v - jnp.mean(v, axis=-1, keepdims=True)
    inverse = lax.rsqrt(jnp.mean(centre * centre, axis=-1, keepdims=True) + epsilon)
    return centre * inverse, inverse


class Exchange:
    def __init__(self, n, me, place, src, dst, send_sem, recv_sem):
        self.n, self.me, self.place, self.src, self.dst = n, me, place, src, dst
        self.send_sem, self.recv_sem = send_sem, recv_sem

    def out(self, q):
        return pltpu.make_async_remote_copy(
            src_ref=self.src(q),
            dst_ref=self.dst(self.me),
            send_sem=self.send_sem,
            recv_sem=self.recv_sem.at[self.me],
            device_id=self.place(q),
            device_id_type=pl.DeviceIdType.MESH,
        )

    def into(self, q):
        return pltpu.make_async_remote_copy(
            src_ref=self.dst(q),
            dst_ref=self.dst(q),
            send_sem=self.send_sem,
            recv_sem=self.recv_sem.at[q],
            device_id=self.place(q),
            device_id_type=pl.DeviceIdType.MESH,
        )

    def peer(self, k):
        return lax.rem(self.me + k, self.n)

    def send(self):
        loop(1, self.n, lambda k: self.out(self.peer(k)).start())

    def wait(self):
        loop(1, self.n, lambda k: self.into(self.peer(k)).wait_recv())

    def drain(self):
        loop(1, self.n, lambda k: self.out(self.peer(k)).wait_send())


def fused_layer(layer_input, grad_out, lengths, w_qkv, w_out, w_fc, w_proj, b_fc, norm_gains, biases):
    seqs, _, sl, width = layer_input.shape
    hs = lax.axis_size("head")
    ss = lax.axis_size("seq")
    zs = ss // seqs
    ps = hs * seqs
    group = sl * hs
    tw = width // zs
    heads = tw // HEAD_DIM
    rows = w_qkv.shape[0]
    ff_rows = w_proj.shape[0]
    part = ff_rows * zs
    home = seqs * sl
    qn = ss * sl
    slab = ps * home
    hidden_width = part * ps
    query_block = 256
    chunk = 16
    pair = 2 * rows
    scale = HEAD_DIM ** (-0.5)

    head_at = lax.axis_index("head")
    seq_at = lax.axis_index("seq")
    z_at = seq_at // seqs
    dev = head_at * ss + seq_at

    lanes = jnp.arange(width, dtype=jnp.int32)
    own = lanes // rows == dev
    small = jnp.concatenate([norm_gains, biases], axis=0).astype(f32)
    spread = jnp.where(own[None, :], jnp.tile(small, (1, width // rows)), 0.0)
    lane_z = lanes // ff_rows == z_at
    up_row = jnp.where(
        lane_z & (lanes < part), jnp.tile(b_fc.astype(f32), width // ff_rows), 0.0
    )[None, :]
    per_triple = tw // rows
    local = (lanes % tw) // rows == dev % per_triple
    q_part = jnp.where(local & (lanes < tw), jnp.tile(small[3], width // rows), 0.0)
    v_part = jnp.where(
        local & (lanes >= 2 * tw) & (lanes < 3 * tw), jnp.tile(small[4], width // rows), 0.0
    )
    triple_rows = jnp.where(
        (jnp.arange(zs) == dev // per_triple)[:, None], (q_part + v_part)[None, :], 0.0
    )
    params = jnp.concatenate(
        [spread, up_row, triple_rows, jnp.zeros((16 - 9 - zs, width), f32)], axis=0
    )

    qkv_in = w_qkv.reshape(rows, 3, zs, tw).transpose(2, 0, 1, 3).reshape(zs, rows, 3 * tw)
    fc_in = w_fc.reshape(rows, hs, zs, seqs, ff_rows).transpose(1, 3, 0, 2, 4).reshape(ps, rows, part)

    def kernel(
        len_ref, x_ref, go_ref, wqkv_ref, wout_ref, wfc_ref, wproj_ref, prm_ref,
        out_ref, gin_ref, gqkv_ref, gout_ref, gfc_ref, gproj_ref, ar_ref,
        prmg, prm_slab, prms, prm,
        wqg, wog, wfg, wpg, wq, wo, wf,
        xg, fi, q_s, ktg, vtg, kneg, probs, s_scr, pb_scr, ds_scr, o_s, o_st, og, mixt,
        branch_s, middle_s, gm_s,
        x2g, gog, act, gh, x2t, actt, gs_st, gsg, fd_st, fdg,
        do_st, dog, dot_s, qt_s, dq_s, dkt, dvt, dk_st, dv_st, dkg, dvg, gpt, gp,
        gf_st, gfg, wos, wor, woz, wozr, wqs, wqr, wqz, wqzr, wfs, wfr, wfz, wfzr, wps, wpr,
        arg, arz,
        send, zsem, psem, lsem, hsem,
    ):
        h = lax.axis_index("head")
        s = lax.axis_index("seq")
        z = s // seqs
        y = lax.rem(s, seqs)
        p = h * seqs + y

        def slab_place(q):
            return (q // seqs, z * seqs + lax.rem(q, seqs))

        def line_place(q):
            return (h, q)

        def z_place(q):
            return (h, q * seqs + y)

        def h_place(q):
            return (q, s)

        counts = {"z": 0, "p": 0, "l": 0, "h": 0, "all": 0}
        kinds = {
            "z": (zs, z, z_place, zsem),
            "p": (ps, p, slab_place, psem),
            "l": (ss, s, line_place, lsem),
            "h": (hs, h, h_place, hsem),
        }

        def exchange(kind, src, dst):
            n, me, place, sems = kinds[kind]
            number = counts[kind]
            counts[kind] += 1
            total = counts["all"]
            counts["all"] += 1
            return Exchange(n, me, place, src, dst, send.at[total], sems.at[number])

        ex_prm_z = exchange("z", lambda q: prm_ref, lambda q: prmg.at[q])
        ex_wq_z = exchange("z", lambda q: wqkv_ref.at[q], lambda q: wqg.at[p, q])
        ex_wo_z = exchange("z", lambda q: wout_ref, lambda q: wog.at[p, q])
        ex_x = exchange("l", lambda q: x_ref.at[lax.rem(q, seqs)], lambda q: xg.at[q])
        ex_prm_p = exchange("p", lambda q: prms, lambda q: prm_slab.at[q])
        ex_wq_p = exchange("p", lambda q: wqg.at[p], lambda q: wqg.at[q])
        ex_wo_p = exchange("p", lambda q: wog.at[p], lambda q: wog.at[q])
        ex_wf_p = exchange("p", lambda q: wfc_ref.at[q], lambda q: wfg.at[z, q])
        ex_wf_z = exchange("z", lambda q: wfg.at[z], lambda q: wfg.at[q])
        ex_wp_z = exchange("z", lambda q: wproj_ref, lambda q: wpg.at[q])
        ex_go = exchange("p", lambda q: gog.at[p], lambda q: gog.at[q])
        ex_k = exchange("h", lambda q: ktg.at[h], lambda q: ktg.at[q])
        ex_v = exchange("h", lambda q: vtg.at[h], lambda q: vtg.at[q])
        ex_o = exchange("l", lambda q: o_st.at[q], lambda q: og.at[lax.rem(q, seqs), q // seqs])
        ex_x2 = exchange("p", lambda q: x2g.at[p], lambda q: x2g.at[q])
        ex_gs = exchange("p", lambda q: gs_st.at[q], lambda q: gsg.at[q])
        ex_fd = exchange("p", lambda q: fd_st.at[q], lambda q: fdg.at[q])
        ex_do = exchange(
            "l", lambda q: do_st.at[q // seqs, lax.rem(q, seqs)], lambda q: dog.at[q]
        )
        ex_dk = exchange("h", lambda q: dk_st.at[q], lambda q: dkg.at[q])
        ex_dv = exchange("h", lambda q: dv_st.at[q], lambda q: dvg.at[q])
        ex_gf = exchange("l", lambda q: gf_st.at[q], lambda q: gfg.at[lax.rem(q, seqs), q // seqs])
        ex_go_w = exchange("p", lambda q: wos.at[q], lambda q: wor.at[q])
        ex_go_z = exchange("z", lambda q: woz.at[q], lambda q: wozr.at[q])
        ex_gq_w = exchange("p", lambda q: wqs.at[q], lambda q: wqr.at[q])
        ex_gq_z = exchange("z", lambda q: wqz.at[q], lambda q: wqzr.at[q])
        ex_gfc_z = exchange("z", lambda q: wfs.at[q], lambda q: wfr.at[q])
        ex_gfc_p = exchange("p", lambda q: wfz.at[q], lambda q: wfzr.at[q])
        ex_gp_z = exchange("z", lambda q: wps.at[q], lambda q: wpr.at[q])
        ex_ar_p = exchange("p", lambda q: arg.at[p], lambda q: arg.at[q])
        ex_ar_z = exchange("z", lambda q: arz.at[z], lambda q: arz.at[q])

        barrier = pltpu.get_barrier_semaphore()

        def greet(place, me, n):
            def one(k):
                pl.semaphore_signal(
                    barrier, inc=1, device_id=place(lax.rem(me + k, n)),
                    device_id_type=pl.DeviceIdType.MESH,
                )

            loop(1, n, one)

        greet(slab_place, p, ps)
        greet(line_place, s, ss)
        pl.semaphore_wait(barrier, ps - 1 + ss - 1)

        ex_prm_z.send()
        ex_wq_z.send()
        ex_x.send()

        len_0 = len_ref[0]
        len_1 = len_ref[1]
        len_y = jnp.where(y == 0, len_0, len_1)

        prmg[z] = prm_ref[...]
        wqg[p, z] = wqkv_ref[z]
        wog[p, z] = wout_ref[...]
        wfg[z, p] = wfc_ref[p]
        wpg[z] = wproj_ref[...]
        xg[s] = x_ref[y]
        home_row = lax.broadcasted_iota(jnp.int32, (home, 1), 0)
        home_place = s * group + h * sl + lax.rem(home_row, sl)
        keep = jnp.where(home_place < jnp.where(home_row < sl, len_0, len_1), 1.0, 0.0)
        gfin = go_ref[...].reshape(home, width).astype(f32) * keep
        gog[p] = gfin.astype(bf16)

        def mask_block(q):
            column = lax.broadcasted_iota(jnp.int32, (chunk, qn), 1)
            place = (column // sl) * group + q * sl + lax.rem(column, sl)
            kneg[q] = jnp.where(place < len_y, 0.0, masked_score)

        loop(0, hs, mask_block)

        ex_wq_z.wait()
        ex_wq_p.send()
        ex_prm_z.wait()
        summed = jnp.sum(prmg[...], axis=0)
        prms[...] = summed
        prm_slab[p] = summed
        ex_prm_p.send()
        ex_wo_z.send()

        ex_wq_p.wait()

        def assemble(src, dst):
            def one(i):
                a = src(i // zs * seqs, lax.rem(i, zs)).astype(f32)
                b = src(i // zs * seqs + 1, lax.rem(i, zs)).astype(f32)
                dst[pl.ds(pl.multiple_of(i * pair, pair), pair), :] = jnp.concatenate(
                    [a, b], axis=0
                ).astype(bf16)

            loop(0, width // pair, one)

        assemble(lambda a, b: wqg[a, b], wq)
        ex_prm_p.wait()
        prm[...] = jnp.sum(prm_slab[...], axis=0)

        ex_x.wait()

        def project(i):
            xv = xg[pl.ds(2 * i, 2)].reshape(2 * sl, width).astype(f32)
            normed, _ = norm_parts(xv)
            first = (normed * prm[0:1, :] + prm[2:3, :]).astype(bf16)
            at = pl.ds(pl.multiple_of(i * 2 * sl, 2 * sl), 2 * sl)
            fi[at, :] = first
            projected = nn(first, wq[...]) + prm[pl.ds(9 + z, 1), 0 : 3 * tw]
            q_s[at, :] = (projected[:, 0:tw] * scale).astype(bf16)
            turned = projected[:, tw:].T.astype(bf16)
            ktg[h, :, at] = turned[0:tw, :]
            vtg[h, :, at] = turned[tw : 2 * tw, :]

        loop(0, ss // 2, project)
        ex_k.send()
        ex_v.send()
        ex_wo_z.wait()
        ex_go.send()
        ex_wo_p.send()
        ex_wf_p.send()
        ex_wp_z.send()
        ex_wf_p.wait()
        ex_wf_z.send()

        lane_head = lax.broadcasted_iota(jnp.int32, (query_block, tw), 1) // HEAD_DIM
        blocks = qn // query_block

        ex_k.wait()
        ex_v.wait()

        def attend(i):
            at = pl.ds(pl.multiple_of(i * query_block, query_block), query_block)
            queries = q_s[at, :]
            total = jnp.zeros((query_block, tw), f32)
            for n in range(heads):
                masked = jnp.where(lane_head == n, queries, jnp.zeros_like(queries))
                for b in range(hs):
                    s_scr[:, b * qn : (b + 1) * qn] = nn(masked, ktg[b])

                def soft(r):
                    rat = pl.ds(pl.multiple_of(r * chunk, chunk), chunk)
                    sv = [s_scr[rat, b * qn : (b + 1) * qn] + kneg[b] for b in range(hs)]
                    top = jnp.max(functools.reduce(jnp.maximum, sv), axis=-1, keepdims=True)
                    ev = [jnp.exp(v - top) for v in sv]
                    inv = 1.0 / jnp.sum(functools.reduce(jnp.add, ev), axis=-1, keepdims=True)
                    for b in range(hs):
                        value = ev[b] * inv
                        probs[n, i, rat, b * qn : (b + 1) * qn] = value
                        pb_scr[rat, b * qn : (b + 1) * qn] = value.astype(bf16)

                loop(0, query_block // chunk, soft)
                head_out = nt(pb_scr[:, 0:qn], vtg[0])
                for b in range(1, hs):
                    head_out = head_out + nt(pb_scr[:, b * qn : (b + 1) * qn], vtg[b])
                total = jnp.where(lane_head == n, head_out, total)
            o_s[at, :] = total.astype(bf16)

        loop(0, blocks, attend)

        def lay_out(q):
            o_st[q] = o_s[pl.ds(pl.multiple_of(q * sl, sl), sl), :]

        loop(0, ss, lay_out)
        ex_o.send()
        og[y, z] = o_st[s]

        ex_wo_p.wait()
        assemble(lambda a, b: wog[a, b], wo)
        ex_wp_z.wait()
        ex_wf_z.wait()
        assemble(lambda a, b: wfg[b, a], wf)
        ex_o.wait()
        branch = jnp.broadcast_to(prm[5:6, :], (home, width))
        for t in range(zs):
            mixed = og[:, t].reshape(home, tw)
            branch = branch + nn(mixed, wo[t * tw : (t + 1) * tw, :])
            mixt[t * tw : (t + 1) * tw, :] = mixed.T
        middle = x_ref[...].reshape(home, width).astype(f32) + branch
        branch_s[...] = branch
        middle_s[...] = middle
        normed, _ = norm_parts(middle)
        x2g[p] = (normed * prm[1:2, :] + prm[6:7, :]).astype(bf16)
        ex_x2.send()
        ex_go.wait()

        up_bias = jnp.sum(prmg[...], axis=0)[8:9, 0:part]

        def feed(k, running):
            q = lax.rem(p + k, ps)

            @pl.when(k > 0)
            def _():
                ex_x2.into(q).wait_recv()

            at = pl.ds(pl.multiple_of(q * home, home), home)
            hid = nn(x2g[q], wf[...]) + up_bias
            gate = 1.0 / (1.0 + jnp.exp(-quick_slope * hid))
            act[at, :] = (hid * gate).astype(bf16)
            flow = nt(gog[q], wpg[...].reshape(part, width))
            slope = gate + quick_slope * hid * gate * (1.0 - gate)
            back = (flow * slope).astype(bf16)
            gh[at, :] = back
            gs_st[q] = nt(back, wf[...]).astype(bf16)

            @pl.when(k > 0)
            def _():
                ex_gs.out(q).start()

            return running + jnp.sum(back.astype(f32), axis=0, keepdims=True)

        grad_up = lax.fori_loop(0, ps, feed, jnp.zeros((1, part), f32))

        def feed_down(k):
            q = lax.rem(p + k, ps)
            at = pl.ds(pl.multiple_of(q * home, home), home)
            fd_st[q] = nn(act[at, :], wpg[...].reshape(part, width)).astype(bf16)

            @pl.when(k > 0)
            def _():
                ex_fd.out(q).start()

        gsg[p] = gs_st[p]

        ex_gs.wait()
        grad_second = jnp.sum(gsg[...].astype(f32), axis=0)
        g2 = grad_second * prm[1:2, :]
        n2, r2 = norm_parts(middle_s[...])
        grad_middle = go_ref[...].reshape(home, width).astype(f32) * keep + norm_backward(g2, n2, r2)
        gm_s[...] = grad_middle
        arg[p] = jnp.zeros((16, width), f32)
        arg[p, 1:2, :] = jnp.sum(grad_second * n2, axis=0, keepdims=True)
        arg[p, 6:7, :] = jnp.sum(grad_second, axis=0, keepdims=True)
        grad_branch = grad_middle.astype(bf16)
        arg[p, 5:6, :] = jnp.sum(grad_branch.astype(f32), axis=0, keepdims=True)
        for t in range(zs):
            do_st[t] = nt(grad_branch, wo[t * tw : (t + 1) * tw, :]).astype(bf16).reshape(seqs, sl, tw)
        ex_do.send()
        dog[s] = do_st[z, y]

        loop(0, ps, feed_down)
        fdg[p] = fd_st[p]

        def out_grad(c):
            val = nn(mixt[pl.ds(pl.multiple_of(c * 4 * rows, 4 * rows), 4 * rows), :], grad_branch)
            for j in range(4):
                d = c * 4 + j
                sd = lax.rem(d, ss)
                wos[d // ss * seqs + lax.rem(sd, seqs), sd // seqs] = val[
                    j * rows : (j + 1) * rows, :
                ].astype(bf16)

        loop(0, width // (4 * rows), out_grad)
        ex_go_w.send()
        wor[p] = wos[p]

        def turn(q):
            at = pl.ds(pl.multiple_of(q * home, home), home)
            x2t[:, at] = x2g[q].T
            actt[:, at] = act[at, :].T

        loop(0, ps, turn)

        def fc_grad(c):
            val = nn(x2t[pl.ds(pl.multiple_of(c * 4 * rows, 4 * rows), 4 * rows), :], gh[...])
            for j in range(4):
                d = c * 4 + j
                sd = lax.rem(d, ss)
                wfs[sd // seqs, d // ss * seqs + lax.rem(sd, seqs)] = val[
                    j * rows : (j + 1) * rows, :
                ].astype(bf16)

        loop(0, width // (4 * rows), fc_grad)

        def proj_grad(c):
            val = nn(
                actt[pl.ds(pl.multiple_of(c * ff_rows, ff_rows), ff_rows), :],
                gog[...].reshape(slab, width),
            )
            wps[c] = val.astype(bf16)

        loop(0, zs, proj_grad)
        ex_gfc_z.send()
        ex_gp_z.send()
        wfr[z] = wfs[z]
        wpr[z] = wps[z]

        ex_do.wait()

        def gather_do(i):
            at = pl.ds(pl.multiple_of(i * 2 * sl, 2 * sl), 2 * sl)
            dv = dog[pl.ds(2 * i, 2)].reshape(2 * sl, tw)
            o_s[at, :] = dv
            dot_s[:, at] = dv.T
            qt_s[:, at] = q_s[at, :].T

        loop(0, ss // 2, gather_do)

        def back(n):
            lane_own = lane_head == n
            head_rows = pl.ds(pl.multiple_of(n * HEAD_DIM, HEAD_DIM), HEAD_DIM)
            for i in range(blocks):
                at = pl.ds(i * query_block, query_block)
                outer = o_s[at, :]
                masked = jnp.where(lane_own, outer, jnp.zeros_like(outer))
                for b in range(hs):
                    s_scr[:, b * qn : (b + 1) * qn] = nn(masked, vtg[b])

                def soft(r):
                    rat = pl.ds(pl.multiple_of(r * chunk, chunk), chunk)
                    dp = [s_scr[rat, b * qn : (b + 1) * qn] for b in range(hs)]
                    pv = [probs[n, i, rat, b * qn : (b + 1) * qn] for b in range(hs)]
                    delta = jnp.sum(
                        functools.reduce(jnp.add, [a * c for a, c in zip(dp, pv)]),
                        axis=-1, keepdims=True,
                    )
                    for b in range(hs):
                        ds_scr[rat, b * qn : (b + 1) * qn] = (pv[b] * (dp[b] - delta)).astype(bf16)
                        pb_scr[rat, b * qn : (b + 1) * qn] = pv[b].astype(bf16)

                loop(0, query_block // chunk, soft)
                head_dq = nt(ds_scr[:, 0:qn], ktg[0])
                for b in range(1, hs):
                    head_dq = head_dq + nt(ds_scr[:, b * qn : (b + 1) * qn], ktg[b])
                dq_s[at, :] = jnp.where(lane_own, head_dq.astype(bf16).astype(f32) * scale, dq_s[at, :])
                for b in range(hs):
                    new_k = nn(qt_s[head_rows, at], ds_scr[:, b * qn : (b + 1) * qn])
                    new_v = nn(dot_s[head_rows, at], pb_scr[:, b * qn : (b + 1) * qn])
                    if i:
                        new_k = dkt[b] + new_k
                        new_v = dvt[b] + new_v
                    if i < blocks - 1:
                        dkt[b] = new_k
                        dvt[b] = new_v
                    else:
                        dk_st[b, head_rows, :] = new_k.astype(bf16)
                        dv_st[b, head_rows, :] = new_v.astype(bf16)

        loop(0, heads, back)
        ex_dk.send()
        ex_dv.send()
        dkg[h] = dk_st[h]
        dvg[h] = dv_st[h]

        ex_go_w.wait()
        woz[...] = jnp.sum(wor[...].astype(f32), axis=0)
        ex_go_z.send()
        wozr[z] = woz[z]
        ex_gfc_z.wait()
        wfz[...] = jnp.sum(wfr[...].astype(f32), axis=0)
        ex_gfc_p.send()
        wfzr[p] = wfz[p]
        ex_gp_z.wait()
        gproj_ref[...] = jnp.sum(wpr[...].astype(f32), axis=0)
        x2t[:, 0:qn] = fi[...].T
        ex_fd.wait()
        feed_out = jnp.sum(fdg[...].astype(f32), axis=0) + prm[7:8, :]
        final = middle_s[...] + feed_out
        out_ref[...] = (final * keep).astype(bf16).reshape(seqs, sl, width)
        xv = x_ref[...].reshape(home, width).astype(f32)
        br = branch_s[...]
        for row, value in ((3, xv), (4, br), (13, feed_out), (14, final)):
            arg[p, row : row + 1, :] = jnp.sum(keep * value * value, axis=0, keepdims=True)
        arg[p, 7:8, :] = jnp.sum(gog[p].astype(f32), axis=0, keepdims=True)

        ex_dk.wait()
        ex_dv.wait()
        gpt[0:tw, :] = dq_s[...].T.astype(bf16)
        gpt[tw : 2 * tw, :] = jnp.sum(dkg[...].astype(f32), axis=0).astype(bf16)
        gpt[2 * tw : 3 * tw, :] = jnp.sum(dvg[...].astype(f32), axis=0).astype(bf16)
        gp[...] = gpt[...].T

        def first_grad(q):
            gf_st[q] = nt(gp[pl.ds(pl.multiple_of(q * sl, sl), sl), :], wq[...]).astype(bf16)

        loop(0, ss, first_grad)
        ex_gf.send()
        gfg[y, z] = gf_st[s]
        arg[p, pl.ds(9 + z, 1), 0 : 3 * tw] = jnp.sum(gp[...].astype(f32), axis=0, keepdims=True)

        def qkv_grad(c):
            val = nn(x2t[pl.ds(pl.multiple_of(c * 4 * rows, 4 * rows), 4 * rows), 0:qn], gp[...])
            for j in range(4):
                d = c * 4 + j
                sd = lax.rem(d, ss)
                wqs[d // ss * seqs + lax.rem(sd, seqs), sd // seqs] = val[
                    j * rows : (j + 1) * rows, :
                ].astype(bf16)

        loop(0, width // (4 * rows), qkv_grad)
        ex_gq_w.send()
        wqr[p] = wqs[p]

        ex_gf.wait()
        grad_first = jnp.sum(gfg[...].astype(f32), axis=1).reshape(home, width)
        n1, r1 = norm_parts(x_ref[...].reshape(home, width).astype(f32))
        grad_in = gm_s[...] + norm_backward(grad_first * prm[0:1, :], n1, r1)
        gin_ref[...] = grad_in.reshape(seqs, sl, width)
        arg[p, 0:1, :] = jnp.sum(grad_first * n1, axis=0, keepdims=True)
        arg[p, 2:3, :] = jnp.sum(grad_first, axis=0, keepdims=True)
        ex_ar_p.send()

        ex_gq_w.wait()
        wqz[...] = jnp.sum(wqr[...].astype(f32), axis=0)
        ex_gq_z.send()
        wqzr[z] = wqz[z]

        ex_ar_p.wait()
        arz[z] = jnp.sum(arg[...], axis=0)
        arz[z, 8:9, 0:part] = grad_up
        ex_ar_z.send()

        ex_go_z.wait()
        gout_ref[...] = jnp.sum(wozr[...], axis=0)
        ex_gfc_p.wait()
        gfc_ref[...] = wfzr[...]
        ex_gq_z.wait()
        gqkv_ref[...] = wqzr[...]
        ex_ar_z.wait()
        ar_ref[...] = jnp.sum(arz[...], axis=0)

        for ex in (
            ex_prm_z, ex_wq_z, ex_wo_z, ex_x, ex_prm_p, ex_wq_p, ex_wo_p, ex_wf_p, ex_wf_z,
            ex_wp_z, ex_go, ex_k, ex_v, ex_o, ex_x2, ex_gs, ex_fd, ex_do, ex_dk, ex_dv, ex_gf,
            ex_go_w, ex_go_z, ex_gq_w, ex_gq_z, ex_gfc_z, ex_gfc_p, ex_gp_z, ex_ar_p, ex_ar_z,
        ):
            ex.drain()

    vm = pltpu.VMEM
    names = [
        ("prmg", vm((zs, 16, width), f32)),
        ("prm_slab", vm((ps, 16, width), f32)),
        ("prms", vm((16, width), f32)),
        ("prm", vm((16, width), f32)),
        ("wqg", vm((ps, zs, rows, 3 * tw), bf16)),
        ("wog", vm((ps, zs, rows, width), bf16)),
        ("wfg", vm((zs, ps, rows, part), bf16)),
        ("wpg", vm((zs, ff_rows, width), bf16)),
        ("wq", vm((width, 3 * tw), bf16)),
        ("wo", vm((width, width), bf16)),
        ("wf", vm((width, part), bf16)),
        ("xg", vm((ss, sl, width), bf16)),
        ("fi", vm((qn, width), bf16)),
        ("q_s", vm((qn, tw), bf16)),
        ("ktg", vm((hs, tw, qn), bf16)),
        ("vtg", vm((hs, tw, qn), bf16)),
        ("kneg", vm((hs, chunk, qn), f32)),
        ("probs", vm((heads, qn // query_block, query_block, hs * qn), f32)),
        ("s_scr", vm((query_block, hs * qn), f32)),
        ("pb_scr", vm((query_block, hs * qn), bf16)),
        ("ds_scr", vm((query_block, hs * qn), bf16)),
        ("o_s", vm((qn, tw), bf16)),
        ("o_st", vm((ss, sl, tw), bf16)),
        ("og", vm((seqs, zs, sl, tw), bf16)),
        ("mixt", vm((width, home), bf16)),
        ("branch_s", vm((home, width), f32)),
        ("middle_s", vm((home, width), f32)),
        ("gm_s", vm((home, width), f32)),
        ("x2g", vm((ps, home, width), bf16)),
        ("gog", vm((ps, home, width), bf16)),
        ("act", vm((slab, part), bf16)),
        ("gh", vm((slab, part), bf16)),
        ("x2t", vm((width, slab), bf16)),
        ("actt", vm((part, slab), bf16)),
        ("gs_st", vm((ps, home, width), bf16)),
        ("gsg", vm((ps, home, width), bf16)),
        ("fd_st", vm((ps, home, width), bf16)),
        ("fdg", vm((ps, home, width), bf16)),
        ("do_st", vm((zs, seqs, sl, tw), bf16)),
        ("dog", vm((ss, sl, tw), bf16)),
        ("dot_s", vm((tw, qn), bf16)),
        ("qt_s", vm((tw, qn), bf16)),
        ("dq_s", vm((qn, tw), f32)),
        ("dkt", vm((hs, HEAD_DIM, qn), f32)),
        ("dvt", vm((hs, HEAD_DIM, qn), f32)),
        ("dk_st", vm((hs, tw, qn), bf16)),
        ("dv_st", vm((hs, tw, qn), bf16)),
        ("dkg", vm((hs, tw, qn), bf16)),
        ("dvg", vm((hs, tw, qn), bf16)),
        ("gpt", vm((3 * tw, qn), bf16)),
        ("gp", vm((qn, 3 * tw), bf16)),
        ("gf_st", vm((ss, sl, width), bf16)),
        ("gfg", vm((seqs, zs, sl, width), bf16)),
        ("wos", vm((ps, zs, rows, width), bf16)),
        ("wor", vm((ps, zs, rows, width), bf16)),
        ("woz", vm((zs, rows, width), f32)),
        ("wozr", vm((zs, rows, width), f32)),
        ("wqs", vm((ps, zs, rows, 3 * tw), bf16)),
        ("wqr", vm((ps, zs, rows, 3 * tw), bf16)),
        ("wqz", vm((zs, rows, 3 * tw), f32)),
        ("wqzr", vm((zs, rows, 3 * tw), f32)),
        ("wfs", vm((zs, ps, rows, part), bf16)),
        ("wfr", vm((zs, ps, rows, part), bf16)),
        ("wfz", vm((ps, rows, part), f32)),
        ("wfzr", vm((ps, rows, part), f32)),
        ("wps", vm((zs, ff_rows, width), bf16)),
        ("wpr", vm((zs, ff_rows, width), bf16)),
        ("arg", vm((ps, 16, width), f32)),
        ("arz", vm((zs, 16, width), f32)),
        ("send", pltpu.SemaphoreType.DMA((30,))),
        ("zsem", pltpu.SemaphoreType.DMA((10, zs))),
        ("psem", pltpu.SemaphoreType.DMA((12, ps))),
        ("lsem", pltpu.SemaphoreType.DMA((4, ss))),
        ("hsem", pltpu.SemaphoreType.DMA((4, hs))),
    ]
    in_vmem = pl.BlockSpec(memory_space=pltpu.VMEM)
    results = pl.pallas_call(
        kernel,
        out_shape=(
            jax.ShapeDtypeStruct((seqs, sl, width), bf16),
            jax.ShapeDtypeStruct((seqs, sl, width), f32),
            jax.ShapeDtypeStruct((zs, rows, 3 * tw), f32),
            jax.ShapeDtypeStruct((rows, width), f32),
            jax.ShapeDtypeStruct((ps, rows, part), f32),
            jax.ShapeDtypeStruct((ff_rows, width), f32),
            jax.ShapeDtypeStruct((16, width), f32),
        ),
        in_specs=[pl.BlockSpec(memory_space=pltpu.SMEM)] + [in_vmem] * 7,
        out_specs=(in_vmem,) * 7,
        scratch_shapes=[shape for _, shape in names],
        compiler_params=pltpu.CompilerParams(
            collective_id=0, has_side_effects=True, vmem_limit_bytes=63 * 1024 * 1024
        ),
        name="layer",
    )(
        lengths,
        layer_input.reshape(seqs, sl, width),
        grad_out.reshape(seqs, sl, width),
        qkv_in,
        w_out,
        fc_in,
        w_proj,
        params,
    )
    result, grad_input, gqkv, gout, gfc, gproj, sums = results
    grad_qkv = gqkv.reshape(zs, rows, 3, tw).transpose(1, 2, 0, 3).reshape(rows, 3 * width)
    grad_fc = (
        gfc.reshape(hs, seqs, rows, zs, ff_rows).transpose(2, 0, 3, 1, 4).reshape(rows, ps * part)
    )
    grad_up = lax.dynamic_slice_in_dim(sums[8], z_at * ff_rows, ff_rows, 0)
    triples = sums[9 : 9 + zs]
    table = jnp.stack(
        [
            sums[0],
            sums[1],
            sums[2],
            triples[:, 0:tw].reshape(width),
            triples[:, 2 * tw : 3 * tw].reshape(width),
            sums[5],
            sums[6],
            sums[7],
        ]
    )
    owned = lax.dynamic_slice_in_dim(table, dev * rows, rows, 1)
    squares = jnp.stack(
        [jnp.sum(sums[3]), jnp.sum(sums[4]), jnp.sum(sums[13]), jnp.sum(sums[14])]
    )
    root_means = jnp.sqrt(squares / (jnp.sum(lengths).astype(f32) * width))
    return (
        result.reshape(layer_input.shape),
        grad_input.reshape(layer_input.shape),
        grad_qkv,
        gout,
        grad_fc,
        gproj,
        grad_up,
        owned[0:2],
        owned[2:8],
        root_means,
    )


def fits(seqs, sl, width, hs, ss, qkv_rows, ff_rows):
    if ss % seqs or seqs != 2:
        return False
    zs = ss // seqs
    if width % zs or (width // zs) % HEAD_DIM or 9 + zs > 13:
        return False
    tw = width // zs
    keys = ss * sl * hs
    return tw <= 256 and keys * ss * sl * (tw // HEAD_DIM) * 4 <= 16 * 1024 * 1024 and qkv_rows % 8 == 0


def on_device(layer_input, grad_out, lengths, w_qkv, w_out, w_fc, w_proj, b_fc, norm_gains, biases):
    seqs, _, sl, width = layer_input.shape
    hs, ss = lax.axis_size("head"), lax.axis_size("seq")
    chosen = (
        fused_layer
        if fits(seqs, sl, width, hs, ss, w_qkv.shape[0], w_proj.shape[0])
        else spread_layer
    )
    return chosen(
        layer_input, grad_out, lengths, w_qkv, w_out, w_fc, w_proj, b_fc, norm_gains, biases
    )


def solution(mesh):
    return jax.shard_map(
        on_device,
        mesh=mesh,
        in_specs=(
            P(None, "seq", "head", None),
            P(None, "seq", "head", None),
            P(),
            P(("head", "seq"), None),
            P(("head", "seq"), None),
            P(("head", "seq"), None),
            P(("head", "seq"), None),
            P(("head", "seq")),
            P(None, ("head", "seq")),
            P(None, ("head", "seq")),
        ),
        out_specs=(
            P(None, "seq", "head", None),
            P(None, "seq", "head", None),
            P(("head", "seq"), None),
            P(("head", "seq"), None),
            P(("head", "seq"), None),
            P(("head", "seq"), None),
            P(("head", "seq")),
            P(None, ("head", "seq")),
            P(None, ("head", "seq")),
            P(),
        ),
        check_vma=False,
    )
```

```python
import functools

import jax
import jax.numpy as jnp
from jax import lax
from jax.sharding import PartitionSpec as P
from jax.experimental import pallas as pl
from jax.experimental.pallas import tpu as pltpu

HEAD_DIM = 64


masked_score = -1e30
block_keys = 512
quick_slope = 1.702
epsilon = 1e-05


def layer_norm_parts(inputs):
    centre = inputs - jnp.mean(inputs, axis=-1, keepdims=True)
    inverse = lax.rsqrt(jnp.mean(centre * centre, axis=-1, keepdims=True) + epsilon)
    return (centre * inverse, inverse)


def norm_backward(grad_normed, normed, inverse):
    return inverse * (
        grad_normed
        - jnp.mean(grad_normed, axis=-1, keepdims=True)
        - normed * jnp.mean(grad_normed * normed, axis=-1, keepdims=True)
    )


def split_heads(piece_block):
    return piece_block.reshape(
        piece_block.shape[0], piece_block.shape[1], piece_block.shape[2] // HEAD_DIM, HEAD_DIM
    )


def head_scores(left_side, right_side):
    return jnp.einsum("sqhd,skhd->shqk", left_side, right_side, preferred_element_type=jnp.float32)


def weighted(probabilities, right_side):
    return jnp.einsum(
        "shqk,skhd->sqhd", probabilities, right_side, preferred_element_type=jnp.float32
    )


def transposed(probabilities, right_side):
    return jnp.einsum(
        "shqk,sqhd->skhd", probabilities, right_side, preferred_element_type=jnp.float32
    )


def over_blocks(step_fn, running, pieces):
    extent = pieces[0].shape[1]
    number = extent // block_keys
    parted = tuple(
        (
            piece_part.reshape(
                (piece_part.shape[0], number, block_keys) + piece_part.shape[2:]
            ).swapaxes(0, 1)
            for piece_part in pieces
        )
    )

    def advance(inner_run, element):
        position, blocks = element
        return (step_fn(inner_run, blocks, position * block_keys), None)

    return lax.scan(advance, running, (jnp.arange(number, dtype=jnp.int32), parted))[0]


def spread_layer(layer_input, grad_out, lengths, w_qkv, w_out, w_fc, w_proj, b_fc, norm_gains, biases):
    sequences = layer_input.shape[0]
    slice_len = layer_input.shape[2]
    model_width = layer_input.shape[3]
    head_ways = lax.axis_size("head")
    group_len = slice_len * head_ways
    local_width = model_width // head_ways
    head_count = local_width // HEAD_DIM
    head_place = lax.axis_index("head")
    cycle_place = lax.axis_index("seq")
    flat_rows = sequences * slice_len
    full_qkv, full_out, full_fc, full_proj, full_bias_fc, full_gains, full_biases = (
        lax.all_gather(w_qkv, ("head", "seq"), axis=0, tiled=True),
        lax.all_gather(w_out, ("head", "seq"), axis=0, tiled=True),
        lax.all_gather(w_fc, ("head", "seq"), axis=0, tiled=True),
        lax.all_gather(w_proj, ("head", "seq"), axis=0, tiled=True),
        lax.all_gather(b_fc, ("head", "seq"), axis=0, tiled=True),
        lax.all_gather(norm_gains, ("head", "seq"), axis=1, tiled=True),
        lax.all_gather(biases, ("head", "seq"), axis=1, tiled=True),
    )
    gain_vals = full_gains.astype(jnp.float32)
    shift_vals = full_biases.astype(jnp.float32)
    bias_up = full_bias_fc.astype(jnp.float32)
    token_places = (
        cycle_place * group_len + head_place * slice_len + jnp.arange(slice_len, dtype=jnp.int32)
    )
    token_keep = (
        (token_places[None, :] < lengths[:, None]).astype(jnp.float32).reshape(flat_rows, 1)
    )
    own_places = cycle_place * group_len + jnp.arange(group_len, dtype=jnp.int32)
    own_allowed = (own_places[None, :] < lengths[:, None])[:, None, None, :]

    def allowed_at(offset, extent):
        places = offset + jnp.arange(extent, dtype=jnp.int32)
        return (places[None, :] < lengths[:, None])[:, None, None, :]

    inputs = layer_input.reshape(flat_rows, model_width).astype(jnp.float32)
    normed_one, inverse_one = layer_norm_parts(inputs)
    first_in = (normed_one * gain_vals[0] + shift_vals[0]).astype(jnp.bfloat16)
    projected = jnp.dot(first_in, full_qkv, preferred_element_type=jnp.float32)
    query_scale = HEAD_DIM ** (-0.5)
    queries = ((projected[:, :model_width] + shift_vals[1]) * query_scale).astype(jnp.bfloat16)
    keys_new = projected[:, model_width : 2 * model_width].astype(jnp.bfloat16)
    values_new = (projected[:, 2 * model_width :] + shift_vals[2]).astype(jnp.bfloat16)
    packed = jnp.stack([queries, keys_new, values_new], axis=1).reshape(
        sequences, slice_len, 3, head_ways, local_width
    )
    spread = lax.all_to_all(packed, "head", split_axis=3, concat_axis=1, tiled=True)
    query_block = spread[:, :, 0, 0]
    key_block = spread[:, :, 1, 0]
    value_block = spread[:, :, 2, 0]
    query_heads = split_heads(query_block)
    key_heads = split_heads(key_block)
    value_heads = split_heads(value_block)

    def maxima_step(running, pieces, offset):
        highest, denominator = running
        scores = head_scores(query_heads, split_heads(pieces[0]))
        allowed = allowed_at(offset, pieces[0].shape[1])
        scores = jnp.where(allowed, scores, masked_score)
        raised = jnp.maximum(highest, jnp.max(scores, axis=-1))
        weights = jnp.where(allowed, jnp.exp(scores - raised[..., None]), 0.0)
        denominator = denominator * jnp.exp(highest - raised) + jnp.sum(weights, axis=-1)
        return (raised, denominator)

    zero_rows = jnp.zeros((sequences, head_count, group_len), jnp.float32)
    highest, denominator = over_blocks(
        maxima_step,
        (zero_rows + masked_score, zero_rows),
        (lax.all_gather(key_block, "seq", axis=1, tiled=True),),
    )
    log_total = highest + jnp.log(denominator)

    def attention_weights(key_piece, offset):
        scores = head_scores(query_heads, key_piece)
        allowed = allowed_at(offset, key_piece.shape[1])
        return jnp.where(
            allowed, jnp.exp(jnp.where(allowed, scores, masked_score) - log_total[..., None]), 0.0
        )

    zero_heads = jnp.zeros((sequences, group_len, head_count, HEAD_DIM), jnp.float32)

    def output_step(running, pieces, offset):
        probabilities = attention_weights(split_heads(pieces[0]), offset)
        return running + weighted(probabilities.astype(jnp.bfloat16), split_heads(pieces[1]))

    attended = over_blocks(
        output_step,
        zero_heads,
        (
            lax.all_gather(key_block, "seq", axis=1, tiled=True),
            lax.all_gather(value_block, "seq", axis=1, tiled=True),
        ),
    )
    mixed_heads = attended.astype(jnp.bfloat16).reshape(
        sequences, head_ways, slice_len, local_width
    )
    gathered_out = lax.all_to_all(mixed_heads, "head", split_axis=1, concat_axis=3, tiled=True)
    mixed_rows = gathered_out.reshape(flat_rows, model_width)
    branch = jnp.dot(mixed_rows, full_out, preferred_element_type=jnp.float32) + shift_vals[3]
    middle = inputs + branch
    normed_two, inverse_two = layer_norm_parts(middle)
    second_in = (normed_two * gain_vals[1] + shift_vals[4]).astype(jnp.bfloat16)
    hidden = jnp.dot(second_in, full_fc, preferred_element_type=jnp.float32) + bias_up
    gate_sig = jax.nn.sigmoid(quick_slope * hidden)
    activated = (hidden * gate_sig).astype(jnp.bfloat16)
    feed_out = jnp.dot(activated, full_proj, preferred_element_type=jnp.float32) + shift_vals[5]
    final_rows = middle + feed_out
    result = (final_rows * token_keep).astype(jnp.bfloat16).reshape(layer_input.shape)
    local_squares = jnp.stack(
        [
            jnp.sum(token_keep * inputs * inputs),
            jnp.sum(token_keep * branch * branch),
            jnp.sum(token_keep * feed_out * feed_out),
            jnp.sum(token_keep * final_rows * final_rows),
        ]
    )
    squares = lax.psum(local_squares, ("head", "seq"))
    valid_count = jnp.sum(lengths).astype(jnp.float32) * model_width
    root_means = jnp.sqrt(squares / valid_count)
    grad_final = grad_out.reshape(flat_rows, model_width).astype(jnp.float32) * token_keep
    grad_feed = grad_final.astype(jnp.bfloat16)
    grad_proj = jnp.dot(activated.T, grad_feed, preferred_element_type=jnp.float32)
    grad_shift_proj = jnp.sum(grad_feed.astype(jnp.float32), axis=0)
    grad_act = jnp.dot(grad_feed, full_proj.T, preferred_element_type=jnp.float32)
    grad_hidden = (
        grad_act * (gate_sig + quick_slope * hidden * gate_sig * (1.0 - gate_sig))
    ).astype(jnp.bfloat16)
    grad_fc = jnp.dot(second_in.T, grad_hidden, preferred_element_type=jnp.float32)
    grad_bias_up = jnp.sum(grad_hidden.astype(jnp.float32), axis=0)
    grad_second = jnp.dot(grad_hidden, full_fc.T, preferred_element_type=jnp.float32)
    grad_gain_two = jnp.sum(grad_second * normed_two, axis=0)
    grad_shift_two = jnp.sum(grad_second, axis=0)
    grad_middle = grad_final + norm_backward(grad_second * gain_vals[1], normed_two, inverse_two)
    grad_branch = grad_middle.astype(jnp.bfloat16)
    grad_out_weight = jnp.dot(mixed_rows.T, grad_branch, preferred_element_type=jnp.float32)
    grad_shift_out = jnp.sum(grad_branch.astype(jnp.float32), axis=0)
    grad_mixed = jnp.dot(grad_branch, full_out.T, preferred_element_type=jnp.float32).astype(
        jnp.bfloat16
    )
    grad_spread = lax.all_to_all(
        grad_mixed.reshape(sequences, slice_len, head_ways, local_width),
        "head",
        split_axis=2,
        concat_axis=1,
        tiled=True,
    )
    grad_block = grad_spread[:, :, 0]
    grad_heads = split_heads(grad_block)

    def delta_step(running, pieces, offset):
        probabilities = attention_weights(split_heads(pieces[0]), offset)
        grad_probs = head_scores(grad_heads, split_heads(pieces[1]))
        return running + jnp.sum(probabilities * grad_probs, axis=-1)

    row_delta = over_blocks(
        delta_step,
        zero_rows,
        (
            lax.all_gather(key_block, "seq", axis=1, tiled=True),
            lax.all_gather(value_block, "seq", axis=1, tiled=True),
        ),
    )

    def query_step(running, pieces, offset):
        key_piece = split_heads(pieces[0])
        probabilities = attention_weights(key_piece, offset)
        grad_probs = head_scores(grad_heads, split_heads(pieces[1]))
        slopes = (probabilities * (grad_probs - row_delta[..., None])).astype(jnp.bfloat16)
        return running + weighted(slopes, key_piece)

    grad_query = over_blocks(
        query_step,
        zero_heads,
        (
            lax.all_gather(key_block, "seq", axis=1, tiled=True),
            lax.all_gather(value_block, "seq", axis=1, tiled=True),
        ),
    )
    all_logs, all_deltas = (
        lax.all_gather(log_total.transpose(0, 2, 1), "seq", axis=1, tiled=True),
        lax.all_gather(row_delta.transpose(0, 2, 1), "seq", axis=1, tiled=True),
    )

    def key_step(running, pieces, offset):
        query_piece = split_heads(pieces[0])
        grad_piece = split_heads(pieces[1])
        extent = pieces[0].shape[1]
        log_piece = lax.dynamic_slice_in_dim(all_logs, offset, extent, 1).transpose(0, 2, 1)
        delta_piece = lax.dynamic_slice_in_dim(all_deltas, offset, extent, 1).transpose(0, 2, 1)
        scores = head_scores(query_piece, key_heads)
        probabilities = jnp.where(
            own_allowed,
            jnp.exp(jnp.where(own_allowed, scores, masked_score) - log_piece[..., None]),
            0.0,
        )
        grad_value = running[1] + transposed(probabilities.astype(jnp.bfloat16), grad_piece)
        grad_probs = head_scores(grad_piece, value_heads)
        slopes = (probabilities * (grad_probs - delta_piece[..., None])).astype(jnp.bfloat16)
        grad_key = running[0] + transposed(slopes, query_piece)
        return (grad_key, grad_value)

    grad_key, grad_value = over_blocks(
        key_step,
        (zero_heads, zero_heads),
        (
            lax.all_gather(query_block, "seq", axis=1, tiled=True),
            lax.all_gather(grad_block, "seq", axis=1, tiled=True),
        ),
    )
    stacked = jnp.stack([grad_query, grad_key, grad_value], axis=2).astype(jnp.bfloat16)
    stacked = stacked.reshape(sequences, head_ways, slice_len, 3, local_width)
    returned = lax.all_to_all(stacked, "head", split_axis=1, concat_axis=4, tiled=True)
    column_scale = jnp.concatenate(
        [
            jnp.full((model_width,), query_scale, jnp.float32),
            jnp.ones((2 * model_width,), jnp.float32),
        ]
    )
    grad_projected = returned.reshape(flat_rows, 3 * model_width).astype(jnp.float32) * column_scale
    grad_shift_query = jnp.sum(grad_projected[:, :model_width], axis=0)
    grad_shift_value = jnp.sum(grad_projected[:, 2 * model_width :], axis=0)
    grad_projected_low = grad_projected.astype(jnp.bfloat16)
    grad_qkv = jnp.dot(first_in.T, grad_projected_low, preferred_element_type=jnp.float32)
    grad_first = jnp.dot(grad_projected_low, full_qkv.T, preferred_element_type=jnp.float32)
    grad_gain_one = jnp.sum(grad_first * normed_one, axis=0)
    grad_shift_one = jnp.sum(grad_first, axis=0)
    grad_inputs = grad_middle + norm_backward(grad_first * gain_vals[0], normed_one, inverse_one)
    grad_gain_rows = jnp.stack([grad_gain_one, grad_gain_two])
    grad_shift_rows = jnp.stack(
        [
            grad_shift_one,
            grad_shift_query,
            grad_shift_value,
            grad_shift_out,
            grad_shift_two,
            grad_shift_proj,
        ]
    )
    owned_grads = (
        lax.psum_scatter(grad_qkv, ("head", "seq"), scatter_dimension=0, tiled=True),
        lax.psum_scatter(grad_out_weight, ("head", "seq"), scatter_dimension=0, tiled=True),
        lax.psum_scatter(grad_fc, ("head", "seq"), scatter_dimension=0, tiled=True),
        lax.psum_scatter(grad_proj, ("head", "seq"), scatter_dimension=0, tiled=True),
        lax.psum_scatter(grad_bias_up, ("head", "seq"), scatter_dimension=0, tiled=True),
        lax.psum_scatter(grad_gain_rows, ("head", "seq"), scatter_dimension=1, tiled=True),
        lax.psum_scatter(grad_shift_rows, ("head", "seq"), scatter_dimension=1, tiled=True),
    )
    return (
        result,
        grad_inputs.reshape(layer_input.shape),
        owned_grads[0],
        owned_grads[1],
        owned_grads[2],
        owned_grads[3],
        owned_grads[4],
        owned_grads[5],
        owned_grads[6],
        root_means,
    )


f32 = jnp.float32
bf16 = jnp.bfloat16
cores = 2


def nn(left, right):
    return lax.dot_general(left, right, (((1,), (0,)), ((), ())), preferred_element_type=f32)


def nt(left, right):
    return lax.dot_general(left, right, (((1,), (1,)), ((), ())), preferred_element_type=f32)


def loop(low, high, step_fn, unroll=1):
    def advance(index, carry):
        step_fn(index)
        return carry

    lax.fori_loop(low, high, advance, 0, unroll=unroll)


def aligned(index, extent):
    return pl.ds(pl.multiple_of(index * extent, extent), extent)


def norm_parts(v):
    centre = v - jnp.mean(v, axis=-1, keepdims=True)
    inverse = lax.rsqrt(jnp.mean(centre * centre, axis=-1, keepdims=True) + epsilon)
    return centre * inverse, inverse


def remote(src, dst, send_sem, recv_sem, place):
    return pltpu.make_async_remote_copy(
        src_ref=src,
        dst_ref=dst,
        send_sem=send_sem,
        recv_sem=recv_sem,
        device_id=place,
        device_id_type=pl.DeviceIdType.MESH,
    )


class Exchange:
    def __init__(self, n, me, place, src, dst, send_sem, recv_sem):
        self.n, self.me, self.place, self.src, self.dst = n, me, place, src, dst
        self.send_sem, self.recv_sem = send_sem, recv_sem

    def out(self, q):
        return remote(
            self.src(q), self.dst(self.me), self.send_sem, self.recv_sem.at[self.me], self.place(q)
        )

    def into(self, q):
        return remote(
            self.dst(q), self.dst(q), self.send_sem, self.recv_sem.at[q], self.place(q)
        )

    def peer(self, k):
        return lax.rem(self.me + k, self.n)

    def send(self):
        loop(1, self.n, lambda k: self.out(self.peer(k)).start())

    def wait(self):
        loop(1, self.n, lambda k: self.into(self.peer(k)).wait_recv())

    def drain(self):
        loop(1, self.n, lambda k: self.out(self.peer(k)).wait_send())


class Gather:
    def __init__(self, n, me, core, place, dst, send_sem, recv_sem):
        self.n, self.me, self.core, self.place, self.dst = n, me, core, place, dst
        self.send_sem, self.recv_sem = send_sem, recv_sem
        self.mine = me * cores + core

    def peer(self, k):
        return lax.rem(self.me + k, self.n)

    def move(self, slot, place):
        return remote(
            self.dst(slot), self.dst(slot), self.send_sem, self.recv_sem.at[slot], place
        )

    def out(self, k):
        return self.move(self.mine, self.place(self.peer(k), self.core))

    def aside(self, k):
        return self.move(
            self.peer(k) * cores + self.core, self.place(self.me, 1 - self.core)
        )

    def send(self):
        loop(1, self.n, lambda k: self.out(k).start())
        self.aside(0).start()

    def relay_from(self, k):
        self.out_slot(k, self.core).wait_recv()
        self.aside(k).start()

    def out_slot(self, k, core):
        return self.move(self.peer(k) * cores + core, self.place(self.peer(k), core))

    def wait_from(self, k):
        self.out_slot(k, 1 - self.core).wait_recv()

    def relay(self):
        loop(1, self.n, self.relay_from)

    def wait(self):
        loop(0, self.n, self.wait_from)

    def drain(self):
        loop(1, self.n, lambda k: self.out(k).wait_send())
        loop(0, self.n, lambda k: self.aside(k).wait_send())


class Reduce:
    def __init__(self, n, me, core, place, stage, beside, summed, landed, sems, recv_sems, add):
        self.n, self.me, self.core, self.place = n, me, core, place
        self.stage, self.beside, self.summed, self.landed = stage, beside, summed, landed
        self.sems, self.recv_sems, self.add = sems, recv_sems, add

    def peer(self, k):
        return lax.rem(self.me + k, self.n)

    def aside(self, r):
        return remote(
            self.stage(r * cores + 1 - self.core),
            self.beside(r),
            self.sems.at[0],
            self.recv_sems.at[0, r],
            self.place(self.me, 1 - self.core),
        )

    def out(self, r):
        return remote(
            self.summed(r),
            self.landed(self.me),
            self.sems.at[1],
            self.recv_sems.at[1, self.me],
            self.place(r, self.core),
        )

    def combine(self, r):
        self.aside(r).wait_recv()
        self.add(self.stage(r * cores + self.core), self.beside(r), self.summed(r))

    def combine_out(self, k):
        r = self.peer(k)
        self.combine(r)
        self.out(r).start()

    def send_aside(self):
        loop(0, self.n, lambda k: self.aside(self.peer(k + 1)).start())

    def send(self):
        loop(1, self.n, self.combine_out)
        self.combine(self.me)

    def wait(self):
        def one(k):
            r = self.peer(k)
            remote(
                self.landed(r), self.landed(r), self.sems.at[1], self.recv_sems.at[1, r],
                self.place(r, self.core),
            ).wait_recv()

        loop(1, self.n, one)

    def drain_aside(self):
        loop(0, self.n, lambda k: self.aside(self.peer(k)).wait_send())

    def drain(self):
        self.drain_aside()
        loop(1, self.n, lambda k: self.out(self.peer(k)).wait_send())


def fused_layer(layer_input, grad_out, lengths, w_qkv, w_out, w_fc, w_proj, b_fc, norm_gains, biases):
    seqs, _, sl, width = layer_input.shape
    hs = lax.axis_size("head")
    ss = lax.axis_size("seq")
    zs = ss // seqs
    ps = hs * seqs
    xs = hs // cores
    rs = xs * seqs
    group = sl * hs
    tw = width // zs
    heads = tw // HEAD_DIM
    rows = w_qkv.shape[0]
    ff_rows = w_proj.shape[0]
    part = ff_rows * zs
    home = seqs * sl
    qn = ss * sl
    slab = ps * home
    duo = cores * home
    query_block = 256
    blocks = qn // query_block
    chunk = 32
    pair = 2 * rows
    quad = 4 * rows
    scale = HEAD_DIM ** (-0.5)

    def kernel(
        len_ref, x_ref, go_ref, wqkv_ref, wout_ref, wfc_ref, wproj_ref, bfc_ref, gain_ref, bias_ref,
        out_ref, gin_ref, gqkv_ref, gout_ref, gfc_ref, gproj_ref, ar_ref,
        small, small_z, small_g, prm, up_bias,
        qkv_st, fc_st, wqg, wog, wfg, wpg, wq, wo, wf,
        xg, q_s, kvg, kneg, probs, s_scr, pb_scr, ds_scr, o_s, o_st, og, mixt,
        branch_s, middle_s, gm_s,
        x2g, gog, act, gh, x2t, actt, gs_st, gs_out, gs_in, gs_red, fd_in, fd_red,
        do_st, dog, dot_s, qt_s, dq_s, dkt, dvt, kv_st, kv_in, kv_out, kv_red, gpt, gp,
        gf_st, gfg, wos, wo_in, wo_out, wo_red, woz, wozr, wqs, wq_in, wq_out, wq_red, wqz, wqzr,
        wfs, wfr, wfz, wfzr, wps, wpr, arg, arz,
        send, zsem, lsem, psem, gsem, rsem, ksem, krsem, ssem,
    ):
        h = lax.axis_index("head")
        s = lax.axis_index("seq")
        z = s // seqs
        y = lax.rem(s, seqs)
        core = lax.rem(h, cores)
        r_at = (h // cores) * seqs + y
        x_at = h // cores
        p = r_at * cores + core

        def chip_place(r, c):
            return ((r // seqs) * cores + c, z * seqs + lax.rem(r, seqs))

        def slab_place(q):
            return chip_place(q // cores, lax.rem(q, cores))

        def line_place(q):
            return (h, q)

        def z_place(q):
            return (h, q * seqs + y)

        def x_place(r, c):
            return (r * cores + c, s)

        count = {}

        def take(name):
            number = count.get(name, 0)
            count[name] = number + 1
            return number

        def over_z(src, dst):
            return Exchange(zs, z, z_place, src, dst, send.at[take("s")], zsem.at[take("z")])

        def over_line(src, dst):
            return Exchange(ss, s, line_place, src, dst, send.at[take("s")], lsem.at[take("l")])

        def over_plane(src, dst):
            return Exchange(ps, p, slab_place, src, dst, send.at[take("s")], psem.at[take("p")])

        def gather(dst):
            return Gather(rs, r_at, core, chip_place, dst, send.at[take("s")], gsem.at[take("g")])

        def add_rows(block):
            def add(a, b, c):
                extent = a.shape[0]

                def one(i):
                    at = aligned(i, block)
                    c[at, :] = (a[at, :].astype(f32) + b[at, :].astype(f32)).astype(bf16)

                loop(0, extent // block, one)

            return add

        def add_blocks(a, b, c):
            def one(i):
                c[i] = (a[i].astype(f32) + b[i].astype(f32)).astype(bf16)

            loop(0, a.shape[0], one)

        def reduce(stage, beside, summed, landed, add):
            number = take("r")
            return Reduce(
                rs, r_at, core, chip_place, stage, beside, summed, landed, ssem.at[number],
                rsem.at[number], add,
            )

        ex_small_z = over_z(lambda q: small, lambda q: small_z.at[q])
        ex_wq_z = over_z(lambda q: qkv_st.at[q], lambda q: wqg.at[p, q])
        ex_wo_z = over_z(lambda q: wout_ref, lambda q: wog.at[p, q])
        ex_x = over_line(lambda q: x_ref.at[lax.rem(q, seqs)], lambda q: xg.at[q])
        ga_small = gather(lambda q: small_g.at[q])
        ga_wq = gather(lambda q: wqg.at[q])
        ga_wo = gather(lambda q: wog.at[q])
        ex_wf_p = over_plane(lambda q: fc_st.at[q], lambda q: wfg.at[z, q])
        ex_wf_z = over_z(lambda q: wfg.at[z], lambda q: wfg.at[q])
        ex_wp_z = over_z(lambda q: wproj_ref, lambda q: wpg.at[q])
        ga_go = gather(lambda q: gog.at[q])
        ga_kv = [
            Gather(
                xs, x_at, core, x_place,
                lambda q, i=i: kvg.at[q, :, :, i * 2 * sl : (i + 1) * 2 * sl],
                send.at[take("s")], ksem.at[i],
            )
            for i in range(zs)
        ]
        ex_o = over_line(lambda q: o_st.at[q], lambda q: og.at[lax.rem(q, seqs), q // seqs])
        ga_x2 = gather(lambda q: x2g.at[q])
        re_gs = reduce(
            lambda q: gs_st.at[q], lambda r: gs_in.at[r], lambda r: gs_out.at[r],
            lambda r: gs_red.at[r], add_rows(32),
        )
        re_fd = reduce(
            lambda q: gs_st.at[q], lambda r: fd_in.at[r], lambda r: gs_out.at[r],
            lambda r: fd_red.at[r], add_rows(32),
        )
        ex_do = over_line(
            lambda q: do_st.at[q // seqs, lax.rem(q, seqs)], lambda q: dog.at[q]
        )
        re_kv = [
            Reduce(
                xs, x_at, core, x_place,
                lambda q, n=n: kv_st.at[n, q], lambda r, n=n: kv_in.at[n, r],
                lambda r, n=n: kv_out.at[n, r], lambda r, n=n: kv_red.at[n, r],
                ssem.at[take("r")], krsem.at[n], add_blocks,
            )
            for n in range(heads)
        ]
        ex_gf = over_line(lambda q: gf_st.at[q], lambda q: gfg.at[lax.rem(q, seqs), q // seqs])
        re_wo = reduce(
            lambda q: wos.at[q], lambda r: wo_in.at[r], lambda r: wo_out.at[r],
            lambda r: wo_red.at[r], add_blocks,
        )
        ex_go_z = over_z(lambda q: woz.at[q], lambda q: wozr.at[q])
        re_wq = reduce(
            lambda q: wqs.at[q], lambda r: wq_in.at[r], lambda r: wq_out.at[r],
            lambda r: wq_red.at[r], add_blocks,
        )
        ex_gq_z = over_z(lambda q: wqz.at[q], lambda q: wqzr.at[q])
        ex_gfc_z = over_z(lambda q: wfs.at[q], lambda q: wfr.at[q])
        ex_gfc_p = over_plane(lambda q: wfz.at[q], lambda q: wfzr.at[q])
        ex_gp_z = over_z(lambda q: wps.at[q], lambda q: wpr.at[q])
        ga_ar = gather(lambda q: arg.at[q])
        ex_ar_z = over_z(lambda q: arz.at[z], lambda q: arz.at[q])

        barrier = pltpu.get_barrier_semaphore()

        def greet(place, me, n):
            def one(k):
                pl.semaphore_signal(
                    barrier, inc=1, device_id=place(lax.rem(me + k, n)),
                    device_id_type=pl.DeviceIdType.MESH,
                )

            loop(1, n, one)

        greet(slab_place, p, ps)
        greet(line_place, s, ss)

        small[...] = jnp.zeros_like(small)
        small[0:2, 0:rows] = gain_ref[...].astype(f32)
        small[2:8, 0:rows] = bias_ref[...].astype(f32)
        small[8:9, 0:ff_rows] = bfc_ref[...].astype(f32)
        for t in range(zs):
            for k in range(3):
                qkv_st[t, :, k * tw : (k + 1) * tw] = wqkv_ref[:, k * width + t * tw : k * width + (t + 1) * tw]
        for q in range(ps):
            hq = q // cores // seqs * cores + q % cores
            yq = q // cores % seqs
            for t in range(zs):
                at = ((hq * zs + t) * seqs + yq) * ff_rows
                fc_st[q, :, t * ff_rows : (t + 1) * ff_rows] = wfc_ref[:, at : at + ff_rows]
        small_z[z] = small[...]
        wqg[p, z] = qkv_st[z]
        wog[p, z] = wout_ref[...]
        wfg[z, p] = fc_st[p]
        wpg[z] = wproj_ref[...]
        xg[s] = x_ref[y]
        len_0 = len_ref[0]
        len_1 = len_ref[1]
        len_y = jnp.where(y == 0, len_0, len_1)
        home_row = lax.broadcasted_iota(jnp.int32, (home, 1), 0)
        home_place = s * group + h * sl + lax.rem(home_row, sl)
        keep = jnp.where(home_place < jnp.where(home_row < sl, len_0, len_1), 1.0, 0.0)
        gog[p] = (go_ref[...].reshape(home, width).astype(f32) * keep).astype(bf16)

        def mask_block(q):
            column = lax.broadcasted_iota(jnp.int32, (chunk, qn), 1)
            place = (column // sl) * group + q * sl + lax.rem(column, sl)
            kneg[q] = jnp.where(place < len_y, 0.0, masked_score)

        loop(0, hs, mask_block)
        pl.semaphore_wait(barrier, ps - 1 + ss - 1)

        ex_small_z.send()
        ex_wq_z.send()
        ex_x.send()
        ex_wf_p.send()

        ex_small_z.wait()
        small_g[p] = small_z[...]
        ga_small.send()
        up_bias[...] = jnp.zeros_like(up_bias)
        for t in range(zs):
            up_bias[0:1, t * ff_rows : (t + 1) * ff_rows] = small_z[t, 8:9, 0:ff_rows]
        ex_wq_z.wait()
        ga_wq.send()
        ga_small.relay()
        ga_wq.relay()

        def d_of(q, t):
            hq = q // cores // seqs * cores + q % cores
            return hq * ss + t * seqs + q // cores % seqs

        ga_small.wait()
        prm[...] = jnp.zeros_like(prm)
        for q in range(ps):
            for t in range(zs):
                d = d_of(q, t)
                prm[0:8, d * rows : (d + 1) * rows] = small_g[q, t, 0:8, 0:rows]
                at = (d * rows) % tw
                triple = (d * rows) // tw
                prm[8 + triple : 9 + triple, at : at + rows] = small_g[q, t, 3:4, 0:rows]
                prm[8 + triple : 9 + triple, 2 * tw + at : 2 * tw + at + rows] = small_g[q, t, 4:5, 0:rows]

        def assemble(src, dst):
            def one(i):
                hq = i // zs
                q = hq // cores * seqs * cores + lax.rem(hq, cores)
                t = lax.rem(i, zs)
                dst[aligned(i, pair), :] = jnp.concatenate(
                    [src(q, t).astype(f32), src(q + cores, t).astype(f32)], axis=0
                ).astype(bf16)

            loop(0, width // pair, one)

        ga_wq.wait()
        assemble(lambda a, b: wqg[a, b], wq)

        def first_norm(i):
            xv = xg[pl.ds(2 * i, 2)].reshape(2 * sl, width).astype(f32)
            normed, inverse = norm_parts(xv)
            return normed, (normed * prm[0:1, :] + prm[2:3, :]).astype(bf16)

        for i in range(zs):
            for q in (2 * i, 2 * i + 1):
                @pl.when(s != q)
                def _(q=q):
                    ex_x.into(q).wait_recv()

            _, first = first_norm(i)
            at = slice(i * 2 * sl, (i + 1) * 2 * sl)
            projected = nn(first, wq[...]) + prm[pl.ds(8 + z, 1), 0 : 3 * tw]
            q_s[at, :] = (projected[:, 0:tw] * scale).astype(bf16)
            turned = projected[:, tw:].T.astype(bf16)
            kvg[h, 0, :, at] = turned[0:tw, :]
            kvg[h, 1, :, at] = turned[tw : 2 * tw, :]
            ga_kv[i].send()
        for i in range(zs):
            ga_kv[i].relay()
        ex_wp_z.send()
        ex_wf_p.wait()
        ex_wf_z.send()
        ex_wo_z.send()
        for i in range(zs):
            ga_kv[i].wait()
        ga_go.send()

        lane_head = lax.broadcasted_iota(jnp.int32, (query_block, tw), 1) // HEAD_DIM

        def attend(step):
            n = step // blocks
            i = lax.rem(step, blocks)
            at = aligned(i, query_block)
            lane_own = lane_head == n
            queries = q_s[at, :]
            masked = jnp.where(lane_own, queries, jnp.zeros_like(queries))
            for b in range(hs):
                s_scr[:, b * qn : (b + 1) * qn] = nn(masked, kvg[b, 0])

            def soft(r):
                rat = aligned(r, chunk)
                sv = [s_scr[rat, b * qn : (b + 1) * qn] + kneg[b] for b in range(hs)]
                top = jnp.max(functools.reduce(jnp.maximum, sv), axis=-1, keepdims=True)
                ev = [jnp.exp(v - top) for v in sv]
                inv = 1.0 / jnp.sum(functools.reduce(jnp.add, ev), axis=-1, keepdims=True)
                for b in range(hs):
                    value = ev[b] * inv
                    probs[n, i, rat, b * qn : (b + 1) * qn] = value
                    pb_scr[rat, b * qn : (b + 1) * qn] = value.astype(bf16)

            loop(0, query_block // chunk, soft, unroll=4)
            head_out = nt(pb_scr[:, 0:qn], kvg[0, 1])
            for b in range(1, hs):
                head_out = head_out + nt(pb_scr[:, b * qn : (b + 1) * qn], kvg[b, 1])
            o_s[at, :] = jnp.where(lane_own, head_out.astype(bf16), o_s[at, :])

        o_s[...] = jnp.zeros_like(o_s)
        loop(0, 2 * blocks, attend)
        ga_go.relay()
        ex_wo_z.wait()
        ga_wo.send()
        loop(2 * blocks, heads * blocks, attend)

        def lay_out(q):
            o_st[q] = o_s[aligned(q, sl), :]

        loop(0, ss, lay_out)
        ex_o.send()
        og[y, z] = o_st[s]

        ga_wo.relay()
        ex_wp_z.wait()
        ex_wf_z.wait()
        assemble(lambda a, b: wfg[b, a], wf)
        ga_wo.wait()
        assemble(lambda a, b: wog[a, b], wo)
        ga_go.wait()
        ex_o.wait()
        branch = jnp.broadcast_to(prm[5:6, :], (home, width))
        for t in range(zs):
            mixed = og[:, t].reshape(home, tw)
            branch = branch + nn(mixed, wo[t * tw : (t + 1) * tw, :])
        middle = x_ref[...].reshape(home, width).astype(f32) + branch
        normed, _ = norm_parts(middle)
        x2g[p] = (normed * prm[1:2, :] + prm[6:7, :]).astype(bf16)
        ga_x2.send()
        branch_s[...] = branch
        middle_s[...] = middle

        def feed(k, running):
            r = ga_x2.peer(k)

            @pl.when(k > 0)
            def _():
                ga_x2.relay_from(k)

            ga_x2.wait_from(k)
            at = aligned(r, duo)
            chip = pl.ds(cores * r, cores)
            hid = nn(x2g[chip].reshape(duo, width), wf[...]) + up_bias[0:1, :]
            gate = 1.0 / (1.0 + jnp.exp(-quick_slope * hid))
            act[at, :] = (hid * gate).astype(bf16)
            flow = nt(gog[chip].reshape(duo, width), wpg[...].reshape(part, width))
            slope = gate + quick_slope * hid * gate * (1.0 - gate)
            back = (flow * slope).astype(bf16)
            gh[at, :] = back
            gs_st[chip] = nt(back, wf[...]).astype(bf16).reshape(cores, home, width)
            re_gs.aside(r).start()

            @pl.when(k > 1)
            def _():
                re_gs.combine_out(k - 1)

            return running + jnp.sum(back.astype(f32), axis=0, keepdims=True)

        grad_up = lax.fori_loop(0, rs, feed, jnp.zeros((1, part), f32))
        re_gs.combine_out(rs - 1)
        re_gs.combine(r_at)
        for t in range(zs):
            mixt[t * tw : (t + 1) * tw, :] = og[:, t].reshape(home, tw).T
        grad_final = go_ref[...].reshape(home, width).astype(f32) * keep

        re_gs.wait()

        def landed_sum(re, own):
            total = own
            for k in range(1, rs):
                total = total + re.landed(re.peer(k))[...].astype(f32)
            return total

        grad_second = landed_sum(re_gs, gs_out[r_at].astype(f32))
        n2, r2 = norm_parts(middle_s[...])
        grad_middle = grad_final + norm_backward(grad_second * prm[1:2, :], n2, r2)
        grad_branch = grad_middle.astype(bf16)
        for t in range(zs):
            do_st[t] = nt(grad_branch, wo[t * tw : (t + 1) * tw, :]).astype(bf16).reshape(seqs, sl, tw)
        ex_do.send()
        dog[s] = do_st[z, y]
        gm_s[...] = grad_middle
        arg[p] = jnp.zeros((16, width), f32)
        arg[p, 1:2, :] = jnp.sum(grad_second * n2, axis=0, keepdims=True)
        arg[p, 6:7, :] = jnp.sum(grad_second, axis=0, keepdims=True)
        arg[p, 5:6, :] = jnp.sum(grad_branch.astype(f32), axis=0, keepdims=True)

        def turn(q):
            at = aligned(q, home)
            x2t[:, at] = x2g[q].T
            actt[:, at] = act[at, :].T

        loop(0, ps, turn)

        def scatter_rows(c, val, put):
            for j in range(4):
                d = c * 4 + j
                hq = d // ss
                sd = lax.rem(d, ss)
                q = (hq // cores * seqs + lax.rem(sd, seqs)) * cores + lax.rem(hq, cores)
                put(q, sd // seqs, val[j * rows : (j + 1) * rows, :].astype(bf16))

        def fc_grad(c):
            def put(q, t, value):
                wfs[t, q] = value

            scatter_rows(c, nn(x2t[aligned(c, quad), :], gh[...]), put)

        loop(0, width // quad, fc_grad)
        ex_gfc_z.send()
        wfr[z] = wfs[z]

        def proj_grad(c):
            wps[c] = nn(actt[aligned(c, ff_rows), :], gog[...].reshape(slab, width)).astype(bf16)

        loop(0, zs, proj_grad)
        ex_gp_z.send()
        wpr[z] = wps[z]

        ex_do.wait()

        def gather_do(i):
            at = aligned(i, 2 * sl)
            value = dog[pl.ds(2 * i, 2)].reshape(2 * sl, tw)
            o_s[at, :] = value
            dot_s[:, at] = value.T
            qt_s[:, at] = q_s[at, :].T

        loop(0, ss // 2, gather_do)
        dq_s[...] = jnp.zeros_like(dq_s)

        for n in range(heads):
            lane_own = lane_head == n
            head_rows = slice(n * HEAD_DIM, (n + 1) * HEAD_DIM)

            def back(i, n=n, lane_own=lane_own, head_rows=head_rows):
                at = aligned(i, query_block)
                outer = o_s[at, :]
                masked = jnp.where(lane_own, outer, jnp.zeros_like(outer))
                for b in range(hs):
                    s_scr[:, b * qn : (b + 1) * qn] = nn(masked, kvg[b, 1])

                def soft(r):
                    rat = aligned(r, chunk)
                    dp = [s_scr[rat, b * qn : (b + 1) * qn] for b in range(hs)]
                    pv = [probs[n, i, rat, b * qn : (b + 1) * qn] for b in range(hs)]
                    delta = jnp.sum(
                        functools.reduce(jnp.add, [a * c for a, c in zip(dp, pv)]),
                        axis=-1, keepdims=True,
                    )
                    for b in range(hs):
                        ds_scr[rat, b * qn : (b + 1) * qn] = (pv[b] * (dp[b] - delta)).astype(bf16)
                        pb_scr[rat, b * qn : (b + 1) * qn] = pv[b].astype(bf16)

                loop(0, query_block // chunk, soft, unroll=4)
                head_dq = nt(ds_scr[:, 0:qn], kvg[0, 0])
                for b in range(1, hs):
                    head_dq = head_dq + nt(ds_scr[:, b * qn : (b + 1) * qn], kvg[b, 0])
                dq_s[at, :] = jnp.where(lane_own, (head_dq.astype(bf16).astype(f32) * scale).astype(bf16), dq_s[at, :])
                for b in range(hs):
                    dkt[b] = dkt[b] + nn(qt_s[head_rows, at], ds_scr[:, b * qn : (b + 1) * qn])
                    dvt[b] = dvt[b] + nn(dot_s[head_rows, at], pb_scr[:, b * qn : (b + 1) * qn])

            dkt[...] = jnp.zeros_like(dkt)
            dvt[...] = jnp.zeros_like(dvt)
            loop(0, blocks, back)
            for b in range(hs):
                kv_st[n, b, 0] = dkt[b].astype(bf16)
                kv_st[n, b, 1] = dvt[b].astype(bf16)
            re_kv[n].send_aside()
            if n:
                re_kv[n - 1].send()
        re_kv[heads - 1].send()

        re_gs.drain()

        def feed_down(r):
            chip = pl.ds(cores * r, cores)
            gs_st[chip] = nn(act[aligned(r, duo), :], wpg[...].reshape(part, width)).astype(bf16).reshape(
                cores, home, width
            )
            re_fd.aside(r).start()

        loop(0, rs, feed_down)
        gpt[0:tw, :] = dq_s[...].T
        for n in range(heads):
            re_kv[n].wait()
            for k in range(2):
                at = (1 + k) * tw + n * HEAD_DIM
                gpt[at : at + HEAD_DIM, :] = (
                    kv_out[n, x_at, k].astype(f32) + kv_red[n, re_kv[n].peer(1), k].astype(f32)
                ).astype(bf16)
        gp[...] = gpt[...].T

        gain_sum = jnp.zeros((1, width), f32)
        shift_sum = jnp.zeros((1, width), f32)
        for k in range(zs):
            i = lax.rem(z + 1 + k, zs)
            at = aligned(i, 2 * sl)
            value = nt(gp[at, :], wq[...])
            gf_st[pl.ds(2 * i, 2)] = value.astype(bf16).reshape(2, sl, width)
            for q in (2 * i, 2 * i + 1):
                if k < zs - 1:
                    ex_gf.out(q).start()
                else:
                    @pl.when(s != q)
                    def _(q=q):
                        ex_gf.out(q).start()
            normed, first = first_norm(i)
            x2t[:, at] = first.T
            gain_sum = gain_sum + jnp.sum(value * normed, axis=0, keepdims=True)
            shift_sum = shift_sum + jnp.sum(value, axis=0, keepdims=True)
        gfg[y, z] = gf_st[s]

        def qkv_grad(c):
            def put(q, t, value):
                wqs[q, t] = value

            scatter_rows(c, nn(x2t[aligned(c, quad), 0:qn], gp[...]), put)

        loop(0, width // quad, qkv_grad)
        re_wq.send_aside()
        arg[p, 0:1, :] = gain_sum
        arg[p, 2:3, :] = shift_sum
        arg[p, pl.ds(9 + z, 1), 0 : 3 * tw] = jnp.sum(gp[...].astype(f32), axis=0, keepdims=True)
        arg[p, 7:8, :] = jnp.sum(gog[p].astype(f32), axis=0, keepdims=True)
        re_wq.send()

        re_fd.send()
        re_fd.wait()
        feed_out = landed_sum(re_fd, gs_out[r_at].astype(f32)) + prm[7:8, :]
        final = middle_s[...] + feed_out
        out_ref[...] = (final * keep).astype(bf16).reshape(seqs, sl, width)
        xv = x_ref[...].reshape(home, width).astype(f32)
        br = branch_s[...]
        for row, value in ((3, xv), (4, br), (13, feed_out), (14, final)):
            arg[p, row : row + 1, :] = jnp.sum(keep * value * value, axis=0, keepdims=True)
        ga_ar.send()

        def out_grad(c):
            def put(q, t, value):
                wos[q, t] = value

            scatter_rows(c, nn(mixt[aligned(c, quad), :], gm_s[...].astype(bf16)), put)

        loop(0, width // quad, out_grad)
        re_wo.send_aside()

        ex_gfc_z.wait()

        def fc_sum(q):
            wfz[q] = functools.reduce(jnp.add, [wfr[t, q].astype(f32) for t in range(zs)])

        loop(0, ps, fc_sum)
        ex_gfc_p.send()
        wfzr[p] = wfz[p]
        re_wo.send()
        ex_gp_z.wait()
        gproj_ref[...] = functools.reduce(jnp.add, [wpr[t].astype(f32) for t in range(zs)])

        def final_rows(re, out, landed, dst):
            def one(t):
                total = out[r_at, t].astype(f32)
                for k in range(1, rs):
                    total = total + landed[re.peer(k), t].astype(f32)
                dst[t] = total

            loop(0, zs, one)

        re_wq.wait()
        final_rows(re_wq, wq_out, wq_red, wqz)
        ex_gq_z.send()
        wqzr[z] = wqz[z]
        ga_ar.relay()
        ga_ar.wait()
        arz[z] = functools.reduce(jnp.add, [arg[q] for q in range(ps)])
        arz[z, 8:9, 0:part] = grad_up
        ex_ar_z.send()
        re_wo.wait()
        final_rows(re_wo, wo_out, wo_red, woz)
        ex_go_z.send()
        wozr[z] = woz[z]

        ex_gf.wait()
        grad_first = functools.reduce(jnp.add, [gfg[:, t].astype(f32) for t in range(zs)]).reshape(home, width)
        n1, r1 = norm_parts(x_ref[...].reshape(home, width).astype(f32))
        grad_in = gm_s[...] + norm_backward(grad_first * prm[0:1, :], n1, r1)
        gin_ref[...] = grad_in.reshape(seqs, sl, width)

        ex_gfc_p.wait()
        gfc_ref[...] = wfzr[...]
        ex_gq_z.wait()
        gqkv_ref[...] = wqzr[...]
        ex_ar_z.wait()
        ar_ref[...] = functools.reduce(jnp.add, [arz[t] for t in range(zs)])
        ex_go_z.wait()
        gout_ref[...] = functools.reduce(jnp.add, [wozr[t] for t in range(zs)])

        for ex in (
            ex_small_z, ex_wq_z, ex_wo_z, ex_x, ga_small, ga_wq, ga_wo, ex_wf_p, ex_wf_z, ex_wp_z,
            ga_go, *ga_kv, ex_o, ga_x2, re_fd, ex_do, *re_kv, ex_gf, re_wo, ex_go_z, re_wq, ex_gq_z,
            ex_gfc_z, ex_gfc_p, ex_gp_z, ga_ar, ex_ar_z,
        ):
            ex.drain()

    vm = pltpu.VMEM
    scratch = [
        vm((16, 128), f32),
        vm((zs, 16, 128), f32),
        vm((ps, zs, 16, 128), f32),
        vm((16, width), f32),
        vm((8, part), f32),
        vm((zs, rows, 3 * tw), bf16),
        vm((ps, rows, part), bf16),
        vm((ps, zs, rows, 3 * tw), bf16),
        vm((ps, zs, rows, width), bf16),
        vm((zs, ps, rows, part), bf16),
        vm((zs, ff_rows, width), bf16),
        vm((width, 3 * tw), bf16),
        vm((width, width), bf16),
        vm((width, part), bf16),
        vm((ss, sl, width), bf16),
        vm((qn, tw), bf16),
        vm((hs, 2, tw, qn), bf16),
        vm((hs, chunk, qn), f32),
        vm((heads, blocks, query_block, hs * qn), f32),
        vm((query_block, hs * qn), f32),
        vm((query_block, hs * qn), bf16),
        vm((query_block, hs * qn), bf16),
        vm((qn, tw), bf16),
        vm((ss, sl, tw), bf16),
        vm((seqs, zs, sl, tw), bf16),
        vm((width, home), bf16),
        vm((home, width), f32),
        vm((home, width), f32),
        vm((home, width), f32),
        vm((ps, home, width), bf16),
        vm((ps, home, width), bf16),
        vm((slab, part), bf16),
        vm((slab, part), bf16),
        vm((width, slab), bf16),
        vm((part, slab), bf16),
        vm((ps, home, width), bf16),
        vm((rs, home, width), bf16),
        vm((rs, home, width), bf16),
        vm((rs, home, width), bf16),
        vm((rs, home, width), bf16),
        vm((rs, home, width), bf16),
        vm((zs, seqs, sl, tw), bf16),
        vm((ss, sl, tw), bf16),
        vm((tw, qn), bf16),
        vm((tw, qn), bf16),
        vm((qn, tw), bf16),
        vm((hs, HEAD_DIM, qn), f32),
        vm((hs, HEAD_DIM, qn), f32),
        vm((heads, hs, 2, HEAD_DIM, qn), bf16),
        vm((heads, xs, 2, HEAD_DIM, qn), bf16),
        vm((heads, xs, 2, HEAD_DIM, qn), bf16),
        vm((heads, xs, 2, HEAD_DIM, qn), bf16),
        vm((3 * tw, qn), bf16),
        vm((qn, 3 * tw), bf16),
        vm((ss, sl, width), bf16),
        vm((seqs, zs, sl, width), bf16),
        vm((ps, zs, rows, width), bf16),
        vm((rs, zs, rows, width), bf16),
        vm((rs, zs, rows, width), bf16),
        vm((rs, zs, rows, width), bf16),
        vm((zs, rows, width), f32),
        vm((zs, rows, width), f32),
        vm((ps, zs, rows, 3 * tw), bf16),
        vm((rs, zs, rows, 3 * tw), bf16),
        vm((rs, zs, rows, 3 * tw), bf16),
        vm((rs, zs, rows, 3 * tw), bf16),
        vm((zs, rows, 3 * tw), f32),
        vm((zs, rows, 3 * tw), f32),
        vm((zs, ps, rows, part), bf16),
        vm((zs, ps, rows, part), bf16),
        vm((ps, rows, part), f32),
        vm((ps, rows, part), f32),
        vm((zs, ff_rows, width), bf16),
        vm((zs, ff_rows, width), bf16),
        vm((ps, 16, width), f32),
        vm((zs, 16, width), f32),
        pltpu.SemaphoreType.DMA((26,)),
        pltpu.SemaphoreType.DMA((10, zs)),
        pltpu.SemaphoreType.DMA((4, ss)),
        pltpu.SemaphoreType.DMA((2, ps)),
        pltpu.SemaphoreType.DMA((6, ps)),
        pltpu.SemaphoreType.DMA((7, 2, rs)),
        pltpu.SemaphoreType.DMA((zs, hs)),
        pltpu.SemaphoreType.DMA((heads, 2, xs)),
        pltpu.SemaphoreType.DMA((7, 2)),
    ]
    in_vmem = pl.BlockSpec(memory_space=pltpu.VMEM)
    in_smem = pl.BlockSpec(memory_space=pltpu.SMEM)
    results = pl.pallas_call(
        kernel,
        out_shape=(
            jax.ShapeDtypeStruct((seqs, sl, width), bf16),
            jax.ShapeDtypeStruct((seqs, sl, width), f32),
            jax.ShapeDtypeStruct((zs, rows, 3 * tw), f32),
            jax.ShapeDtypeStruct((rows, width), f32),
            jax.ShapeDtypeStruct((ps, rows, part), f32),
            jax.ShapeDtypeStruct((ff_rows, width), f32),
            jax.ShapeDtypeStruct((16, width), f32),
        ),
        in_specs=[in_smem] + [in_vmem] * 9,
        out_specs=(in_vmem,) * 7,
        scratch_shapes=scratch,
        compiler_params=pltpu.CompilerParams(
            collective_id=0, has_side_effects=True, vmem_limit_bytes=63 * 1024 * 1024
        ),
        name="layer",
    )(
        lengths,
        layer_input.reshape(seqs, sl, width),
        grad_out.reshape(seqs, sl, width),
        w_qkv,
        w_out,
        w_fc,
        w_proj,
        b_fc.reshape(1, ff_rows),
        norm_gains,
        biases,
    )

    def finish(
        len_ref, a_out, a_gin, a_gqkv, a_gout, a_gfc, a_gproj, sums,
        out_ref, gin_ref, gqkv_ref, gout_ref, gfc_ref, gproj_ref, gup_ref, ggain_ref, gbias_ref, rms_ref,
        table,
    ):
        h = lax.axis_index("head")
        s = lax.axis_index("seq")
        z = s // seqs
        out_ref[...] = a_out[...]
        gin_ref[...] = a_gin[...]
        gout_ref[...] = a_gout[...]
        gproj_ref[...] = a_gproj[...]
        for t in range(zs):
            for k in range(3):
                gqkv_ref[:, k * width + t * tw : k * width + (t + 1) * tw] = a_gqkv[t, :, k * tw : (k + 1) * tw]
        for q in range(ps):
            hq = q // cores // seqs * cores + q % cores
            yq = q // cores % seqs
            for t in range(zs):
                at = ((hq * zs + t) * seqs + yq) * ff_rows
                gfc_ref[:, at : at + ff_rows] = a_gfc[q, :, t * ff_rows : (t + 1) * ff_rows]
        table[0:3, :] = sums[0:3, :]
        for t in range(zs):
            table[3:4, t * tw : (t + 1) * tw] = sums[9 + t : 10 + t, 0:tw]
            table[4:5, t * tw : (t + 1) * tw] = sums[9 + t : 10 + t, 2 * tw : 3 * tw]
        table[5:8, :] = sums[5:8, :]
        back = lax.rem(width - (h * ss + s) * rows, width)
        turned = pltpu.roll(table[...], back, 1)
        ggain_ref[...] = turned[0:2, 0:rows]
        gbias_ref[...] = turned[2:8, 0:rows]
        up = jnp.zeros((1, ff_rows), f32)
        for t in range(zs):
            up = up + jnp.where(z == t, sums[8:9, t * ff_rows : (t + 1) * ff_rows], 0.0)
        gup_ref[...] = up
        valid = (len_ref[0] + len_ref[1]).astype(f32) * width
        place = lax.broadcasted_iota(jnp.int32, (1, 4), 1)
        squares = jnp.zeros((1, 4), f32)
        for k, row in enumerate((3, 4, 13, 14)):
            squares = squares + jnp.where(
                place == k, jnp.sum(sums[row : row + 1, :], axis=1, keepdims=True), 0.0
            )
        rms_ref[...] = jnp.sqrt(squares / valid)

    final = pl.pallas_call(
        finish,
        out_shape=(
            jax.ShapeDtypeStruct((seqs, sl, width), bf16),
            jax.ShapeDtypeStruct((seqs, sl, width), f32),
            jax.ShapeDtypeStruct((rows, 3 * width), f32),
            jax.ShapeDtypeStruct((rows, width), f32),
            jax.ShapeDtypeStruct((rows, ps * part), f32),
            jax.ShapeDtypeStruct((ff_rows, width), f32),
            jax.ShapeDtypeStruct((1, ff_rows), f32),
            jax.ShapeDtypeStruct((2, rows), f32),
            jax.ShapeDtypeStruct((6, rows), f32),
            jax.ShapeDtypeStruct((1, 4), f32),
        ),
        in_specs=[in_smem] + [in_vmem] * 7,
        out_specs=(in_vmem,) * 10,
        scratch_shapes=[vm((8, width), f32)],
        name="finish",
    )(lengths, *results)
    return (
        final[0].reshape(layer_input.shape),
        final[1].reshape(layer_input.shape),
        *final[2:6],
        final[6].reshape(ff_rows),
        final[7],
        final[8],
        final[9].reshape(4),
    )


def fits(seqs, sl, width, hs, ss, qkv_rows):
    if seqs != 2 or ss % seqs or hs % cores:
        return False
    zs = ss // seqs
    if width % zs or (width // zs) % HEAD_DIM or zs > 4 or qkv_rows % 8:
        return False
    tw = width // zs
    keys = ss * sl * hs
    return tw <= 256 and keys * ss * sl * (tw // HEAD_DIM) * 4 <= 16 * 1024 * 1024


def on_device(layer_input, grad_out, lengths, w_qkv, w_out, w_fc, w_proj, b_fc, norm_gains, biases):
    seqs, _, sl, width = layer_input.shape
    hs, ss = lax.axis_size("head"), lax.axis_size("seq")
    chosen = fused_layer if fits(seqs, sl, width, hs, ss, w_qkv.shape[0]) else spread_layer
    return chosen(
        layer_input, grad_out, lengths, w_qkv, w_out, w_fc, w_proj, b_fc, norm_gains, biases
    )


def solution(mesh):
    return jax.shard_map(
        on_device,
        mesh=mesh,
        in_specs=(
            P(None, "seq", "head", None),
            P(None, "seq", "head", None),
            P(),
            P(("head", "seq"), None),
            P(("head", "seq"), None),
            P(("head", "seq"), None),
            P(("head", "seq"), None),
            P(("head", "seq")),
            P(None, ("head", "seq")),
            P(None, ("head", "seq")),
        ),
        out_specs=(
            P(None, "seq", "head", None),
            P(None, "seq", "head", None),
            P(("head", "seq"), None),
            P(("head", "seq"), None),
            P(("head", "seq"), None),
            P(("head", "seq"), None),
            P(("head", "seq")),
            P(None, ("head", "seq")),
            P(None, ("head", "seq")),
            P(),
        ),
        check_vma=False,
    )
```

```python
import functools

import jax
import jax.numpy as jnp
from jax import lax
from jax.sharding import PartitionSpec as P
from jax.experimental import pallas as pl
from jax.experimental.pallas import tpu as pltpu

HEAD_DIM = 64


masked_score = -1e30
block_keys = 512
quick_slope = 1.702
epsilon = 1e-05


def layer_norm_parts(inputs):
    centre = inputs - jnp.mean(inputs, axis=-1, keepdims=True)
    inverse = lax.rsqrt(jnp.mean(centre * centre, axis=-1, keepdims=True) + epsilon)
    return (centre * inverse, inverse)


def norm_backward(grad_normed, normed, inverse):
    return inverse * (
        grad_normed
        - jnp.mean(grad_normed, axis=-1, keepdims=True)
        - normed * jnp.mean(grad_normed * normed, axis=-1, keepdims=True)
    )


def split_heads(piece_block):
    return piece_block.reshape(
        piece_block.shape[0], piece_block.shape[1], piece_block.shape[2] // HEAD_DIM, HEAD_DIM
    )


def head_scores(left_side, right_side):
    return jnp.einsum("sqhd,skhd->shqk", left_side, right_side, preferred_element_type=jnp.float32)


def weighted(probabilities, right_side):
    return jnp.einsum(
        "shqk,skhd->sqhd", probabilities, right_side, preferred_element_type=jnp.float32
    )


def transposed(probabilities, right_side):
    return jnp.einsum(
        "shqk,sqhd->skhd", probabilities, right_side, preferred_element_type=jnp.float32
    )


def over_blocks(step_fn, running, pieces):
    extent = pieces[0].shape[1]
    number = extent // block_keys
    parted = tuple(
        (
            piece_part.reshape(
                (piece_part.shape[0], number, block_keys) + piece_part.shape[2:]
            ).swapaxes(0, 1)
            for piece_part in pieces
        )
    )

    def advance(inner_run, element):
        position, blocks = element
        return (step_fn(inner_run, blocks, position * block_keys), None)

    return lax.scan(advance, running, (jnp.arange(number, dtype=jnp.int32), parted))[0]


def spread_layer(layer_input, grad_out, lengths, w_qkv, w_out, w_fc, w_proj, b_fc, norm_gains, biases):
    sequences = layer_input.shape[0]
    slice_len = layer_input.shape[2]
    model_width = layer_input.shape[3]
    head_ways = lax.axis_size("head")
    group_len = slice_len * head_ways
    local_width = model_width // head_ways
    head_count = local_width // HEAD_DIM
    head_place = lax.axis_index("head")
    cycle_place = lax.axis_index("seq")
    flat_rows = sequences * slice_len
    full_qkv, full_out, full_fc, full_proj, full_bias_fc, full_gains, full_biases = (
        lax.all_gather(w_qkv, ("head", "seq"), axis=0, tiled=True),
        lax.all_gather(w_out, ("head", "seq"), axis=0, tiled=True),
        lax.all_gather(w_fc, ("head", "seq"), axis=0, tiled=True),
        lax.all_gather(w_proj, ("head", "seq"), axis=0, tiled=True),
        lax.all_gather(b_fc, ("head", "seq"), axis=0, tiled=True),
        lax.all_gather(norm_gains, ("head", "seq"), axis=1, tiled=True),
        lax.all_gather(biases, ("head", "seq"), axis=1, tiled=True),
    )
    gain_vals = full_gains.astype(jnp.float32)
    shift_vals = full_biases.astype(jnp.float32)
    bias_up = full_bias_fc.astype(jnp.float32)
    token_places = (
        cycle_place * group_len + head_place * slice_len + jnp.arange(slice_len, dtype=jnp.int32)
    )
    token_keep = (
        (token_places[None, :] < lengths[:, None]).astype(jnp.float32).reshape(flat_rows, 1)
    )
    own_places = cycle_place * group_len + jnp.arange(group_len, dtype=jnp.int32)
    own_allowed = (own_places[None, :] < lengths[:, None])[:, None, None, :]

    def allowed_at(offset, extent):
        places = offset + jnp.arange(extent, dtype=jnp.int32)
        return (places[None, :] < lengths[:, None])[:, None, None, :]

    inputs = layer_input.reshape(flat_rows, model_width).astype(jnp.float32)
    normed_one, inverse_one = layer_norm_parts(inputs)
    first_in = (normed_one * gain_vals[0] + shift_vals[0]).astype(jnp.bfloat16)
    projected = jnp.dot(first_in, full_qkv, preferred_element_type=jnp.float32)
    query_scale = HEAD_DIM ** (-0.5)
    queries = ((projected[:, :model_width] + shift_vals[1]) * query_scale).astype(jnp.bfloat16)
    keys_new = projected[:, model_width : 2 * model_width].astype(jnp.bfloat16)
    values_new = (projected[:, 2 * model_width :] + shift_vals[2]).astype(jnp.bfloat16)
    packed = jnp.stack([queries, keys_new, values_new], axis=1).reshape(
        sequences, slice_len, 3, head_ways, local_width
    )
    spread = lax.all_to_all(packed, "head", split_axis=3, concat_axis=1, tiled=True)
    query_block = spread[:, :, 0, 0]
    key_block = spread[:, :, 1, 0]
    value_block = spread[:, :, 2, 0]
    query_heads = split_heads(query_block)
    key_heads = split_heads(key_block)
    value_heads = split_heads(value_block)

    def maxima_step(running, pieces, offset):
        highest, denominator = running
        scores = head_scores(query_heads, split_heads(pieces[0]))
        allowed = allowed_at(offset, pieces[0].shape[1])
        scores = jnp.where(allowed, scores, masked_score)
        raised = jnp.maximum(highest, jnp.max(scores, axis=-1))
        weights = jnp.where(allowed, jnp.exp(scores - raised[..., None]), 0.0)
        denominator = denominator * jnp.exp(highest - raised) + jnp.sum(weights, axis=-1)
        return (raised, denominator)

    zero_rows = jnp.zeros((sequences, head_count, group_len), jnp.float32)
    highest, denominator = over_blocks(
        maxima_step,
        (zero_rows + masked_score, zero_rows),
        (lax.all_gather(key_block, "seq", axis=1, tiled=True),),
    )
    log_total = highest + jnp.log(denominator)

    def attention_weights(key_piece, offset):
        scores = head_scores(query_heads, key_piece)
        allowed = allowed_at(offset, key_piece.shape[1])
        return jnp.where(
            allowed, jnp.exp(jnp.where(allowed, scores, masked_score) - log_total[..., None]), 0.0
        )

    zero_heads = jnp.zeros((sequences, group_len, head_count, HEAD_DIM), jnp.float32)

    def output_step(running, pieces, offset):
        probabilities = attention_weights(split_heads(pieces[0]), offset)
        return running + weighted(probabilities.astype(jnp.bfloat16), split_heads(pieces[1]))

    attended = over_blocks(
        output_step,
        zero_heads,
        (
            lax.all_gather(key_block, "seq", axis=1, tiled=True),
            lax.all_gather(value_block, "seq", axis=1, tiled=True),
        ),
    )
    mixed_heads = attended.astype(jnp.bfloat16).reshape(
        sequences, head_ways, slice_len, local_width
    )
    gathered_out = lax.all_to_all(mixed_heads, "head", split_axis=1, concat_axis=3, tiled=True)
    mixed_rows = gathered_out.reshape(flat_rows, model_width)
    branch = jnp.dot(mixed_rows, full_out, preferred_element_type=jnp.float32) + shift_vals[3]
    middle = inputs + branch
    normed_two, inverse_two = layer_norm_parts(middle)
    second_in = (normed_two * gain_vals[1] + shift_vals[4]).astype(jnp.bfloat16)
    hidden = jnp.dot(second_in, full_fc, preferred_element_type=jnp.float32) + bias_up
    gate_sig = jax.nn.sigmoid(quick_slope * hidden)
    activated = (hidden * gate_sig).astype(jnp.bfloat16)
    feed_out = jnp.dot(activated, full_proj, preferred_element_type=jnp.float32) + shift_vals[5]
    final_rows = middle + feed_out
    result = (final_rows * token_keep).astype(jnp.bfloat16).reshape(layer_input.shape)
    local_squares = jnp.stack(
        [
            jnp.sum(token_keep * inputs * inputs),
            jnp.sum(token_keep * branch * branch),
            jnp.sum(token_keep * feed_out * feed_out),
            jnp.sum(token_keep * final_rows * final_rows),
        ]
    )
    squares = lax.psum(local_squares, ("head", "seq"))
    valid_count = jnp.sum(lengths).astype(jnp.float32) * model_width
    root_means = jnp.sqrt(squares / valid_count)
    grad_final = grad_out.reshape(flat_rows, model_width).astype(jnp.float32) * token_keep
    grad_feed = grad_final.astype(jnp.bfloat16)
    grad_proj = jnp.dot(activated.T, grad_feed, preferred_element_type=jnp.float32)
    grad_shift_proj = jnp.sum(grad_feed.astype(jnp.float32), axis=0)
    grad_act = jnp.dot(grad_feed, full_proj.T, preferred_element_type=jnp.float32)
    grad_hidden = (
        grad_act * (gate_sig + quick_slope * hidden * gate_sig * (1.0 - gate_sig))
    ).astype(jnp.bfloat16)
    grad_fc = jnp.dot(second_in.T, grad_hidden, preferred_element_type=jnp.float32)
    grad_bias_up = jnp.sum(grad_hidden.astype(jnp.float32), axis=0)
    grad_second = jnp.dot(grad_hidden, full_fc.T, preferred_element_type=jnp.float32)
    grad_gain_two = jnp.sum(grad_second * normed_two, axis=0)
    grad_shift_two = jnp.sum(grad_second, axis=0)
    grad_middle = grad_final + norm_backward(grad_second * gain_vals[1], normed_two, inverse_two)
    grad_branch = grad_middle.astype(jnp.bfloat16)
    grad_out_weight = jnp.dot(mixed_rows.T, grad_branch, preferred_element_type=jnp.float32)
    grad_shift_out = jnp.sum(grad_branch.astype(jnp.float32), axis=0)
    grad_mixed = jnp.dot(grad_branch, full_out.T, preferred_element_type=jnp.float32).astype(
        jnp.bfloat16
    )
    grad_spread = lax.all_to_all(
        grad_mixed.reshape(sequences, slice_len, head_ways, local_width),
        "head",
        split_axis=2,
        concat_axis=1,
        tiled=True,
    )
    grad_block = grad_spread[:, :, 0]
    grad_heads = split_heads(grad_block)

    def delta_step(running, pieces, offset):
        probabilities = attention_weights(split_heads(pieces[0]), offset)
        grad_probs = head_scores(grad_heads, split_heads(pieces[1]))
        return running + jnp.sum(probabilities * grad_probs, axis=-1)

    row_delta = over_blocks(
        delta_step,
        zero_rows,
        (
            lax.all_gather(key_block, "seq", axis=1, tiled=True),
            lax.all_gather(value_block, "seq", axis=1, tiled=True),
        ),
    )

    def query_step(running, pieces, offset):
        key_piece = split_heads(pieces[0])
        probabilities = attention_weights(key_piece, offset)
        grad_probs = head_scores(grad_heads, split_heads(pieces[1]))
        slopes = (probabilities * (grad_probs - row_delta[..., None])).astype(jnp.bfloat16)
        return running + weighted(slopes, key_piece)

    grad_query = over_blocks(
        query_step,
        zero_heads,
        (
            lax.all_gather(key_block, "seq", axis=1, tiled=True),
            lax.all_gather(value_block, "seq", axis=1, tiled=True),
        ),
    )
    all_logs, all_deltas = (
        lax.all_gather(log_total.transpose(0, 2, 1), "seq", axis=1, tiled=True),
        lax.all_gather(row_delta.transpose(0, 2, 1), "seq", axis=1, tiled=True),
    )

    def key_step(running, pieces, offset):
        query_piece = split_heads(pieces[0])
        grad_piece = split_heads(pieces[1])
        extent = pieces[0].shape[1]
        log_piece = lax.dynamic_slice_in_dim(all_logs, offset, extent, 1).transpose(0, 2, 1)
        delta_piece = lax.dynamic_slice_in_dim(all_deltas, offset, extent, 1).transpose(0, 2, 1)
        scores = head_scores(query_piece, key_heads)
        probabilities = jnp.where(
            own_allowed,
            jnp.exp(jnp.where(own_allowed, scores, masked_score) - log_piece[..., None]),
            0.0,
        )
        grad_value = running[1] + transposed(probabilities.astype(jnp.bfloat16), grad_piece)
        grad_probs = head_scores(grad_piece, value_heads)
        slopes = (probabilities * (grad_probs - delta_piece[..., None])).astype(jnp.bfloat16)
        grad_key = running[0] + transposed(slopes, query_piece)
        return (grad_key, grad_value)

    grad_key, grad_value = over_blocks(
        key_step,
        (zero_heads, zero_heads),
        (
            lax.all_gather(query_block, "seq", axis=1, tiled=True),
            lax.all_gather(grad_block, "seq", axis=1, tiled=True),
        ),
    )
    stacked = jnp.stack([grad_query, grad_key, grad_value], axis=2).astype(jnp.bfloat16)
    stacked = stacked.reshape(sequences, head_ways, slice_len, 3, local_width)
    returned = lax.all_to_all(stacked, "head", split_axis=1, concat_axis=4, tiled=True)
    column_scale = jnp.concatenate(
        [
            jnp.full((model_width,), query_scale, jnp.float32),
            jnp.ones((2 * model_width,), jnp.float32),
        ]
    )
    grad_projected = returned.reshape(flat_rows, 3 * model_width).astype(jnp.float32) * column_scale
    grad_shift_query = jnp.sum(grad_projected[:, :model_width], axis=0)
    grad_shift_value = jnp.sum(grad_projected[:, 2 * model_width :], axis=0)
    grad_projected_low = grad_projected.astype(jnp.bfloat16)
    grad_qkv = jnp.dot(first_in.T, grad_projected_low, preferred_element_type=jnp.float32)
    grad_first = jnp.dot(grad_projected_low, full_qkv.T, preferred_element_type=jnp.float32)
    grad_gain_one = jnp.sum(grad_first * normed_one, axis=0)
    grad_shift_one = jnp.sum(grad_first, axis=0)
    grad_inputs = grad_middle + norm_backward(grad_first * gain_vals[0], normed_one, inverse_one)
    grad_gain_rows = jnp.stack([grad_gain_one, grad_gain_two])
    grad_shift_rows = jnp.stack(
        [
            grad_shift_one,
            grad_shift_query,
            grad_shift_value,
            grad_shift_out,
            grad_shift_two,
            grad_shift_proj,
        ]
    )
    owned_grads = (
        lax.psum_scatter(grad_qkv, ("head", "seq"), scatter_dimension=0, tiled=True),
        lax.psum_scatter(grad_out_weight, ("head", "seq"), scatter_dimension=0, tiled=True),
        lax.psum_scatter(grad_fc, ("head", "seq"), scatter_dimension=0, tiled=True),
        lax.psum_scatter(grad_proj, ("head", "seq"), scatter_dimension=0, tiled=True),
        lax.psum_scatter(grad_bias_up, ("head", "seq"), scatter_dimension=0, tiled=True),
        lax.psum_scatter(grad_gain_rows, ("head", "seq"), scatter_dimension=1, tiled=True),
        lax.psum_scatter(grad_shift_rows, ("head", "seq"), scatter_dimension=1, tiled=True),
    )
    return (
        result,
        grad_inputs.reshape(layer_input.shape),
        owned_grads[0],
        owned_grads[1],
        owned_grads[2],
        owned_grads[3],
        owned_grads[4],
        owned_grads[5],
        owned_grads[6],
        root_means,
    )


f32 = jnp.float32
bf16 = jnp.bfloat16
cores = 2


def nn(left, right):
    return lax.dot_general(left, right, (((1,), (0,)), ((), ())), preferred_element_type=f32)


def nt(left, right):
    return lax.dot_general(left, right, (((1,), (1,)), ((), ())), preferred_element_type=f32)


def loop(low, high, step_fn, unroll=1):
    def advance(index, carry):
        step_fn(index)
        return carry

    lax.fori_loop(low, high, advance, 0, unroll=unroll)


def aligned(index, extent):
    return pl.ds(pl.multiple_of(index * extent, extent), extent)


def norm_parts(v):
    centre = v - jnp.mean(v, axis=-1, keepdims=True)
    inverse = lax.rsqrt(jnp.mean(centre * centre, axis=-1, keepdims=True) + epsilon)
    return centre * inverse, inverse


def remote(src, dst, send_sem, recv_sem, place):
    return pltpu.make_async_remote_copy(
        src_ref=src,
        dst_ref=dst,
        send_sem=send_sem,
        recv_sem=recv_sem,
        device_id=place,
        device_id_type=pl.DeviceIdType.MESH,
    )


class Exchange:
    def __init__(self, n, me, place, src, dst, send_sem, recv_sem):
        self.n, self.me, self.place, self.src, self.dst = n, me, place, src, dst
        self.send_sem, self.recv_sem = send_sem, recv_sem

    def out(self, q):
        return remote(
            self.src(q), self.dst(self.me), self.send_sem, self.recv_sem.at[self.me], self.place(q)
        )

    def into(self, q):
        return remote(
            self.dst(q), self.dst(q), self.send_sem, self.recv_sem.at[q], self.place(q)
        )

    def peer(self, k):
        return lax.rem(self.me + k, self.n)

    def send(self):
        loop(1, self.n, lambda k: self.out(self.peer(k)).start())

    def wait(self):
        loop(1, self.n, lambda k: self.into(self.peer(k)).wait_recv())

    def drain(self):
        loop(1, self.n, lambda k: self.out(self.peer(k)).wait_send())


def chip_peer(n, inner, me, k):
    outer = n // inner
    a = lax.rem(me // inner + lax.rem(k, outer), outer)
    b = lax.rem(lax.rem(me, inner) + k // outer, inner)
    return a * inner + b


class Gather:
    def __init__(self, n, inner, me, core, place, dst, send_sem, recv_sem):
        self.n, self.inner, self.me, self.core, self.place, self.dst = n, inner, me, core, place, dst
        self.send_sem, self.recv_sem = send_sem, recv_sem
        self.mine = me * cores + core

    def peer(self, k):
        return chip_peer(self.n, self.inner, self.me, k)

    def move(self, slot, place):
        return remote(
            self.dst(slot), self.dst(slot), self.send_sem, self.recv_sem.at[slot], place
        )

    def out(self, k):
        return self.move(self.mine, self.place(self.peer(k), self.core))

    def aside(self, k):
        return self.move(
            self.peer(k) * cores + self.core, self.place(self.me, 1 - self.core)
        )

    def send(self, last=None):
        loop(1, last or self.n, lambda k: self.out(k).start())
        self.aside(0).start()

    def send_last(self):
        loop(1, self.n - 1, lambda k: self.out(k).wait_send())
        self.out(self.n - 1).start()

    def relay_from(self, k):
        self.out_slot(k, self.core).wait_recv()
        self.aside(k).start()

    def out_slot(self, k, core):
        return self.move(self.peer(k) * cores + core, self.place(self.peer(k), core))

    def wait_from(self, k):
        self.out_slot(k, 1 - self.core).wait_recv()

    def relay(self):
        loop(1, self.n, self.relay_from)

    def wait(self):
        loop(0, self.n, self.wait_from)

    def drain(self, first=1):
        loop(first, self.n, lambda k: self.out(k).wait_send())
        loop(0, self.n, lambda k: self.aside(k).wait_send())


class Reduce:
    def __init__(self, n, inner, me, core, place, stage, beside, summed, landed, sems, recv_sems, add):
        self.n, self.inner, self.me, self.core, self.place = n, inner, me, core, place
        self.stage, self.beside, self.summed, self.landed = stage, beside, summed, landed
        self.sems, self.recv_sems, self.add = sems, recv_sems, add

    def peer(self, k):
        return chip_peer(self.n, self.inner, self.me, k)

    def aside(self, r):
        return remote(
            self.stage(r * cores + 1 - self.core),
            self.beside(r),
            self.sems.at[0],
            self.recv_sems.at[0, r],
            self.place(self.me, 1 - self.core),
        )

    def out(self, r):
        return remote(
            self.summed(r),
            self.landed(self.me),
            self.sems.at[1],
            self.recv_sems.at[1, self.me],
            self.place(r, self.core),
        )

    def combine(self, r):
        self.aside(r).wait_recv()
        self.add(self.stage(r * cores + self.core), self.beside(r), self.summed(r))

    def combine_out(self, k):
        r = self.peer(k)
        self.combine(r)
        self.out(r).start()

    def send_aside(self):
        loop(1, self.n, lambda k: self.aside(self.peer(k)).start())
        self.aside(self.me).start()

    def send(self):
        loop(1, self.n, self.combine_out)
        self.combine(self.me)

    def wait(self):
        def one(k):
            r = self.peer(k)
            remote(
                self.landed(r), self.landed(r), self.sems.at[1], self.recv_sems.at[1, r],
                self.place(r, self.core),
            ).wait_recv()

        loop(1, self.n, one)

    def drain_aside(self):
        loop(0, self.n, lambda k: self.aside(self.peer(k)).wait_send())

    def drain(self):
        self.drain_aside()
        loop(1, self.n, lambda k: self.out(self.peer(k)).wait_send())


def fused_layer(layer_input, grad_out, lengths, w_qkv, w_out, w_fc, w_proj, b_fc, norm_gains, biases):
    seqs, _, sl, width = layer_input.shape
    hs = lax.axis_size("head")
    ss = lax.axis_size("seq")
    zs = ss // seqs
    ps = hs * seqs
    xs = hs // cores
    rs = xs * seqs
    group = sl * hs
    tw = width // zs
    heads = tw // HEAD_DIM
    rows = w_qkv.shape[0]
    ff_rows = w_proj.shape[0]
    part = ff_rows * zs
    home = seqs * sl
    qn = ss * sl
    slab = ps * home
    duo = cores * home
    query_block = 256
    blocks = qn // query_block
    chunk = 32
    pair = 2 * rows
    quad = 4 * rows
    scale = HEAD_DIM ** (-0.5)

    def kernel(
        len_ref, x_ref, go_ref, wqkv_ref, wout_ref, wfc_ref, wproj_ref, bfc_ref, gain_ref, bias_ref,
        out_ref, gin_ref, gqkv_ref, gout_ref, gfc_ref, gproj_ref, ar_ref,
        small, small_z, small_g, prm, up_bias,
        qkv_st, fc_st, wqg, wog, wfg, wpg, wq, wo, wf,
        xg, q_s, kvg, kneg, probs, s_scr, pb_scr, ds_scr, o_s, o_st, og,
        branch_s, middle_s, gm_s,
        x2g, gog, act, gh, x2t, gs_st, gs_out, gs_in, gs_red, fd_st, fd_out, fd_in, fd_red,
        do_st, dog, dot_s, qt_s, dq_s, dkt, dvt, kv_st, kv_in, kv_out, kv_red, gpt, gp,
        gf_st, gfg, wos, wo_in, wo_out, wo_red, woz, wozr, wqs, wq_in, wq_out, wq_red, wqz, wqzr,
        wfs, wfr, wfz, wfzr, wps, wpr, arg, sums, ar_st, arz,
        send, zsem, lsem, psem, gsem, rsem, ksem, krsem, ssem,
    ):
        h = lax.axis_index("head")
        s = lax.axis_index("seq")
        z = s // seqs
        y = lax.rem(s, seqs)
        core = lax.rem(h, cores)
        r_at = (h // cores) * seqs + y
        x_at = h // cores
        p = r_at * cores + core

        def chip_place(r, c):
            return ((r // seqs) * cores + c, z * seqs + lax.rem(r, seqs))

        def slab_place(q):
            return chip_place(q // cores, lax.rem(q, cores))

        def line_place(q):
            return (h, q)

        def z_place(q):
            return (h, q * seqs + y)

        def x_place(r, c):
            return (r * cores + c, s)

        count = {}

        def take(name):
            number = count.get(name, 0)
            count[name] = number + 1
            return number

        def over_z(src, dst):
            return Exchange(zs, z, z_place, src, dst, send.at[take("s")], zsem.at[take("z")])

        def over_line(src, dst):
            return Exchange(ss, s, line_place, src, dst, send.at[take("s")], lsem.at[take("l")])

        def over_plane(src, dst):
            return Exchange(ps, p, slab_place, src, dst, send.at[take("s")], psem.at[take("p")])

        def gather(dst):
            return Gather(rs, seqs, r_at, core, chip_place, dst, send.at[take("s")], gsem.at[take("g")])

        def add_rows(block):
            def add(a, b, c):
                extent = a.shape[0]

                def one(i):
                    at = aligned(i, block)
                    c[at, :] = (a[at, :].astype(f32) + b[at, :].astype(f32)).astype(bf16)

                loop(0, extent // block, one)

            return add

        def add_blocks(a, b, c):
            def one(i):
                c[i] = (a[i].astype(f32) + b[i].astype(f32)).astype(bf16)

            loop(0, a.shape[0], one)

        def reduce(stage, beside, summed, landed, add):
            number = take("r")
            return Reduce(
                rs, seqs, r_at, core, chip_place, stage, beside, summed, landed, ssem.at[number],
                rsem.at[number], add,
            )

        ex_small_z = over_z(lambda q: small, lambda q: small_z.at[q])
        ex_wq_z = over_z(lambda q: qkv_st.at[q], lambda q: wqg.at[p, q])
        ex_wo_z = over_z(lambda q: wout_ref, lambda q: wog.at[p, q])
        ex_x = over_line(lambda q: x_ref.at[lax.rem(q, seqs)], lambda q: xg.at[q])
        ga_small = gather(lambda q: small_g.at[q])
        ga_wq = gather(lambda q: wqg.at[q])
        ga_wo = gather(lambda q: wog.at[q])
        ex_wf_p = over_plane(lambda q: fc_st.at[q], lambda q: wfg.at[z, q])
        ex_wf_z = over_z(lambda q: wfg.at[z], lambda q: wfg.at[q])
        ex_wp_z = over_z(lambda q: wproj_ref, lambda q: wpg.at[q])
        ga_go = gather(lambda q: gog.at[q])
        ga_kv = [
            Gather(
                xs, 1, x_at, core, x_place,
                lambda q, i=i: kvg.at[q, :, :, i * 2 * sl : (i + 1) * 2 * sl],
                send.at[take("s")], ksem.at[i],
            )
            for i in range(zs)
        ]
        ex_o = over_line(lambda q: o_st.at[q], lambda q: og.at[lax.rem(q, seqs), q // seqs])
        ga_x2 = gather(lambda q: x2g.at[q])
        re_gs = reduce(
            lambda q: gs_st.at[q], lambda r: gs_in.at[r], lambda r: gs_out.at[r],
            lambda r: gs_red.at[r], add_rows(32),
        )
        re_fd = reduce(
            lambda q: fd_st.at[q], lambda r: fd_in.at[r], lambda r: fd_out.at[r],
            lambda r: fd_red.at[r], add_rows(32),
        )
        ex_do = over_line(
            lambda q: do_st.at[q // seqs, lax.rem(q, seqs)], lambda q: dog.at[q]
        )
        re_kv = [
            Reduce(
                xs, 1, x_at, core, x_place,
                lambda q, n=n: kv_st.at[n, q], lambda r, n=n: kv_in.at[n, r],
                lambda r, n=n: kv_out.at[n, r], lambda r, n=n: kv_red.at[n, r],
                ssem.at[take("r")], krsem.at[n], add_blocks,
            )
            for n in range(heads)
        ]
        ex_gf = over_line(lambda q: gf_st.at[q], lambda q: gfg.at[lax.rem(q, seqs), q // seqs])
        re_wo = reduce(
            lambda q: wos.at[q], lambda r: wo_in.at[r], lambda r: wo_out.at[r],
            lambda r: wo_red.at[r], add_blocks,
        )
        ex_go_z = over_z(lambda q: woz.at[q], lambda q: wozr.at[q])
        re_wq = reduce(
            lambda q: wqs.at[q], lambda r: wq_in.at[r], lambda r: wq_out.at[r],
            lambda r: wq_red.at[r], add_blocks,
        )
        ex_gq_z = over_z(lambda q: wqz.at[q], lambda q: wqzr.at[q])
        ex_gfc_z = over_z(lambda q: wfs.at[q], lambda q: wfr.at[q])
        ex_gfc_p = over_plane(lambda q: wfz.at[q], lambda q: wfzr.at[q])
        ex_gp_z = over_z(lambda q: wps.at[q], lambda q: wpr.at[q])
        ga_ar = gather(lambda q: arg.at[q])
        ex_ar_z = over_z(lambda q: ar_st.at[q], lambda q: arz.at[q])

        barrier = pltpu.get_barrier_semaphore()

        def greet(place, me, n):
            def one(k):
                pl.semaphore_signal(
                    barrier, inc=1, device_id=place(lax.rem(me + k, n)),
                    device_id_type=pl.DeviceIdType.MESH,
                )

            loop(1, n, one)

        greet(slab_place, p, ps)
        greet(line_place, s, ss)

        small[...] = jnp.zeros_like(small)
        small[0:2, 0:rows] = gain_ref[...].astype(f32)
        small[2:8, 0:rows] = bias_ref[...].astype(f32)
        small[8:9, 0:ff_rows] = bfc_ref[...].astype(f32)
        for t in range(zs):
            for k in range(3):
                qkv_st[t, :, k * tw : (k + 1) * tw] = wqkv_ref[:, k * width + t * tw : k * width + (t + 1) * tw]
        for q in range(ps):
            hq = q // cores // seqs * cores + q % cores
            yq = q // cores % seqs
            for t in range(zs):
                at = ((hq * zs + t) * seqs + yq) * ff_rows
                fc_st[q, :, t * ff_rows : (t + 1) * ff_rows] = wfc_ref[:, at : at + ff_rows]
        small_z[z] = small[...]
        wqg[p, z] = qkv_st[z]
        wog[p, z] = wout_ref[...]
        wfg[z, p] = fc_st[p]
        wpg[z] = wproj_ref[...]
        xg[s] = x_ref[y]
        ar_st[...] = jnp.zeros_like(ar_st)
        len_0 = len_ref[0]
        len_1 = len_ref[1]
        len_y = jnp.where(y == 0, len_0, len_1)
        home_row = lax.broadcasted_iota(jnp.int32, (home, 1), 0)
        home_place = s * group + h * sl + lax.rem(home_row, sl)
        keep = jnp.where(home_place < jnp.where(home_row < sl, len_0, len_1), 1.0, 0.0)
        gog[p] = (go_ref[...].reshape(home, width).astype(f32) * keep).astype(bf16)

        def mask_block(q):
            column = lax.broadcasted_iota(jnp.int32, (chunk, qn), 1)
            place = (column // sl) * group + q * sl + lax.rem(column, sl)
            kneg[q] = jnp.where(place < len_y, 0.0, masked_score)

        loop(0, hs, mask_block)
        pl.semaphore_wait(barrier, ps - 1 + ss - 1)

        ex_small_z.send()
        ex_wq_z.send()
        ex_x.send()
        ex_wo_z.send()
        ex_wf_p.send()

        ex_small_z.wait()
        small_g[p] = small_z[...]
        ga_small.send()
        up_bias[...] = jnp.zeros_like(up_bias)
        for t in range(zs):
            up_bias[0:1, t * ff_rows : (t + 1) * ff_rows] = small_z[t, 8:9, 0:ff_rows]
        ex_wq_z.wait()
        ga_wq.send()
        ga_small.relay()
        ga_wq.relay()

        def d_of(q, t):
            hq = q // cores // seqs * cores + q % cores
            return hq * ss + t * seqs + q // cores % seqs

        ga_small.wait()
        prm[...] = jnp.zeros_like(prm)
        for q in range(ps):
            for t in range(zs):
                d = d_of(q, t)
                prm[0:8, d * rows : (d + 1) * rows] = small_g[q, t, 0:8, 0:rows]
                at = (d * rows) % tw
                triple = (d * rows) // tw
                prm[8 + triple : 9 + triple, at : at + rows] = small_g[q, t, 3:4, 0:rows]
                prm[8 + triple : 9 + triple, 2 * tw + at : 2 * tw + at + rows] = small_g[q, t, 4:5, 0:rows]

        def assemble(src, dst):
            def one(i):
                hq = i // zs
                q = hq // cores * seqs * cores + lax.rem(hq, cores)
                t = lax.rem(i, zs)
                dst[aligned(i, pair), :] = jnp.concatenate(
                    [src(q, t).astype(f32), src(q + cores, t).astype(f32)], axis=0
                ).astype(bf16)

            loop(0, width // pair, one)

        ga_wq.wait()
        assemble(lambda a, b: wqg[a, b], wq)

        def first_norm(i):
            xv = xg[pl.ds(2 * i, 2)].reshape(2 * sl, width).astype(f32)
            normed, inverse = norm_parts(xv)
            return normed, (normed * prm[0:1, :] + prm[2:3, :]).astype(bf16)

        for i in range(zs):
            for q in (2 * i, 2 * i + 1):
                @pl.when(s != q)
                def _(q=q):
                    ex_x.into(q).wait_recv()

            _, first = first_norm(i)
            at = slice(i * 2 * sl, (i + 1) * 2 * sl)
            projected = nn(first, wq[...]) + prm[pl.ds(8 + z, 1), 0 : 3 * tw]
            q_s[at, :] = (projected[:, 0:tw] * scale).astype(bf16)
            turned = projected[:, tw:].T.astype(bf16)
            kvg[h, 0, :, at] = turned[0:tw, :]
            kvg[h, 1, :, at] = turned[tw : 2 * tw, :]
            ga_kv[i].send()
        ex_wf_p.wait()
        ex_wf_z.send()
        ex_wp_z.send()
        for i in range(zs):
            ga_kv[i].relay()
        ex_wo_z.wait()
        ga_wo.send()
        for i in range(zs):
            ga_kv[i].wait()

        lane_head = lax.broadcasted_iota(jnp.int32, (query_block, tw), 1) // HEAD_DIM

        def attend(step):
            n = step // blocks
            i = lax.rem(step, blocks)
            at = aligned(i, query_block)
            lane_own = lane_head == n
            queries = q_s[at, :]
            masked = jnp.where(lane_own, queries, jnp.zeros_like(queries))
            for b in range(hs):
                s_scr[:, b * qn : (b + 1) * qn] = nn(masked, kvg[b, 0])

            def soft(r):
                rat = aligned(r, chunk)
                sv = [s_scr[rat, b * qn : (b + 1) * qn] + kneg[b] for b in range(hs)]
                top = jnp.max(functools.reduce(jnp.maximum, sv), axis=-1, keepdims=True)
                ev = [jnp.exp(v - top) for v in sv]
                inv = 1.0 / jnp.sum(functools.reduce(jnp.add, ev), axis=-1, keepdims=True)
                for b in range(hs):
                    value = ev[b] * inv
                    probs[n, i, rat, b * qn : (b + 1) * qn] = value
                    pb_scr[rat, b * qn : (b + 1) * qn] = value.astype(bf16)

            loop(0, query_block // chunk, soft, unroll=4)
            head_out = nt(pb_scr[:, 0:qn], kvg[0, 1])
            for b in range(1, hs):
                head_out = head_out + nt(pb_scr[:, b * qn : (b + 1) * qn], kvg[b, 1])
            o_s[at, :] = jnp.where(lane_own, head_out.astype(bf16), o_s[at, :])

        o_s[...] = jnp.zeros_like(o_s)
        loop(0, heads * blocks - 1, attend)
        ga_wo.relay()
        ga_go.send()
        loop(heads * blocks - 1, heads * blocks, attend)

        def lay_out(q):
            o_st[q] = o_s[aligned(q, sl), :]

        loop(0, ss, lay_out)
        ex_o.send()
        og[y, z] = o_st[s]

        ga_wo.wait()
        assemble(lambda a, b: wog[a, b], wo)
        ex_o.wait()
        branch = jnp.broadcast_to(prm[5:6, :], (home, width))
        for t in range(zs):
            mixed = og[:, t].reshape(home, tw)
            branch = branch + nn(mixed, wo[t * tw : (t + 1) * tw, :])
        middle = x_ref[...].reshape(home, width).astype(f32) + branch
        normed, _ = norm_parts(middle)
        x2g[p] = (normed * prm[1:2, :] + prm[6:7, :]).astype(bf16)
        ga_x2.send(rs - 1)
        branch_s[...] = branch
        middle_s[...] = middle
        ex_wp_z.wait()
        ex_wf_z.wait()
        assemble(lambda a, b: wfg[b, a], wf)

        def feed(k, running):
            r = ga_x2.peer(k)

            @pl.when(k > 0)
            def _():
                ga_go.relay_from(k)
                ga_x2.relay_from(k)

            ga_go.wait_from(k)
            ga_x2.wait_from(k)
            at = aligned(r, duo)
            chip = pl.ds(cores * r, cores)
            hid = nn(x2g[chip].reshape(duo, width), wf[...]) + up_bias[0:1, :]
            gate = 1.0 / (1.0 + jnp.exp(-quick_slope * hid))
            act[at, :] = (hid * gate).astype(bf16)
            flow = nt(gog[chip].reshape(duo, width), wpg[...].reshape(part, width))
            slope = gate + quick_slope * hid * gate * (1.0 - gate)
            back = (flow * slope).astype(bf16)
            gh[at, :] = back
            gs_st[chip] = nt(back, wf[...]).astype(bf16).reshape(cores, home, width)
            re_gs.aside(r).start()

            @pl.when(k == 0)
            def _():
                ga_x2.send_last()

            @pl.when(k > 1)
            def _():
                re_gs.combine_out(k - 1)

            return running + jnp.sum(back.astype(f32), axis=0, keepdims=True)

        grad_up = lax.fori_loop(0, rs, feed, jnp.zeros((1, part), f32))

        def turn_act(q):
            at = aligned(q, home)
            x2t[0:part, at] = act[at, :].T

        loop(0, ps, turn_act)
        re_gs.combine_out(rs - 1)
        re_gs.combine(r_at)

        def proj_grad(c):
            wps[c] = nn(x2t[aligned(c, ff_rows), :], gog[...].reshape(slab, width)).astype(bf16)

        loop(0, zs, proj_grad)
        ex_gp_z.send()
        wpr[z] = wps[z]

        def feed_down(r):
            chip = pl.ds(cores * r, cores)
            fd_st[chip] = nn(act[aligned(r, duo), :], wpg[...].reshape(part, width)).astype(bf16).reshape(
                cores, home, width
            )
            re_fd.aside(r).start()

        loop(0, rs, feed_down)
        for t in range(zs):
            x2t[t * tw : (t + 1) * tw, 0:home] = og[:, t].reshape(home, tw).T
        grad_final = go_ref[...].reshape(home, width).astype(f32) * keep

        re_gs.wait()

        def landed_sum(re, own):
            total = own
            for k in range(1, rs):
                total = total + re.landed(re.peer(k))[...].astype(f32)
            return total

        grad_second = landed_sum(re_gs, gs_out[r_at].astype(f32))
        n2, r2 = norm_parts(middle_s[...])
        grad_middle = grad_final + norm_backward(grad_second * prm[1:2, :], n2, r2)
        grad_branch = grad_middle.astype(bf16)
        for t in range(zs):
            do_st[t] = nt(grad_branch, wo[t * tw : (t + 1) * tw, :]).astype(bf16).reshape(seqs, sl, tw)
        ex_do.send()
        dog[s] = do_st[z, y]
        gm_s[...] = grad_middle
        arg[p] = jnp.zeros((16, width), f32)
        arg[p, 1:2, :] = jnp.sum(grad_second * n2, axis=0, keepdims=True)
        arg[p, 6:7, :] = jnp.sum(grad_second, axis=0, keepdims=True)
        arg[p, 5:6, :] = jnp.sum(grad_branch.astype(f32), axis=0, keepdims=True)

        re_fd.send()

        def scatter_rows(c, val, put):
            for j in range(4):
                d = c * 4 + j
                hq = d // ss
                sd = lax.rem(d, ss)
                q = (hq // cores * seqs + lax.rem(sd, seqs)) * cores + lax.rem(hq, cores)
                put(q, sd // seqs, val[j * rows : (j + 1) * rows, :].astype(bf16))

        def out_grad(c):
            def put(q, t, value):
                wos[q, t] = value

            scatter_rows(c, nn(x2t[aligned(c, quad), 0:home], gm_s[...].astype(bf16)), put)

        loop(0, width // quad, out_grad)
        re_wo.send_aside()

        def turn_in(q):
            x2t[:, aligned(q, home)] = x2g[q].T

        loop(0, ps, turn_in)

        def fc_grad(c):
            def put(q, t, value):
                wfs[t, q] = value

            scatter_rows(c, nn(x2t[aligned(c, quad), :], gh[...]), put)

        loop(0, width // quad, fc_grad)

        ex_do.wait()
        ex_gfc_z.send()
        wfr[z] = wfs[z]
        re_wo.send()

        def gather_do(i):
            at = aligned(i, 2 * sl)
            value = dog[pl.ds(2 * i, 2)].reshape(2 * sl, tw)
            o_s[at, :] = value
            dot_s[:, at] = value.T
            qt_s[:, at] = q_s[at, :].T

        loop(0, ss // 2, gather_do)
        dq_s[...] = jnp.zeros_like(dq_s)

        for n in range(heads):
            lane_own = lane_head == n
            head_rows = slice(n * HEAD_DIM, (n + 1) * HEAD_DIM)

            def back(i, n=n, lane_own=lane_own, head_rows=head_rows):
                at = aligned(i, query_block)
                outer = o_s[at, :]
                masked = jnp.where(lane_own, outer, jnp.zeros_like(outer))
                for b in range(hs):
                    s_scr[:, b * qn : (b + 1) * qn] = nn(masked, kvg[b, 1])

                def soft(r):
                    rat = aligned(r, chunk)
                    dp = [s_scr[rat, b * qn : (b + 1) * qn] for b in range(hs)]
                    pv = [probs[n, i, rat, b * qn : (b + 1) * qn] for b in range(hs)]
                    delta = jnp.sum(
                        functools.reduce(jnp.add, [a * c for a, c in zip(dp, pv)]),
                        axis=-1, keepdims=True,
                    )
                    for b in range(hs):
                        ds_scr[rat, b * qn : (b + 1) * qn] = (pv[b] * (dp[b] - delta)).astype(bf16)
                        pb_scr[rat, b * qn : (b + 1) * qn] = pv[b].astype(bf16)

                loop(0, query_block // chunk, soft, unroll=4)
                head_dq = nt(ds_scr[:, 0:qn], kvg[0, 0])
                for b in range(1, hs):
                    head_dq = head_dq + nt(ds_scr[:, b * qn : (b + 1) * qn], kvg[b, 0])
                dq_s[at, :] = jnp.where(lane_own, (head_dq.astype(bf16).astype(f32) * scale).astype(bf16), dq_s[at, :])
                for b in range(hs):
                    dkt[b] = dkt[b] + nn(qt_s[head_rows, at], ds_scr[:, b * qn : (b + 1) * qn])
                    dvt[b] = dvt[b] + nn(dot_s[head_rows, at], pb_scr[:, b * qn : (b + 1) * qn])

            dkt[...] = jnp.zeros_like(dkt)
            dvt[...] = jnp.zeros_like(dvt)
            loop(0, blocks, back)
            for b in range(hs):
                kv_st[n, b, 0] = dkt[b].astype(bf16)
                kv_st[n, b, 1] = dvt[b].astype(bf16)
            re_kv[n].send_aside()
            if n:
                re_kv[n - 1].send()
        re_kv[heads - 1].send()

        gpt[0:tw, :] = dq_s[...].T
        for n in range(heads):
            re_kv[n].wait()
            for k in range(2):
                at = (1 + k) * tw + n * HEAD_DIM
                gpt[at : at + HEAD_DIM, :] = (
                    kv_out[n, x_at, k].astype(f32) + kv_red[n, re_kv[n].peer(1), k].astype(f32)
                ).astype(bf16)
        gp[...] = gpt[...].T

        gain_sum = jnp.zeros((1, width), f32)
        shift_sum = jnp.zeros((1, width), f32)
        for k in range(zs):
            i = lax.rem(z + 1 + k, zs)
            at = aligned(i, 2 * sl)
            value = nt(gp[at, :], wq[...])
            gf_st[pl.ds(2 * i, 2)] = value.astype(bf16).reshape(2, sl, width)
            for q in (2 * i, 2 * i + 1):
                if k < zs - 1:
                    ex_gf.out(q).start()
                else:
                    @pl.when(s != q)
                    def _(q=q):
                        ex_gf.out(q).start()
            normed, first = first_norm(i)
            x2t[:, at] = first.T
            gain_sum = gain_sum + jnp.sum(value * normed, axis=0, keepdims=True)
            shift_sum = shift_sum + jnp.sum(value, axis=0, keepdims=True)
        gfg[y, z] = gf_st[s]

        def qkv_grad(c):
            def put(q, t, value):
                wqs[q, t] = value

            scatter_rows(c, nn(x2t[aligned(c, quad), 0:qn], gp[...]), put)

        loop(0, width // quad, qkv_grad)
        re_wq.send_aside()
        arg[p, 0:1, :] = gain_sum
        arg[p, 2:3, :] = shift_sum
        arg[p, pl.ds(9 + z, 1), 0 : 3 * tw] = jnp.sum(gp[...].astype(f32), axis=0, keepdims=True)
        arg[p, 7:8, :] = jnp.sum(gog[p].astype(f32), axis=0, keepdims=True)
        re_wq.send()

        re_fd.wait()
        feed_out = landed_sum(re_fd, fd_out[r_at].astype(f32)) + prm[7:8, :]
        final = middle_s[...] + feed_out
        out_ref[...] = (final * keep).astype(bf16).reshape(seqs, sl, width)
        xv = x_ref[...].reshape(home, width).astype(f32)
        br = branch_s[...]
        for row, value in ((3, xv), (4, br), (13, feed_out), (14, final)):
            arg[p, row : row + 1, :] = jnp.sum(keep * value * value, axis=0, keepdims=True)
        ga_ar.send()

        ex_gfc_z.wait()

        def fc_sum(q):
            wfz[q] = functools.reduce(jnp.add, [wfr[t, q].astype(f32) for t in range(zs)]).astype(bf16)

        loop(0, ps, fc_sum)
        ex_gfc_p.send()
        wfzr[p] = wfz[p]
        ex_gp_z.wait()
        gproj_ref[...] = functools.reduce(jnp.add, [wpr[t].astype(f32) for t in range(zs)])

        def final_rows(re, out, landed, dst):
            def one(t):
                total = out[r_at, t].astype(f32)
                for k in range(1, rs):
                    total = total + landed[re.peer(k), t].astype(f32)
                dst[t] = total.astype(bf16)

            loop(0, zs, one)

        re_wo.wait()
        final_rows(re_wo, wo_out, wo_red, woz)
        ex_go_z.send()
        wozr[z] = woz[z]
        re_wq.wait()
        final_rows(re_wq, wq_out, wq_red, wqz)
        ex_gq_z.send()
        wqzr[z] = wqz[z]
        ga_ar.relay()
        ga_ar.wait()
        total = functools.reduce(jnp.add, [arg[q] for q in range(ps)])
        sums[...] = total
        for t in range(zs):
            sums[3:4, t * tw : (t + 1) * tw] = total[9 + t : 10 + t, 0:tw]
            sums[4:5, t * tw : (t + 1) * tw] = total[9 + t : 10 + t, 2 * tw : 3 * tw]
        place = lax.broadcasted_iota(jnp.int32, (1, 128), 1)
        squares = jnp.zeros((1, 128), f32)
        for k, row in enumerate((3, 4, 13, 14)):
            squares = squares + jnp.where(
                place == k, jnp.sum(total[row : row + 1, :], axis=1, keepdims=True), 0.0
            )
        for t in range(zs):
            back_by = lax.rem(width - (h * ss + t * seqs + y) * rows, width)
            ar_st[t, 0:8, :] = pltpu.roll(sums[0:8, :], back_by, 1)[:, 0:128]
            ar_st[t, 8:9, 0:ff_rows] = grad_up[:, t * ff_rows : (t + 1) * ff_rows]
            ar_st[t, 9:10, :] = squares
        ex_ar_z.send()
        arz[z] = ar_st[z]

        ex_gf.wait()
        grad_first = functools.reduce(jnp.add, [gfg[:, t].astype(f32) for t in range(zs)]).reshape(home, width)
        n1, r1 = norm_parts(x_ref[...].reshape(home, width).astype(f32))
        grad_in = gm_s[...] + norm_backward(grad_first * prm[0:1, :], n1, r1)
        gin_ref[...] = grad_in.reshape(seqs, sl, width)

        ex_gfc_p.wait()
        gfc_ref[...] = wfzr[...].astype(f32)
        ex_gq_z.wait()
        gqkv_ref[...] = wqzr[...].astype(f32)
        ex_ar_z.wait()
        ar_ref[...] = functools.reduce(jnp.add, [arz[t] for t in range(zs)])
        ex_go_z.wait()
        gout_ref[...] = functools.reduce(jnp.add, [wozr[t].astype(f32) for t in range(zs)])

        for ex in (
            ex_small_z, ex_wq_z, ex_wo_z, ex_x, ga_small, ga_wq, ga_wo, ex_wf_p, ex_wf_z, ex_wp_z,
            ga_go, *ga_kv, ex_o, re_gs, re_fd, ex_do, *re_kv, ex_gf, re_wo, ex_go_z, re_wq, ex_gq_z,
            ex_gfc_z, ex_gfc_p, ex_gp_z, ga_ar, ex_ar_z,
        ):
            ex.drain()
        ga_x2.drain(rs - 1)

    vm = pltpu.VMEM
    scratch = [
        vm((16, 128), f32),
        vm((zs, 16, 128), f32),
        vm((ps, zs, 16, 128), f32),
        vm((16, width), f32),
        vm((8, part), f32),
        vm((zs, rows, 3 * tw), bf16),
        vm((ps, rows, part), bf16),
        vm((ps, zs, rows, 3 * tw), bf16),
        vm((ps, zs, rows, width), bf16),
        vm((zs, ps, rows, part), bf16),
        vm((zs, ff_rows, width), bf16),
        vm((width, 3 * tw), bf16),
        vm((width, width), bf16),
        vm((width, part), bf16),
        vm((ss, sl, width), bf16),
        vm((qn, tw), bf16),
        vm((hs, 2, tw, qn), bf16),
        vm((hs, chunk, qn), f32),
        vm((heads, blocks, query_block, hs * qn), f32),
        vm((query_block, hs * qn), f32),
        vm((query_block, hs * qn), bf16),
        vm((query_block, hs * qn), bf16),
        vm((qn, tw), bf16),
        vm((ss, sl, tw), bf16),
        vm((seqs, zs, sl, tw), bf16),
        vm((home, width), f32),
        vm((home, width), f32),
        vm((home, width), f32),
        vm((ps, home, width), bf16),
        vm((ps, home, width), bf16),
        vm((slab, part), bf16),
        vm((slab, part), bf16),
        vm((width, slab), bf16),
        vm((ps, home, width), bf16),
        vm((rs, home, width), bf16),
        vm((rs, home, width), bf16),
        vm((rs, home, width), bf16),
        vm((ps, home, width), bf16),
        vm((rs, home, width), bf16),
        vm((rs, home, width), bf16),
        vm((rs, home, width), bf16),
        vm((zs, seqs, sl, tw), bf16),
        vm((ss, sl, tw), bf16),
        vm((tw, qn), bf16),
        vm((tw, qn), bf16),
        vm((qn, tw), bf16),
        vm((hs, HEAD_DIM, qn), f32),
        vm((hs, HEAD_DIM, qn), f32),
        vm((heads, hs, 2, HEAD_DIM, qn), bf16),
        vm((heads, xs, 2, HEAD_DIM, qn), bf16),
        vm((heads, xs, 2, HEAD_DIM, qn), bf16),
        vm((heads, xs, 2, HEAD_DIM, qn), bf16),
        vm((3 * tw, qn), bf16),
        vm((qn, 3 * tw), bf16),
        vm((ss, sl, width), bf16),
        vm((seqs, zs, sl, width), bf16),
        vm((ps, zs, rows, width), bf16),
        vm((rs, zs, rows, width), bf16),
        vm((rs, zs, rows, width), bf16),
        vm((rs, zs, rows, width), bf16),
        vm((zs, rows, width), bf16),
        vm((zs, rows, width), bf16),
        vm((ps, zs, rows, 3 * tw), bf16),
        vm((rs, zs, rows, 3 * tw), bf16),
        vm((rs, zs, rows, 3 * tw), bf16),
        vm((rs, zs, rows, 3 * tw), bf16),
        vm((zs, rows, 3 * tw), bf16),
        vm((zs, rows, 3 * tw), bf16),
        vm((zs, ps, rows, part), bf16),
        vm((zs, ps, rows, part), bf16),
        vm((ps, rows, part), bf16),
        vm((ps, rows, part), bf16),
        vm((zs, ff_rows, width), bf16),
        vm((zs, ff_rows, width), bf16),
        vm((ps, 16, width), f32),
        vm((16, width), f32),
        vm((zs, 16, 128), f32),
        vm((zs, 16, 128), f32),
        pltpu.SemaphoreType.DMA((26,)),
        pltpu.SemaphoreType.DMA((10, zs)),
        pltpu.SemaphoreType.DMA((4, ss)),
        pltpu.SemaphoreType.DMA((2, ps)),
        pltpu.SemaphoreType.DMA((6, ps)),
        pltpu.SemaphoreType.DMA((7, 2, rs)),
        pltpu.SemaphoreType.DMA((zs, hs)),
        pltpu.SemaphoreType.DMA((heads, 2, xs)),
        pltpu.SemaphoreType.DMA((7, 2)),
    ]
    in_vmem = pl.BlockSpec(memory_space=pltpu.VMEM)
    in_smem = pl.BlockSpec(memory_space=pltpu.SMEM)
    results = pl.pallas_call(
        kernel,
        out_shape=(
            jax.ShapeDtypeStruct((seqs, sl, width), bf16),
            jax.ShapeDtypeStruct((seqs, sl, width), f32),
            jax.ShapeDtypeStruct((zs, rows, 3 * tw), f32),
            jax.ShapeDtypeStruct((rows, width), f32),
            jax.ShapeDtypeStruct((ps, rows, part), f32),
            jax.ShapeDtypeStruct((ff_rows, width), f32),
            jax.ShapeDtypeStruct((16, 128), f32),
        ),
        in_specs=[in_smem] + [in_vmem] * 9,
        out_specs=(in_vmem,) * 7,
        scratch_shapes=scratch,
        compiler_params=pltpu.CompilerParams(
            collective_id=0, has_side_effects=True, vmem_limit_bytes=63 * 1024 * 1024
        ),
        name="layer",
    )(
        lengths,
        layer_input.reshape(seqs, sl, width),
        grad_out.reshape(seqs, sl, width),
        w_qkv,
        w_out,
        w_fc,
        w_proj,
        b_fc.reshape(1, ff_rows),
        norm_gains,
        biases,
    )

    def finish(
        len_ref, a_out, a_gin, a_gqkv, a_gout, a_gfc, a_gproj, sums,
        out_ref, gin_ref, gqkv_ref, gout_ref, gfc_ref, gproj_ref, gup_ref, ggain_ref, gbias_ref, rms_ref,
    ):
        out_ref[...] = a_out[...]
        gin_ref[...] = a_gin[...]
        gout_ref[...] = a_gout[...]
        gproj_ref[...] = a_gproj[...]
        for t in range(zs):
            for k in range(3):
                gqkv_ref[:, k * width + t * tw : k * width + (t + 1) * tw] = a_gqkv[t, :, k * tw : (k + 1) * tw]
        for q in range(ps):
            hq = q // cores // seqs * cores + q % cores
            yq = q // cores % seqs
            for t in range(zs):
                at = ((hq * zs + t) * seqs + yq) * ff_rows
                gfc_ref[:, at : at + ff_rows] = a_gfc[q, :, t * ff_rows : (t + 1) * ff_rows]
        ggain_ref[...] = sums[0:2, 0:rows]
        gbias_ref[...] = sums[2:8, 0:rows]
        gup_ref[...] = sums[8:9, 0:ff_rows]
        valid = (len_ref[0] + len_ref[1]).astype(f32) * width
        rms_ref[...] = jnp.sqrt(sums[9:10, 0:4] / valid)

    final = pl.pallas_call(
        finish,
        out_shape=(
            jax.ShapeDtypeStruct((seqs, sl, width), bf16),
            jax.ShapeDtypeStruct((seqs, sl, width), f32),
            jax.ShapeDtypeStruct((rows, 3 * width), f32),
            jax.ShapeDtypeStruct((rows, width), f32),
            jax.ShapeDtypeStruct((rows, ps * part), f32),
            jax.ShapeDtypeStruct((ff_rows, width), f32),
            jax.ShapeDtypeStruct((1, ff_rows), f32),
            jax.ShapeDtypeStruct((2, rows), f32),
            jax.ShapeDtypeStruct((6, rows), f32),
            jax.ShapeDtypeStruct((1, 4), f32),
        ),
        in_specs=[in_smem] + [in_vmem] * 7,
        out_specs=(in_vmem,) * 10,
        name="finish",
    )(lengths, *results)
    return (
        final[0].reshape(layer_input.shape),
        final[1].reshape(layer_input.shape),
        *final[2:6],
        final[6].reshape(ff_rows),
        final[7],
        final[8],
        final[9].reshape(4),
    )


def fits(seqs, sl, width, hs, ss, qkv_rows):
    if seqs != 2 or ss % seqs or hs % cores:
        return False
    zs = ss // seqs
    if width % zs or (width // zs) % HEAD_DIM or zs > 4 or qkv_rows % 8:
        return False
    tw = width // zs
    keys = ss * sl * hs
    return tw <= 256 and keys * ss * sl * (tw // HEAD_DIM) * 4 <= 16 * 1024 * 1024


def on_device(layer_input, grad_out, lengths, w_qkv, w_out, w_fc, w_proj, b_fc, norm_gains, biases):
    seqs, _, sl, width = layer_input.shape
    hs, ss = lax.axis_size("head"), lax.axis_size("seq")
    chosen = fused_layer if fits(seqs, sl, width, hs, ss, w_qkv.shape[0]) else spread_layer
    return chosen(
        layer_input, grad_out, lengths, w_qkv, w_out, w_fc, w_proj, b_fc, norm_gains, biases
    )


def solution(mesh):
    return jax.shard_map(
        on_device,
        mesh=mesh,
        in_specs=(
            P(None, "seq", "head", None),
            P(None, "seq", "head", None),
            P(),
            P(("head", "seq"), None),
            P(("head", "seq"), None),
            P(("head", "seq"), None),
            P(("head", "seq"), None),
            P(("head", "seq")),
            P(None, ("head", "seq")),
            P(None, ("head", "seq")),
        ),
        out_specs=(
            P(None, "seq", "head", None),
            P(None, "seq", "head", None),
            P(("head", "seq"), None),
            P(("head", "seq"), None),
            P(("head", "seq"), None),
            P(("head", "seq"), None),
            P(("head", "seq")),
            P(None, ("head", "seq")),
            P(None, ("head", "seq")),
            P(),
        ),
        check_vma=False,
    )
```

```python
import functools

import jax
import jax.numpy as jnp
from jax import lax
from jax.sharding import PartitionSpec as P
from jax.experimental import pallas as pl
from jax.experimental.pallas import tpu as pltpu

HEAD_DIM = 64


masked_score = -1e30
block_keys = 512
quick_slope = 1.702
epsilon = 1e-05


def layer_norm_parts(inputs):
    centre = inputs - jnp.mean(inputs, axis=-1, keepdims=True)
    inverse = lax.rsqrt(jnp.mean(centre * centre, axis=-1, keepdims=True) + epsilon)
    return (centre * inverse, inverse)


def norm_backward(grad_normed, normed, inverse):
    return inverse * (
        grad_normed
        - jnp.mean(grad_normed, axis=-1, keepdims=True)
        - normed * jnp.mean(grad_normed * normed, axis=-1, keepdims=True)
    )


def split_heads(piece_block):
    return piece_block.reshape(
        piece_block.shape[0], piece_block.shape[1], piece_block.shape[2] // HEAD_DIM, HEAD_DIM
    )


def head_scores(left_side, right_side):
    return jnp.einsum("sqhd,skhd->shqk", left_side, right_side, preferred_element_type=jnp.float32)


def weighted(probabilities, right_side):
    return jnp.einsum(
        "shqk,skhd->sqhd", probabilities, right_side, preferred_element_type=jnp.float32
    )


def transposed(probabilities, right_side):
    return jnp.einsum(
        "shqk,sqhd->skhd", probabilities, right_side, preferred_element_type=jnp.float32
    )


def over_blocks(step_fn, running, pieces):
    extent = pieces[0].shape[1]
    number = extent // block_keys
    parted = tuple(
        (
            piece_part.reshape(
                (piece_part.shape[0], number, block_keys) + piece_part.shape[2:]
            ).swapaxes(0, 1)
            for piece_part in pieces
        )
    )

    def advance(inner_run, element):
        position, blocks = element
        return (step_fn(inner_run, blocks, position * block_keys), None)

    return lax.scan(advance, running, (jnp.arange(number, dtype=jnp.int32), parted))[0]


def spread_layer(layer_input, grad_out, lengths, w_qkv, w_out, w_fc, w_proj, b_fc, norm_gains, biases):
    sequences = layer_input.shape[0]
    slice_len = layer_input.shape[2]
    model_width = layer_input.shape[3]
    head_ways = lax.axis_size("head")
    group_len = slice_len * head_ways
    local_width = model_width // head_ways
    head_count = local_width // HEAD_DIM
    head_place = lax.axis_index("head")
    cycle_place = lax.axis_index("seq")
    flat_rows = sequences * slice_len
    full_qkv, full_out, full_fc, full_proj, full_bias_fc, full_gains, full_biases = (
        lax.all_gather(w_qkv, ("head", "seq"), axis=0, tiled=True),
        lax.all_gather(w_out, ("head", "seq"), axis=0, tiled=True),
        lax.all_gather(w_fc, ("head", "seq"), axis=0, tiled=True),
        lax.all_gather(w_proj, ("head", "seq"), axis=0, tiled=True),
        lax.all_gather(b_fc, ("head", "seq"), axis=0, tiled=True),
        lax.all_gather(norm_gains, ("head", "seq"), axis=1, tiled=True),
        lax.all_gather(biases, ("head", "seq"), axis=1, tiled=True),
    )
    gain_vals = full_gains.astype(jnp.float32)
    shift_vals = full_biases.astype(jnp.float32)
    bias_up = full_bias_fc.astype(jnp.float32)
    token_places = (
        cycle_place * group_len + head_place * slice_len + jnp.arange(slice_len, dtype=jnp.int32)
    )
    token_keep = (
        (token_places[None, :] < lengths[:, None]).astype(jnp.float32).reshape(flat_rows, 1)
    )
    own_places = cycle_place * group_len + jnp.arange(group_len, dtype=jnp.int32)
    own_allowed = (own_places[None, :] < lengths[:, None])[:, None, None, :]

    def allowed_at(offset, extent):
        places = offset + jnp.arange(extent, dtype=jnp.int32)
        return (places[None, :] < lengths[:, None])[:, None, None, :]

    inputs = layer_input.reshape(flat_rows, model_width).astype(jnp.float32)
    normed_one, inverse_one = layer_norm_parts(inputs)
    first_in = (normed_one * gain_vals[0] + shift_vals[0]).astype(jnp.bfloat16)
    projected = jnp.dot(first_in, full_qkv, preferred_element_type=jnp.float32)
    query_scale = HEAD_DIM ** (-0.5)
    queries = ((projected[:, :model_width] + shift_vals[1]) * query_scale).astype(jnp.bfloat16)
    keys_new = projected[:, model_width : 2 * model_width].astype(jnp.bfloat16)
    values_new = (projected[:, 2 * model_width :] + shift_vals[2]).astype(jnp.bfloat16)
    packed = jnp.stack([queries, keys_new, values_new], axis=1).reshape(
        sequences, slice_len, 3, head_ways, local_width
    )
    spread = lax.all_to_all(packed, "head", split_axis=3, concat_axis=1, tiled=True)
    query_block = spread[:, :, 0, 0]
    key_block = spread[:, :, 1, 0]
    value_block = spread[:, :, 2, 0]
    query_heads = split_heads(query_block)
    key_heads = split_heads(key_block)
    value_heads = split_heads(value_block)

    def maxima_step(running, pieces, offset):
        highest, denominator = running
        scores = head_scores(query_heads, split_heads(pieces[0]))
        allowed = allowed_at(offset, pieces[0].shape[1])
        scores = jnp.where(allowed, scores, masked_score)
        raised = jnp.maximum(highest, jnp.max(scores, axis=-1))
        weights = jnp.where(allowed, jnp.exp(scores - raised[..., None]), 0.0)
        denominator = denominator * jnp.exp(highest - raised) + jnp.sum(weights, axis=-1)
        return (raised, denominator)

    zero_rows = jnp.zeros((sequences, head_count, group_len), jnp.float32)
    highest, denominator = over_blocks(
        maxima_step,
        (zero_rows + masked_score, zero_rows),
        (lax.all_gather(key_block, "seq", axis=1, tiled=True),),
    )
    log_total = highest + jnp.log(denominator)

    def attention_weights(key_piece, offset):
        scores = head_scores(query_heads, key_piece)
        allowed = allowed_at(offset, key_piece.shape[1])
        return jnp.where(
            allowed, jnp.exp(jnp.where(allowed, scores, masked_score) - log_total[..., None]), 0.0
        )

    zero_heads = jnp.zeros((sequences, group_len, head_count, HEAD_DIM), jnp.float32)

    def output_step(running, pieces, offset):
        probabilities = attention_weights(split_heads(pieces[0]), offset)
        return running + weighted(probabilities.astype(jnp.bfloat16), split_heads(pieces[1]))

    attended = over_blocks(
        output_step,
        zero_heads,
        (
            lax.all_gather(key_block, "seq", axis=1, tiled=True),
            lax.all_gather(value_block, "seq", axis=1, tiled=True),
        ),
    )
    mixed_heads = attended.astype(jnp.bfloat16).reshape(
        sequences, head_ways, slice_len, local_width
    )
    gathered_out = lax.all_to_all(mixed_heads, "head", split_axis=1, concat_axis=3, tiled=True)
    mixed_rows = gathered_out.reshape(flat_rows, model_width)
    branch = jnp.dot(mixed_rows, full_out, preferred_element_type=jnp.float32) + shift_vals[3]
    middle = inputs + branch
    normed_two, inverse_two = layer_norm_parts(middle)
    second_in = (normed_two * gain_vals[1] + shift_vals[4]).astype(jnp.bfloat16)
    hidden = jnp.dot(second_in, full_fc, preferred_element_type=jnp.float32) + bias_up
    gate_sig = jax.nn.sigmoid(quick_slope * hidden)
    activated = (hidden * gate_sig).astype(jnp.bfloat16)
    feed_out = jnp.dot(activated, full_proj, preferred_element_type=jnp.float32) + shift_vals[5]
    final_rows = middle + feed_out
    result = (final_rows * token_keep).astype(jnp.bfloat16).reshape(layer_input.shape)
    local_squares = jnp.stack(
        [
            jnp.sum(token_keep * inputs * inputs),
            jnp.sum(token_keep * branch * branch),
            jnp.sum(token_keep * feed_out * feed_out),
            jnp.sum(token_keep * final_rows * final_rows),
        ]
    )
    squares = lax.psum(local_squares, ("head", "seq"))
    valid_count = jnp.sum(lengths).astype(jnp.float32) * model_width
    root_means = jnp.sqrt(squares / valid_count)
    grad_final = grad_out.reshape(flat_rows, model_width).astype(jnp.float32) * token_keep
    grad_feed = grad_final.astype(jnp.bfloat16)
    grad_proj = jnp.dot(activated.T, grad_feed, preferred_element_type=jnp.float32)
    grad_shift_proj = jnp.sum(grad_feed.astype(jnp.float32), axis=0)
    grad_act = jnp.dot(grad_feed, full_proj.T, preferred_element_type=jnp.float32)
    grad_hidden = (
        grad_act * (gate_sig + quick_slope * hidden * gate_sig * (1.0 - gate_sig))
    ).astype(jnp.bfloat16)
    grad_fc = jnp.dot(second_in.T, grad_hidden, preferred_element_type=jnp.float32)
    grad_bias_up = jnp.sum(grad_hidden.astype(jnp.float32), axis=0)
    grad_second = jnp.dot(grad_hidden, full_fc.T, preferred_element_type=jnp.float32)
    grad_gain_two = jnp.sum(grad_second * normed_two, axis=0)
    grad_shift_two = jnp.sum(grad_second, axis=0)
    grad_middle = grad_final + norm_backward(grad_second * gain_vals[1], normed_two, inverse_two)
    grad_branch = grad_middle.astype(jnp.bfloat16)
    grad_out_weight = jnp.dot(mixed_rows.T, grad_branch, preferred_element_type=jnp.float32)
    grad_shift_out = jnp.sum(grad_branch.astype(jnp.float32), axis=0)
    grad_mixed = jnp.dot(grad_branch, full_out.T, preferred_element_type=jnp.float32).astype(
        jnp.bfloat16
    )
    grad_spread = lax.all_to_all(
        grad_mixed.reshape(sequences, slice_len, head_ways, local_width),
        "head",
        split_axis=2,
        concat_axis=1,
        tiled=True,
    )
    grad_block = grad_spread[:, :, 0]
    grad_heads = split_heads(grad_block)

    def delta_step(running, pieces, offset):
        probabilities = attention_weights(split_heads(pieces[0]), offset)
        grad_probs = head_scores(grad_heads, split_heads(pieces[1]))
        return running + jnp.sum(probabilities * grad_probs, axis=-1)

    row_delta = over_blocks(
        delta_step,
        zero_rows,
        (
            lax.all_gather(key_block, "seq", axis=1, tiled=True),
            lax.all_gather(value_block, "seq", axis=1, tiled=True),
        ),
    )

    def query_step(running, pieces, offset):
        key_piece = split_heads(pieces[0])
        probabilities = attention_weights(key_piece, offset)
        grad_probs = head_scores(grad_heads, split_heads(pieces[1]))
        slopes = (probabilities * (grad_probs - row_delta[..., None])).astype(jnp.bfloat16)
        return running + weighted(slopes, key_piece)

    grad_query = over_blocks(
        query_step,
        zero_heads,
        (
            lax.all_gather(key_block, "seq", axis=1, tiled=True),
            lax.all_gather(value_block, "seq", axis=1, tiled=True),
        ),
    )
    all_logs, all_deltas = (
        lax.all_gather(log_total.transpose(0, 2, 1), "seq", axis=1, tiled=True),
        lax.all_gather(row_delta.transpose(0, 2, 1), "seq", axis=1, tiled=True),
    )

    def key_step(running, pieces, offset):
        query_piece = split_heads(pieces[0])
        grad_piece = split_heads(pieces[1])
        extent = pieces[0].shape[1]
        log_piece = lax.dynamic_slice_in_dim(all_logs, offset, extent, 1).transpose(0, 2, 1)
        delta_piece = lax.dynamic_slice_in_dim(all_deltas, offset, extent, 1).transpose(0, 2, 1)
        scores = head_scores(query_piece, key_heads)
        probabilities = jnp.where(
            own_allowed,
            jnp.exp(jnp.where(own_allowed, scores, masked_score) - log_piece[..., None]),
            0.0,
        )
        grad_value = running[1] + transposed(probabilities.astype(jnp.bfloat16), grad_piece)
        grad_probs = head_scores(grad_piece, value_heads)
        slopes = (probabilities * (grad_probs - delta_piece[..., None])).astype(jnp.bfloat16)
        grad_key = running[0] + transposed(slopes, query_piece)
        return (grad_key, grad_value)

    grad_key, grad_value = over_blocks(
        key_step,
        (zero_heads, zero_heads),
        (
            lax.all_gather(query_block, "seq", axis=1, tiled=True),
            lax.all_gather(grad_block, "seq", axis=1, tiled=True),
        ),
    )
    stacked = jnp.stack([grad_query, grad_key, grad_value], axis=2).astype(jnp.bfloat16)
    stacked = stacked.reshape(sequences, head_ways, slice_len, 3, local_width)
    returned = lax.all_to_all(stacked, "head", split_axis=1, concat_axis=4, tiled=True)
    column_scale = jnp.concatenate(
        [
            jnp.full((model_width,), query_scale, jnp.float32),
            jnp.ones((2 * model_width,), jnp.float32),
        ]
    )
    grad_projected = returned.reshape(flat_rows, 3 * model_width).astype(jnp.float32) * column_scale
    grad_shift_query = jnp.sum(grad_projected[:, :model_width], axis=0)
    grad_shift_value = jnp.sum(grad_projected[:, 2 * model_width :], axis=0)
    grad_projected_low = grad_projected.astype(jnp.bfloat16)
    grad_qkv = jnp.dot(first_in.T, grad_projected_low, preferred_element_type=jnp.float32)
    grad_first = jnp.dot(grad_projected_low, full_qkv.T, preferred_element_type=jnp.float32)
    grad_gain_one = jnp.sum(grad_first * normed_one, axis=0)
    grad_shift_one = jnp.sum(grad_first, axis=0)
    grad_inputs = grad_middle + norm_backward(grad_first * gain_vals[0], normed_one, inverse_one)
    grad_gain_rows = jnp.stack([grad_gain_one, grad_gain_two])
    grad_shift_rows = jnp.stack(
        [
            grad_shift_one,
            grad_shift_query,
            grad_shift_value,
            grad_shift_out,
            grad_shift_two,
            grad_shift_proj,
        ]
    )
    owned_grads = (
        lax.psum_scatter(grad_qkv, ("head", "seq"), scatter_dimension=0, tiled=True),
        lax.psum_scatter(grad_out_weight, ("head", "seq"), scatter_dimension=0, tiled=True),
        lax.psum_scatter(grad_fc, ("head", "seq"), scatter_dimension=0, tiled=True),
        lax.psum_scatter(grad_proj, ("head", "seq"), scatter_dimension=0, tiled=True),
        lax.psum_scatter(grad_bias_up, ("head", "seq"), scatter_dimension=0, tiled=True),
        lax.psum_scatter(grad_gain_rows, ("head", "seq"), scatter_dimension=1, tiled=True),
        lax.psum_scatter(grad_shift_rows, ("head", "seq"), scatter_dimension=1, tiled=True),
    )
    return (
        result,
        grad_inputs.reshape(layer_input.shape),
        owned_grads[0],
        owned_grads[1],
        owned_grads[2],
        owned_grads[3],
        owned_grads[4],
        owned_grads[5],
        owned_grads[6],
        root_means,
    )


f32 = jnp.float32
bf16 = jnp.bfloat16
cores = 2
halves = 2
lanes_per = 128


def nn(left, right):
    return lax.dot_general(left, right, (((1,), (0,)), ((), ())), preferred_element_type=f32)


def nt(left, right):
    return lax.dot_general(left, right, (((1,), (1,)), ((), ())), preferred_element_type=f32)


def loop(low, high, step_fn, unroll=1):
    def advance(index, carry):
        step_fn(index)
        return carry

    lax.fori_loop(low, high, advance, 0, unroll=unroll)


def aligned(index, extent):
    return pl.ds(pl.multiple_of(index * extent, extent), extent)


def norm_parts(v):
    centre = v - jnp.mean(v, axis=-1, keepdims=True)
    inverse = lax.rsqrt(jnp.mean(centre * centre, axis=-1, keepdims=True) + epsilon)
    return centre * inverse, inverse


def remote(src, dst, send_sem, recv_sem, place):
    return pltpu.make_async_remote_copy(
        src_ref=src,
        dst_ref=dst,
        send_sem=send_sem,
        recv_sem=recv_sem,
        device_id=place,
        device_id_type=pl.DeviceIdType.MESH,
    )


def dense(v):
    n = v.shape[0]
    low = v[:, 0:lanes_per]
    rest = v[:, lanes_per:]
    return low, jnp.concatenate([rest[0 : n // 2], rest[n // 2 :]], axis=1)


def loose(low, rest):
    wide = rest.shape[1] // 2
    return jnp.concatenate(
        [low, jnp.concatenate([rest[:, 0:wide], rest[:, wide:]], axis=0)], axis=1
    )


class Exchange:
    def __init__(self, n, me, place, src, dst, send_sem, recv_sem, order=None):
        self.n, self.me, self.place, self.src, self.dst = n, me, place, src, dst
        self.send_sem, self.recv_sem, self.order = send_sem, recv_sem, order

    def out(self, q):
        return remote(
            self.src(q), self.dst(self.me), self.send_sem, self.recv_sem.at[self.me], self.place(q)
        )

    def into(self, q):
        return remote(
            self.dst(q), self.dst(q), self.send_sem, self.recv_sem.at[q], self.place(q)
        )

    def peer(self, k):
        return lax.rem(self.me + k, self.n)

    def send(self, low=0, high=None):
        if self.order is None:
            loop(1, self.n, lambda k: self.out(self.peer(k)).start())
        else:
            for q in self.order[low:high]:
                self.out(q).start()

    def wait(self):
        loop(1, self.n, lambda k: self.into(self.peer(k)).wait_recv())

    def drain(self):
        loop(1, self.n, lambda k: self.out(self.peer(k)).wait_send())


def chip_peer(n, inner, me, k):
    outer = n // inner
    a = lax.rem(me // inner + lax.rem(k, outer), outer)
    b = lax.rem(lax.rem(me, inner) + k // outer, inner)
    return a * inner + b


class Gather:
    def __init__(self, n, inner, me, core, place, dst, send_sem, recv_sem):
        self.n, self.inner, self.me, self.core, self.place, self.dst = n, inner, me, core, place, dst
        self.send_sem, self.recv_sem = send_sem, recv_sem
        self.mine = me * cores + core

    def peer(self, k):
        return chip_peer(self.n, self.inner, self.me, k)

    def move(self, slot, place):
        return remote(
            self.dst(slot), self.dst(slot), self.send_sem, self.recv_sem.at[slot], place
        )

    def out(self, k):
        return self.move(self.mine, self.place(self.peer(k), self.core))

    def aside(self, k):
        return self.move(
            self.peer(k) * cores + self.core, self.place(self.me, 1 - self.core)
        )

    def send(self, last=None):
        loop(1, last or self.n, lambda k: self.out(k).start())
        self.aside(0).start()

    def send_last(self):
        loop(1, self.n - 1, lambda k: self.out(k).wait_send())
        self.out(self.n - 1).start()

    def relay_from(self, k):
        self.out_slot(k, self.core).wait_recv()
        self.aside(k).start()

    def out_slot(self, k, core):
        return self.move(self.peer(k) * cores + core, self.place(self.peer(k), core))

    def wait_from(self, k):
        self.out_slot(k, 1 - self.core).wait_recv()

    def relay(self):
        loop(1, self.n, self.relay_from)

    def wait(self):
        loop(0, self.n, self.wait_from)

    def drain(self, first=1):
        loop(first, self.n, lambda k: self.out(k).wait_send())
        loop(0, self.n, lambda k: self.aside(k).wait_send())


class Reduce:
    def __init__(self, n, inner, me, core, place, stage, beside, landed, sems, recv_sems, add):
        self.n, self.inner, self.me, self.core, self.place = n, inner, me, core, place
        self.stage, self.beside, self.landed = stage, beside, landed
        self.sems, self.recv_sems, self.add = sems, recv_sems, add

    def peer(self, k):
        return chip_peer(self.n, self.inner, self.me, k)

    def own(self, r):
        return self.stage(r * cores + self.core)

    def aside(self, r):
        return remote(
            self.stage(r * cores + 1 - self.core),
            self.beside(r),
            self.sems.at[0],
            self.recv_sems.at[0, r],
            self.place(self.me, 1 - self.core),
        )

    def out(self, r):
        return remote(
            self.own(r),
            self.landed(self.me),
            self.sems.at[1],
            self.recv_sems.at[1, self.me],
            self.place(r, self.core),
        )

    def combine(self, r):
        self.aside(r).wait_recv()
        self.add(self.own(r), self.beside(r))

    def combine_out(self, k):
        r = self.peer(k)
        self.combine(r)
        self.out(r).start()

    def send_aside(self):
        loop(1, self.n, lambda k: self.aside(self.peer(k)).start())
        self.aside(self.me).start()

    def send(self):
        loop(1, self.n, self.combine_out)
        self.combine(self.me)

    def wait(self):
        def one(k):
            r = self.peer(k)
            remote(
                self.landed(r), self.landed(r), self.sems.at[1], self.recv_sems.at[1, r],
                self.place(r, self.core),
            ).wait_recv()

        loop(1, self.n, one)

    def drain_aside(self):
        loop(0, self.n, lambda k: self.aside(self.peer(k)).wait_send())

    def drain(self):
        self.drain_aside()
        loop(1, self.n, lambda k: self.out(self.peer(k)).wait_send())


def fused_layer(layer_input, grad_out, lengths, w_qkv, w_out, w_fc, w_proj, b_fc, norm_gains, biases):
    seqs, _, sl, width = layer_input.shape
    hs = lax.axis_size("head")
    ss = lax.axis_size("seq")
    zs = ss // seqs
    ps = hs * seqs
    xs = hs // cores
    rs = xs * seqs
    group = sl * hs
    tw = width // zs
    heads = tw // HEAD_DIM
    rows = w_qkv.shape[0]
    ff_rows = w_proj.shape[0]
    part = ff_rows * zs
    home = seqs * sl
    qn = ss * sl
    slab = ps * home
    near = zs // halves
    us = near * seqs
    duo = cores * home
    query_block = 256
    blocks = qn // query_block
    chunk = 32
    pair = 2 * rows
    quad = 8 * rows
    scale = HEAD_DIM ** (-0.5)

    def ff_place(q, b):
        u, c = q // cores, q % cores
        head_of = (b // halves) * cores + c
        return head_of * ss + ((b % halves) * near + u // seqs) * seqs + u % seqs

    def kernel(
        len_ref, x_ref, go_ref, wqkv_ref, wout_ref, wfc_ref, wproj_ref, bfc_ref, gain_ref, bias_ref,
        out_ref, gin_ref, gqkv_ref, gout_ref, gfc_ref, gproj_ref, ar_ref,
        small, small_z, small_g, prm, up_bias,
        qkv_st, fc_st, wqg, wog, wfg, wpg, wq, wo, wf,
        xg, q_s, kvg, kneg, probs, s_scr, pb_scr, ds_scr, o_s, o_st, og, mixed_s,
        middle_s, gm_s,
        x2g, gog, act, gh, x2t, gs_st, gs_in, gs_red, fd_st, fd_in, fd_red,
        do_st, dog, dot_s, qt_s, dq_s, dkt, dvt, kv_st, kv_in, kv_red, gpt, gp,
        gf_st, gfg, wos, wo_in, wo_red, woz, wozr, wqs, wq_in, wq_red, wqz, wqzr,
        wfs, wfr, wfm, wfq, wfz, wfzr, wps, wpr, wpm, wpq, arg, ard, sums, ar_st, arz,
        send, zsem, lsem, psem, bsem, gsem, rsem, ksem, krsem, ssem,
    ):
        h = lax.axis_index("head")
        s = lax.axis_index("seq")
        z = s // seqs
        y = lax.rem(s, seqs)
        core = lax.rem(h, cores)
        r_at = (h // cores) * seqs + y
        x_at = h // cores
        p = r_at * cores + core
        zh = z // near
        zl = lax.rem(z, near)
        u_at = zl * seqs + y
        pf = u_at * cores + core
        t_at = x_at * halves + zh
        t_far = x_at * halves + 1 - zh

        def chip_place(r, c):
            return ((r // seqs) * cores + c, z * seqs + lax.rem(r, seqs))

        def slab_place(q):
            return chip_place(q // cores, lax.rem(q, cores))

        def square_place(u, c):
            return (x_at * cores + c, (zh * near + u // seqs) * seqs + lax.rem(u, seqs))

        def ring_place(q):
            return square_place(q // cores, lax.rem(q, cores))

        def half_place(q):
            return (h, (q * near + zl) * seqs + y)

        def beside_place(q):
            return (q * cores + core, s)

        def line_place(q):
            return (h, q)

        def z_place(q):
            return (h, q * seqs + y)

        def x_place(r, c):
            return (r * cores + c, s)

        count = {}

        def take(name):
            number = count.get(name, 0)
            count[name] = number + 1
            return number

        z_order = [(1 - zh) * (zs - 1), near - zh, zh * zs + 1 - z]
        line_order = [q * seqs + b for q in z_order for b in range(seqs)] + [z * seqs + 1 - y]

        def over_z(src, dst):
            return Exchange(
                zs, z, z_place, src, dst, send.at[take("s")], zsem.at[take("z")], z_order
            )

        def over_line(src, dst):
            return Exchange(
                ss, s, line_place, src, dst, send.at[take("s")], lsem.at[take("l")], line_order
            )

        def over_plane(src, dst):
            return Exchange(ps, p, slab_place, src, dst, send.at[take("s")], psem.at[take("p")])

        def over_square(src, dst):
            return Exchange(ps, pf, ring_place, src, dst, send.at[take("s")], psem.at[take("p")])

        def over_half(src, dst):
            return Exchange(halves, zh, half_place, src, dst, send.at[take("s")], bsem.at[take("b")])

        def over_x(src, dst):
            return Exchange(xs, x_at, beside_place, src, dst, send.at[take("s")], bsem.at[take("b")])

        def gather(dst):
            return Gather(rs, seqs, r_at, core, chip_place, dst, send.at[take("s")], gsem.at[take("g")])

        def gather_square(dst):
            return Gather(us, seqs, u_at, core, square_place, dst, send.at[take("s")], gsem.at[take("g")])

        def add_rows(block):
            def add(a, b):
                extent = a.shape[0]

                def one(i):
                    at = aligned(i, block)
                    a[at, :] = (a[at, :].astype(f32) + b[at, :].astype(f32)).astype(bf16)

                loop(0, extent // block, one)

            return add

        def add_blocks(a, b):
            def one(i):
                a[i] = (a[i].astype(f32) + b[i].astype(f32)).astype(bf16)

            loop(0, a.shape[0], one)

        def reduce(stage, beside, landed, add):
            number = take("r")
            return Reduce(
                rs, seqs, r_at, core, chip_place, stage, beside, landed, ssem.at[number],
                rsem.at[number], add,
            )

        def reduce_square(stage, beside, landed, add):
            number = take("r")
            return Reduce(
                us, seqs, u_at, core, square_place, stage, beside, landed, ssem.at[number],
                rsem.at[number], add,
            )

        ex_small_z = over_z(lambda q: small, lambda q: small_z.at[q])
        ex_wq_z = over_z(lambda q: qkv_st.at[q], lambda q: wqg.at[p, q])
        ex_wo_z = over_z(lambda q: wout_ref, lambda q: wog.at[p, q])
        ex_x = over_line(lambda q: x_ref.at[lax.rem(q, seqs)], lambda q: xg.at[q])
        ga_small = gather(lambda q: small_g.at[q])
        ga_wq = gather(lambda q: wqg.at[q])
        ga_wo = gather(lambda q: wog.at[q])
        ex_wf_p = over_square(lambda q: fc_st.at[q], lambda q: wfg.at[t_at, q])
        ex_wf_1 = over_half(lambda q: wfg.at[t_at], lambda q: wfg.at[x_at * halves + q])
        ex_wf_2 = over_x(lambda q: wfg.at[t_at], lambda q: wfg.at[q * halves + zh])
        ex_wf_3 = over_x(lambda q: wfg.at[t_far], lambda q: wfg.at[q * halves + 1 - zh])
        ex_wp_1 = over_half(lambda q: wproj_ref, lambda q: wpg.at[x_at * halves + q])
        ex_wp_2 = over_x(lambda q: wproj_ref, lambda q: wpg.at[q * halves + zh])
        ex_wp_3 = over_x(lambda q: wpg.at[t_far], lambda q: wpg.at[q * halves + 1 - zh])
        ga_go = gather_square(lambda q: gog.at[q])
        ga_kv = [
            Gather(
                xs, 1, x_at, core, x_place,
                lambda q, i=i: kvg.at[q, :, :, i * query_block : (i + 1) * query_block],
                send.at[take("s")], ksem.at[i],
            )
            for i in range(halves)
        ]
        ex_o = over_line(lambda q: o_st.at[q], lambda q: og.at[lax.rem(q, seqs), q // seqs])
        ga_x2 = gather_square(lambda q: x2g.at[q])
        re_gs = reduce_square(
            lambda q: gs_st.at[q], lambda r: gs_in.at[r], lambda r: gs_red.at[r], add_rows(32),
        )
        re_fd = reduce_square(
            lambda q: fd_st.at[q], lambda r: fd_in.at[r], lambda r: fd_red.at[r], add_rows(32),
        )
        ex_do = over_line(
            lambda q: do_st.at[q // seqs, lax.rem(q, seqs)], lambda q: dog.at[q]
        )
        re_kv = [
            Reduce(
                xs, 1, x_at, core, x_place,
                lambda q, n=n: kv_st.at[n, q], lambda r, n=n: kv_in.at[n, r],
                lambda r, n=n: kv_red.at[n, r],
                ssem.at[take("r")], krsem.at[n], add_blocks,
            )
            for n in range(heads)
        ]
        ex_gf = over_line(lambda q: gf_st.at[q], lambda q: gfg.at[lax.rem(q, seqs), q // seqs])
        re_wo = reduce(
            lambda q: wos.at[q], lambda r: wo_in.at[r], lambda r: wo_red.at[r], add_blocks,
        )
        ex_go_z = over_z(lambda q: woz.at[q], lambda q: wozr.at[q])
        re_wq = reduce(
            lambda q: wqs.at[q], lambda r: wq_in.at[r], lambda r: wq_red.at[r], add_blocks,
        )
        ex_gq_z = over_z(lambda q: wqz.at[q], lambda q: wqzr.at[q])
        ex_gf_1 = over_x(lambda q: wfs.at[pl.ds(q * halves, halves)], lambda q: wfr)
        ex_gf_2 = over_half(lambda q: wfm.at[q], lambda q: wfq)
        ex_gf_3 = over_square(lambda q: wfz.at[q], lambda q: wfzr.at[q])
        ex_gp_1 = over_x(lambda q: wps.at[pl.ds(q * halves, halves)], lambda q: wpr)
        ex_gp_2 = over_half(lambda q: wpm.at[q], lambda q: wpq)
        ex_ar_p = over_plane(lambda q: arg.at[q], lambda q: ard.at[q])
        ex_ar_z = over_z(lambda q: ar_st.at[q], lambda q: arz.at[q])

        barrier = pltpu.get_barrier_semaphore()

        def greet(place, me, n):
            def one(k):
                pl.semaphore_signal(
                    barrier, inc=1, device_id=place(lax.rem(me + k, n)),
                    device_id_type=pl.DeviceIdType.MESH,
                )

            loop(1, n, one)

        greet(slab_place, p, ps)
        greet(line_place, s, ss)
        greet(ring_place, pf, ps)

        small[...] = jnp.zeros_like(small)
        small[0:2, 0:rows] = gain_ref[...].astype(f32)
        small[2:8, 0:rows] = bias_ref[...].astype(f32)
        small[8:9, 0:ff_rows] = bfc_ref[...].astype(f32)
        for t in range(zs):
            for k in range(3):
                qkv_st[t, :, k * tw : (k + 1) * tw] = wqkv_ref[:, k * width + t * tw : k * width + (t + 1) * tw]
        for q in range(ps):
            for b in range(zs):
                at = ff_place(q, b) * ff_rows
                fc_st[q, :, b * ff_rows : (b + 1) * ff_rows] = wfc_ref[:, at : at + ff_rows]
        small_z[z] = small[...]
        wqg[p, z] = qkv_st[z]
        wog[p, z] = wout_ref[...]
        wfg[t_at, pf] = fc_st[pf]
        wpg[t_at] = wproj_ref[...]
        xg[s] = x_ref[y]
        ar_st[...] = jnp.zeros_like(ar_st)
        len_0 = len_ref[0]
        len_1 = len_ref[1]
        len_y = jnp.where(y == 0, len_0, len_1)
        home_row = lax.broadcasted_iota(jnp.int32, (home, 1), 0)
        home_place = s * group + h * sl + lax.rem(home_row, sl)
        keep = jnp.where(home_place < jnp.where(home_row < sl, len_0, len_1), 1.0, 0.0)
        gog[pf] = (go_ref[...].reshape(home, width).astype(f32) * keep).astype(bf16)

        def mask_block(q):
            column = lax.broadcasted_iota(jnp.int32, (8, qn), 1)
            place = (column // sl) * group + q * sl + lax.rem(column, sl)
            kneg[q] = jnp.where(place < len_y, 0.0, masked_score)

        loop(0, hs, mask_block)
        pl.semaphore_wait(barrier, 2 * (ps - 1) + ss - 1)

        ex_small_z.send()
        ex_wq_z.send()
        ex_x.send(0, 1)

        ex_small_z.wait()
        small_g[p] = small_z[...]
        ga_small.send()
        ex_wq_z.wait()
        ga_wq.send()
        ex_x.send(1)
        ex_wo_z.send()
        ex_wf_p.send()
        ga_small.relay()
        ga_wq.relay()

        def d_of(q, t):
            hq = q // cores // seqs * cores + q % cores
            return hq * ss + t * seqs + q // cores % seqs

        ga_small.wait()
        prm[...] = jnp.zeros_like(prm)
        for q in range(ps):
            for t in range(zs):
                d = d_of(q, t)
                prm[0:8, d * rows : (d + 1) * rows] = small_g[q, t, 0:8, 0:rows]
                at = (d * rows) % tw
                triple = (d * rows) // tw
                prm[8 + triple : 9 + triple, at : at + rows] = small_g[q, t, 3:4, 0:rows]
                prm[8 + triple : 9 + triple, 2 * tw + at : 2 * tw + at + rows] = small_g[q, t, 4:5, 0:rows]

        up_bias[...] = jnp.zeros_like(up_bias)
        for b in range(zs):
            q = ((b // halves) * seqs + y) * cores + core
            up_bias[0:1, b * ff_rows : (b + 1) * ff_rows] = small_g[q, (b % halves) * near + zl, 8:9, 0:ff_rows]

        def assemble(src, dst):
            def one(i):
                hq = i // zs
                xq = hq // cores
                cq = lax.rem(hq, cores)
                t = lax.rem(i, zs)
                dst[aligned(i, pair), :] = jnp.concatenate(
                    [src(xq, cq, 0, t).astype(f32), src(xq, cq, 1, t).astype(f32)], axis=0
                ).astype(bf16)

            loop(0, width // pair, one)

        ga_wq.wait()
        assemble(lambda a, c, b, t: wqg[(a * seqs + b) * cores + c, t], wq)

        def first_norm(i):
            xv = xg[pl.ds(2 * i, 2)].reshape(2 * sl, width).astype(f32)
            normed, inverse = norm_parts(xv)
            return normed, (normed * prm[0:1, :] + prm[2:3, :]).astype(bf16)

        for i in range(halves):
            for q in range(ss // halves * i, ss // halves * (i + 1)):
                @pl.when(s != q)
                def _(q=q):
                    ex_x.into(q).wait_recv()

            for j in range(zs // halves):
                _, first = first_norm(zs // halves * i + j)
                x2t[(zs // halves * i + j) * 2 * sl : (zs // halves * i + j + 1) * 2 * sl, 0:width] = first
            at = slice(i * query_block, (i + 1) * query_block)
            projected = nn(x2t[at, 0:width], wq[...]) + prm[pl.ds(8 + z, 1), 0 : 3 * tw]
            q_s[at, :] = (projected[:, 0:tw] * scale).astype(bf16)
            turned = projected[:, tw:].T.astype(bf16)
            kvg[h, 0, :, at] = turned[0:tw, :]
            kvg[h, 1, :, at] = turned[tw : 2 * tw, :]
            ga_kv[i].send()
        ex_wf_p.wait()
        ga_go.send()
        ex_wf_1.send()
        ex_wp_1.send()
        for i in range(halves):
            ga_kv[i].relay()
        ex_wo_z.wait()
        ga_wo.send()
        for i in range(halves):
            ga_kv[i].wait()

        lane_head = lax.broadcasted_iota(jnp.int32, (query_block, tw), 1) // HEAD_DIM

        def attend(step):
            n = step // blocks
            i = lax.rem(step, blocks)
            at = aligned(i, query_block)
            lane_own = lane_head == n
            queries = q_s[at, :]
            masked = jnp.where(lane_own, queries, jnp.zeros_like(queries))
            for b in range(hs):
                s_scr[:, b * qn : (b + 1) * qn] = nn(masked, kvg[b, 0])

            def soft(r):
                rat = aligned(r, chunk)
                sv = [s_scr[rat, b * qn : (b + 1) * qn] + kneg[b, 0:1, :] for b in range(hs)]
                top = jnp.max(functools.reduce(jnp.maximum, sv), axis=-1, keepdims=True)
                ev = [jnp.exp(v - top) for v in sv]
                inv = 1.0 / jnp.sum(functools.reduce(jnp.add, ev), axis=-1, keepdims=True)
                for b in range(hs):
                    value = ev[b] * inv
                    probs[n, i, rat, b * qn : (b + 1) * qn] = value
                    pb_scr[rat, b * qn : (b + 1) * qn] = value.astype(bf16)

            loop(0, query_block // chunk, soft, unroll=4)
            head_out = nt(pb_scr[:, 0:qn], kvg[0, 1])
            for b in range(1, hs):
                head_out = head_out + nt(pb_scr[:, b * qn : (b + 1) * qn], kvg[b, 1])
            o_s[at, :] = jnp.where(lane_own, head_out.astype(bf16), o_s[at, :])

        o_s[...] = jnp.zeros_like(o_s)
        loop(0, blocks, attend)
        ex_wf_2.send()
        ex_wp_2.send()
        loop(blocks, heads * blocks - 2, attend)
        ex_wf_1.wait()
        ex_wf_3.send()
        ex_wp_1.wait()
        ex_wp_3.send()
        loop(heads * blocks - 2, heads * blocks, attend)

        def pack(ref, v):
            ref[0:sl, :], ref[sl:, :] = dense(v)

        def unpack(ref):
            return loose(ref[0:sl, :], ref[sl:, :])

        def lay_out(q):
            pack(o_st.at[q], o_s[aligned(q, sl), :])

        loop(0, ss, lay_out)
        ex_o.send()
        og[y, z] = o_st[s]
        ga_wo.relay()
        ga_go.relay()

        ga_wo.wait()
        assemble(lambda a, c, b, t: wog[(a * seqs + b) * cores + c, t], wo)
        ex_o.wait()
        branch = jnp.broadcast_to(prm[5:6, :], (home, width))
        for t in range(zs):
            mixed = jnp.concatenate([unpack(og.at[a, t]) for a in range(seqs)], axis=0)
            mixed_s[t] = mixed
            branch = branch + nn(mixed, wo[t * tw : (t + 1) * tw, :])
        middle = x_ref[...].reshape(home, width).astype(f32) + branch
        normed, _ = norm_parts(middle)
        x2g[pf] = (normed * prm[1:2, :] + prm[6:7, :]).astype(bf16)
        ga_x2.send(us - 1)
        middle_s[...] = middle
        for ex in (ga_go, ex_wf_2, ex_wp_2, ex_wf_3, ex_wp_3):
            ex.wait()
        assemble(
            lambda a, c, b, t: wfg[a * halves + t // near, (lax.rem(t, near) * seqs + b) * cores + c], wf
        )

        def feed(k, running):
            r = ga_x2.peer(k)

            @pl.when(k > 0)
            def _():
                ga_x2.relay_from(k)

            ga_x2.wait_from(k)
            at = aligned(r, duo)
            chip = pl.ds(cores * r, cores)
            hid = nn(x2g[chip].reshape(duo, width), wf[...]) + up_bias[0:1, :]
            gate = 1.0 / (1.0 + jnp.exp(-quick_slope * hid))
            act[at, :] = (hid * gate).astype(bf16)
            flow = nt(gog[chip].reshape(duo, width), wpg[...].reshape(part, width))
            slope = gate + quick_slope * hid * gate * (1.0 - gate)
            back = (flow * slope).astype(bf16)
            gh[at, :] = back
            gs_st[chip] = nt(back, wf[...]).astype(bf16).reshape(cores, home, width)
            re_gs.aside(r).start()

            @pl.when(k == 0)
            def _():
                ga_x2.send_last()

            @pl.when(k > 1)
            def _():
                re_gs.combine_out(k - 1)

            return running + jnp.sum(back.astype(f32), axis=0, keepdims=True)

        grad_up = lax.fori_loop(0, us, feed, jnp.zeros((1, part), f32))

        def turn_act(q):
            at = aligned(q, home)
            x2t[0:part, at] = act[at, :].T

        loop(0, ps, turn_act)
        re_gs.combine_out(us - 1)
        re_gs.combine(u_at)

        def proj_grad(c):
            wps[pl.ds(2 * c, 2)] = nn(
                x2t[aligned(c, 2 * ff_rows), :], gog[...].reshape(slab, width)
            ).astype(bf16).reshape(2, ff_rows, width)

        loop(0, zs // 2, proj_grad)
        ex_gp_1.send()

        def feed_down(r):
            chip = pl.ds(cores * r, cores)
            fd_st[chip] = nn(act[aligned(r, duo), :], wpg[...].reshape(part, width)).astype(bf16).reshape(
                cores, home, width
            )
            re_fd.aside(r).start()

        loop(0, us, feed_down)

        def scatter_rows(c, val, put):
            for j in range(val.shape[0] // rows):
                d = c * (val.shape[0] // rows) + j
                hq = d // ss
                sd = lax.rem(d, ss)
                put(
                    hq // cores, lax.rem(hq, cores), lax.rem(sd, seqs), sd // seqs,
                    val[j * rows : (j + 1) * rows, :].astype(bf16),
                )

        def turn_in(q):
            x2t[:, aligned(q, home)] = x2g[q].T

        loop(0, ps, turn_in)

        def fc_grad(c):
            def put(a, c, b, t, value):
                wfs[a * halves + t // near, (lax.rem(t, near) * seqs + b) * cores + c] = value

            scatter_rows(c, nn(x2t[aligned(c, quad), :], gh[...]), put)

        loop(0, width // quad, fc_grad)
        ex_gf_1.send()

        for t in range(zs):
            x2t[t * tw : (t + 1) * tw, 0:home] = mixed_s[t].T
        grad_final = go_ref[...].reshape(home, width).astype(f32) * keep

        re_gs.wait()

        def landed_sum(re, own):
            total = own
            for k in range(1, us):
                total = total + re.landed(re.peer(k))[...].astype(f32)
            return total

        grad_second = landed_sum(re_gs, gs_st[pf].astype(f32))
        n2, r2 = norm_parts(middle_s[...])
        grad_middle = grad_final + norm_backward(grad_second * prm[1:2, :], n2, r2)
        grad_branch = grad_middle.astype(bf16)
        for t in range(zs):
            value = nt(grad_branch, wo[t * tw : (t + 1) * tw, :]).astype(bf16)
            for a in range(seqs):
                pack(do_st.at[t, a], value[a * sl : (a + 1) * sl, :])
        ex_do.send()
        dog[s] = do_st[z, y]
        gm_s[...] = grad_middle
        sums[...] = jnp.zeros_like(sums)
        arg[...] = jnp.zeros_like(arg)
        for q in range(ps):
            c, b, a = q % cores, q // cores % seqs, q // cores // seqs
            for i in range(zs):
                at = (a * halves + i // near) * ff_rows
                arg[q, 8 + i : 9 + i, 0:ff_rows] = jnp.where(
                    (core == c) & (y == b) & (zl == i % near), grad_up[:, at : at + ff_rows], 0.0
                )
        sums[1:2, :] = jnp.sum(grad_second * n2, axis=0, keepdims=True)
        sums[6:7, :] = jnp.sum(grad_second, axis=0, keepdims=True)
        sums[5:6, :] = jnp.sum(grad_branch.astype(f32), axis=0, keepdims=True)


        def out_grad(c):
            def put(a, c, b, t, value):
                wos[(a * seqs + b) * cores + c, t] = value

            scatter_rows(c, nn(x2t[aligned(c, quad), 0:home], gm_s[...].astype(bf16)), put)

        loop(0, width // quad, out_grad)
        re_wo.send_aside()

        ex_do.wait()
        ex_gp_1.wait()

        def proj_sum(q):
            wpm[q] = (wps[t_at - zh + q].astype(f32) + wpr[q].astype(f32)).astype(bf16)

        loop(0, halves, proj_sum)
        ex_gp_2.send()
        re_fd.send()
        re_wo.send()

        def gather_do(i):
            at = aligned(i, 2 * sl)
            value = jnp.concatenate([unpack(dog.at[2 * i]), unpack(dog.at[2 * i + 1])], axis=0)
            o_s[at, :] = value
            dot_s[:, at] = value.T
            qt_s[:, at] = q_s[at, :].T

        loop(0, ss // 2, gather_do)
        dq_s[...] = jnp.zeros_like(dq_s)

        for n in range(heads):
            lane_own = lane_head == n
            head_rows = slice(n * HEAD_DIM, (n + 1) * HEAD_DIM)

            def back(i, n=n, lane_own=lane_own, head_rows=head_rows):
                at = aligned(i, query_block)
                outer = o_s[at, :]
                masked = jnp.where(lane_own, outer, jnp.zeros_like(outer))
                for b in range(hs):
                    s_scr[:, b * qn : (b + 1) * qn] = nn(masked, kvg[b, 1])

                def soft(r):
                    rat = aligned(r, chunk)
                    dp = [s_scr[rat, b * qn : (b + 1) * qn] for b in range(hs)]
                    pv = [probs[n, i, rat, b * qn : (b + 1) * qn] for b in range(hs)]
                    delta = jnp.sum(
                        functools.reduce(jnp.add, [a * c for a, c in zip(dp, pv)]),
                        axis=-1, keepdims=True,
                    )
                    for b in range(hs):
                        ds_scr[rat, b * qn : (b + 1) * qn] = (pv[b] * (dp[b] - delta)).astype(bf16)
                        pb_scr[rat, b * qn : (b + 1) * qn] = pv[b].astype(bf16)

                loop(0, query_block // chunk, soft, unroll=4)
                head_dq = nt(ds_scr[:, 0:qn], kvg[0, 0])
                for b in range(1, hs):
                    head_dq = head_dq + nt(ds_scr[:, b * qn : (b + 1) * qn], kvg[b, 0])
                dq_s[at, :] = jnp.where(lane_own, (head_dq.astype(bf16).astype(f32) * scale).astype(bf16), dq_s[at, :])
                for b in range(hs):
                    dkt[b] = dkt[b] + nn(qt_s[head_rows, at], ds_scr[:, b * qn : (b + 1) * qn])
                    dvt[b] = dvt[b] + nn(dot_s[head_rows, at], pb_scr[:, b * qn : (b + 1) * qn])

            dkt[...] = jnp.zeros_like(dkt)
            dvt[...] = jnp.zeros_like(dvt)
            loop(0, blocks, back)
            for b in range(hs):
                kv_st[n, b, 0] = dkt[b].astype(bf16)
                kv_st[n, b, 1] = dvt[b].astype(bf16)
            re_kv[n].send_aside()
            if n:
                re_kv[n - 1].send()
            if n == 0:
                ex_gf_1.wait()

                def fc_sum(i):
                    q, b = i // ps, lax.rem(i, ps)
                    wfm[q, b] = (wfs[t_at - zh + q, b].astype(f32) + wfr[q, b].astype(f32)).astype(bf16)

                loop(0, halves * ps, fc_sum)
                ex_gf_2.send()
        re_kv[heads - 1].send()

        gpt[0:tw, :] = dq_s[...].T

        def turn_first(i):
            _, first = first_norm(i)
            x2t[:, aligned(i, 2 * sl)] = first.T

        loop(0, zs, turn_first)

        def final_rows(re, own, landed, dst):
            def one(t):
                total = own[p, t].astype(f32)
                for k in range(1, rs):
                    total = total + landed[re.peer(k), t].astype(f32)
                dst[t] = total.astype(bf16)

            loop(0, zs, one)

        re_wo.wait()
        final_rows(re_wo, wos, wo_red, woz)
        ex_go_z.send()
        wozr[z] = woz[z]
        ex_gf_2.wait()

        def fc_last(q):
            wfz[q] = (wfm[zh, q].astype(f32) + wfq[q].astype(f32)).astype(bf16)

        loop(0, ps, fc_last)
        ex_gf_3.send()
        wfzr[pf] = wfz[pf]
        re_fd.wait()
        feed_out = landed_sum(re_fd, fd_st[pf].astype(f32)) + prm[7:8, :]
        final = middle_s[...] + feed_out
        out_ref[...] = (final * keep).astype(bf16).reshape(seqs, sl, width)
        xv = x_ref[...].reshape(home, width).astype(f32)
        br = middle_s[...] - xv
        place = lax.broadcasted_iota(jnp.int32, (1, 128), 1)
        squares = jnp.zeros((1, 128), f32)
        for k, value in enumerate((xv, br, feed_out, final)):
            squares = squares + jnp.where(place == k, jnp.sum(keep * value * value), 0.0)
        for q in range(ps):
            arg[q, 12:13, :] = squares
        for n in range(heads):
            re_kv[n].wait()
            for k in range(2):
                at = (1 + k) * tw + n * HEAD_DIM
                gpt[at : at + HEAD_DIM, :] = (
                    kv_st[n, h, k].astype(f32) + kv_red[n, re_kv[n].peer(1), k].astype(f32)
                ).astype(bf16)
        gp[...] = gpt[...].T

        gain_sum = jnp.zeros((1, width), f32)
        shift_sum = jnp.zeros((1, width), f32)
        block = ss // halves

        def first_grad(i):
            value = nt(gp[aligned(i, block * sl), :], wq[...])
            gf_st[pl.ds(block * i, block)] = value.astype(bf16).reshape(block, sl, width)

        first_grad(1 - zh)
        ex_gf.send(0, 1)

        def qkv_grad(c):
            def put(a, c, b, t, value):
                wqs[(a * seqs + b) * cores + c, t] = value

            scatter_rows(c, nn(x2t[aligned(c, quad), 0:qn], gp[...]), put)

        loop(0, width // quad, qkv_grad)
        re_wq.send_aside()
        first_grad(zh)
        re_wq.send()
        ex_gf.send(1)
        gfg[y, z] = gf_st[s]
        for i in range(zs):
            value = gf_st[2 * i : 2 * i + 2].reshape(2 * sl, width).astype(f32)
            normed, _ = first_norm(i)
            gain_sum = gain_sum + jnp.sum(value * normed, axis=0, keepdims=True)
            shift_sum = shift_sum + jnp.sum(value, axis=0, keepdims=True)

        sums[0:1, :] = gain_sum
        sums[2:3, :] = shift_sum
        projected_sum = jnp.sum(gp[...].astype(f32), axis=0, keepdims=True)
        for i in range(zs):
            at = slice(i * tw, (i + 1) * tw)
            sums[3:4, at] = jnp.where(z == i, projected_sum[:, 0:tw], 0.0)
            sums[4:5, at] = jnp.where(z == i, projected_sum[:, 2 * tw :], 0.0)
        sums[7:8, :] = jnp.sum(gog[pf].astype(f32), axis=0, keepdims=True)

        for q in range(ps):
            for i in range(zs):
                at = d_of(q, i) * rows
                arg[q, 0:8, i * rows : (i + 1) * rows] = sums[0:8, at : at + rows]
        ex_ar_p.send()
        ard[p] = arg[p]

        ex_gp_2.wait()
        gproj_ref[...] = wpm[zh].astype(f32) + wpq[...].astype(f32)

        re_wq.wait()
        final_rows(re_wq, wqs, wq_red, wqz)
        ex_gq_z.send()
        wqzr[z] = wqz[z]
        ex_ar_p.wait()
        total = functools.reduce(jnp.add, [ard[q] for q in range(ps)])
        for i in range(zs):
            ar_st[i, 0:8, 0:rows] = total[0:8, i * rows : (i + 1) * rows]
            ar_st[i, 8:9, :] = total[8 + i : 9 + i, :]
            ar_st[i, 9:10, :] = total[12:13, :]
        ex_ar_z.send()
        arz[z] = ar_st[z]
        ex_gf.wait()
        grad_first = functools.reduce(jnp.add, [gfg[:, t].astype(f32) for t in range(zs)]).reshape(home, width)
        n1, r1 = norm_parts(x_ref[...].reshape(home, width).astype(f32))
        grad_in = gm_s[...] + norm_backward(grad_first * prm[0:1, :], n1, r1)
        gin_ref[...] = grad_in.reshape(seqs, sl, width)

        ex_gf_3.wait()
        gfc_ref[...] = wfzr[...].astype(f32)
        ex_gq_z.wait()
        gqkv_ref[...] = wqzr[...].astype(f32)
        ex_ar_z.wait()
        ar_ref[...] = functools.reduce(jnp.add, [arz[t] for t in range(zs)])
        ex_go_z.wait()
        gout_ref[...] = functools.reduce(jnp.add, [wozr[t].astype(f32) for t in range(zs)])

        for ex in (
            ex_small_z, ex_wq_z, ex_wo_z, ex_x, ga_small, ga_wq, ga_wo, ex_wf_p, ex_wf_1, ex_wf_2, ex_wf_3,
            ex_wp_1, ex_wp_2, ex_wp_3,
            ga_go, *ga_kv, ex_o, re_gs, re_fd, ex_do, *re_kv, ex_gf, re_wo, ex_go_z, re_wq, ex_gq_z,
            ex_gf_1, ex_gf_2, ex_gf_3, ex_gp_1, ex_gp_2, ex_ar_p, ex_ar_z,
        ):
            ex.drain()
        ga_x2.drain(us - 1)

    vm = pltpu.VMEM
    scratch = [
        vm((16, 128), f32),
        vm((zs, 16, 128), f32),
        vm((ps, zs, 16, 128), f32),
        vm((16, width), f32),
        vm((8, part), f32),
        vm((zs, rows, 3 * tw), bf16),
        vm((ps, rows, part), bf16),
        vm((ps, zs, rows, 3 * tw), bf16),
        vm((ps, zs, rows, width), bf16),
        vm((zs, ps, rows, part), bf16),
        vm((zs, ff_rows, width), bf16),
        vm((width, 3 * tw), bf16),
        vm((width, width), bf16),
        vm((width, part), bf16),
        vm((ss, sl, width), bf16),
        vm((qn, tw), bf16),
        vm((hs, 2, tw, qn), bf16),
        vm((hs, 8, qn), f32),
        vm((heads, blocks, query_block, hs * qn), f32),
        vm((query_block, hs * qn), f32),
        vm((query_block, hs * qn), bf16),
        vm((query_block, hs * qn), bf16),
        vm((qn, tw), bf16),
        vm((ss, sl * tw // lanes_per, lanes_per), bf16),
        vm((seqs, zs, sl * tw // lanes_per, lanes_per), bf16),
        vm((zs, home, tw), bf16),
        vm((home, width), f32),
        vm((home, width), f32),
        vm((ps, home, width), bf16),
        vm((ps, home, width), bf16),
        vm((slab, part), bf16),
        vm((slab, part), bf16),
        vm((width, slab), bf16),
        vm((ps, home, width), bf16),
        vm((rs, home, width), bf16),
        vm((rs, home, width), bf16),
        vm((ps, home, width), bf16),
        vm((rs, home, width), bf16),
        vm((rs, home, width), bf16),
        vm((zs, seqs, sl * tw // lanes_per, lanes_per), bf16),
        vm((ss, sl * tw // lanes_per, lanes_per), bf16),
        vm((tw, qn), bf16),
        vm((tw, qn), bf16),
        vm((qn, tw), bf16),
        vm((hs, HEAD_DIM, qn), f32),
        vm((hs, HEAD_DIM, qn), f32),
        vm((heads, hs, 2, HEAD_DIM, qn), bf16),
        vm((heads, xs, 2, HEAD_DIM, qn), bf16),
        vm((heads, xs, 2, HEAD_DIM, qn), bf16),
        vm((3 * tw, qn), bf16),
        vm((qn, 3 * tw), bf16),
        vm((ss, sl, width), bf16),
        vm((seqs, zs, sl, width), bf16),
        vm((ps, zs, rows, width), bf16),
        vm((rs, zs, rows, width), bf16),
        vm((rs, zs, rows, width), bf16),
        vm((zs, rows, width), bf16),
        vm((zs, rows, width), bf16),
        vm((ps, zs, rows, 3 * tw), bf16),
        vm((rs, zs, rows, 3 * tw), bf16),
        vm((rs, zs, rows, 3 * tw), bf16),
        vm((zs, rows, 3 * tw), bf16),
        vm((zs, rows, 3 * tw), bf16),
        vm((zs, ps, rows, part), bf16),
        vm((halves, ps, rows, part), bf16),
        vm((halves, ps, rows, part), bf16),
        vm((ps, rows, part), bf16),
        vm((ps, rows, part), bf16),
        vm((ps, rows, part), bf16),
        vm((zs, ff_rows, width), bf16),
        vm((halves, ff_rows, width), bf16),
        vm((halves, ff_rows, width), bf16),
        vm((ff_rows, width), bf16),
        vm((ps, 16, 128), f32),
        vm((ps, 16, 128), f32),
        vm((8, width), f32),
        vm((zs, 16, 128), f32),
        vm((zs, 16, 128), f32),
        pltpu.SemaphoreType.DMA((33,)),
        pltpu.SemaphoreType.DMA((10, zs)),
        pltpu.SemaphoreType.DMA((4, ss)),
        pltpu.SemaphoreType.DMA((3, ps)),
        pltpu.SemaphoreType.DMA((10, 2)),
        pltpu.SemaphoreType.DMA((6, ps)),
        pltpu.SemaphoreType.DMA((7, 2, rs)),
        pltpu.SemaphoreType.DMA((zs, hs)),
        pltpu.SemaphoreType.DMA((heads, 2, xs)),
        pltpu.SemaphoreType.DMA((7, 2)),
    ]
    in_vmem = pl.BlockSpec(memory_space=pltpu.VMEM)
    in_smem = pl.BlockSpec(memory_space=pltpu.SMEM)
    results = pl.pallas_call(
        kernel,
        out_shape=(
            jax.ShapeDtypeStruct((seqs, sl, width), bf16),
            jax.ShapeDtypeStruct((seqs, sl, width), f32),
            jax.ShapeDtypeStruct((zs, rows, 3 * tw), f32),
            jax.ShapeDtypeStruct((rows, width), f32),
            jax.ShapeDtypeStruct((ps, rows, part), f32),
            jax.ShapeDtypeStruct((ff_rows, width), f32),
            jax.ShapeDtypeStruct((16, 128), f32),
        ),
        in_specs=[in_smem] + [in_vmem] * 9,
        out_specs=(in_vmem,) * 7,
        scratch_shapes=scratch,
        compiler_params=pltpu.CompilerParams(
            collective_id=0, has_side_effects=True, vmem_limit_bytes=63 * 1024 * 1024
        ),
        name="layer",
    )(
        lengths,
        layer_input.reshape(seqs, sl, width),
        grad_out.reshape(seqs, sl, width),
        w_qkv,
        w_out,
        w_fc,
        w_proj,
        b_fc.reshape(1, ff_rows),
        norm_gains,
        biases,
    )

    def finish(
        len_ref, a_out, a_gin, a_gqkv, a_gout, a_gfc, a_gproj, sums,
        out_ref, gin_ref, gqkv_ref, gout_ref, gfc_ref, gproj_ref, gup_ref, ggain_ref, gbias_ref, rms_ref,
    ):
        out_ref[...] = a_out[...]
        gin_ref[...] = a_gin[...]
        gout_ref[...] = a_gout[...]
        gproj_ref[...] = a_gproj[...]
        for t in range(zs):
            for k in range(3):
                gqkv_ref[:, k * width + t * tw : k * width + (t + 1) * tw] = a_gqkv[t, :, k * tw : (k + 1) * tw]
        for q in range(ps):
            for b in range(zs):
                at = ff_place(q, b) * ff_rows
                gfc_ref[:, at : at + ff_rows] = a_gfc[q, :, b * ff_rows : (b + 1) * ff_rows]
        ggain_ref[...] = sums[0:2, 0:rows]
        gbias_ref[...] = sums[2:8, 0:rows]
        gup_ref[...] = sums[8:9, 0:ff_rows]
        valid = (len_ref[0] + len_ref[1]).astype(f32) * width
        rms_ref[...] = jnp.sqrt(sums[9:10, 0:4] / valid)

    final = pl.pallas_call(
        finish,
        out_shape=(
            jax.ShapeDtypeStruct((seqs, sl, width), bf16),
            jax.ShapeDtypeStruct((seqs, sl, width), f32),
            jax.ShapeDtypeStruct((rows, 3 * width), f32),
            jax.ShapeDtypeStruct((rows, width), f32),
            jax.ShapeDtypeStruct((rows, ps * part), f32),
            jax.ShapeDtypeStruct((ff_rows, width), f32),
            jax.ShapeDtypeStruct((1, ff_rows), f32),
            jax.ShapeDtypeStruct((2, rows), f32),
            jax.ShapeDtypeStruct((6, rows), f32),
            jax.ShapeDtypeStruct((1, 4), f32),
        ),
        in_specs=[in_smem] + [in_vmem] * 7,
        out_specs=(in_vmem,) * 10,
        name="finish",
    )(lengths, *results)
    return (
        final[0].reshape(layer_input.shape),
        final[1].reshape(layer_input.shape),
        *final[2:6],
        final[6].reshape(ff_rows),
        final[7],
        final[8],
        final[9].reshape(4),
    )


def fits(seqs, sl, width, hs, ss, qkv_rows):
    if seqs != 2 or ss % seqs or hs % cores:
        return False
    zs = ss // seqs
    if width % zs or (width // zs) % HEAD_DIM or zs != 4 or hs != zs or qkv_rows % 8:
        return False
    tw = width // zs
    keys = ss * sl * hs
    return tw <= 256 and keys * ss * sl * (tw // HEAD_DIM) * 4 <= 16 * 1024 * 1024


def on_device(layer_input, grad_out, lengths, w_qkv, w_out, w_fc, w_proj, b_fc, norm_gains, biases):
    seqs, _, sl, width = layer_input.shape
    hs, ss = lax.axis_size("head"), lax.axis_size("seq")
    chosen = fused_layer if fits(seqs, sl, width, hs, ss, w_qkv.shape[0]) else spread_layer
    return chosen(
        layer_input, grad_out, lengths, w_qkv, w_out, w_fc, w_proj, b_fc, norm_gains, biases
    )


def solution(mesh):
    return jax.shard_map(
        on_device,
        mesh=mesh,
        in_specs=(
            P(None, "seq", "head", None),
            P(None, "seq", "head", None),
            P(),
            P(("head", "seq"), None),
            P(("head", "seq"), None),
            P(("head", "seq"), None),
            P(("head", "seq"), None),
            P(("head", "seq")),
            P(None, ("head", "seq")),
            P(None, ("head", "seq")),
        ),
        out_specs=(
            P(None, "seq", "head", None),
            P(None, "seq", "head", None),
            P(("head", "seq"), None),
            P(("head", "seq"), None),
            P(("head", "seq"), None),
            P(("head", "seq"), None),
            P(("head", "seq")),
            P(None, ("head", "seq")),
            P(None, ("head", "seq")),
            P(),
        ),
        check_vma=False,
    )
```

```python
import functools

import jax
import jax.numpy as jnp
from jax import lax
from jax.sharding import PartitionSpec as P
from jax.experimental import pallas as pl
from jax.experimental.pallas import tpu as pltpu

HEAD_DIM = 64


masked_score = -1e30
block_keys = 512
quick_slope = 1.702
epsilon = 1e-05


def layer_norm_parts(inputs):
    centre = inputs - jnp.mean(inputs, axis=-1, keepdims=True)
    inverse = lax.rsqrt(jnp.mean(centre * centre, axis=-1, keepdims=True) + epsilon)
    return (centre * inverse, inverse)


def norm_backward(grad_normed, normed, inverse):
    return inverse * (
        grad_normed
        - jnp.mean(grad_normed, axis=-1, keepdims=True)
        - normed * jnp.mean(grad_normed * normed, axis=-1, keepdims=True)
    )


def split_heads(piece_block):
    return piece_block.reshape(
        piece_block.shape[0], piece_block.shape[1], piece_block.shape[2] // HEAD_DIM, HEAD_DIM
    )


def head_scores(left_side, right_side):
    return jnp.einsum("sqhd,skhd->shqk", left_side, right_side, preferred_element_type=jnp.float32)


def weighted(probabilities, right_side):
    return jnp.einsum(
        "shqk,skhd->sqhd", probabilities, right_side, preferred_element_type=jnp.float32
    )


def transposed(probabilities, right_side):
    return jnp.einsum(
        "shqk,sqhd->skhd", probabilities, right_side, preferred_element_type=jnp.float32
    )


def over_blocks(step_fn, running, pieces):
    extent = pieces[0].shape[1]
    number = extent // block_keys
    parted = tuple(
        (
            piece_part.reshape(
                (piece_part.shape[0], number, block_keys) + piece_part.shape[2:]
            ).swapaxes(0, 1)
            for piece_part in pieces
        )
    )

    def advance(inner_run, element):
        position, blocks = element
        return (step_fn(inner_run, blocks, position * block_keys), None)

    return lax.scan(advance, running, (jnp.arange(number, dtype=jnp.int32), parted))[0]


def spread_layer(layer_input, grad_out, lengths, w_qkv, w_out, w_fc, w_proj, b_fc, norm_gains, biases):
    sequences = layer_input.shape[0]
    slice_len = layer_input.shape[2]
    model_width = layer_input.shape[3]
    head_ways = lax.axis_size("head")
    group_len = slice_len * head_ways
    local_width = model_width // head_ways
    head_count = local_width // HEAD_DIM
    head_place = lax.axis_index("head")
    cycle_place = lax.axis_index("seq")
    flat_rows = sequences * slice_len
    full_qkv, full_out, full_fc, full_proj, full_bias_fc, full_gains, full_biases = (
        lax.all_gather(w_qkv, ("head", "seq"), axis=0, tiled=True),
        lax.all_gather(w_out, ("head", "seq"), axis=0, tiled=True),
        lax.all_gather(w_fc, ("head", "seq"), axis=0, tiled=True),
        lax.all_gather(w_proj, ("head", "seq"), axis=0, tiled=True),
        lax.all_gather(b_fc, ("head", "seq"), axis=0, tiled=True),
        lax.all_gather(norm_gains, ("head", "seq"), axis=1, tiled=True),
        lax.all_gather(biases, ("head", "seq"), axis=1, tiled=True),
    )
    gain_vals = full_gains.astype(jnp.float32)
    shift_vals = full_biases.astype(jnp.float32)
    bias_up = full_bias_fc.astype(jnp.float32)
    token_places = (
        cycle_place * group_len + head_place * slice_len + jnp.arange(slice_len, dtype=jnp.int32)
    )
    token_keep = (
        (token_places[None, :] < lengths[:, None]).astype(jnp.float32).reshape(flat_rows, 1)
    )
    own_places = cycle_place * group_len + jnp.arange(group_len, dtype=jnp.int32)
    own_allowed = (own_places[None, :] < lengths[:, None])[:, None, None, :]

    def allowed_at(offset, extent):
        places = offset + jnp.arange(extent, dtype=jnp.int32)
        return (places[None, :] < lengths[:, None])[:, None, None, :]

    inputs = layer_input.reshape(flat_rows, model_width).astype(jnp.float32)
    normed_one, inverse_one = layer_norm_parts(inputs)
    first_in = (normed_one * gain_vals[0] + shift_vals[0]).astype(jnp.bfloat16)
    projected = jnp.dot(first_in, full_qkv, preferred_element_type=jnp.float32)
    query_scale = HEAD_DIM ** (-0.5)
    queries = ((projected[:, :model_width] + shift_vals[1]) * query_scale).astype(jnp.bfloat16)
    keys_new = projected[:, model_width : 2 * model_width].astype(jnp.bfloat16)
    values_new = (projected[:, 2 * model_width :] + shift_vals[2]).astype(jnp.bfloat16)
    packed = jnp.stack([queries, keys_new, values_new], axis=1).reshape(
        sequences, slice_len, 3, head_ways, local_width
    )
    spread = lax.all_to_all(packed, "head", split_axis=3, concat_axis=1, tiled=True)
    query_block = spread[:, :, 0, 0]
    key_block = spread[:, :, 1, 0]
    value_block = spread[:, :, 2, 0]
    query_heads = split_heads(query_block)
    key_heads = split_heads(key_block)
    value_heads = split_heads(value_block)

    def maxima_step(running, pieces, offset):
        highest, denominator = running
        scores = head_scores(query_heads, split_heads(pieces[0]))
        allowed = allowed_at(offset, pieces[0].shape[1])
        scores = jnp.where(allowed, scores, masked_score)
        raised = jnp.maximum(highest, jnp.max(scores, axis=-1))
        weights = jnp.where(allowed, jnp.exp(scores - raised[..., None]), 0.0)
        denominator = denominator * jnp.exp(highest - raised) + jnp.sum(weights, axis=-1)
        return (raised, denominator)

    zero_rows = jnp.zeros((sequences, head_count, group_len), jnp.float32)
    highest, denominator = over_blocks(
        maxima_step,
        (zero_rows + masked_score, zero_rows),
        (lax.all_gather(key_block, "seq", axis=1, tiled=True),),
    )
    log_total = highest + jnp.log(denominator)

    def attention_weights(key_piece, offset):
        scores = head_scores(query_heads, key_piece)
        allowed = allowed_at(offset, key_piece.shape[1])
        return jnp.where(
            allowed, jnp.exp(jnp.where(allowed, scores, masked_score) - log_total[..., None]), 0.0
        )

    zero_heads = jnp.zeros((sequences, group_len, head_count, HEAD_DIM), jnp.float32)

    def output_step(running, pieces, offset):
        probabilities = attention_weights(split_heads(pieces[0]), offset)
        return running + weighted(probabilities.astype(jnp.bfloat16), split_heads(pieces[1]))

    attended = over_blocks(
        output_step,
        zero_heads,
        (
            lax.all_gather(key_block, "seq", axis=1, tiled=True),
            lax.all_gather(value_block, "seq", axis=1, tiled=True),
        ),
    )
    mixed_heads = attended.astype(jnp.bfloat16).reshape(
        sequences, head_ways, slice_len, local_width
    )
    gathered_out = lax.all_to_all(mixed_heads, "head", split_axis=1, concat_axis=3, tiled=True)
    mixed_rows = gathered_out.reshape(flat_rows, model_width)
    branch = jnp.dot(mixed_rows, full_out, preferred_element_type=jnp.float32) + shift_vals[3]
    middle = inputs + branch
    normed_two, inverse_two = layer_norm_parts(middle)
    second_in = (normed_two * gain_vals[1] + shift_vals[4]).astype(jnp.bfloat16)
    hidden = jnp.dot(second_in, full_fc, preferred_element_type=jnp.float32) + bias_up
    gate_sig = jax.nn.sigmoid(quick_slope * hidden)
    activated = (hidden * gate_sig).astype(jnp.bfloat16)
    feed_out = jnp.dot(activated, full_proj, preferred_element_type=jnp.float32) + shift_vals[5]
    final_rows = middle + feed_out
    result = (final_rows * token_keep).astype(jnp.bfloat16).reshape(layer_input.shape)
    local_squares = jnp.stack(
        [
            jnp.sum(token_keep * inputs * inputs),
            jnp.sum(token_keep * branch * branch),
            jnp.sum(token_keep * feed_out * feed_out),
            jnp.sum(token_keep * final_rows * final_rows),
        ]
    )
    squares = lax.psum(local_squares, ("head", "seq"))
    valid_count = jnp.sum(lengths).astype(jnp.float32) * model_width
    root_means = jnp.sqrt(squares / valid_count)
    grad_final = grad_out.reshape(flat_rows, model_width).astype(jnp.float32) * token_keep
    grad_feed = grad_final.astype(jnp.bfloat16)
    grad_proj = jnp.dot(activated.T, grad_feed, preferred_element_type=jnp.float32)
    grad_shift_proj = jnp.sum(grad_feed.astype(jnp.float32), axis=0)
    grad_act = jnp.dot(grad_feed, full_proj.T, preferred_element_type=jnp.float32)
    grad_hidden = (
        grad_act * (gate_sig + quick_slope * hidden * gate_sig * (1.0 - gate_sig))
    ).astype(jnp.bfloat16)
    grad_fc = jnp.dot(second_in.T, grad_hidden, preferred_element_type=jnp.float32)
    grad_bias_up = jnp.sum(grad_hidden.astype(jnp.float32), axis=0)
    grad_second = jnp.dot(grad_hidden, full_fc.T, preferred_element_type=jnp.float32)
    grad_gain_two = jnp.sum(grad_second * normed_two, axis=0)
    grad_shift_two = jnp.sum(grad_second, axis=0)
    grad_middle = grad_final + norm_backward(grad_second * gain_vals[1], normed_two, inverse_two)
    grad_branch = grad_middle.astype(jnp.bfloat16)
    grad_out_weight = jnp.dot(mixed_rows.T, grad_branch, preferred_element_type=jnp.float32)
    grad_shift_out = jnp.sum(grad_branch.astype(jnp.float32), axis=0)
    grad_mixed = jnp.dot(grad_branch, full_out.T, preferred_element_type=jnp.float32).astype(
        jnp.bfloat16
    )
    grad_spread = lax.all_to_all(
        grad_mixed.reshape(sequences, slice_len, head_ways, local_width),
        "head",
        split_axis=2,
        concat_axis=1,
        tiled=True,
    )
    grad_block = grad_spread[:, :, 0]
    grad_heads = split_heads(grad_block)

    def delta_step(running, pieces, offset):
        probabilities = attention_weights(split_heads(pieces[0]), offset)
        grad_probs = head_scores(grad_heads, split_heads(pieces[1]))
        return running + jnp.sum(probabilities * grad_probs, axis=-1)

    row_delta = over_blocks(
        delta_step,
        zero_rows,
        (
            lax.all_gather(key_block, "seq", axis=1, tiled=True),
            lax.all_gather(value_block, "seq", axis=1, tiled=True),
        ),
    )

    def query_step(running, pieces, offset):
        key_piece = split_heads(pieces[0])
        probabilities = attention_weights(key_piece, offset)
        grad_probs = head_scores(grad_heads, split_heads(pieces[1]))
        slopes = (probabilities * (grad_probs - row_delta[..., None])).astype(jnp.bfloat16)
        return running + weighted(slopes, key_piece)

    grad_query = over_blocks(
        query_step,
        zero_heads,
        (
            lax.all_gather(key_block, "seq", axis=1, tiled=True),
            lax.all_gather(value_block, "seq", axis=1, tiled=True),
        ),
    )
    all_logs, all_deltas = (
        lax.all_gather(log_total.transpose(0, 2, 1), "seq", axis=1, tiled=True),
        lax.all_gather(row_delta.transpose(0, 2, 1), "seq", axis=1, tiled=True),
    )

    def key_step(running, pieces, offset):
        query_piece = split_heads(pieces[0])
        grad_piece = split_heads(pieces[1])
        extent = pieces[0].shape[1]
        log_piece = lax.dynamic_slice_in_dim(all_logs, offset, extent, 1).transpose(0, 2, 1)
        delta_piece = lax.dynamic_slice_in_dim(all_deltas, offset, extent, 1).transpose(0, 2, 1)
        scores = head_scores(query_piece, key_heads)
        probabilities = jnp.where(
            own_allowed,
            jnp.exp(jnp.where(own_allowed, scores, masked_score) - log_piece[..., None]),
            0.0,
        )
        grad_value = running[1] + transposed(probabilities.astype(jnp.bfloat16), grad_piece)
        grad_probs = head_scores(grad_piece, value_heads)
        slopes = (probabilities * (grad_probs - delta_piece[..., None])).astype(jnp.bfloat16)
        grad_key = running[0] + transposed(slopes, query_piece)
        return (grad_key, grad_value)

    grad_key, grad_value = over_blocks(
        key_step,
        (zero_heads, zero_heads),
        (
            lax.all_gather(query_block, "seq", axis=1, tiled=True),
            lax.all_gather(grad_block, "seq", axis=1, tiled=True),
        ),
    )
    stacked = jnp.stack([grad_query, grad_key, grad_value], axis=2).astype(jnp.bfloat16)
    stacked = stacked.reshape(sequences, head_ways, slice_len, 3, local_width)
    returned = lax.all_to_all(stacked, "head", split_axis=1, concat_axis=4, tiled=True)
    column_scale = jnp.concatenate(
        [
            jnp.full((model_width,), query_scale, jnp.float32),
            jnp.ones((2 * model_width,), jnp.float32),
        ]
    )
    grad_projected = returned.reshape(flat_rows, 3 * model_width).astype(jnp.float32) * column_scale
    grad_shift_query = jnp.sum(grad_projected[:, :model_width], axis=0)
    grad_shift_value = jnp.sum(grad_projected[:, 2 * model_width :], axis=0)
    grad_projected_low = grad_projected.astype(jnp.bfloat16)
    grad_qkv = jnp.dot(first_in.T, grad_projected_low, preferred_element_type=jnp.float32)
    grad_first = jnp.dot(grad_projected_low, full_qkv.T, preferred_element_type=jnp.float32)
    grad_gain_one = jnp.sum(grad_first * normed_one, axis=0)
    grad_shift_one = jnp.sum(grad_first, axis=0)
    grad_inputs = grad_middle + norm_backward(grad_first * gain_vals[0], normed_one, inverse_one)
    grad_gain_rows = jnp.stack([grad_gain_one, grad_gain_two])
    grad_shift_rows = jnp.stack(
        [
            grad_shift_one,
            grad_shift_query,
            grad_shift_value,
            grad_shift_out,
            grad_shift_two,
            grad_shift_proj,
        ]
    )
    owned_grads = (
        lax.psum_scatter(grad_qkv, ("head", "seq"), scatter_dimension=0, tiled=True),
        lax.psum_scatter(grad_out_weight, ("head", "seq"), scatter_dimension=0, tiled=True),
        lax.psum_scatter(grad_fc, ("head", "seq"), scatter_dimension=0, tiled=True),
        lax.psum_scatter(grad_proj, ("head", "seq"), scatter_dimension=0, tiled=True),
        lax.psum_scatter(grad_bias_up, ("head", "seq"), scatter_dimension=0, tiled=True),
        lax.psum_scatter(grad_gain_rows, ("head", "seq"), scatter_dimension=1, tiled=True),
        lax.psum_scatter(grad_shift_rows, ("head", "seq"), scatter_dimension=1, tiled=True),
    )
    return (
        result,
        grad_inputs.reshape(layer_input.shape),
        owned_grads[0],
        owned_grads[1],
        owned_grads[2],
        owned_grads[3],
        owned_grads[4],
        owned_grads[5],
        owned_grads[6],
        root_means,
    )


f32 = jnp.float32
bf16 = jnp.bfloat16
cores = 2
halves = 2
lanes_per = 128


def nn(left, right):
    return lax.dot_general(left, right, (((1,), (0,)), ((), ())), preferred_element_type=f32)


def nt(left, right):
    return lax.dot_general(left, right, (((1,), (1,)), ((), ())), preferred_element_type=f32)


def loop(low, high, step_fn, unroll=1):
    def advance(index, carry):
        step_fn(index)
        return carry

    lax.fori_loop(low, high, advance, 0, unroll=unroll)


def aligned(index, extent):
    return pl.ds(pl.multiple_of(index * extent, extent), extent)


def norm_parts(v):
    centre = v - jnp.mean(v, axis=-1, keepdims=True)
    inverse = lax.rsqrt(jnp.mean(centre * centre, axis=-1, keepdims=True) + epsilon)
    return centre * inverse, inverse


def remote(src, dst, send_sem, recv_sem, place):
    return pltpu.make_async_remote_copy(
        src_ref=src,
        dst_ref=dst,
        send_sem=send_sem,
        recv_sem=recv_sem,
        device_id=place,
        device_id_type=pl.DeviceIdType.MESH,
    )


def dense(v):
    n = v.shape[0]
    low = v[:, 0:lanes_per]
    rest = v[:, lanes_per:]
    return low, jnp.concatenate([rest[0 : n // 2], rest[n // 2 :]], axis=1)


def loose(low, rest):
    wide = rest.shape[1] // 2
    return jnp.concatenate(
        [low, jnp.concatenate([rest[:, 0:wide], rest[:, wide:]], axis=0)], axis=1
    )


class Exchange:
    def __init__(self, n, me, place, src, dst, send_sem, recv_sem, order=None):
        self.n, self.me, self.place, self.src, self.dst = n, me, place, src, dst
        self.send_sem, self.recv_sem, self.order = send_sem, recv_sem, order

    def out(self, q):
        return remote(
            self.src(q), self.dst(self.me), self.send_sem, self.recv_sem.at[self.me], self.place(q)
        )

    def into(self, q):
        return remote(
            self.dst(q), self.dst(q), self.send_sem, self.recv_sem.at[q], self.place(q)
        )

    def peer(self, k):
        return lax.rem(self.me + k, self.n)

    def send(self, low=0, high=None):
        if self.order is None:
            loop(1, self.n, lambda k: self.out(self.peer(k)).start())
        else:
            for q in self.order[low:high]:
                self.out(q).start()

    def wait(self):
        loop(1, self.n, lambda k: self.into(self.peer(k)).wait_recv())

    def drain(self):
        loop(1, self.n, lambda k: self.out(self.peer(k)).wait_send())


def chip_peer(n, inner, me, k):
    outer = n // inner
    a = lax.rem(me // inner + lax.rem(k, outer), outer)
    b = lax.rem(lax.rem(me, inner) + k // outer, inner)
    return a * inner + b


class Gather:
    def __init__(self, n, inner, me, core, place, dst, send_sem, recv_sem):
        self.n, self.inner, self.me, self.core, self.place, self.dst = n, inner, me, core, place, dst
        self.send_sem, self.recv_sem = send_sem, recv_sem
        self.mine = me * cores + core

    def peer(self, k):
        return chip_peer(self.n, self.inner, self.me, k)

    def move(self, slot, place):
        return remote(
            self.dst(slot), self.dst(slot), self.send_sem, self.recv_sem.at[slot], place
        )

    def out(self, k):
        return self.move(self.mine, self.place(self.peer(k), self.core))

    def aside(self, k):
        return self.move(
            self.peer(k) * cores + self.core, self.place(self.me, 1 - self.core)
        )

    def send(self, last=None):
        loop(1, last or self.n, lambda k: self.out(k).start())
        self.aside(0).start()

    def send_last(self):
        loop(1, self.n - 1, lambda k: self.out(k).wait_send())
        self.out(self.n - 1).start()

    def relay_from(self, k):
        self.out_slot(k, self.core).wait_recv()
        self.aside(k).start()

    def out_slot(self, k, core):
        return self.move(self.peer(k) * cores + core, self.place(self.peer(k), core))

    def wait_from(self, k):
        self.out_slot(k, 1 - self.core).wait_recv()

    def relay(self):
        loop(1, self.n, self.relay_from)

    def wait(self):
        loop(0, self.n, self.wait_from)

    def drain(self, first=1):
        loop(first, self.n, lambda k: self.out(k).wait_send())
        loop(0, self.n, lambda k: self.aside(k).wait_send())


class Reduce:
    def __init__(self, n, inner, me, core, place, stage, beside, landed, sems, recv_sems, add):
        self.n, self.inner, self.me, self.core, self.place = n, inner, me, core, place
        self.stage, self.beside, self.landed = stage, beside, landed
        self.sems, self.recv_sems, self.add = sems, recv_sems, add

    def peer(self, k):
        return chip_peer(self.n, self.inner, self.me, k)

    def own(self, r):
        return self.stage(r * cores + self.core)

    def aside(self, r):
        return remote(
            self.stage(r * cores + 1 - self.core),
            self.beside(r),
            self.sems.at[0],
            self.recv_sems.at[0, r],
            self.place(self.me, 1 - self.core),
        )

    def out(self, r):
        return remote(
            self.own(r),
            self.landed(self.me),
            self.sems.at[1],
            self.recv_sems.at[1, self.me],
            self.place(r, self.core),
        )

    def combine(self, r):
        self.aside(r).wait_recv()
        self.add(self.own(r), self.beside(r))

    def combine_out(self, k):
        r = self.peer(k)
        self.combine(r)
        self.out(r).start()

    def send_aside(self):
        loop(1, self.n, lambda k: self.aside(self.peer(k)).start())
        self.aside(self.me).start()

    def send(self):
        loop(1, self.n, self.combine_out)
        self.combine(self.me)

    def wait(self):
        def one(k):
            r = self.peer(k)
            remote(
                self.landed(r), self.landed(r), self.sems.at[1], self.recv_sems.at[1, r],
                self.place(r, self.core),
            ).wait_recv()

        loop(1, self.n, one)

    def drain_aside(self):
        loop(0, self.n, lambda k: self.aside(self.peer(k)).wait_send())

    def drain(self):
        self.drain_aside()
        loop(1, self.n, lambda k: self.out(self.peer(k)).wait_send())


def fused_layer(layer_input, grad_out, lengths, w_qkv, w_out, w_fc, w_proj, b_fc, norm_gains, biases):
    seqs, _, sl, width = layer_input.shape
    hs = lax.axis_size("head")
    ss = lax.axis_size("seq")
    zs = ss // seqs
    ps = hs * seqs
    xs = hs // cores
    rs = xs * seqs
    group = sl * hs
    tw = width // zs
    heads = tw // HEAD_DIM
    rows = w_qkv.shape[0]
    ff_rows = w_proj.shape[0]
    part = ff_rows * zs
    home = seqs * sl
    qn = ss * sl
    slab = ps * home
    near = zs // halves
    us = near * seqs
    duo = cores * home
    query_block = 256
    blocks = qn // query_block
    chunk = 32
    pair = 2 * rows
    quad = 8 * rows
    scale = HEAD_DIM ** (-0.5)

    def ff_place(q, b):
        u, c = q // cores, q % cores
        head_of = (b // halves) * cores + c
        return head_of * ss + ((b % halves) * near + u // seqs) * seqs + u % seqs

    def kernel(
        len_ref, x_ref, go_ref, wqkv_ref, wout_ref, wfc_ref, wproj_ref, bfc_ref, gain_ref, bias_ref,
        out_ref, gin_ref, gqkv_ref, gout_ref, gfc_ref, gproj_ref, ar_ref,
        small, small_z, small_g, prm, up_bias,
        qkv_st, fc_st, wqg, wog, wfg, wpg, wq, wo, wf,
        xg, q_s, kvg, kneg, probs, s_scr, t_scr, pb_scr, ds_scr, o_s, o_st, og, mixed_s,
        middle_s, gm_s,
        x2g, gog, act, gh, x2t, gs_st, gs_in, gs_red, fd_st, fd_in, fd_red,
        do_st, dog, dot_s, qt_s, dq_s, dkt, dvt, kv_st, kv_in, kv_red, gpt, gp,
        gf_st, gfg, wo_in, wo_red, woz, wozr, wq_in, wq_red, wqz, wqzr,
        wfs, wfr, wfm, wfq, wfz, wfzr, wps, wpr, wpm, wpq, arg, ard, sums, ar_st, arz,
        send, zsem, lsem, psem, bsem, gsem, rsem, ksem, krsem, ssem,
    ):
        h = lax.axis_index("head")
        s = lax.axis_index("seq")
        z = s // seqs
        y = lax.rem(s, seqs)
        core = lax.rem(h, cores)
        r_at = (h // cores) * seqs + y
        x_at = h // cores
        p = r_at * cores + core
        zh = z // near
        zl = lax.rem(z, near)
        u_at = zl * seqs + y
        pf = u_at * cores + core
        t_at = x_at * halves + zh
        t_far = x_at * halves + 1 - zh

        def chip_place(r, c):
            return ((r // seqs) * cores + c, z * seqs + lax.rem(r, seqs))

        def slab_place(q):
            return chip_place(q // cores, lax.rem(q, cores))

        def square_place(u, c):
            return (x_at * cores + c, (zh * near + u // seqs) * seqs + lax.rem(u, seqs))

        def ring_place(q):
            return square_place(q // cores, lax.rem(q, cores))

        def half_place(q):
            return (h, (q * near + zl) * seqs + y)

        def beside_place(q):
            return (q * cores + core, s)

        def line_place(q):
            return (h, q)

        def z_place(q):
            return (h, q * seqs + y)

        def x_place(r, c):
            return (r * cores + c, s)

        count = {}

        def take(name):
            number = count.get(name, 0)
            count[name] = number + 1
            return number

        z_order = [(1 - zh) * (zs - 1), near - zh, zh * zs + 1 - z]
        line_order = [q * seqs + b for q in z_order for b in range(seqs)] + [z * seqs + 1 - y]

        def over_z(src, dst):
            return Exchange(
                zs, z, z_place, src, dst, send.at[take("s")], zsem.at[take("z")], z_order
            )

        def over_line(src, dst):
            return Exchange(
                ss, s, line_place, src, dst, send.at[take("s")], lsem.at[take("l")], line_order
            )

        def over_plane(src, dst):
            return Exchange(ps, p, slab_place, src, dst, send.at[take("s")], psem.at[take("p")])

        def over_square(src, dst):
            return Exchange(ps, pf, ring_place, src, dst, send.at[take("s")], psem.at[take("p")])

        def over_half(src, dst):
            return Exchange(halves, zh, half_place, src, dst, send.at[take("s")], bsem.at[take("b")])

        def over_x(src, dst):
            return Exchange(xs, x_at, beside_place, src, dst, send.at[take("s")], bsem.at[take("b")])

        def gather(dst):
            return Gather(rs, seqs, r_at, core, chip_place, dst, send.at[take("s")], gsem.at[take("g")])

        def gather_square(dst):
            return Gather(us, seqs, u_at, core, square_place, dst, send.at[take("s")], gsem.at[take("g")])

        def add_rows(block):
            def add(a, b):
                extent = a.shape[0]

                def one(i):
                    at = aligned(i, block)
                    a[at, :] = (a[at, :].astype(f32) + b[at, :].astype(f32)).astype(bf16)

                loop(0, extent // block, one)

            return add

        def add_blocks(a, b):
            def one(i):
                a[i] = (a[i].astype(f32) + b[i].astype(f32)).astype(bf16)

            loop(0, a.shape[0], one)

        def reduce(stage, beside, landed, add):
            number = take("r")
            return Reduce(
                rs, seqs, r_at, core, chip_place, stage, beside, landed, ssem.at[number],
                rsem.at[number], add,
            )

        def reduce_square(stage, beside, landed, add):
            number = take("r")
            return Reduce(
                us, seqs, u_at, core, square_place, stage, beside, landed, ssem.at[number],
                rsem.at[number], add,
            )

        ex_small_z = over_z(lambda q: small, lambda q: small_z.at[q])
        ex_wq_z = over_z(lambda q: qkv_st.at[q], lambda q: wqg.at[p, q])
        ex_wo_z = over_z(lambda q: wout_ref, lambda q: wog.at[p, q])
        ex_x = over_line(lambda q: x_ref.at[lax.rem(q, seqs)], lambda q: xg.at[q])
        ga_small = gather(lambda q: small_g.at[q])
        ga_wq = gather(lambda q: wqg.at[q])
        ga_wo = gather(lambda q: wog.at[q])
        ex_wf_p = over_square(lambda q: fc_st.at[q], lambda q: wfg.at[t_at, q])
        ex_wf_1 = over_half(lambda q: wfg.at[t_at], lambda q: wfg.at[x_at * halves + q])
        ex_wf_2 = over_x(lambda q: wfg.at[t_at], lambda q: wfg.at[q * halves + zh])
        ex_wf_3 = over_x(lambda q: wfg.at[t_far], lambda q: wfg.at[q * halves + 1 - zh])
        ex_wp_1 = over_half(lambda q: wproj_ref, lambda q: wpg.at[x_at * halves + q])
        ex_wp_2 = over_x(lambda q: wproj_ref, lambda q: wpg.at[q * halves + zh])
        ex_wp_3 = over_x(lambda q: wpg.at[t_far], lambda q: wpg.at[q * halves + 1 - zh])
        ga_go = gather_square(lambda q: gog.at[q])
        ga_kv = [
            Gather(
                xs, 1, x_at, core, x_place,
                lambda q, i=i: kvg.at[q, :, :, i * query_block : (i + 1) * query_block],
                send.at[take("s")], ksem.at[i],
            )
            for i in range(halves)
        ]
        ex_o = over_line(lambda q: o_st.at[q], lambda q: og.at[lax.rem(q, seqs), q // seqs])
        ga_x2 = gather_square(lambda q: x2g.at[q])
        re_gs = reduce_square(
            lambda q: gs_st.at[q], lambda r: gs_in.at[r], lambda r: gs_red.at[r], add_rows(32),
        )
        re_fd = reduce_square(
            lambda q: fd_st.at[q], lambda r: fd_in.at[r], lambda r: fd_red.at[r], add_rows(32),
        )
        ex_do = over_line(
            lambda q: do_st.at[q // seqs, lax.rem(q, seqs)], lambda q: dog.at[q]
        )
        re_kv = [
            Reduce(
                xs, 1, x_at, core, x_place,
                lambda q, n=n: kv_st.at[n, q], lambda r, n=n: kv_in.at[n, r],
                lambda r, n=n: kv_red.at[n, r],
                ssem.at[take("r")], krsem.at[n], add_blocks,
            )
            for n in range(heads)
        ]
        ex_gf = over_line(lambda q: gf_st.at[q], lambda q: gfg.at[lax.rem(q, seqs), q // seqs])
        re_wo = reduce(
            lambda q: wog.at[q], lambda r: wo_in.at[r], lambda r: wo_red.at[r], add_blocks,
        )
        ex_go_z = over_z(lambda q: woz.at[q], lambda q: wozr.at[q])
        re_wq = reduce(
            lambda q: wqg.at[q], lambda r: wq_in.at[r], lambda r: wq_red.at[r], add_blocks,
        )
        ex_gq_z = over_z(lambda q: wqz.at[q], lambda q: wqzr.at[q])
        ex_gf_1 = over_x(lambda q: wfs.at[pl.ds(q * halves, halves)], lambda q: wfr)
        ex_gf_2 = over_half(lambda q: wfm.at[q], lambda q: wfq)
        ex_gf_3 = over_square(lambda q: wfz.at[q], lambda q: wfzr.at[q])
        ex_gp_1 = over_x(lambda q: wps.at[pl.ds(q * halves, halves)], lambda q: wpr)
        ex_gp_2 = over_half(lambda q: wpm.at[q], lambda q: wpq)
        ex_ar_p = over_plane(lambda q: arg.at[q], lambda q: ard.at[q])
        ex_ar_z = over_z(lambda q: ar_st.at[q], lambda q: arz.at[q])

        barrier = pltpu.get_barrier_semaphore()

        def greet(place, me, n):
            def one(k):
                pl.semaphore_signal(
                    barrier, inc=1, device_id=place(lax.rem(me + k, n)),
                    device_id_type=pl.DeviceIdType.MESH,
                )

            loop(1, n, one)

        greet(slab_place, p, ps)
        greet(line_place, s, ss)
        greet(ring_place, pf, ps)

        small[...] = jnp.zeros_like(small)
        small[0:2, 0:rows] = gain_ref[...].astype(f32)
        small[2:8, 0:rows] = bias_ref[...].astype(f32)
        small[8:9, 0:ff_rows] = bfc_ref[...].astype(f32)
        for t in range(zs):
            for k in range(3):
                qkv_st[t, :, k * tw : (k + 1) * tw] = wqkv_ref[:, k * width + t * tw : k * width + (t + 1) * tw]
        for q in range(ps):
            for b in range(zs):
                at = ff_place(q, b) * ff_rows
                fc_st[q, :, b * ff_rows : (b + 1) * ff_rows] = wfc_ref[:, at : at + ff_rows]
        small_z[z] = small[...]
        wqg[p, z] = qkv_st[z]
        wog[p, z] = wout_ref[...]
        wfg[t_at, pf] = fc_st[pf]
        wpg[t_at] = wproj_ref[...]
        xg[s] = x_ref[y]
        ar_st[...] = jnp.zeros_like(ar_st)
        len_0 = len_ref[0]
        len_1 = len_ref[1]
        len_y = jnp.where(y == 0, len_0, len_1)
        home_row = lax.broadcasted_iota(jnp.int32, (home, 1), 0)
        home_place = s * group + h * sl + lax.rem(home_row, sl)
        keep = jnp.where(home_place < jnp.where(home_row < sl, len_0, len_1), 1.0, 0.0)
        gog[pf] = (go_ref[...].reshape(home, width).astype(f32) * keep).astype(bf16)

        def mask_block(q):
            column = lax.broadcasted_iota(jnp.int32, (8, qn), 1)
            place = (column // sl) * group + q * sl + lax.rem(column, sl)
            kneg[q] = jnp.where(place < len_y, 0.0, masked_score)

        loop(0, hs, mask_block)
        pl.semaphore_wait(barrier, 2 * (ps - 1) + ss - 1)

        ex_small_z.send()
        ex_wq_z.send()
        ex_x.send(0, 1)

        ex_small_z.wait()
        small_g[p] = small_z[...]
        ga_small.send()
        ex_wq_z.wait()
        ga_wq.send()
        ex_wp_2.send()
        ex_x.send(1)
        ex_wo_z.send()
        ex_wf_p.send()
        ex_wp_1.send()
        ga_small.relay()
        ga_wq.relay()

        def d_of(q, t):
            hq = q // cores // seqs * cores + q % cores
            return hq * ss + t * seqs + q // cores % seqs

        ga_small.wait()
        prm[...] = jnp.zeros_like(prm)
        for q in range(ps):
            for t in range(zs):
                d = d_of(q, t)
                prm[0:8, d * rows : (d + 1) * rows] = small_g[q, t, 0:8, 0:rows]
                at = (d * rows) % tw
                triple = (d * rows) // tw
                prm[8 + triple : 9 + triple, at : at + rows] = small_g[q, t, 3:4, 0:rows]
                prm[8 + triple : 9 + triple, 2 * tw + at : 2 * tw + at + rows] = small_g[q, t, 4:5, 0:rows]

        up_bias[...] = jnp.zeros_like(up_bias)
        for b in range(zs):
            q = ((b // halves) * seqs + y) * cores + core
            up_bias[0:1, b * ff_rows : (b + 1) * ff_rows] = small_g[q, (b % halves) * near + zl, 8:9, 0:ff_rows]

        def assemble(src, dst):
            def one(i):
                hq = i // zs
                xq = hq // cores
                cq = lax.rem(hq, cores)
                t = lax.rem(i, zs)
                dst[aligned(i, pair), :] = jnp.concatenate(
                    [src(xq, cq, 0, t).astype(f32), src(xq, cq, 1, t).astype(f32)], axis=0
                ).astype(bf16)

            loop(0, width // pair, one)

        ga_wq.wait()
        assemble(lambda a, c, b, t: wqg[(a * seqs + b) * cores + c, t], wq)

        def first_norm(i):
            xv = xg[pl.ds(2 * i, 2)].reshape(2 * sl, width).astype(f32)
            normed, inverse = norm_parts(xv)
            return normed, (normed * prm[0:1, :] + prm[2:3, :]).astype(bf16)

        for i in range(halves):
            for q in range(ss // halves * i, ss // halves * (i + 1)):
                @pl.when(s != q)
                def _(q=q):
                    ex_x.into(q).wait_recv()

            for j in range(zs // halves):
                _, first = first_norm(zs // halves * i + j)
                x2t[(zs // halves * i + j) * 2 * sl : (zs // halves * i + j + 1) * 2 * sl, 0:width] = first
            at = slice(i * query_block, (i + 1) * query_block)
            projected = nn(x2t[at, 0:width], wq[...]) + prm[pl.ds(8 + z, 1), 0 : 3 * tw]
            q_s[at, :] = (projected[:, 0:tw] * scale).astype(bf16)
            turned = projected[:, tw:].T.astype(bf16)
            kvg[h, 0, :, at] = turned[0:tw, :]
            kvg[h, 1, :, at] = turned[tw : 2 * tw, :]
            ga_kv[i].send()
        ex_wf_p.wait()
        ga_go.send()
        ex_wf_1.send()
        for i in range(halves):
            ga_kv[i].relay()
        ex_wo_z.wait()
        ga_wo.send()
        for i in range(halves):
            ga_kv[i].wait()

        lane_head = lax.broadcasted_iota(jnp.int32, (query_block, tw), 1) // HEAD_DIM

        def score(n, i):
            queries = q_s[i * query_block : (i + 1) * query_block, :]
            masked = jnp.where(lane_head == n, queries, jnp.zeros_like(queries))
            for b in range(hs):
                probs[n, i, :, b * qn : (b + 1) * qn] = nn(masked, kvg[b, 0])

        def soften(n, i, low_ref):
            for r in range(query_block // chunk):
                rat = slice(r * chunk, (r + 1) * chunk)
                sv = [probs[n, i, rat, b * qn : (b + 1) * qn] + kneg[b, 0:1, :] for b in range(hs)]
                top = jnp.max(functools.reduce(jnp.maximum, sv), axis=-1, keepdims=True)
                ev = [jnp.exp(v - top) for v in sv]
                inv = 1.0 / jnp.sum(functools.reduce(jnp.add, ev), axis=-1, keepdims=True)
                for b in range(hs):
                    value = ev[b] * inv
                    probs[n, i, rat, b * qn : (b + 1) * qn] = value
                    low_ref[rat, b * qn : (b + 1) * qn] = value.astype(bf16)

        def mix(n, i, low_ref):
            head_out = nt(low_ref[:, 0:qn], kvg[0, 1])
            for b in range(1, hs):
                head_out = head_out + nt(low_ref[:, b * qn : (b + 1) * qn], kvg[b, 1])
            at = slice(i * query_block, (i + 1) * query_block)
            o_s[at, :] = jnp.where(lane_head == n, head_out.astype(bf16), o_s[at, :])

        o_s[...] = jnp.zeros_like(o_s)
        score(0, 0)
        for n in range(heads):
            soften(n, 0, pb_scr)
            score(n, 1)
            if n:
                mix(n - 1, 1, ds_scr)
            soften(n, 1, ds_scr)
            if n < heads - 1:
                score(n + 1, 0)
            mix(n, 0, pb_scr)
            if n == 0:
                ex_wf_2.send()
        mix(heads - 1, 1, ds_scr)

        def pack(ref, v):
            ref[0:sl, :], ref[sl:, :] = dense(v)

        def unpack(ref):
            return loose(ref[0:sl, :], ref[sl:, :])

        def lay_out(q):
            pack(o_st.at[q], o_s[aligned(q, sl), :])

        loop(0, ss, lay_out)
        ex_o.send()
        og[y, z] = o_st[s]
        ex_wf_1.wait()
        ex_wf_3.send()
        ex_wp_1.wait()
        ex_wp_3.send()
        ga_wo.relay()
        ga_go.relay()

        ga_wo.wait()
        assemble(lambda a, c, b, t: wog[(a * seqs + b) * cores + c, t], wo)
        ex_o.wait()
        branch = jnp.broadcast_to(prm[5:6, :], (home, width))
        for t in range(zs):
            mixed = jnp.concatenate([unpack(og.at[a, t]) for a in range(seqs)], axis=0)
            mixed_s[t] = mixed
            branch = branch + nn(mixed, wo[t * tw : (t + 1) * tw, :])
        middle = x_ref[...].reshape(home, width).astype(f32) + branch
        normed, _ = norm_parts(middle)
        x2g[pf] = (normed * prm[1:2, :] + prm[6:7, :]).astype(bf16)
        ga_x2.send(us - 1)
        middle_s[...] = middle
        for ex in (ga_go, ex_wf_2, ex_wp_2, ex_wf_3, ex_wp_3):
            ex.wait()
        assemble(
            lambda a, c, b, t: wfg[a * halves + t // near, (lax.rem(t, near) * seqs + b) * cores + c], wf
        )

        def feed(k, running):
            r = ga_x2.peer(k)

            @pl.when(k > 0)
            def _():
                ga_x2.relay_from(k)

            ga_x2.wait_from(k)
            at = aligned(r, duo)
            chip = pl.ds(cores * r, cores)
            hid = nn(x2g[chip].reshape(duo, width), wf[...]) + up_bias[0:1, :]
            gate = 1.0 / (1.0 + jnp.exp(-quick_slope * hid))
            act[at, :] = (hid * gate).astype(bf16)
            flow = nt(gog[chip].reshape(duo, width), wpg[...].reshape(part, width))
            slope = gate + quick_slope * hid * gate * (1.0 - gate)
            back = (flow * slope).astype(bf16)
            gh[at, :] = back
            gs_st[chip] = nt(back, wf[...]).astype(bf16).reshape(cores, home, width)
            re_gs.aside(r).start()

            @pl.when(k == 0)
            def _():
                ga_x2.send_last()

            @pl.when(k > 1)
            def _():
                re_gs.combine_out(k - 1)

            return running + jnp.sum(back.astype(f32), axis=0, keepdims=True)

        grad_up = lax.fori_loop(0, us, feed, jnp.zeros((1, part), f32))

        def turn_act(q):
            at = aligned(q, home)
            x2t[0:part, at] = act[at, :].T

        loop(0, ps, turn_act)
        re_gs.combine_out(us - 1)
        re_gs.combine(u_at)

        def proj_grad(c):
            wps[pl.ds(2 * c, 2)] = nn(
                x2t[aligned(c, 2 * ff_rows), :], gog[...].reshape(slab, width)
            ).astype(bf16).reshape(2, ff_rows, width)

        loop(0, zs // 2, proj_grad)
        ex_gp_1.send()

        def feed_down(r):
            chip = pl.ds(cores * r, cores)
            fd_st[chip] = nn(act[aligned(r, duo), :], wpg[...].reshape(part, width)).astype(bf16).reshape(
                cores, home, width
            )
            re_fd.aside(r).start()

        loop(0, us, feed_down)

        def scatter_rows(c, val, put):
            for j in range(val.shape[0] // rows):
                d = c * (val.shape[0] // rows) + j
                hq = d // ss
                sd = lax.rem(d, ss)
                put(
                    hq // cores, lax.rem(hq, cores), lax.rem(sd, seqs), sd // seqs,
                    val[j * rows : (j + 1) * rows, :].astype(bf16),
                )

        def turn_in(q):
            x2t[:, aligned(q, home)] = x2g[q].T

        loop(0, ps, turn_in)

        def fc_grad(c):
            def put(a, c, b, t, value):
                wfs[a * halves + t // near, (lax.rem(t, near) * seqs + b) * cores + c] = value

            scatter_rows(c, nn(x2t[aligned(c, quad), :], gh[...]), put)

        loop(0, width // quad, fc_grad)
        ex_gf_1.send()

        for t in range(zs):
            x2t[t * tw : (t + 1) * tw, 0:home] = mixed_s[t].T
        grad_final = go_ref[...].reshape(home, width).astype(f32) * keep

        re_gs.wait()

        def landed_sum(re, own):
            total = own
            for k in range(1, us):
                total = total + re.landed(re.peer(k))[...].astype(f32)
            return total

        grad_second = landed_sum(re_gs, gs_st[pf].astype(f32))
        n2, r2 = norm_parts(middle_s[...])
        grad_middle = grad_final + norm_backward(grad_second * prm[1:2, :], n2, r2)
        grad_branch = grad_middle.astype(bf16)
        for t in range(zs):
            value = nt(grad_branch, wo[t * tw : (t + 1) * tw, :]).astype(bf16)
            for a in range(seqs):
                pack(do_st.at[t, a], value[a * sl : (a + 1) * sl, :])
        ex_do.send()
        dog[s] = do_st[z, y]
        gm_s[...] = grad_middle
        sums[...] = jnp.zeros_like(sums)
        arg[...] = jnp.zeros_like(arg)
        for q in range(ps):
            c, b, a = q % cores, q // cores % seqs, q // cores // seqs
            for i in range(zs):
                at = (a * halves + i // near) * ff_rows
                arg[q, 8 + i : 9 + i, 0:ff_rows] = jnp.where(
                    (core == c) & (y == b) & (zl == i % near), grad_up[:, at : at + ff_rows], 0.0
                )
        sums[1:2, :] = jnp.sum(grad_second * n2, axis=0, keepdims=True)
        sums[6:7, :] = jnp.sum(grad_second, axis=0, keepdims=True)
        sums[5:6, :] = jnp.sum(grad_branch.astype(f32), axis=0, keepdims=True)


        def out_grad(c):
            def put(a, c, b, t, value):
                wog[(a * seqs + b) * cores + c, t] = value

            scatter_rows(c, nn(x2t[aligned(c, quad), 0:home], gm_s[...].astype(bf16)), put)

        ga_wo.drain()
        loop(0, width // quad, out_grad)
        re_wo.send_aside()

        ex_do.wait()
        ex_gp_1.wait()

        def proj_sum(q):
            wpm[q] = (wps[t_at - zh + q].astype(f32) + wpr[q].astype(f32)).astype(bf16)

        loop(0, halves, proj_sum)
        ex_gp_2.send()
        re_fd.send()
        re_wo.send()

        def gather_do(i):
            at = aligned(i, 2 * sl)
            value = jnp.concatenate([unpack(dog.at[2 * i]), unpack(dog.at[2 * i + 1])], axis=0)
            o_s[at, :] = value
            dot_s[:, at] = value.T
            qt_s[:, at] = q_s[at, :].T

        loop(0, ss // 2, gather_do)
        dq_s[...] = jnp.zeros_like(dq_s)

        def slope_in(n, i, out_ref):
            outer = o_s[i * query_block : (i + 1) * query_block, :]
            masked = jnp.where(lane_head == n, outer, jnp.zeros_like(outer))
            for b in range(hs):
                out_ref[:, b * qn : (b + 1) * qn] = nn(masked, kvg[b, 1])

        def slopes(n, i, in_ref, slope_ref, low_ref):
            for r in range(query_block // chunk):
                rat = slice(r * chunk, (r + 1) * chunk)
                dp = [in_ref[rat, b * qn : (b + 1) * qn] for b in range(hs)]
                pv = [probs[n, i, rat, b * qn : (b + 1) * qn] for b in range(hs)]
                delta = jnp.sum(
                    functools.reduce(jnp.add, [a * c for a, c in zip(dp, pv)]), axis=-1, keepdims=True
                )
                for b in range(hs):
                    slope_ref[rat, b * qn : (b + 1) * qn] = (pv[b] * (dp[b] - delta)).astype(bf16)
                    low_ref[rat, b * qn : (b + 1) * qn] = pv[b].astype(bf16)

        def slope_out(n, i, slope_ref, low_ref):
            at = slice(i * query_block, (i + 1) * query_block)
            head_rows = slice(n * HEAD_DIM, (n + 1) * HEAD_DIM)
            head_dq = nt(slope_ref[:, 0:qn], kvg[0, 0])
            for b in range(1, hs):
                head_dq = head_dq + nt(slope_ref[:, b * qn : (b + 1) * qn], kvg[b, 0])
            dq_s[at, :] = jnp.where(
                lane_head == n, (head_dq.astype(bf16).astype(f32) * scale).astype(bf16), dq_s[at, :]
            )
            for b in range(hs):
                new_k = nn(qt_s[head_rows, at], slope_ref[:, b * qn : (b + 1) * qn])
                new_v = nn(dot_s[head_rows, at], low_ref[:, b * qn : (b + 1) * qn])
                if i == 0:
                    dkt[b] = new_k
                    dvt[b] = new_v
                else:
                    kv_st[n, b, 0] = (dkt[b] + new_k).astype(bf16)
                    kv_st[n, b, 1] = (dvt[b] + new_v).astype(bf16)

        slope_in(0, 0, s_scr)
        for n in range(heads):
            slopes(n, 0, s_scr, ds_scr, pb_scr)
            slope_in(n, 1, t_scr)
            slope_out(n, 0, ds_scr, pb_scr)
            slopes(n, 1, t_scr, ds_scr, pb_scr)
            if n < heads - 1:
                slope_in(n + 1, 0, s_scr)
            slope_out(n, 1, ds_scr, pb_scr)
            re_kv[n].send_aside()
            if n:
                re_kv[n - 1].send()
            if n == 0:
                ex_gf_1.wait()

                def fc_sum(i):
                    q, b = i // ps, lax.rem(i, ps)
                    wfm[q, b] = (wfs[t_at - zh + q, b].astype(f32) + wfr[q, b].astype(f32)).astype(bf16)

                loop(0, halves * ps, fc_sum)
                ex_gf_2.send()
        re_kv[heads - 1].send()

        gpt[0:tw, :] = dq_s[...].T

        def turn_first(i):
            _, first = first_norm(i)
            x2t[:, aligned(i, 2 * sl)] = first.T

        loop(0, zs, turn_first)

        def final_rows(re, own, landed, dst):
            def one(t):
                total = own[p, t].astype(f32)
                for k in range(1, rs):
                    total = total + landed[re.peer(k), t].astype(f32)
                dst[t] = total.astype(bf16)

            loop(0, zs, one)

        re_wo.wait()
        final_rows(re_wo, wog, wo_red, woz)
        ex_go_z.send()
        wozr[z] = woz[z]
        ex_gf_2.wait()

        def fc_last(q):
            wfz[q] = (wfm[zh, q].astype(f32) + wfq[q].astype(f32)).astype(bf16)

        loop(0, ps, fc_last)
        ex_gf_3.send()
        wfzr[pf] = wfz[pf]
        for n in range(heads):
            re_kv[n].wait()
            for k in range(2):
                at = (1 + k) * tw + n * HEAD_DIM
                gpt[at : at + HEAD_DIM, :] = (
                    kv_st[n, h, k].astype(f32) + kv_red[n, re_kv[n].peer(1), k].astype(f32)
                ).astype(bf16)
        gp[...] = gpt[...].T

        gain_sum = jnp.zeros((1, width), f32)
        shift_sum = jnp.zeros((1, width), f32)
        block = ss // halves

        def first_grad(i):
            value = nt(gp[aligned(i, block * sl), :], wq[...])
            gf_st[pl.ds(block * i, block)] = value.astype(bf16).reshape(block, sl, width)

        first_grad(1 - zh)
        ex_gf.send(0, 1)

        def qkv_grad(c):
            def put(a, c, b, t, value):
                wqg[(a * seqs + b) * cores + c, t] = value

            scatter_rows(c, nn(x2t[aligned(c, quad), 0:qn], gp[...]), put)

        ga_wq.drain()
        loop(0, width // quad, qkv_grad)
        re_wq.send_aside()
        first_grad(zh)
        re_wq.send()
        ex_gf.send(1)
        gfg[y, z] = gf_st[s]
        for i in range(zs):
            value = gf_st[2 * i : 2 * i + 2].reshape(2 * sl, width).astype(f32)
            normed, _ = first_norm(i)
            gain_sum = gain_sum + jnp.sum(value * normed, axis=0, keepdims=True)
            shift_sum = shift_sum + jnp.sum(value, axis=0, keepdims=True)

        sums[0:1, :] = gain_sum
        sums[2:3, :] = shift_sum
        re_fd.wait()
        feed_out = landed_sum(re_fd, fd_st[pf].astype(f32)) + prm[7:8, :]
        final = middle_s[...] + feed_out
        out_ref[...] = (final * keep).astype(bf16).reshape(seqs, sl, width)
        xv = x_ref[...].reshape(home, width).astype(f32)
        br = middle_s[...] - xv
        place = lax.broadcasted_iota(jnp.int32, (1, 128), 1)
        squares = jnp.zeros((1, 128), f32)
        for k, value in enumerate((xv, br, feed_out, final)):
            squares = squares + jnp.where(place == k, jnp.sum(keep * value * value), 0.0)
        for q in range(ps):
            arg[q, 12:13, :] = squares
        projected_sum = jnp.sum(gp[...].astype(f32), axis=0, keepdims=True)
        for i in range(zs):
            at = slice(i * tw, (i + 1) * tw)
            sums[3:4, at] = jnp.where(z == i, projected_sum[:, 0:tw], 0.0)
            sums[4:5, at] = jnp.where(z == i, projected_sum[:, 2 * tw :], 0.0)
        sums[7:8, :] = jnp.sum(gog[pf].astype(f32), axis=0, keepdims=True)

        for q in range(ps):
            for i in range(zs):
                at = d_of(q, i) * rows
                arg[q, 0:8, i * rows : (i + 1) * rows] = sums[0:8, at : at + rows]
        ex_ar_p.send()
        ard[p] = arg[p]

        ex_gp_2.wait()
        gproj_ref[...] = wpm[zh].astype(f32) + wpq[...].astype(f32)

        re_wq.wait()
        final_rows(re_wq, wqg, wq_red, wqz)
        ex_gq_z.send()
        wqzr[z] = wqz[z]
        ex_ar_p.wait()
        total = functools.reduce(jnp.add, [ard[q] for q in range(ps)])
        for i in range(zs):
            ar_st[i, 0:8, 0:rows] = total[0:8, i * rows : (i + 1) * rows]
            ar_st[i, 8:9, :] = total[8 + i : 9 + i, :]
            ar_st[i, 9:10, :] = total[12:13, :]
        ex_ar_z.send()
        arz[z] = ar_st[z]
        ex_gf.wait()
        grad_first = functools.reduce(jnp.add, [gfg[:, t].astype(f32) for t in range(zs)]).reshape(home, width)
        n1, r1 = norm_parts(x_ref[...].reshape(home, width).astype(f32))
        grad_in = gm_s[...] + norm_backward(grad_first * prm[0:1, :], n1, r1)
        gin_ref[...] = grad_in.reshape(seqs, sl, width)

        ex_gf_3.wait()
        gfc_ref[...] = wfzr[...].astype(f32)
        ex_gq_z.wait()
        gqkv_ref[...] = wqzr[...].astype(f32)
        ex_ar_z.wait()
        ar_ref[...] = functools.reduce(jnp.add, [arz[t] for t in range(zs)])
        ex_go_z.wait()
        gout_ref[...] = functools.reduce(jnp.add, [wozr[t].astype(f32) for t in range(zs)])

        for ex in (
            ex_small_z, ex_wq_z, ex_wo_z, ex_x, ga_small, ex_wf_p, ex_wf_1, ex_wf_2, ex_wf_3,
            ex_wp_1, ex_wp_2, ex_wp_3,
            ga_go, *ga_kv, ex_o, re_gs, re_fd, ex_do, *re_kv, ex_gf, re_wo, ex_go_z, re_wq, ex_gq_z,
            ex_gf_1, ex_gf_2, ex_gf_3, ex_gp_1, ex_gp_2, ex_ar_p, ex_ar_z,
        ):
            ex.drain()
        ga_x2.drain(us - 1)

    vm = pltpu.VMEM
    scratch = [
        vm((16, 128), f32),
        vm((zs, 16, 128), f32),
        vm((ps, zs, 16, 128), f32),
        vm((16, width), f32),
        vm((8, part), f32),
        vm((zs, rows, 3 * tw), bf16),
        vm((ps, rows, part), bf16),
        vm((ps, zs, rows, 3 * tw), bf16),
        vm((ps, zs, rows, width), bf16),
        vm((zs, ps, rows, part), bf16),
        vm((zs, ff_rows, width), bf16),
        vm((width, 3 * tw), bf16),
        vm((width, width), bf16),
        vm((width, part), bf16),
        vm((ss, sl, width), bf16),
        vm((qn, tw), bf16),
        vm((hs, 2, tw, qn), bf16),
        vm((hs, 8, qn), f32),
        vm((heads, blocks, query_block, hs * qn), f32),
        vm((query_block, hs * qn), f32),
        vm((query_block, hs * qn), f32),
        vm((query_block, hs * qn), bf16),
        vm((query_block, hs * qn), bf16),
        vm((qn, tw), bf16),
        vm((ss, sl * tw // lanes_per, lanes_per), bf16),
        vm((seqs, zs, sl * tw // lanes_per, lanes_per), bf16),
        vm((zs, home, tw), bf16),
        vm((home, width), f32),
        vm((home, width), f32),
        vm((ps, home, width), bf16),
        vm((ps, home, width), bf16),
        vm((slab, part), bf16),
        vm((slab, part), bf16),
        vm((width, slab), bf16),
        vm((ps, home, width), bf16),
        vm((rs, home, width), bf16),
        vm((rs, home, width), bf16),
        vm((ps, home, width), bf16),
        vm((rs, home, width), bf16),
        vm((rs, home, width), bf16),
        vm((zs, seqs, sl * tw // lanes_per, lanes_per), bf16),
        vm((ss, sl * tw // lanes_per, lanes_per), bf16),
        vm((tw, qn), bf16),
        vm((tw, qn), bf16),
        vm((qn, tw), bf16),
        vm((hs, HEAD_DIM, qn), f32),
        vm((hs, HEAD_DIM, qn), f32),
        vm((heads, hs, 2, HEAD_DIM, qn), bf16),
        vm((heads, xs, 2, HEAD_DIM, qn), bf16),
        vm((heads, xs, 2, HEAD_DIM, qn), bf16),
        vm((3 * tw, qn), bf16),
        vm((qn, 3 * tw), bf16),
        vm((ss, sl, width), bf16),
        vm((seqs, zs, sl, width), bf16),
        vm((rs, zs, rows, width), bf16),
        vm((rs, zs, rows, width), bf16),
        vm((zs, rows, width), bf16),
        vm((zs, rows, width), bf16),
        vm((rs, zs, rows, 3 * tw), bf16),
        vm((rs, zs, rows, 3 * tw), bf16),
        vm((zs, rows, 3 * tw), bf16),
        vm((zs, rows, 3 * tw), bf16),
        vm((zs, ps, rows, part), bf16),
        vm((halves, ps, rows, part), bf16),
        vm((halves, ps, rows, part), bf16),
        vm((ps, rows, part), bf16),
        vm((ps, rows, part), bf16),
        vm((ps, rows, part), bf16),
        vm((zs, ff_rows, width), bf16),
        vm((halves, ff_rows, width), bf16),
        vm((halves, ff_rows, width), bf16),
        vm((ff_rows, width), bf16),
        vm((ps, 16, 128), f32),
        vm((ps, 16, 128), f32),
        vm((8, width), f32),
        vm((zs, 16, 128), f32),
        vm((zs, 16, 128), f32),
        pltpu.SemaphoreType.DMA((33,)),
        pltpu.SemaphoreType.DMA((10, zs)),
        pltpu.SemaphoreType.DMA((4, ss)),
        pltpu.SemaphoreType.DMA((3, ps)),
        pltpu.SemaphoreType.DMA((10, 2)),
        pltpu.SemaphoreType.DMA((6, ps)),
        pltpu.SemaphoreType.DMA((7, 2, rs)),
        pltpu.SemaphoreType.DMA((zs, hs)),
        pltpu.SemaphoreType.DMA((heads, 2, xs)),
        pltpu.SemaphoreType.DMA((7, 2)),
    ]
    in_vmem = pl.BlockSpec(memory_space=pltpu.VMEM)
    in_smem = pl.BlockSpec(memory_space=pltpu.SMEM)
    results = pl.pallas_call(
        kernel,
        out_shape=(
            jax.ShapeDtypeStruct((seqs, sl, width), bf16),
            jax.ShapeDtypeStruct((seqs, sl, width), f32),
            jax.ShapeDtypeStruct((zs, rows, 3 * tw), f32),
            jax.ShapeDtypeStruct((rows, width), f32),
            jax.ShapeDtypeStruct((ps, rows, part), f32),
            jax.ShapeDtypeStruct((ff_rows, width), f32),
            jax.ShapeDtypeStruct((16, 128), f32),
        ),
        in_specs=[in_smem] + [in_vmem] * 9,
        out_specs=(in_vmem,) * 7,
        scratch_shapes=scratch,
        compiler_params=pltpu.CompilerParams(
            collective_id=0, has_side_effects=True, vmem_limit_bytes=63 * 1024 * 1024
        ),
        name="layer",
    )(
        lengths,
        layer_input.reshape(seqs, sl, width),
        grad_out.reshape(seqs, sl, width),
        w_qkv,
        w_out,
        w_fc,
        w_proj,
        b_fc.reshape(1, ff_rows),
        norm_gains,
        biases,
    )

    def finish(
        len_ref, a_out, a_gin, a_gqkv, a_gout, a_gfc, a_gproj, sums,
        out_ref, gin_ref, gqkv_ref, gout_ref, gfc_ref, gproj_ref, gup_ref, ggain_ref, gbias_ref, rms_ref,
    ):
        out_ref[...] = a_out[...]
        gin_ref[...] = a_gin[...]
        gout_ref[...] = a_gout[...]
        gproj_ref[...] = a_gproj[...]
        for t in range(zs):
            for k in range(3):
                gqkv_ref[:, k * width + t * tw : k * width + (t + 1) * tw] = a_gqkv[t, :, k * tw : (k + 1) * tw]
        for q in range(ps):
            for b in range(zs):
                at = ff_place(q, b) * ff_rows
                gfc_ref[:, at : at + ff_rows] = a_gfc[q, :, b * ff_rows : (b + 1) * ff_rows]
        ggain_ref[...] = sums[0:2, 0:rows]
        gbias_ref[...] = sums[2:8, 0:rows]
        gup_ref[...] = sums[8:9, 0:ff_rows]
        valid = (len_ref[0] + len_ref[1]).astype(f32) * width
        rms_ref[...] = jnp.sqrt(sums[9:10, 0:4] / valid)

    final = pl.pallas_call(
        finish,
        out_shape=(
            jax.ShapeDtypeStruct((seqs, sl, width), bf16),
            jax.ShapeDtypeStruct((seqs, sl, width), f32),
            jax.ShapeDtypeStruct((rows, 3 * width), f32),
            jax.ShapeDtypeStruct((rows, width), f32),
            jax.ShapeDtypeStruct((rows, ps * part), f32),
            jax.ShapeDtypeStruct((ff_rows, width), f32),
            jax.ShapeDtypeStruct((1, ff_rows), f32),
            jax.ShapeDtypeStruct((2, rows), f32),
            jax.ShapeDtypeStruct((6, rows), f32),
            jax.ShapeDtypeStruct((1, 4), f32),
        ),
        in_specs=[in_smem] + [in_vmem] * 7,
        out_specs=(in_vmem,) * 10,
        name="finish",
    )(lengths, *results)
    return (
        final[0].reshape(layer_input.shape),
        final[1].reshape(layer_input.shape),
        *final[2:6],
        final[6].reshape(ff_rows),
        final[7],
        final[8],
        final[9].reshape(4),
    )


def fits(seqs, sl, width, hs, ss, qkv_rows):
    if seqs != 2 or ss % seqs or hs % cores:
        return False
    zs = ss // seqs
    if width % zs or (width // zs) % HEAD_DIM or zs != 4 or hs != zs or qkv_rows % 8:
        return False
    tw = width // zs
    keys = ss * sl * hs
    return tw <= 256 and keys * ss * sl * (tw // HEAD_DIM) * 4 <= 16 * 1024 * 1024


def on_device(layer_input, grad_out, lengths, w_qkv, w_out, w_fc, w_proj, b_fc, norm_gains, biases):
    seqs, _, sl, width = layer_input.shape
    hs, ss = lax.axis_size("head"), lax.axis_size("seq")
    chosen = fused_layer if fits(seqs, sl, width, hs, ss, w_qkv.shape[0]) else spread_layer
    return chosen(
        layer_input, grad_out, lengths, w_qkv, w_out, w_fc, w_proj, b_fc, norm_gains, biases
    )


def solution(mesh):
    return jax.shard_map(
        on_device,
        mesh=mesh,
        in_specs=(
            P(None, "seq", "head", None),
            P(None, "seq", "head", None),
            P(),
            P(("head", "seq"), None),
            P(("head", "seq"), None),
            P(("head", "seq"), None),
            P(("head", "seq"), None),
            P(("head", "seq")),
            P(None, ("head", "seq")),
            P(None, ("head", "seq")),
        ),
        out_specs=(
            P(None, "seq", "head", None),
            P(None, "seq", "head", None),
            P(("head", "seq"), None),
            P(("head", "seq"), None),
            P(("head", "seq"), None),
            P(("head", "seq"), None),
            P(("head", "seq")),
            P(None, ("head", "seq")),
            P(None, ("head", "seq")),
            P(),
        ),
        check_vma=False,
    )
```

```python
import functools

import jax
import jax.numpy as jnp
from jax import lax
from jax.sharding import PartitionSpec as P
from jax.experimental import pallas as pl
from jax.experimental.pallas import tpu as pltpu

HEAD_DIM = 64


masked_score = -1e30
block_keys = 512
quick_slope = 1.702
epsilon = 1e-05


def layer_norm_parts(inputs):
    centre = inputs - jnp.mean(inputs, axis=-1, keepdims=True)
    inverse = lax.rsqrt(jnp.mean(centre * centre, axis=-1, keepdims=True) + epsilon)
    return (centre * inverse, inverse)


def norm_backward(grad_normed, normed, inverse):
    return inverse * (
        grad_normed
        - jnp.mean(grad_normed, axis=-1, keepdims=True)
        - normed * jnp.mean(grad_normed * normed, axis=-1, keepdims=True)
    )


def split_heads(piece_block):
    return piece_block.reshape(
        piece_block.shape[0], piece_block.shape[1], piece_block.shape[2] // HEAD_DIM, HEAD_DIM
    )


def head_scores(left_side, right_side):
    return jnp.einsum("sqhd,skhd->shqk", left_side, right_side, preferred_element_type=jnp.float32)


def weighted(probabilities, right_side):
    return jnp.einsum(
        "shqk,skhd->sqhd", probabilities, right_side, preferred_element_type=jnp.float32
    )


def transposed(probabilities, right_side):
    return jnp.einsum(
        "shqk,sqhd->skhd", probabilities, right_side, preferred_element_type=jnp.float32
    )


def over_blocks(step_fn, running, pieces):
    extent = pieces[0].shape[1]
    number = extent // block_keys
    parted = tuple(
        (
            piece_part.reshape(
                (piece_part.shape[0], number, block_keys) + piece_part.shape[2:]
            ).swapaxes(0, 1)
            for piece_part in pieces
        )
    )

    def advance(inner_run, element):
        position, blocks = element
        return (step_fn(inner_run, blocks, position * block_keys), None)

    return lax.scan(advance, running, (jnp.arange(number, dtype=jnp.int32), parted))[0]


def spread_layer(layer_input, grad_out, lengths, w_qkv, w_out, w_fc, w_proj, b_fc, norm_gains, biases):
    sequences = layer_input.shape[0]
    slice_len = layer_input.shape[2]
    model_width = layer_input.shape[3]
    head_ways = lax.axis_size("head")
    group_len = slice_len * head_ways
    local_width = model_width // head_ways
    head_count = local_width // HEAD_DIM
    head_place = lax.axis_index("head")
    cycle_place = lax.axis_index("seq")
    flat_rows = sequences * slice_len
    full_qkv, full_out, full_fc, full_proj, full_bias_fc, full_gains, full_biases = (
        lax.all_gather(w_qkv, ("head", "seq"), axis=0, tiled=True),
        lax.all_gather(w_out, ("head", "seq"), axis=0, tiled=True),
        lax.all_gather(w_fc, ("head", "seq"), axis=0, tiled=True),
        lax.all_gather(w_proj, ("head", "seq"), axis=0, tiled=True),
        lax.all_gather(b_fc, ("head", "seq"), axis=0, tiled=True),
        lax.all_gather(norm_gains, ("head", "seq"), axis=1, tiled=True),
        lax.all_gather(biases, ("head", "seq"), axis=1, tiled=True),
    )
    gain_vals = full_gains.astype(jnp.float32)
    shift_vals = full_biases.astype(jnp.float32)
    bias_up = full_bias_fc.astype(jnp.float32)
    token_places = (
        cycle_place * group_len + head_place * slice_len + jnp.arange(slice_len, dtype=jnp.int32)
    )
    token_keep = (
        (token_places[None, :] < lengths[:, None]).astype(jnp.float32).reshape(flat_rows, 1)
    )
    own_places = cycle_place * group_len + jnp.arange(group_len, dtype=jnp.int32)
    own_allowed = (own_places[None, :] < lengths[:, None])[:, None, None, :]

    def allowed_at(offset, extent):
        places = offset + jnp.arange(extent, dtype=jnp.int32)
        return (places[None, :] < lengths[:, None])[:, None, None, :]

    inputs = layer_input.reshape(flat_rows, model_width).astype(jnp.float32)
    normed_one, inverse_one = layer_norm_parts(inputs)
    first_in = (normed_one * gain_vals[0] + shift_vals[0]).astype(jnp.bfloat16)
    projected = jnp.dot(first_in, full_qkv, preferred_element_type=jnp.float32)
    query_scale = HEAD_DIM ** (-0.5)
    queries = ((projected[:, :model_width] + shift_vals[1]) * query_scale).astype(jnp.bfloat16)
    keys_new = projected[:, model_width : 2 * model_width].astype(jnp.bfloat16)
    values_new = (projected[:, 2 * model_width :] + shift_vals[2]).astype(jnp.bfloat16)
    packed = jnp.stack([queries, keys_new, values_new], axis=1).reshape(
        sequences, slice_len, 3, head_ways, local_width
    )
    spread = lax.all_to_all(packed, "head", split_axis=3, concat_axis=1, tiled=True)
    query_block = spread[:, :, 0, 0]
    key_block = spread[:, :, 1, 0]
    value_block = spread[:, :, 2, 0]
    query_heads = split_heads(query_block)
    key_heads = split_heads(key_block)
    value_heads = split_heads(value_block)

    def maxima_step(running, pieces, offset):
        highest, denominator = running
        scores = head_scores(query_heads, split_heads(pieces[0]))
        allowed = allowed_at(offset, pieces[0].shape[1])
        scores = jnp.where(allowed, scores, masked_score)
        raised = jnp.maximum(highest, jnp.max(scores, axis=-1))
        weights = jnp.where(allowed, jnp.exp(scores - raised[..., None]), 0.0)
        denominator = denominator * jnp.exp(highest - raised) + jnp.sum(weights, axis=-1)
        return (raised, denominator)

    zero_rows = jnp.zeros((sequences, head_count, group_len), jnp.float32)
    highest, denominator = over_blocks(
        maxima_step,
        (zero_rows + masked_score, zero_rows),
        (lax.all_gather(key_block, "seq", axis=1, tiled=True),),
    )
    log_total = highest + jnp.log(denominator)

    def attention_weights(key_piece, offset):
        scores = head_scores(query_heads, key_piece)
        allowed = allowed_at(offset, key_piece.shape[1])
        return jnp.where(
            allowed, jnp.exp(jnp.where(allowed, scores, masked_score) - log_total[..., None]), 0.0
        )

    zero_heads = jnp.zeros((sequences, group_len, head_count, HEAD_DIM), jnp.float32)

    def output_step(running, pieces, offset):
        probabilities = attention_weights(split_heads(pieces[0]), offset)
        return running + weighted(probabilities.astype(jnp.bfloat16), split_heads(pieces[1]))

    attended = over_blocks(
        output_step,
        zero_heads,
        (
            lax.all_gather(key_block, "seq", axis=1, tiled=True),
            lax.all_gather(value_block, "seq", axis=1, tiled=True),
        ),
    )
    mixed_heads = attended.astype(jnp.bfloat16).reshape(
        sequences, head_ways, slice_len, local_width
    )
    gathered_out = lax.all_to_all(mixed_heads, "head", split_axis=1, concat_axis=3, tiled=True)
    mixed_rows = gathered_out.reshape(flat_rows, model_width)
    branch = jnp.dot(mixed_rows, full_out, preferred_element_type=jnp.float32) + shift_vals[3]
    middle = inputs + branch
    normed_two, inverse_two = layer_norm_parts(middle)
    second_in = (normed_two * gain_vals[1] + shift_vals[4]).astype(jnp.bfloat16)
    hidden = jnp.dot(second_in, full_fc, preferred_element_type=jnp.float32) + bias_up
    gate_sig = jax.nn.sigmoid(quick_slope * hidden)
    activated = (hidden * gate_sig).astype(jnp.bfloat16)
    feed_out = jnp.dot(activated, full_proj, preferred_element_type=jnp.float32) + shift_vals[5]
    final_rows = middle + feed_out
    result = (final_rows * token_keep).astype(jnp.bfloat16).reshape(layer_input.shape)
    local_squares = jnp.stack(
        [
            jnp.sum(token_keep * inputs * inputs),
            jnp.sum(token_keep * branch * branch),
            jnp.sum(token_keep * feed_out * feed_out),
            jnp.sum(token_keep * final_rows * final_rows),
        ]
    )
    squares = lax.psum(local_squares, ("head", "seq"))
    valid_count = jnp.sum(lengths).astype(jnp.float32) * model_width
    root_means = jnp.sqrt(squares / valid_count)
    grad_final = grad_out.reshape(flat_rows, model_width).astype(jnp.float32) * token_keep
    grad_feed = grad_final.astype(jnp.bfloat16)
    grad_proj = jnp.dot(activated.T, grad_feed, preferred_element_type=jnp.float32)
    grad_shift_proj = jnp.sum(grad_feed.astype(jnp.float32), axis=0)
    grad_act = jnp.dot(grad_feed, full_proj.T, preferred_element_type=jnp.float32)
    grad_hidden = (
        grad_act * (gate_sig + quick_slope * hidden * gate_sig * (1.0 - gate_sig))
    ).astype(jnp.bfloat16)
    grad_fc = jnp.dot(second_in.T, grad_hidden, preferred_element_type=jnp.float32)
    grad_bias_up = jnp.sum(grad_hidden.astype(jnp.float32), axis=0)
    grad_second = jnp.dot(grad_hidden, full_fc.T, preferred_element_type=jnp.float32)
    grad_gain_two = jnp.sum(grad_second * normed_two, axis=0)
    grad_shift_two = jnp.sum(grad_second, axis=0)
    grad_middle = grad_final + norm_backward(grad_second * gain_vals[1], normed_two, inverse_two)
    grad_branch = grad_middle.astype(jnp.bfloat16)
    grad_out_weight = jnp.dot(mixed_rows.T, grad_branch, preferred_element_type=jnp.float32)
    grad_shift_out = jnp.sum(grad_branch.astype(jnp.float32), axis=0)
    grad_mixed = jnp.dot(grad_branch, full_out.T, preferred_element_type=jnp.float32).astype(
        jnp.bfloat16
    )
    grad_spread = lax.all_to_all(
        grad_mixed.reshape(sequences, slice_len, head_ways, local_width),
        "head",
        split_axis=2,
        concat_axis=1,
        tiled=True,
    )
    grad_block = grad_spread[:, :, 0]
    grad_heads = split_heads(grad_block)

    def delta_step(running, pieces, offset):
        probabilities = attention_weights(split_heads(pieces[0]), offset)
        grad_probs = head_scores(grad_heads, split_heads(pieces[1]))
        return running + jnp.sum(probabilities * grad_probs, axis=-1)

    row_delta = over_blocks(
        delta_step,
        zero_rows,
        (
            lax.all_gather(key_block, "seq", axis=1, tiled=True),
            lax.all_gather(value_block, "seq", axis=1, tiled=True),
        ),
    )

    def query_step(running, pieces, offset):
        key_piece = split_heads(pieces[0])
        probabilities = attention_weights(key_piece, offset)
        grad_probs = head_scores(grad_heads, split_heads(pieces[1]))
        slopes = (probabilities * (grad_probs - row_delta[..., None])).astype(jnp.bfloat16)
        return running + weighted(slopes, key_piece)

    grad_query = over_blocks(
        query_step,
        zero_heads,
        (
            lax.all_gather(key_block, "seq", axis=1, tiled=True),
            lax.all_gather(value_block, "seq", axis=1, tiled=True),
        ),
    )
    all_logs, all_deltas = (
        lax.all_gather(log_total.transpose(0, 2, 1), "seq", axis=1, tiled=True),
        lax.all_gather(row_delta.transpose(0, 2, 1), "seq", axis=1, tiled=True),
    )

    def key_step(running, pieces, offset):
        query_piece = split_heads(pieces[0])
        grad_piece = split_heads(pieces[1])
        extent = pieces[0].shape[1]
        log_piece = lax.dynamic_slice_in_dim(all_logs, offset, extent, 1).transpose(0, 2, 1)
        delta_piece = lax.dynamic_slice_in_dim(all_deltas, offset, extent, 1).transpose(0, 2, 1)
        scores = head_scores(query_piece, key_heads)
        probabilities = jnp.where(
            own_allowed,
            jnp.exp(jnp.where(own_allowed, scores, masked_score) - log_piece[..., None]),
            0.0,
        )
        grad_value = running[1] + transposed(probabilities.astype(jnp.bfloat16), grad_piece)
        grad_probs = head_scores(grad_piece, value_heads)
        slopes = (probabilities * (grad_probs - delta_piece[..., None])).astype(jnp.bfloat16)
        grad_key = running[0] + transposed(slopes, query_piece)
        return (grad_key, grad_value)

    grad_key, grad_value = over_blocks(
        key_step,
        (zero_heads, zero_heads),
        (
            lax.all_gather(query_block, "seq", axis=1, tiled=True),
            lax.all_gather(grad_block, "seq", axis=1, tiled=True),
        ),
    )
    stacked = jnp.stack([grad_query, grad_key, grad_value], axis=2).astype(jnp.bfloat16)
    stacked = stacked.reshape(sequences, head_ways, slice_len, 3, local_width)
    returned = lax.all_to_all(stacked, "head", split_axis=1, concat_axis=4, tiled=True)
    column_scale = jnp.concatenate(
        [
            jnp.full((model_width,), query_scale, jnp.float32),
            jnp.ones((2 * model_width,), jnp.float32),
        ]
    )
    grad_projected = returned.reshape(flat_rows, 3 * model_width).astype(jnp.float32) * column_scale
    grad_shift_query = jnp.sum(grad_projected[:, :model_width], axis=0)
    grad_shift_value = jnp.sum(grad_projected[:, 2 * model_width :], axis=0)
    grad_projected_low = grad_projected.astype(jnp.bfloat16)
    grad_qkv = jnp.dot(first_in.T, grad_projected_low, preferred_element_type=jnp.float32)
    grad_first = jnp.dot(grad_projected_low, full_qkv.T, preferred_element_type=jnp.float32)
    grad_gain_one = jnp.sum(grad_first * normed_one, axis=0)
    grad_shift_one = jnp.sum(grad_first, axis=0)
    grad_inputs = grad_middle + norm_backward(grad_first * gain_vals[0], normed_one, inverse_one)
    grad_gain_rows = jnp.stack([grad_gain_one, grad_gain_two])
    grad_shift_rows = jnp.stack(
        [
            grad_shift_one,
            grad_shift_query,
            grad_shift_value,
            grad_shift_out,
            grad_shift_two,
            grad_shift_proj,
        ]
    )
    owned_grads = (
        lax.psum_scatter(grad_qkv, ("head", "seq"), scatter_dimension=0, tiled=True),
        lax.psum_scatter(grad_out_weight, ("head", "seq"), scatter_dimension=0, tiled=True),
        lax.psum_scatter(grad_fc, ("head", "seq"), scatter_dimension=0, tiled=True),
        lax.psum_scatter(grad_proj, ("head", "seq"), scatter_dimension=0, tiled=True),
        lax.psum_scatter(grad_bias_up, ("head", "seq"), scatter_dimension=0, tiled=True),
        lax.psum_scatter(grad_gain_rows, ("head", "seq"), scatter_dimension=1, tiled=True),
        lax.psum_scatter(grad_shift_rows, ("head", "seq"), scatter_dimension=1, tiled=True),
    )
    return (
        result,
        grad_inputs.reshape(layer_input.shape),
        owned_grads[0],
        owned_grads[1],
        owned_grads[2],
        owned_grads[3],
        owned_grads[4],
        owned_grads[5],
        owned_grads[6],
        root_means,
    )


f32 = jnp.float32
bf16 = jnp.bfloat16
cores = 2
halves = 2
lanes_per = 128


def nn(left, right):
    return lax.dot_general(left, right, (((1,), (0,)), ((), ())), preferred_element_type=f32)


def nt(left, right):
    return lax.dot_general(left, right, (((1,), (1,)), ((), ())), preferred_element_type=f32)


def loop(low, high, step_fn, unroll=1):
    def advance(index, carry):
        step_fn(index)
        return carry

    lax.fori_loop(low, high, advance, 0, unroll=unroll)


def aligned(index, extent):
    return pl.ds(pl.multiple_of(index * extent, extent), extent)


def norm_parts(v):
    centre = v - jnp.mean(v, axis=-1, keepdims=True)
    inverse = lax.rsqrt(jnp.mean(centre * centre, axis=-1, keepdims=True) + epsilon)
    return centre * inverse, inverse


def remote(src, dst, send_sem, recv_sem, place):
    return pltpu.make_async_remote_copy(
        src_ref=src,
        dst_ref=dst,
        send_sem=send_sem,
        recv_sem=recv_sem,
        device_id=place,
        device_id_type=pl.DeviceIdType.MESH,
    )


def dense(v):
    n = v.shape[0]
    low = v[:, 0:lanes_per]
    rest = v[:, lanes_per:]
    return low, jnp.concatenate([rest[0 : n // 2], rest[n // 2 :]], axis=1)


def loose(low, rest):
    wide = rest.shape[1] // 2
    return jnp.concatenate(
        [low, jnp.concatenate([rest[:, 0:wide], rest[:, wide:]], axis=0)], axis=1
    )


class Exchange:
    def __init__(self, n, me, place, src, dst, send_sem, recv_sem, order=None):
        self.n, self.me, self.place, self.src, self.dst = n, me, place, src, dst
        self.send_sem, self.recv_sem, self.order = send_sem, recv_sem, order

    def out(self, q):
        return remote(
            self.src(q), self.dst(self.me), self.send_sem, self.recv_sem.at[self.me], self.place(q)
        )

    def into(self, q):
        return remote(
            self.dst(q), self.dst(q), self.send_sem, self.recv_sem.at[q], self.place(q)
        )

    def peer(self, k):
        return lax.rem(self.me + k, self.n)

    def send(self, low=0, high=None):
        if self.order is None:
            loop(1, self.n, lambda k: self.out(self.peer(k)).start())
        else:
            for q in self.order[low:high]:
                self.out(q).start()

    def wait(self):
        loop(1, self.n, lambda k: self.into(self.peer(k)).wait_recv())

    def drain(self):
        loop(1, self.n, lambda k: self.out(self.peer(k)).wait_send())


def chip_peer(n, inner, me, k):
    outer = n // inner
    a = lax.rem(me // inner + lax.rem(k, outer), outer)
    b = lax.rem(lax.rem(me, inner) + k // outer, inner)
    return a * inner + b


class Gather:
    def __init__(self, n, inner, me, core, place, dst, send_sem, recv_sem):
        self.n, self.inner, self.me, self.core, self.place, self.dst = n, inner, me, core, place, dst
        self.send_sem, self.recv_sem = send_sem, recv_sem
        self.mine = me * cores + core

    def peer(self, k):
        return chip_peer(self.n, self.inner, self.me, k)

    def move(self, slot, place):
        return remote(
            self.dst(slot), self.dst(slot), self.send_sem, self.recv_sem.at[slot], place
        )

    def out(self, k):
        return self.move(self.mine, self.place(self.peer(k), self.core))

    def aside(self, k):
        return self.move(
            self.peer(k) * cores + self.core, self.place(self.me, 1 - self.core)
        )

    def send(self, last=None):
        loop(1, last or self.n, lambda k: self.out(k).start())
        self.aside(0).start()

    def send_last(self):
        loop(1, self.n - 1, lambda k: self.out(k).wait_send())
        self.out(self.n - 1).start()

    def relay_from(self, k):
        self.out_slot(k, self.core).wait_recv()
        self.aside(k).start()

    def out_slot(self, k, core):
        return self.move(self.peer(k) * cores + core, self.place(self.peer(k), core))

    def wait_from(self, k):
        self.out_slot(k, 1 - self.core).wait_recv()

    def relay(self):
        loop(1, self.n, self.relay_from)

    def wait(self):
        loop(0, self.n, self.wait_from)

    def drain(self, first=1):
        loop(first, self.n, lambda k: self.out(k).wait_send())
        loop(0, self.n, lambda k: self.aside(k).wait_send())


class Reduce:
    def __init__(self, n, inner, me, core, place, stage, beside, landed, sems, recv_sems, add):
        self.n, self.inner, self.me, self.core, self.place = n, inner, me, core, place
        self.stage, self.beside, self.landed = stage, beside, landed
        self.sems, self.recv_sems, self.add = sems, recv_sems, add

    def peer(self, k):
        return chip_peer(self.n, self.inner, self.me, k)

    def own(self, r):
        return self.stage(r * cores + self.core)

    def aside(self, r):
        return remote(
            self.stage(r * cores + 1 - self.core),
            self.beside(r),
            self.sems.at[0],
            self.recv_sems.at[0, r],
            self.place(self.me, 1 - self.core),
        )

    def out(self, r):
        return remote(
            self.own(r),
            self.landed(self.me),
            self.sems.at[1],
            self.recv_sems.at[1, self.me],
            self.place(r, self.core),
        )

    def combine(self, r):
        self.aside(r).wait_recv()
        self.add(self.own(r), self.beside(r))

    def combine_out(self, k):
        r = self.peer(k)
        self.combine(r)
        self.out(r).start()

    def send_aside(self):
        loop(1, self.n, lambda k: self.aside(self.peer(k)).start())
        self.aside(self.me).start()

    def send(self):
        loop(1, self.n, self.combine_out)
        self.combine(self.me)

    def wait(self):
        def one(k):
            r = self.peer(k)
            remote(
                self.landed(r), self.landed(r), self.sems.at[1], self.recv_sems.at[1, r],
                self.place(r, self.core),
            ).wait_recv()

        loop(1, self.n, one)

    def drain_aside(self):
        loop(0, self.n, lambda k: self.aside(self.peer(k)).wait_send())

    def drain(self):
        self.drain_aside()
        loop(1, self.n, lambda k: self.out(self.peer(k)).wait_send())


def fused_layer(layer_input, grad_out, lengths, w_qkv, w_out, w_fc, w_proj, b_fc, norm_gains, biases):
    seqs, _, sl, width = layer_input.shape
    hs = lax.axis_size("head")
    ss = lax.axis_size("seq")
    zs = ss // seqs
    ps = hs * seqs
    xs = hs // cores
    rs = xs * seqs
    group = sl * hs
    tw = width // zs
    heads = tw // HEAD_DIM
    rows = w_qkv.shape[0]
    ff_rows = w_proj.shape[0]
    part = ff_rows * zs
    home = seqs * sl
    qn = ss * sl
    slab = ps * home
    near = zs // halves
    us = near * seqs
    duo = cores * home
    query_block = 256
    blocks = qn // query_block
    chunk = 32
    pair = 2 * rows
    quad = 8 * rows
    scale = HEAD_DIM ** (-0.5)

    def ff_place(q, b):
        u, c = q // cores, q % cores
        head_of = (b // halves) * cores + c
        return head_of * ss + ((b % halves) * near + u // seqs) * seqs + u % seqs

    def kernel(
        len_ref, x_hbm, go_hbm, wqkv_hbm, wout_hbm, wfc_hbm, wproj_hbm, bfc_hbm, gain_hbm, bias_hbm,
        out_hbm, gin_hbm, gqkv_hbm, gout_hbm, gfc_hbm, gproj_hbm, owned_hbm,
        x_ref, go_ref, wqkv_ref, wout_ref, wfc_ref, wproj_ref, bfc_ref, gain_ref, bias_ref, in_sem,
        out_ref, gin_ref, gqkv_ref, gout_ref, gfc_ref, gproj_ref, owned_ref, home_sem,
        small, small_z, small_g, prm, up_bias,
        qkv_st, fc_st, wqg, wog, wfg, wpg, wq, wo, wf,
        xg, q_s, kvg, kneg, probs, s_scr, t_scr, pb_scr, ds_scr, o_s, o_st, og, mixed_s,
        middle_s, gm_s,
        x2g, gog, act, gh, x2t, gs_st, gs_in, gs_red, fd_st, fd_in, fd_red,
        do_st, dog, dot_s, qt_s, dq_s, dkt, dvt, kv_st, kv_in, kv_red, gpt, gp,
        gf_st, gfg, wo_in, wo_red, woz, wozr, wq_in, wq_red, wqz, wqzr,
        wfs, wfr, wfm, wfq, wfz, wfzr, wps, wpr, wpm, wpq, arg, ard, sums, ar_st, arz,
        send, zsem, lsem, psem, bsem, gsem, rsem, ksem, krsem, ssem,
    ):
        h = lax.axis_index("head")
        s = lax.axis_index("seq")
        z = s // seqs
        y = lax.rem(s, seqs)
        core = lax.rem(h, cores)
        r_at = (h // cores) * seqs + y
        x_at = h // cores
        p = r_at * cores + core
        zh = z // near
        zl = lax.rem(z, near)
        u_at = zl * seqs + y
        pf = u_at * cores + core
        t_at = x_at * halves + zh
        t_far = x_at * halves + 1 - zh

        def chip_place(r, c):
            return ((r // seqs) * cores + c, z * seqs + lax.rem(r, seqs))

        def slab_place(q):
            return chip_place(q // cores, lax.rem(q, cores))

        def square_place(u, c):
            return (x_at * cores + c, (zh * near + u // seqs) * seqs + lax.rem(u, seqs))

        def ring_place(q):
            return square_place(q // cores, lax.rem(q, cores))

        def half_place(q):
            return (h, (q * near + zl) * seqs + y)

        def beside_place(q):
            return (q * cores + core, s)

        def line_place(q):
            return (h, q)

        def z_place(q):
            return (h, q * seqs + y)

        def x_place(r, c):
            return (r * cores + c, s)

        count = {}

        def take(name):
            number = count.get(name, 0)
            count[name] = number + 1
            return number

        z_order = [(1 - zh) * (zs - 1), near - zh, zh * zs + 1 - z]
        line_order = [q * seqs + b for q in z_order for b in range(seqs)] + [z * seqs + 1 - y]

        def over_z(src, dst):
            return Exchange(
                zs, z, z_place, src, dst, send.at[take("s")], zsem.at[take("z")], z_order
            )

        def over_line(src, dst):
            return Exchange(
                ss, s, line_place, src, dst, send.at[take("s")], lsem.at[take("l")], line_order
            )

        def over_plane(src, dst):
            return Exchange(ps, p, slab_place, src, dst, send.at[take("s")], psem.at[take("p")])

        def over_square(src, dst):
            return Exchange(ps, pf, ring_place, src, dst, send.at[take("s")], psem.at[take("p")])

        def over_half(src, dst):
            return Exchange(halves, zh, half_place, src, dst, send.at[take("s")], bsem.at[take("b")])

        def over_x(src, dst):
            return Exchange(xs, x_at, beside_place, src, dst, send.at[take("s")], bsem.at[take("b")])

        def gather(dst):
            return Gather(rs, seqs, r_at, core, chip_place, dst, send.at[take("s")], gsem.at[take("g")])

        def gather_square(dst):
            return Gather(us, seqs, u_at, core, square_place, dst, send.at[take("s")], gsem.at[take("g")])

        def add_rows(block):
            def add(a, b):
                extent = a.shape[0]

                def one(i):
                    at = aligned(i, block)
                    a[at, :] = (a[at, :].astype(f32) + b[at, :].astype(f32)).astype(bf16)

                loop(0, extent // block, one)

            return add

        def add_blocks(a, b):
            def one(i):
                a[i] = (a[i].astype(f32) + b[i].astype(f32)).astype(bf16)

            loop(0, a.shape[0], one)

        def reduce(stage, beside, landed, add):
            number = take("r")
            return Reduce(
                rs, seqs, r_at, core, chip_place, stage, beside, landed, ssem.at[number],
                rsem.at[number], add,
            )

        def reduce_square(stage, beside, landed, add):
            number = take("r")
            return Reduce(
                us, seqs, u_at, core, square_place, stage, beside, landed, ssem.at[number],
                rsem.at[number], add,
            )

        ex_small_z = over_z(lambda q: small, lambda q: small_z.at[q])
        ex_wq_z = over_z(lambda q: qkv_st.at[q], lambda q: wqg.at[p, q])
        ex_wo_z = over_z(lambda q: wout_ref, lambda q: wog.at[p, q])
        ex_x = over_line(lambda q: x_ref.at[lax.rem(q, seqs)], lambda q: xg.at[q])
        ga_small = gather(lambda q: small_g.at[q])
        ga_wq = gather(lambda q: wqg.at[q])
        ga_wo = gather(lambda q: wog.at[q])
        ex_wf_p = over_square(lambda q: fc_st.at[q], lambda q: wfg.at[t_at, q])
        ex_wf_1 = over_half(lambda q: wfg.at[t_at], lambda q: wfg.at[x_at * halves + q])
        ex_wf_2 = over_x(lambda q: wfg.at[t_at], lambda q: wfg.at[q * halves + zh])
        ex_wf_3 = over_x(lambda q: wfg.at[t_far], lambda q: wfg.at[q * halves + 1 - zh])
        ex_wp_1 = over_half(lambda q: wproj_ref, lambda q: wpg.at[x_at * halves + q])
        ex_wp_2 = over_x(lambda q: wproj_ref, lambda q: wpg.at[q * halves + zh])
        ex_wp_3 = over_x(lambda q: wpg.at[t_far], lambda q: wpg.at[q * halves + 1 - zh])
        ga_go = gather_square(lambda q: gog.at[q])
        ga_kv = [
            Gather(
                xs, 1, x_at, core, x_place,
                lambda q, i=i: kvg.at[q, :, :, i * query_block : (i + 1) * query_block],
                send.at[take("s")], ksem.at[i],
            )
            for i in range(halves)
        ]
        ex_o = over_line(lambda q: o_st.at[q], lambda q: og.at[lax.rem(q, seqs), q // seqs])
        ga_x2 = gather_square(lambda q: x2g.at[q])
        re_gs = reduce_square(
            lambda q: gs_st.at[q], lambda r: gs_in.at[r], lambda r: gs_red.at[r], add_rows(32),
        )
        re_fd = reduce_square(
            lambda q: fd_st.at[q], lambda r: fd_in.at[r], lambda r: fd_red.at[r], add_rows(32),
        )
        ex_do = over_line(
            lambda q: do_st.at[q // seqs, lax.rem(q, seqs)], lambda q: dog.at[q]
        )
        re_kv = [
            Reduce(
                xs, 1, x_at, core, x_place,
                lambda q, n=n: kv_st.at[n, q], lambda r, n=n: kv_in.at[n, r],
                lambda r, n=n: kv_red.at[n, r],
                ssem.at[take("r")], krsem.at[n], add_blocks,
            )
            for n in range(heads)
        ]
        ex_gf = over_line(lambda q: gf_st.at[q], lambda q: gfg.at[lax.rem(q, seqs), q // seqs])
        re_wo = reduce(
            lambda q: wog.at[q], lambda r: wo_in.at[r], lambda r: wo_red.at[r], add_blocks,
        )
        ex_go_z = over_z(lambda q: woz.at[q], lambda q: wozr.at[q])
        re_wq = reduce(
            lambda q: wqg.at[q], lambda r: wq_in.at[r], lambda r: wq_red.at[r], add_blocks,
        )
        ex_gq_z = over_z(lambda q: wqz.at[q], lambda q: wqzr.at[q])
        ex_gf_1 = over_x(lambda q: wfs.at[pl.ds(q * halves, halves)], lambda q: wfr)
        ex_gf_2 = over_half(lambda q: wfm.at[q], lambda q: wfq)
        ex_gf_3 = over_square(lambda q: wfz.at[q], lambda q: wfzr.at[q])
        ex_gp_1 = over_x(lambda q: wps.at[pl.ds(q * halves, halves)], lambda q: wpr)
        ex_gp_2 = over_half(lambda q: wpm.at[q], lambda q: wpq)
        ex_ar_p = over_plane(lambda q: arg.at[q], lambda q: ard.at[q])
        ex_ar_z = over_z(lambda q: ar_st.at[q], lambda q: arz.at[q])

        coming = [
            pltpu.make_async_copy(kept, held, in_sem.at[i])
            for i, (kept, held) in enumerate(
                (
                    (gain_hbm, gain_ref), (bias_hbm, bias_ref), (bfc_hbm, bfc_ref), (wqkv_hbm, wqkv_ref),
                    (wfc_hbm, wfc_ref), (x_hbm, x_ref), (wout_hbm, wout_ref), (wproj_hbm, wproj_ref),
                    (go_hbm, go_ref),
                )
            )
        ]
        for copy in coming:
            copy.start()
        leaving = [
            pltpu.make_async_copy(held, kept, home_sem.at[i])
            for i, (held, kept) in enumerate(
                (
                    (out_ref, out_hbm), (gin_ref, gin_hbm), (gqkv_ref, gqkv_hbm), (gout_ref, gout_hbm),
                    (gfc_ref, gfc_hbm), (gproj_ref, gproj_hbm), (owned_ref, owned_hbm),
                )
            )
        ]

        def leave(i):
            leaving[i].start()

        barrier = pltpu.get_barrier_semaphore()

        def greet(place, me, n):
            def one(k):
                pl.semaphore_signal(
                    barrier, inc=1, device_id=place(lax.rem(me + k, n)),
                    device_id_type=pl.DeviceIdType.MESH,
                )

            loop(1, n, one)

        greet(slab_place, p, ps)
        greet(line_place, s, ss)
        greet(ring_place, pf, ps)

        for copy in coming:
            copy.wait()
        small[...] = jnp.zeros_like(small)
        small[0:2, 0:rows] = gain_ref[...].astype(f32)
        small[2:8, 0:rows] = bias_ref[...].astype(f32)
        small[8:9, 0:ff_rows] = bfc_ref[...].astype(f32)
        for t in range(zs):
            for k in range(3):
                qkv_st[t, :, k * tw : (k + 1) * tw] = wqkv_ref[:, k * width + t * tw : k * width + (t + 1) * tw]
        for q in range(ps):
            for b in range(zs):
                at = ff_place(q, b) * ff_rows
                fc_st[q, :, b * ff_rows : (b + 1) * ff_rows] = wfc_ref[:, at : at + ff_rows]
        small_z[z] = small[...]
        wqg[p, z] = qkv_st[z]
        wog[p, z] = wout_ref[...]
        wfg[t_at, pf] = fc_st[pf]
        wpg[t_at] = wproj_ref[...]
        xg[s] = x_ref[y]
        ar_st[...] = jnp.zeros_like(ar_st)
        len_0 = len_ref[0]
        len_1 = len_ref[1]
        len_y = jnp.where(y == 0, len_0, len_1)
        home_row = lax.broadcasted_iota(jnp.int32, (home, 1), 0)
        home_place = s * group + h * sl + lax.rem(home_row, sl)
        keep = jnp.where(home_place < jnp.where(home_row < sl, len_0, len_1), 1.0, 0.0)
        gog[pf] = (go_ref[...].reshape(home, width).astype(f32) * keep).astype(bf16)

        def mask_block(q):
            column = lax.broadcasted_iota(jnp.int32, (8, qn), 1)
            place = (column // sl) * group + q * sl + lax.rem(column, sl)
            kneg[q] = jnp.where(place < len_y, 0.0, masked_score)

        loop(0, hs, mask_block)
        pl.semaphore_wait(barrier, 2 * (ps - 1) + ss - 1)

        ex_small_z.send()
        ex_wq_z.send()
        ex_x.send(0, 1)

        ex_small_z.wait()
        small_g[p] = small_z[...]
        ga_small.send()
        ex_wq_z.wait()
        ga_wq.send()
        ex_wp_2.send()
        ex_x.send(1)
        ex_wo_z.send()
        ex_wf_p.send()
        ex_wp_1.send()
        ga_small.relay()
        ga_wq.relay()

        def d_of(q, t):
            hq = q // cores // seqs * cores + q % cores
            return hq * ss + t * seqs + q // cores % seqs

        ga_small.wait()
        prm[...] = jnp.zeros_like(prm)
        for q in range(ps):
            for t in range(zs):
                d = d_of(q, t)
                prm[0:8, d * rows : (d + 1) * rows] = small_g[q, t, 0:8, 0:rows]
                at = (d * rows) % tw
                triple = (d * rows) // tw
                prm[8 + triple : 9 + triple, at : at + rows] = small_g[q, t, 3:4, 0:rows]
                prm[8 + triple : 9 + triple, 2 * tw + at : 2 * tw + at + rows] = small_g[q, t, 4:5, 0:rows]

        up_bias[...] = jnp.zeros_like(up_bias)
        for b in range(zs):
            q = ((b // halves) * seqs + y) * cores + core
            up_bias[0:1, b * ff_rows : (b + 1) * ff_rows] = small_g[q, (b % halves) * near + zl, 8:9, 0:ff_rows]

        def assemble(src, dst):
            def one(i):
                hq = i // zs
                xq = hq // cores
                cq = lax.rem(hq, cores)
                t = lax.rem(i, zs)
                dst[aligned(i, pair), :] = jnp.concatenate(
                    [src(xq, cq, 0, t).astype(f32), src(xq, cq, 1, t).astype(f32)], axis=0
                ).astype(bf16)

            loop(0, width // pair, one)

        ga_wq.wait()
        assemble(lambda a, c, b, t: wqg[(a * seqs + b) * cores + c, t], wq)

        def first_norm(i):
            xv = xg[pl.ds(2 * i, 2)].reshape(2 * sl, width).astype(f32)
            normed, inverse = norm_parts(xv)
            return normed, (normed * prm[0:1, :] + prm[2:3, :]).astype(bf16)

        for i in range(halves):
            for q in range(ss // halves * i, ss // halves * (i + 1)):
                @pl.when(s != q)
                def _(q=q):
                    ex_x.into(q).wait_recv()

            for j in range(zs // halves):
                _, first = first_norm(zs // halves * i + j)
                x2t[(zs // halves * i + j) * 2 * sl : (zs // halves * i + j + 1) * 2 * sl, 0:width] = first
            at = slice(i * query_block, (i + 1) * query_block)
            projected = nn(x2t[at, 0:width], wq[...]) + prm[pl.ds(8 + z, 1), 0 : 3 * tw]
            q_s[at, :] = (projected[:, 0:tw] * scale).astype(bf16)
            turned = projected[:, tw:].T.astype(bf16)
            kvg[h, 0, :, at] = turned[0:tw, :]
            kvg[h, 1, :, at] = turned[tw : 2 * tw, :]
            ga_kv[i].send()
        ex_wf_p.wait()
        ga_go.send()
        ex_wf_1.send()
        for i in range(halves):
            ga_kv[i].relay()
        ex_wo_z.wait()
        ga_wo.send()
        for i in range(halves):
            ga_kv[i].wait()

        lane_head = lax.broadcasted_iota(jnp.int32, (query_block, tw), 1) // HEAD_DIM

        def score(n, i):
            queries = q_s[i * query_block : (i + 1) * query_block, :]
            masked = jnp.where(lane_head == n, queries, jnp.zeros_like(queries))
            for b in range(hs):
                probs[n, i, :, b * qn : (b + 1) * qn] = nn(masked, kvg[b, 0])

        def soften(n, i, low_ref):
            for r in range(query_block // chunk):
                rat = slice(r * chunk, (r + 1) * chunk)
                sv = [probs[n, i, rat, b * qn : (b + 1) * qn] + kneg[b, 0:1, :] for b in range(hs)]
                top = jnp.max(functools.reduce(jnp.maximum, sv), axis=-1, keepdims=True)
                ev = [jnp.exp(v - top) for v in sv]
                inv = 1.0 / jnp.sum(functools.reduce(jnp.add, ev), axis=-1, keepdims=True)
                for b in range(hs):
                    value = ev[b] * inv
                    probs[n, i, rat, b * qn : (b + 1) * qn] = value
                    low_ref[rat, b * qn : (b + 1) * qn] = value.astype(bf16)

        def mix(n, i, low_ref):
            head_out = nt(low_ref[:, 0:qn], kvg[0, 1])
            for b in range(1, hs):
                head_out = head_out + nt(low_ref[:, b * qn : (b + 1) * qn], kvg[b, 1])
            at = slice(i * query_block, (i + 1) * query_block)
            o_s[at, :] = jnp.where(lane_head == n, head_out.astype(bf16), o_s[at, :])

        o_s[...] = jnp.zeros_like(o_s)
        score(0, 0)
        for n in range(heads):
            soften(n, 0, pb_scr)
            score(n, 1)
            if n:
                mix(n - 1, 1, ds_scr)
            soften(n, 1, ds_scr)
            if n < heads - 1:
                score(n + 1, 0)
            mix(n, 0, pb_scr)
            if n == 0:
                ex_wf_2.send()
        mix(heads - 1, 1, ds_scr)

        def pack(ref, v):
            ref[0:sl, :], ref[sl:, :] = dense(v)

        def unpack(ref):
            return loose(ref[0:sl, :], ref[sl:, :])

        def lay_out(q):
            pack(o_st.at[q], o_s[aligned(q, sl), :])

        loop(0, ss, lay_out)
        ex_o.send()
        og[y, z] = o_st[s]
        ex_wf_1.wait()
        ex_wf_3.send()
        ex_wp_1.wait()
        ex_wp_3.send()
        ga_wo.relay()
        ga_go.relay()

        ga_wo.wait()
        assemble(lambda a, c, b, t: wog[(a * seqs + b) * cores + c, t], wo)
        ex_o.wait()
        branch = jnp.broadcast_to(prm[5:6, :], (home, width))
        for t in range(zs):
            mixed = jnp.concatenate([unpack(og.at[a, t]) for a in range(seqs)], axis=0)
            mixed_s[t] = mixed
            branch = branch + nn(mixed, wo[t * tw : (t + 1) * tw, :])
        middle = x_ref[...].reshape(home, width).astype(f32) + branch
        normed, _ = norm_parts(middle)
        x2g[pf] = (normed * prm[1:2, :] + prm[6:7, :]).astype(bf16)
        ga_x2.send(us - 1)
        middle_s[...] = middle
        for ex in (ga_go, ex_wf_2, ex_wp_2, ex_wf_3, ex_wp_3):
            ex.wait()
        assemble(
            lambda a, c, b, t: wfg[a * halves + t // near, (lax.rem(t, near) * seqs + b) * cores + c], wf
        )

        def feed(k, running):
            r = ga_x2.peer(k)

            @pl.when(k > 0)
            def _():
                ga_x2.relay_from(k)

            ga_x2.wait_from(k)
            at = aligned(r, duo)
            chip = pl.ds(cores * r, cores)
            hid = nn(x2g[chip].reshape(duo, width), wf[...]) + up_bias[0:1, :]
            gate = 1.0 / (1.0 + jnp.exp(-quick_slope * hid))
            act[at, :] = (hid * gate).astype(bf16)
            flow = nt(gog[chip].reshape(duo, width), wpg[...].reshape(part, width))
            slope = gate + quick_slope * hid * gate * (1.0 - gate)
            back = (flow * slope).astype(bf16)
            gh[at, :] = back
            gs_st[chip] = nt(back, wf[...]).astype(bf16).reshape(cores, home, width)
            re_gs.aside(r).start()

            @pl.when(k == 0)
            def _():
                ga_x2.send_last()

            @pl.when(k > 1)
            def _():
                re_gs.combine_out(k - 1)

            return running + jnp.sum(back.astype(f32), axis=0, keepdims=True)

        grad_up = lax.fori_loop(0, us, feed, jnp.zeros((1, part), f32))

        def turn_act(q):
            at = aligned(q, home)
            x2t[0:part, at] = act[at, :].T

        loop(0, ps, turn_act)
        re_gs.combine_out(us - 1)
        re_gs.combine(u_at)

        def proj_grad(c):
            wps[pl.ds(2 * c, 2)] = nn(
                x2t[aligned(c, 2 * ff_rows), :], gog[...].reshape(slab, width)
            ).astype(bf16).reshape(2, ff_rows, width)

        loop(0, zs // 2, proj_grad)
        ex_gp_1.send()

        def feed_down(r):
            chip = pl.ds(cores * r, cores)
            fd_st[chip] = nn(act[aligned(r, duo), :], wpg[...].reshape(part, width)).astype(bf16).reshape(
                cores, home, width
            )
            re_fd.aside(r).start()

        loop(0, us, feed_down)

        def scatter_rows(c, val, put):
            for j in range(val.shape[0] // rows):
                d = c * (val.shape[0] // rows) + j
                hq = d // ss
                sd = lax.rem(d, ss)
                put(
                    hq // cores, lax.rem(hq, cores), lax.rem(sd, seqs), sd // seqs,
                    val[j * rows : (j + 1) * rows, :].astype(bf16),
                )

        def turn_in(q):
            x2t[:, aligned(q, home)] = x2g[q].T

        loop(0, ps, turn_in)

        def fc_grad(c):
            def put(a, c, b, t, value):
                wfs[a * halves + t // near, (lax.rem(t, near) * seqs + b) * cores + c] = value

            scatter_rows(c, nn(x2t[aligned(c, quad), :], gh[...]), put)

        loop(0, width // quad, fc_grad)
        ex_gf_1.send()

        for t in range(zs):
            x2t[t * tw : (t + 1) * tw, 0:home] = mixed_s[t].T
        grad_final = go_ref[...].reshape(home, width).astype(f32) * keep

        re_gs.wait()

        def landed_sum(re, own):
            total = own
            for k in range(1, us):
                total = total + re.landed(re.peer(k))[...].astype(f32)
            return total

        grad_second = landed_sum(re_gs, gs_st[pf].astype(f32))
        n2, r2 = norm_parts(middle_s[...])
        grad_middle = grad_final + norm_backward(grad_second * prm[1:2, :], n2, r2)
        grad_branch = grad_middle.astype(bf16)
        for t in range(zs):
            value = nt(grad_branch, wo[t * tw : (t + 1) * tw, :]).astype(bf16)
            for a in range(seqs):
                pack(do_st.at[t, a], value[a * sl : (a + 1) * sl, :])
        ex_do.send()
        dog[s] = do_st[z, y]
        gm_s[...] = grad_middle
        sums[...] = jnp.zeros_like(sums)
        arg[...] = jnp.zeros_like(arg)
        for q in range(ps):
            c, b, a = q % cores, q // cores % seqs, q // cores // seqs
            for i in range(zs):
                at = (a * halves + i // near) * ff_rows
                arg[q, 8 + i : 9 + i, 0:ff_rows] = jnp.where(
                    (core == c) & (y == b) & (zl == i % near), grad_up[:, at : at + ff_rows], 0.0
                )
        sums[1:2, :] = jnp.sum(grad_second * n2, axis=0, keepdims=True)
        sums[6:7, :] = jnp.sum(grad_second, axis=0, keepdims=True)
        sums[5:6, :] = jnp.sum(grad_branch.astype(f32), axis=0, keepdims=True)


        def out_grad(c):
            def put(a, c, b, t, value):
                wog[(a * seqs + b) * cores + c, t] = value

            scatter_rows(c, nn(x2t[aligned(c, quad), 0:home], gm_s[...].astype(bf16)), put)

        ga_wo.drain()
        loop(0, width // quad, out_grad)
        re_wo.send_aside()
        re_wo.send()

        ex_do.wait()
        ex_gp_1.wait()

        def proj_sum(q):
            wpm[q] = (wps[t_at - zh + q].astype(f32) + wpr[q].astype(f32)).astype(bf16)

        loop(0, halves, proj_sum)
        ex_gp_2.send()
        re_fd.send()

        def gather_do(i):
            at = aligned(i, 2 * sl)
            value = jnp.concatenate([unpack(dog.at[2 * i]), unpack(dog.at[2 * i + 1])], axis=0)
            o_s[at, :] = value
            dot_s[:, at] = value.T
            qt_s[:, at] = q_s[at, :].T

        loop(0, ss // 2, gather_do)
        dq_s[...] = jnp.zeros_like(dq_s)

        def slope_in(n, i, out_ref):
            outer = o_s[i * query_block : (i + 1) * query_block, :]
            masked = jnp.where(lane_head == n, outer, jnp.zeros_like(outer))
            for b in range(hs):
                out_ref[:, b * qn : (b + 1) * qn] = nn(masked, kvg[b, 1])

        def slopes(n, i, in_ref, slope_ref, low_ref):
            for r in range(query_block // chunk):
                rat = slice(r * chunk, (r + 1) * chunk)
                dp = [in_ref[rat, b * qn : (b + 1) * qn] for b in range(hs)]
                pv = [probs[n, i, rat, b * qn : (b + 1) * qn] for b in range(hs)]
                delta = jnp.sum(
                    functools.reduce(jnp.add, [a * c for a, c in zip(dp, pv)]), axis=-1, keepdims=True
                )
                for b in range(hs):
                    slope_ref[rat, b * qn : (b + 1) * qn] = (pv[b] * (dp[b] - delta)).astype(bf16)
                    low_ref[rat, b * qn : (b + 1) * qn] = pv[b].astype(bf16)

        def slope_out(n, i, slope_ref, low_ref):
            at = slice(i * query_block, (i + 1) * query_block)
            head_rows = slice(n * HEAD_DIM, (n + 1) * HEAD_DIM)
            head_dq = nt(slope_ref[:, 0:qn], kvg[0, 0])
            for b in range(1, hs):
                head_dq = head_dq + nt(slope_ref[:, b * qn : (b + 1) * qn], kvg[b, 0])
            dq_s[at, :] = jnp.where(
                lane_head == n, (head_dq.astype(bf16).astype(f32) * scale).astype(bf16), dq_s[at, :]
            )
            for b in range(hs):
                new_k = nn(qt_s[head_rows, at], slope_ref[:, b * qn : (b + 1) * qn])
                new_v = nn(dot_s[head_rows, at], low_ref[:, b * qn : (b + 1) * qn])
                if i == 0:
                    dkt[b] = new_k
                    dvt[b] = new_v
                else:
                    kv_st[n, b, 0] = (dkt[b] + new_k).astype(bf16)
                    kv_st[n, b, 1] = (dvt[b] + new_v).astype(bf16)

        def final_rows(re, own, landed, dst):
            def one(t):
                total = own[p, t].astype(f32)
                for k in range(1, rs):
                    total = total + landed[re.peer(k), t].astype(f32)
                dst[t] = total.astype(bf16)

            loop(0, zs, one)

        slope_in(0, 0, s_scr)
        for n in range(heads):
            slopes(n, 0, s_scr, ds_scr, pb_scr)
            slope_in(n, 1, t_scr)
            slope_out(n, 0, ds_scr, pb_scr)
            slopes(n, 1, t_scr, ds_scr, pb_scr)
            if n < heads - 1:
                slope_in(n + 1, 0, s_scr)
            slope_out(n, 1, ds_scr, pb_scr)
            re_kv[n].send_aside()
            if n:
                re_kv[n - 1].send()
            if n == heads - 1:
                re_wo.wait()
                final_rows(re_wo, wog, wo_red, woz)
                ex_go_z.send()
                wozr[z] = woz[z]
            if n == 0:
                ex_gf_1.wait()

                def fc_sum(i):
                    q, b = i // ps, lax.rem(i, ps)
                    wfm[q, b] = (wfs[t_at - zh + q, b].astype(f32) + wfr[q, b].astype(f32)).astype(bf16)

                loop(0, halves * ps, fc_sum)
                ex_gf_2.send()
        re_kv[heads - 1].send()

        gpt[0:tw, :] = dq_s[...].T

        def turn_first(i):
            _, first = first_norm(i)
            x2t[:, aligned(i, 2 * sl)] = first.T

        loop(0, zs, turn_first)

        for n in range(heads):
            re_kv[n].wait()
            for k in range(2):
                at = (1 + k) * tw + n * HEAD_DIM
                gpt[at : at + HEAD_DIM, :] = (
                    kv_st[n, h, k].astype(f32) + kv_red[n, re_kv[n].peer(1), k].astype(f32)
                ).astype(bf16)
        gp[...] = gpt[...].T

        gain_sum = jnp.zeros((1, width), f32)
        shift_sum = jnp.zeros((1, width), f32)
        block = ss // halves

        def first_grad(i):
            value = nt(gp[aligned(i, block * sl), :], wq[...])
            gf_st[pl.ds(block * i, block)] = value.astype(bf16).reshape(block, sl, width)

        first_grad(1 - zh)
        ex_gf.send(0, 1)

        def qkv_grad(c):
            def put(a, c, b, t, value):
                wqg[(a * seqs + b) * cores + c, t] = value

            scatter_rows(c, nn(x2t[aligned(c, quad), 0:qn], gp[...]), put)

        ga_wq.drain()
        loop(0, width // quad, qkv_grad)
        re_wq.send_aside()
        first_grad(zh)
        re_wq.send()
        ex_gf.send(1)
        gfg[y, z] = gf_st[s]
        ex_gf_2.wait()

        def fc_last(q):
            wfz[q] = (wfm[zh, q].astype(f32) + wfq[q].astype(f32)).astype(bf16)

        loop(0, ps, fc_last)
        ex_gf_3.send()
        wfzr[pf] = wfz[pf]
        for i in range(zs):
            value = gf_st[2 * i : 2 * i + 2].reshape(2 * sl, width).astype(f32)
            normed, _ = first_norm(i)
            gain_sum = gain_sum + jnp.sum(value * normed, axis=0, keepdims=True)
            shift_sum = shift_sum + jnp.sum(value, axis=0, keepdims=True)

        sums[0:1, :] = gain_sum
        sums[2:3, :] = shift_sum
        re_fd.wait()
        feed_out = landed_sum(re_fd, fd_st[pf].astype(f32)) + prm[7:8, :]
        final = middle_s[...] + feed_out
        out_ref[...] = (final * keep).astype(bf16).reshape(seqs, sl, width)
        leave(0)
        xv = x_ref[...].reshape(home, width).astype(f32)
        br = middle_s[...] - xv
        place = lax.broadcasted_iota(jnp.int32, (1, 128), 1)
        squares = jnp.zeros((1, 128), f32)
        for k, value in enumerate((xv, br, feed_out, final)):
            squares = squares + jnp.where(place == k, jnp.sum(keep * value * value), 0.0)
        for q in range(ps):
            arg[q, 12:13, :] = squares
        projected_sum = jnp.sum(gp[...].astype(f32), axis=0, keepdims=True)
        for i in range(zs):
            at = slice(i * tw, (i + 1) * tw)
            sums[3:4, at] = jnp.where(z == i, projected_sum[:, 0:tw], 0.0)
            sums[4:5, at] = jnp.where(z == i, projected_sum[:, 2 * tw :], 0.0)
        sums[7:8, :] = jnp.sum(gog[pf].astype(f32), axis=0, keepdims=True)

        for q in range(ps):
            for i in range(zs):
                at = d_of(q, i) * rows
                arg[q, 0:8, i * rows : (i + 1) * rows] = sums[0:8, at : at + rows]
        ex_ar_p.send()
        ard[p] = arg[p]

        ex_gp_2.wait()
        gproj_ref[...] = wpm[zh].astype(f32) + wpq[...].astype(f32)
        leave(5)

        re_wq.wait()
        final_rows(re_wq, wqg, wq_red, wqz)
        ex_gq_z.send()
        wqzr[z] = wqz[z]
        ex_ar_p.wait()
        total = functools.reduce(jnp.add, [ard[q] for q in range(ps)])
        for i in range(zs):
            ar_st[i, 0:8, 0:rows] = total[0:8, i * rows : (i + 1) * rows]
            ar_st[i, 8:9, :] = total[8 + i : 9 + i, :]
            ar_st[i, 9:10, :] = total[12:13, :]
        ex_ar_z.send()
        arz[z] = ar_st[z]
        ex_go_z.wait()
        gout_ref[...] = functools.reduce(jnp.add, [wozr[t].astype(f32) for t in range(zs)])
        leave(3)

        for ex in (
            ex_small_z, ex_wq_z, ex_wo_z, ex_x, ga_small, ex_wf_p, ex_wf_1, ex_wf_2, ex_wf_3,
            ex_wp_1, ex_wp_2, ex_wp_3,
            ga_go, *ga_kv, ex_o, re_gs, re_fd, ex_do, *re_kv, re_wo, ex_go_z, re_wq,
            ex_gf_1, ex_gf_2, ex_gf_3, ex_gp_1, ex_gp_2, ex_ar_p,
        ):
            ex.drain()
        ga_x2.drain(us - 1)

        ex_gf.wait()
        grad_first = functools.reduce(jnp.add, [gfg[:, t].astype(f32) for t in range(zs)]).reshape(home, width)
        n1, r1 = norm_parts(x_ref[...].reshape(home, width).astype(f32))
        grad_in = gm_s[...] + norm_backward(grad_first * prm[0:1, :], n1, r1)
        gin_ref[...] = grad_in.reshape(seqs, sl, width)
        leave(1)

        ex_gf_3.wait()
        for q in range(ps):
            for b in range(zs):
                at = ff_place(q, b) * ff_rows
                gfc_ref[:, at : at + ff_rows] = wfzr[q, :, b * ff_rows : (b + 1) * ff_rows].astype(f32)
        leave(4)
        ex_gq_z.wait()
        for i in range(zs):
            for k in range(3):
                at = k * width + i * tw
                gqkv_ref[:, at : at + tw] = wqzr[i, :, k * tw : (k + 1) * tw].astype(f32)
        leave(2)
        ex_ar_z.wait()
        owned = functools.reduce(jnp.add, [arz[t] for t in range(zs)])
        owned_ref[...] = owned
        leave(6)
        for ex in (ex_gf, ex_gq_z, ex_ar_z):
            ex.drain()
        for copy in leaving:
            copy.wait()

    vm = pltpu.VMEM
    scratch = [
        vm((seqs, sl, width), bf16),
        vm((seqs, sl, width), bf16),
        vm((rows, 3 * width), bf16),
        vm((rows, width), bf16),
        vm((rows, ps * part), bf16),
        vm((ff_rows, width), bf16),
        vm((1, ff_rows), bf16),
        vm((2, rows), bf16),
        vm((6, rows), bf16),
        pltpu.SemaphoreType.DMA((9,)),
        vm((seqs, sl, width), bf16),
        vm((seqs, sl, width), f32),
        vm((rows, 3 * width), f32),
        vm((rows, width), f32),
        vm((rows, ps * part), f32),
        vm((ff_rows, width), f32),
        vm((16, 128), f32),
        pltpu.SemaphoreType.DMA((7,)),
        vm((16, 128), f32),
        vm((zs, 16, 128), f32),
        vm((ps, zs, 16, 128), f32),
        vm((16, width), f32),
        vm((8, part), f32),
        vm((zs, rows, 3 * tw), bf16),
        vm((ps, rows, part), bf16),
        vm((ps, zs, rows, 3 * tw), bf16),
        vm((ps, zs, rows, width), bf16),
        vm((zs, ps, rows, part), bf16),
        vm((zs, ff_rows, width), bf16),
        vm((width, 3 * tw), bf16),
        vm((width, width), bf16),
        vm((width, part), bf16),
        vm((ss, sl, width), bf16),
        vm((qn, tw), bf16),
        vm((hs, 2, tw, qn), bf16),
        vm((hs, 8, qn), f32),
        vm((heads, blocks, query_block, hs * qn), f32),
        vm((query_block, hs * qn), f32),
        vm((query_block, hs * qn), f32),
        vm((query_block, hs * qn), bf16),
        vm((query_block, hs * qn), bf16),
        vm((qn, tw), bf16),
        vm((ss, sl * tw // lanes_per, lanes_per), bf16),
        vm((seqs, zs, sl * tw // lanes_per, lanes_per), bf16),
        vm((zs, home, tw), bf16),
        vm((home, width), f32),
        vm((home, width), f32),
        vm((ps, home, width), bf16),
        vm((ps, home, width), bf16),
        vm((slab, part), bf16),
        vm((slab, part), bf16),
        vm((width, slab), bf16),
        vm((ps, home, width), bf16),
        vm((rs, home, width), bf16),
        vm((rs, home, width), bf16),
        vm((ps, home, width), bf16),
        vm((rs, home, width), bf16),
        vm((rs, home, width), bf16),
        vm((zs, seqs, sl * tw // lanes_per, lanes_per), bf16),
        vm((ss, sl * tw // lanes_per, lanes_per), bf16),
        vm((tw, qn), bf16),
        vm((tw, qn), bf16),
        vm((qn, tw), bf16),
        vm((hs, HEAD_DIM, qn), f32),
        vm((hs, HEAD_DIM, qn), f32),
        vm((heads, hs, 2, HEAD_DIM, qn), bf16),
        vm((heads, xs, 2, HEAD_DIM, qn), bf16),
        vm((heads, xs, 2, HEAD_DIM, qn), bf16),
        vm((3 * tw, qn), bf16),
        vm((qn, 3 * tw), bf16),
        vm((ss, sl, width), bf16),
        vm((seqs, zs, sl, width), bf16),
        vm((rs, zs, rows, width), bf16),
        vm((rs, zs, rows, width), bf16),
        vm((zs, rows, width), bf16),
        vm((zs, rows, width), bf16),
        vm((rs, zs, rows, 3 * tw), bf16),
        vm((rs, zs, rows, 3 * tw), bf16),
        vm((zs, rows, 3 * tw), bf16),
        vm((zs, rows, 3 * tw), bf16),
        vm((zs, ps, rows, part), bf16),
        vm((halves, ps, rows, part), bf16),
        vm((halves, ps, rows, part), bf16),
        vm((ps, rows, part), bf16),
        vm((ps, rows, part), bf16),
        vm((ps, rows, part), bf16),
        vm((zs, ff_rows, width), bf16),
        vm((halves, ff_rows, width), bf16),
        vm((halves, ff_rows, width), bf16),
        vm((ff_rows, width), bf16),
        vm((ps, 16, 128), f32),
        vm((ps, 16, 128), f32),
        vm((8, width), f32),
        vm((zs, 16, 128), f32),
        vm((zs, 16, 128), f32),
        pltpu.SemaphoreType.DMA((33,)),
        pltpu.SemaphoreType.DMA((10, zs)),
        pltpu.SemaphoreType.DMA((4, ss)),
        pltpu.SemaphoreType.DMA((3, ps)),
        pltpu.SemaphoreType.DMA((10, 2)),
        pltpu.SemaphoreType.DMA((6, ps)),
        pltpu.SemaphoreType.DMA((7, 2, rs)),
        pltpu.SemaphoreType.DMA((zs, hs)),
        pltpu.SemaphoreType.DMA((heads, 2, xs)),
        pltpu.SemaphoreType.DMA((7, 2)),
    ]
    in_smem = pl.BlockSpec(memory_space=pltpu.SMEM)
    in_place = pl.BlockSpec(memory_space=pl.ANY)
    shapes = (
        jax.ShapeDtypeStruct((seqs, sl, width), bf16),
        jax.ShapeDtypeStruct((seqs, sl, width), f32),
        jax.ShapeDtypeStruct((rows, 3 * width), f32),
        jax.ShapeDtypeStruct((rows, width), f32),
        jax.ShapeDtypeStruct((rows, ps * part), f32),
        jax.ShapeDtypeStruct((ff_rows, width), f32),
        jax.ShapeDtypeStruct((1, ff_rows), f32),
        jax.ShapeDtypeStruct((2, rows), f32),
        jax.ShapeDtypeStruct((6, rows), f32),
        jax.ShapeDtypeStruct((1, 4), f32),
    )
    results = pl.pallas_call(
        kernel,
        out_shape=shapes[0:6] + (jax.ShapeDtypeStruct((16, 128), f32),),
        in_specs=[in_smem] + [in_place] * 9,
        out_specs=(in_place,) * 7,
        scratch_shapes=scratch,
        compiler_params=pltpu.CompilerParams(
            collective_id=0, has_side_effects=True, vmem_limit_bytes=63 * 1024 * 1024
        ),
        name="layer",
    )(
        lengths,
        layer_input.reshape(seqs, sl, width),
        grad_out.reshape(seqs, sl, width),
        w_qkv,
        w_out,
        w_fc,
        w_proj,
        b_fc.reshape(1, ff_rows),
        norm_gains,
        biases,
    )

    def finish(len_ref, *refs):
        given, kept, held, small_held = refs[0:7], refs[7:17], refs[17:24], refs[24:28]
        in_sem, out_sem = refs[28:]
        arrive = [pltpu.make_async_copy(given[i], held[i], in_sem.at[i]) for i in range(7)]
        leave = [
            pltpu.make_async_copy(ref, kept[i], out_sem.at[i])
            for i, ref in enumerate(held[0:6] + small_held)
        ]
        for i in (6, 1, 4, 5, 2, 0, 3):
            arrive[i].start()
        arrive[6].wait()
        owned = held[6]
        small_held[0][...] = owned[8:9, 0:ff_rows]
        small_held[1][...] = owned[0:2, 0:rows]
        small_held[2][...] = owned[2:8, 0:rows]
        valid = (len_ref[0] + len_ref[1]).astype(f32) * width
        small_held[3][...] = jnp.sqrt(owned[9:10, 0:4] / valid)
        for i in range(6, 10):
            leave[i].start()
        for i in (1, 4, 5, 2, 0, 3):
            arrive[i].wait()
            leave[i].start()
        for copy in leave:
            copy.wait()

    final = pl.pallas_call(
        finish,
        out_shape=shapes,
        in_specs=[in_smem] + [in_place] * 7,
        out_specs=(in_place,) * 10,
        scratch_shapes=[vm(s.shape, s.dtype) for s in shapes[0:6]]
        + [vm((16, 128), f32)]
        + [vm(s.shape, s.dtype) for s in shapes[6:]]
        + [pltpu.SemaphoreType.DMA((7,)), pltpu.SemaphoreType.DMA((10,))],
        name="finish",
    )(lengths, *results)
    return (
        final[0].reshape(layer_input.shape),
        final[1].reshape(layer_input.shape),
        *final[2:6],
        final[6].reshape(ff_rows),
        final[7],
        final[8],
        final[9].reshape(4),
    )


def fits(seqs, sl, width, hs, ss, qkv_rows):
    if seqs != 2 or ss % seqs or hs % cores:
        return False
    zs = ss // seqs
    if width % zs or (width // zs) % HEAD_DIM or zs != 4 or hs != zs or qkv_rows % 8:
        return False
    tw = width // zs
    keys = ss * sl * hs
    return tw <= 256 and keys * ss * sl * (tw // HEAD_DIM) * 4 <= 16 * 1024 * 1024


def on_device(layer_input, grad_out, lengths, w_qkv, w_out, w_fc, w_proj, b_fc, norm_gains, biases):
    seqs, _, sl, width = layer_input.shape
    hs, ss = lax.axis_size("head"), lax.axis_size("seq")
    chosen = fused_layer if fits(seqs, sl, width, hs, ss, w_qkv.shape[0]) else spread_layer
    return chosen(
        layer_input, grad_out, lengths, w_qkv, w_out, w_fc, w_proj, b_fc, norm_gains, biases
    )


def solution(mesh):
    return jax.shard_map(
        on_device,
        mesh=mesh,
        in_specs=(
            P(None, "seq", "head", None),
            P(None, "seq", "head", None),
            P(),
            P(("head", "seq"), None),
            P(("head", "seq"), None),
            P(("head", "seq"), None),
            P(("head", "seq"), None),
            P(("head", "seq")),
            P(None, ("head", "seq")),
            P(None, ("head", "seq")),
        ),
        out_specs=(
            P(None, "seq", "head", None),
            P(None, "seq", "head", None),
            P(("head", "seq"), None),
            P(("head", "seq"), None),
            P(("head", "seq"), None),
            P(("head", "seq"), None),
            P(("head", "seq")),
            P(None, ("head", "seq")),
            P(None, ("head", "seq")),
            P(),
        ),
        check_vma=False,
    )
```

```python
import functools

import jax
import jax.numpy as jnp
from jax import lax
from jax.sharding import PartitionSpec as P
from jax.experimental import pallas as pl
from jax.experimental.pallas import tpu as pltpu

HEAD_DIM = 64


masked_score = -1e30
block_keys = 512
quick_slope = 1.702
epsilon = 1e-05


def layer_norm_parts(inputs):
    centre = inputs - jnp.mean(inputs, axis=-1, keepdims=True)
    inverse = lax.rsqrt(jnp.mean(centre * centre, axis=-1, keepdims=True) + epsilon)
    return (centre * inverse, inverse)


def norm_backward(grad_normed, normed, inverse):
    return inverse * (
        grad_normed
        - jnp.mean(grad_normed, axis=-1, keepdims=True)
        - normed * jnp.mean(grad_normed * normed, axis=-1, keepdims=True)
    )


def split_heads(piece_block):
    return piece_block.reshape(
        piece_block.shape[0], piece_block.shape[1], piece_block.shape[2] // HEAD_DIM, HEAD_DIM
    )


def head_scores(left_side, right_side):
    return jnp.einsum("sqhd,skhd->shqk", left_side, right_side, preferred_element_type=jnp.float32)


def weighted(probabilities, right_side):
    return jnp.einsum(
        "shqk,skhd->sqhd", probabilities, right_side, preferred_element_type=jnp.float32
    )


def transposed(probabilities, right_side):
    return jnp.einsum(
        "shqk,sqhd->skhd", probabilities, right_side, preferred_element_type=jnp.float32
    )


def over_blocks(step_fn, running, pieces):
    extent = pieces[0].shape[1]
    number = extent // block_keys
    parted = tuple(
        (
            piece_part.reshape(
                (piece_part.shape[0], number, block_keys) + piece_part.shape[2:]
            ).swapaxes(0, 1)
            for piece_part in pieces
        )
    )

    def advance(inner_run, element):
        position, blocks = element
        return (step_fn(inner_run, blocks, position * block_keys), None)

    return lax.scan(advance, running, (jnp.arange(number, dtype=jnp.int32), parted))[0]


def spread_layer(layer_input, grad_out, lengths, w_qkv, w_out, w_fc, w_proj, b_fc, norm_gains, biases):
    sequences = layer_input.shape[0]
    slice_len = layer_input.shape[2]
    model_width = layer_input.shape[3]
    head_ways = lax.axis_size("head")
    group_len = slice_len * head_ways
    local_width = model_width // head_ways
    head_count = local_width // HEAD_DIM
    head_place = lax.axis_index("head")
    cycle_place = lax.axis_index("seq")
    flat_rows = sequences * slice_len
    full_qkv, full_out, full_fc, full_proj, full_bias_fc, full_gains, full_biases = (
        lax.all_gather(w_qkv, ("head", "seq"), axis=0, tiled=True),
        lax.all_gather(w_out, ("head", "seq"), axis=0, tiled=True),
        lax.all_gather(w_fc, ("head", "seq"), axis=0, tiled=True),
        lax.all_gather(w_proj, ("head", "seq"), axis=0, tiled=True),
        lax.all_gather(b_fc, ("head", "seq"), axis=0, tiled=True),
        lax.all_gather(norm_gains, ("head", "seq"), axis=1, tiled=True),
        lax.all_gather(biases, ("head", "seq"), axis=1, tiled=True),
    )
    gain_vals = full_gains.astype(jnp.float32)
    shift_vals = full_biases.astype(jnp.float32)
    bias_up = full_bias_fc.astype(jnp.float32)
    token_places = (
        cycle_place * group_len + head_place * slice_len + jnp.arange(slice_len, dtype=jnp.int32)
    )
    token_keep = (
        (token_places[None, :] < lengths[:, None]).astype(jnp.float32).reshape(flat_rows, 1)
    )
    own_places = cycle_place * group_len + jnp.arange(group_len, dtype=jnp.int32)
    own_allowed = (own_places[None, :] < lengths[:, None])[:, None, None, :]

    def allowed_at(offset, extent):
        places = offset + jnp.arange(extent, dtype=jnp.int32)
        return (places[None, :] < lengths[:, None])[:, None, None, :]

    inputs = layer_input.reshape(flat_rows, model_width).astype(jnp.float32)
    normed_one, inverse_one = layer_norm_parts(inputs)
    first_in = (normed_one * gain_vals[0] + shift_vals[0]).astype(jnp.bfloat16)
    projected = jnp.dot(first_in, full_qkv, preferred_element_type=jnp.float32)
    query_scale = HEAD_DIM ** (-0.5)
    queries = ((projected[:, :model_width] + shift_vals[1]) * query_scale).astype(jnp.bfloat16)
    keys_new = projected[:, model_width : 2 * model_width].astype(jnp.bfloat16)
    values_new = (projected[:, 2 * model_width :] + shift_vals[2]).astype(jnp.bfloat16)
    packed = jnp.stack([queries, keys_new, values_new], axis=1).reshape(
        sequences, slice_len, 3, head_ways, local_width
    )
    spread = lax.all_to_all(packed, "head", split_axis=3, concat_axis=1, tiled=True)
    query_block = spread[:, :, 0, 0]
    key_block = spread[:, :, 1, 0]
    value_block = spread[:, :, 2, 0]
    query_heads = split_heads(query_block)
    key_heads = split_heads(key_block)
    value_heads = split_heads(value_block)

    def maxima_step(running, pieces, offset):
        highest, denominator = running
        scores = head_scores(query_heads, split_heads(pieces[0]))
        allowed = allowed_at(offset, pieces[0].shape[1])
        scores = jnp.where(allowed, scores, masked_score)
        raised = jnp.maximum(highest, jnp.max(scores, axis=-1))
        weights = jnp.where(allowed, jnp.exp(scores - raised[..., None]), 0.0)
        denominator = denominator * jnp.exp(highest - raised) + jnp.sum(weights, axis=-1)
        return (raised, denominator)

    zero_rows = jnp.zeros((sequences, head_count, group_len), jnp.float32)
    highest, denominator = over_blocks(
        maxima_step,
        (zero_rows + masked_score, zero_rows),
        (lax.all_gather(key_block, "seq", axis=1, tiled=True),),
    )
    log_total = highest + jnp.log(denominator)

    def attention_weights(key_piece, offset):
        scores = head_scores(query_heads, key_piece)
        allowed = allowed_at(offset, key_piece.shape[1])
        return jnp.where(
            allowed, jnp.exp(jnp.where(allowed, scores, masked_score) - log_total[..., None]), 0.0
        )

    zero_heads = jnp.zeros((sequences, group_len, head_count, HEAD_DIM), jnp.float32)

    def output_step(running, pieces, offset):
        probabilities = attention_weights(split_heads(pieces[0]), offset)
        return running + weighted(probabilities.astype(jnp.bfloat16), split_heads(pieces[1]))

    attended = over_blocks(
        output_step,
        zero_heads,
        (
            lax.all_gather(key_block, "seq", axis=1, tiled=True),
            lax.all_gather(value_block, "seq", axis=1, tiled=True),
        ),
    )
    mixed_heads = attended.astype(jnp.bfloat16).reshape(
        sequences, head_ways, slice_len, local_width
    )
    gathered_out = lax.all_to_all(mixed_heads, "head", split_axis=1, concat_axis=3, tiled=True)
    mixed_rows = gathered_out.reshape(flat_rows, model_width)
    branch = jnp.dot(mixed_rows, full_out, preferred_element_type=jnp.float32) + shift_vals[3]
    middle = inputs + branch
    normed_two, inverse_two = layer_norm_parts(middle)
    second_in = (normed_two * gain_vals[1] + shift_vals[4]).astype(jnp.bfloat16)
    hidden = jnp.dot(second_in, full_fc, preferred_element_type=jnp.float32) + bias_up
    gate_sig = jax.nn.sigmoid(quick_slope * hidden)
    activated = (hidden * gate_sig).astype(jnp.bfloat16)
    feed_out = jnp.dot(activated, full_proj, preferred_element_type=jnp.float32) + shift_vals[5]
    final_rows = middle + feed_out
    result = (final_rows * token_keep).astype(jnp.bfloat16).reshape(layer_input.shape)
    local_squares = jnp.stack(
        [
            jnp.sum(token_keep * inputs * inputs),
            jnp.sum(token_keep * branch * branch),
            jnp.sum(token_keep * feed_out * feed_out),
            jnp.sum(token_keep * final_rows * final_rows),
        ]
    )
    squares = lax.psum(local_squares, ("head", "seq"))
    valid_count = jnp.sum(lengths).astype(jnp.float32) * model_width
    root_means = jnp.sqrt(squares / valid_count)
    grad_final = grad_out.reshape(flat_rows, model_width).astype(jnp.float32) * token_keep
    grad_feed = grad_final.astype(jnp.bfloat16)
    grad_proj = jnp.dot(activated.T, grad_feed, preferred_element_type=jnp.float32)
    grad_shift_proj = jnp.sum(grad_feed.astype(jnp.float32), axis=0)
    grad_act = jnp.dot(grad_feed, full_proj.T, preferred_element_type=jnp.float32)
    grad_hidden = (
        grad_act * (gate_sig + quick_slope * hidden * gate_sig * (1.0 - gate_sig))
    ).astype(jnp.bfloat16)
    grad_fc = jnp.dot(second_in.T, grad_hidden, preferred_element_type=jnp.float32)
    grad_bias_up = jnp.sum(grad_hidden.astype(jnp.float32), axis=0)
    grad_second = jnp.dot(grad_hidden, full_fc.T, preferred_element_type=jnp.float32)
    grad_gain_two = jnp.sum(grad_second * normed_two, axis=0)
    grad_shift_two = jnp.sum(grad_second, axis=0)
    grad_middle = grad_final + norm_backward(grad_second * gain_vals[1], normed_two, inverse_two)
    grad_branch = grad_middle.astype(jnp.bfloat16)
    grad_out_weight = jnp.dot(mixed_rows.T, grad_branch, preferred_element_type=jnp.float32)
    grad_shift_out = jnp.sum(grad_branch.astype(jnp.float32), axis=0)
    grad_mixed = jnp.dot(grad_branch, full_out.T, preferred_element_type=jnp.float32).astype(
        jnp.bfloat16
    )
    grad_spread = lax.all_to_all(
        grad_mixed.reshape(sequences, slice_len, head_ways, local_width),
        "head",
        split_axis=2,
        concat_axis=1,
        tiled=True,
    )
    grad_block = grad_spread[:, :, 0]
    grad_heads = split_heads(grad_block)

    def delta_step(running, pieces, offset):
        probabilities = attention_weights(split_heads(pieces[0]), offset)
        grad_probs = head_scores(grad_heads, split_heads(pieces[1]))
        return running + jnp.sum(probabilities * grad_probs, axis=-1)

    row_delta = over_blocks(
        delta_step,
        zero_rows,
        (
            lax.all_gather(key_block, "seq", axis=1, tiled=True),
            lax.all_gather(value_block, "seq", axis=1, tiled=True),
        ),
    )

    def query_step(running, pieces, offset):
        key_piece = split_heads(pieces[0])
        probabilities = attention_weights(key_piece, offset)
        grad_probs = head_scores(grad_heads, split_heads(pieces[1]))
        slopes = (probabilities * (grad_probs - row_delta[..., None])).astype(jnp.bfloat16)
        return running + weighted(slopes, key_piece)

    grad_query = over_blocks(
        query_step,
        zero_heads,
        (
            lax.all_gather(key_block, "seq", axis=1, tiled=True),
            lax.all_gather(value_block, "seq", axis=1, tiled=True),
        ),
    )
    all_logs, all_deltas = (
        lax.all_gather(log_total.transpose(0, 2, 1), "seq", axis=1, tiled=True),
        lax.all_gather(row_delta.transpose(0, 2, 1), "seq", axis=1, tiled=True),
    )

    def key_step(running, pieces, offset):
        query_piece = split_heads(pieces[0])
        grad_piece = split_heads(pieces[1])
        extent = pieces[0].shape[1]
        log_piece = lax.dynamic_slice_in_dim(all_logs, offset, extent, 1).transpose(0, 2, 1)
        delta_piece = lax.dynamic_slice_in_dim(all_deltas, offset, extent, 1).transpose(0, 2, 1)
        scores = head_scores(query_piece, key_heads)
        probabilities = jnp.where(
            own_allowed,
            jnp.exp(jnp.where(own_allowed, scores, masked_score) - log_piece[..., None]),
            0.0,
        )
        grad_value = running[1] + transposed(probabilities.astype(jnp.bfloat16), grad_piece)
        grad_probs = head_scores(grad_piece, value_heads)
        slopes = (probabilities * (grad_probs - delta_piece[..., None])).astype(jnp.bfloat16)
        grad_key = running[0] + transposed(slopes, query_piece)
        return (grad_key, grad_value)

    grad_key, grad_value = over_blocks(
        key_step,
        (zero_heads, zero_heads),
        (
            lax.all_gather(query_block, "seq", axis=1, tiled=True),
            lax.all_gather(grad_block, "seq", axis=1, tiled=True),
        ),
    )
    stacked = jnp.stack([grad_query, grad_key, grad_value], axis=2).astype(jnp.bfloat16)
    stacked = stacked.reshape(sequences, head_ways, slice_len, 3, local_width)
    returned = lax.all_to_all(stacked, "head", split_axis=1, concat_axis=4, tiled=True)
    column_scale = jnp.concatenate(
        [
            jnp.full((model_width,), query_scale, jnp.float32),
            jnp.ones((2 * model_width,), jnp.float32),
        ]
    )
    grad_projected = returned.reshape(flat_rows, 3 * model_width).astype(jnp.float32) * column_scale
    grad_shift_query = jnp.sum(grad_projected[:, :model_width], axis=0)
    grad_shift_value = jnp.sum(grad_projected[:, 2 * model_width :], axis=0)
    grad_projected_low = grad_projected.astype(jnp.bfloat16)
    grad_qkv = jnp.dot(first_in.T, grad_projected_low, preferred_element_type=jnp.float32)
    grad_first = jnp.dot(grad_projected_low, full_qkv.T, preferred_element_type=jnp.float32)
    grad_gain_one = jnp.sum(grad_first * normed_one, axis=0)
    grad_shift_one = jnp.sum(grad_first, axis=0)
    grad_inputs = grad_middle + norm_backward(grad_first * gain_vals[0], normed_one, inverse_one)
    grad_gain_rows = jnp.stack([grad_gain_one, grad_gain_two])
    grad_shift_rows = jnp.stack(
        [
            grad_shift_one,
            grad_shift_query,
            grad_shift_value,
            grad_shift_out,
            grad_shift_two,
            grad_shift_proj,
        ]
    )
    owned_grads = (
        lax.psum_scatter(grad_qkv, ("head", "seq"), scatter_dimension=0, tiled=True),
        lax.psum_scatter(grad_out_weight, ("head", "seq"), scatter_dimension=0, tiled=True),
        lax.psum_scatter(grad_fc, ("head", "seq"), scatter_dimension=0, tiled=True),
        lax.psum_scatter(grad_proj, ("head", "seq"), scatter_dimension=0, tiled=True),
        lax.psum_scatter(grad_bias_up, ("head", "seq"), scatter_dimension=0, tiled=True),
        lax.psum_scatter(grad_gain_rows, ("head", "seq"), scatter_dimension=1, tiled=True),
        lax.psum_scatter(grad_shift_rows, ("head", "seq"), scatter_dimension=1, tiled=True),
    )
    return (
        result,
        grad_inputs.reshape(layer_input.shape),
        owned_grads[0],
        owned_grads[1],
        owned_grads[2],
        owned_grads[3],
        owned_grads[4],
        owned_grads[5],
        owned_grads[6],
        root_means,
    )


f32 = jnp.float32
bf16 = jnp.bfloat16
cores = 2
halves = 2
lanes_per = 128


def nn(left, right):
    return lax.dot_general(left, right, (((1,), (0,)), ((), ())), preferred_element_type=f32)


def nt(left, right):
    return lax.dot_general(left, right, (((1,), (1,)), ((), ())), preferred_element_type=f32)


def loop(low, high, step_fn, unroll=1):
    def advance(index, carry):
        step_fn(index)
        return carry

    lax.fori_loop(low, high, advance, 0, unroll=unroll)


def aligned(index, extent):
    return pl.ds(pl.multiple_of(index * extent, extent), extent)


def norm_parts(v):
    centre = v - jnp.mean(v, axis=-1, keepdims=True)
    inverse = lax.rsqrt(jnp.mean(centre * centre, axis=-1, keepdims=True) + epsilon)
    return centre * inverse, inverse


def remote(src, dst, send_sem, recv_sem, place):
    return pltpu.make_async_remote_copy(
        src_ref=src,
        dst_ref=dst,
        send_sem=send_sem,
        recv_sem=recv_sem,
        device_id=place,
        device_id_type=pl.DeviceIdType.MESH,
    )


def dense(v):
    n = v.shape[0]
    low = v[:, 0:lanes_per]
    rest = v[:, lanes_per:]
    return low, jnp.concatenate([rest[0 : n // 2], rest[n // 2 :]], axis=1)


def loose(low, rest):
    wide = rest.shape[1] // 2
    return jnp.concatenate(
        [low, jnp.concatenate([rest[:, 0:wide], rest[:, wide:]], axis=0)], axis=1
    )


class Exchange:
    def __init__(self, n, me, place, src, dst, send_sem, recv_sem, order=None):
        self.n, self.me, self.place, self.src, self.dst = n, me, place, src, dst
        self.send_sem, self.recv_sem, self.order = send_sem, recv_sem, order

    def out(self, q):
        return remote(
            self.src(q), self.dst(self.me), self.send_sem, self.recv_sem.at[self.me], self.place(q)
        )

    def into(self, q):
        return remote(
            self.dst(q), self.dst(q), self.send_sem, self.recv_sem.at[q], self.place(q)
        )

    def peer(self, k):
        return lax.rem(self.me + k, self.n)

    def send(self, low=0, high=None):
        if self.order is None:
            loop(1, self.n, lambda k: self.out(self.peer(k)).start())
        else:
            for q in self.order[low:high]:
                self.out(q).start()

    def wait(self):
        loop(1, self.n, lambda k: self.into(self.peer(k)).wait_recv())

    def drain(self):
        loop(1, self.n, lambda k: self.out(self.peer(k)).wait_send())


def chip_peer(n, inner, me, k):
    outer = n // inner
    a = lax.rem(me // inner + lax.rem(k, outer), outer)
    b = lax.rem(lax.rem(me, inner) + k // outer, inner)
    return a * inner + b


class Gather:
    def __init__(self, n, inner, me, core, place, dst, send_sem, recv_sem):
        self.n, self.inner, self.me, self.core, self.place, self.dst = n, inner, me, core, place, dst
        self.send_sem, self.recv_sem = send_sem, recv_sem
        self.mine = me * cores + core

    def peer(self, k):
        return chip_peer(self.n, self.inner, self.me, k)

    def move(self, slot, place):
        return remote(
            self.dst(slot), self.dst(slot), self.send_sem, self.recv_sem.at[slot], place
        )

    def out(self, k):
        return self.move(self.mine, self.place(self.peer(k), self.core))

    def aside(self, k):
        return self.move(
            self.peer(k) * cores + self.core, self.place(self.me, 1 - self.core)
        )

    def send(self, last=None):
        loop(1, last or self.n, lambda k: self.out(k).start())
        self.aside(0).start()

    def send_last(self):
        loop(1, self.n - 1, lambda k: self.out(k).wait_send())
        self.out(self.n - 1).start()

    def relay_from(self, k):
        self.out_slot(k, self.core).wait_recv()
        self.aside(k).start()

    def out_slot(self, k, core):
        return self.move(self.peer(k) * cores + core, self.place(self.peer(k), core))

    def wait_from(self, k):
        self.out_slot(k, 1 - self.core).wait_recv()

    def relay(self):
        loop(1, self.n, self.relay_from)

    def wait(self):
        loop(0, self.n, self.wait_from)

    def drain(self, first=1):
        loop(first, self.n, lambda k: self.out(k).wait_send())
        loop(0, self.n, lambda k: self.aside(k).wait_send())


class Reduce:
    def __init__(self, n, inner, me, core, place, stage, beside, landed, sems, recv_sems, add):
        self.n, self.inner, self.me, self.core, self.place = n, inner, me, core, place
        self.stage, self.beside, self.landed = stage, beside, landed
        self.sems, self.recv_sems, self.add = sems, recv_sems, add

    def peer(self, k):
        return chip_peer(self.n, self.inner, self.me, k)

    def own(self, r):
        return self.stage(r * cores + self.core)

    def aside(self, r):
        return remote(
            self.stage(r * cores + 1 - self.core),
            self.beside(r),
            self.sems.at[0],
            self.recv_sems.at[0, r],
            self.place(self.me, 1 - self.core),
        )

    def out(self, r):
        return remote(
            self.own(r),
            self.landed(self.me),
            self.sems.at[1],
            self.recv_sems.at[1, self.me],
            self.place(r, self.core),
        )

    def combine(self, r):
        self.aside(r).wait_recv()
        self.add(self.own(r), self.beside(r))

    def combine_out(self, k):
        r = self.peer(k)
        self.combine(r)
        self.out(r).start()

    def send_aside(self):
        loop(1, self.n, lambda k: self.aside(self.peer(k)).start())
        self.aside(self.me).start()

    def send(self):
        loop(1, self.n, self.combine_out)
        self.combine(self.me)

    def wait(self):
        def one(k):
            r = self.peer(k)
            remote(
                self.landed(r), self.landed(r), self.sems.at[1], self.recv_sems.at[1, r],
                self.place(r, self.core),
            ).wait_recv()

        loop(1, self.n, one)

    def drain_aside(self):
        loop(0, self.n, lambda k: self.aside(self.peer(k)).wait_send())

    def drain(self):
        self.drain_aside()
        loop(1, self.n, lambda k: self.out(self.peer(k)).wait_send())


def fused_layer(layer_input, grad_out, lengths, w_qkv, w_out, w_fc, w_proj, b_fc, norm_gains, biases):
    seqs, _, sl, width = layer_input.shape
    hs = lax.axis_size("head")
    ss = lax.axis_size("seq")
    zs = ss // seqs
    ps = hs * seqs
    xs = hs // cores
    rs = xs * seqs
    group = sl * hs
    tw = width // zs
    heads = tw // HEAD_DIM
    rows = w_qkv.shape[0]
    ff_rows = w_proj.shape[0]
    part = ff_rows * zs
    home = seqs * sl
    qn = ss * sl
    slab = ps * home
    near = zs // halves
    us = near * seqs
    duo = cores * home
    query_block = 256
    blocks = qn // query_block
    chunk = 32
    pair = 2 * rows
    quad = 8 * rows
    scale = HEAD_DIM ** (-0.5)

    def ff_place(q, b):
        u, c = q // cores, q % cores
        head_of = (b // halves) * cores + c
        return head_of * ss + ((b % halves) * near + u // seqs) * seqs + u % seqs

    def kernel(
        len_ref, x_hbm, go_hbm, wqkv_hbm, wout_hbm, wfc_hbm, wproj_hbm, bfc_hbm, gain_hbm, bias_hbm,
        out_hbm, gin_hbm, gqkv_hbm, gout_hbm, gfc_hbm, gproj_hbm, owned_hbm,
        x_ref, go_ref, wqkv_ref, wout_ref, wfc_ref, wproj_ref, bfc_ref, gain_ref, bias_ref, in_sem,
        out_ref, gin_ref, gqkv_ref, gout_ref, gfc_ref, gproj_ref, owned_ref, home_sem,
        small, small_z, small_g, prm, up_bias,
        qkv_st, fc_st, wqg, wog, wfg, wpg, wq, wo, wf,
        xg, q_s, kvg, kneg, probs, s_scr, t_scr, pb_scr, ds_scr, o_s, o_st, og, mixed_s,
        middle_s, gm_s,
        x2g, gog, act, gh, x2t, gs_st, gs_in, gs_red, fd_st, fd_in, fd_red,
        do_st, dog, dot_s, qt_s, dq_s, dkt, dvt, kv_st, kv_in, kv_red, gpt, gp,
        gf_st, gfg, wo_in, wo_red, woz, wozr, wq_in, wq_red, wqz, wqzr,
        wfs, wfr, wfm, wfq, wfz, wfzr, wps, wpr, wpm, wpq, arg, ard, sums, ar_st, arz,
        send, zsem, lsem, psem, bsem, gsem, rsem, ksem, krsem, ssem,
    ):
        h = lax.axis_index("head")
        s = lax.axis_index("seq")
        z = s // seqs
        y = lax.rem(s, seqs)
        core = lax.rem(h, cores)
        r_at = (h // cores) * seqs + y
        x_at = h // cores
        p = r_at * cores + core
        zh = z // near
        zl = lax.rem(z, near)
        u_at = zl * seqs + y
        pf = u_at * cores + core
        t_at = x_at * halves + zh
        t_far = x_at * halves + 1 - zh

        def chip_place(r, c):
            return ((r // seqs) * cores + c, z * seqs + lax.rem(r, seqs))

        def slab_place(q):
            return chip_place(q // cores, lax.rem(q, cores))

        def square_place(u, c):
            return (x_at * cores + c, (zh * near + u // seqs) * seqs + lax.rem(u, seqs))

        def ring_place(q):
            return square_place(q // cores, lax.rem(q, cores))

        def half_place(q):
            return (h, (q * near + zl) * seqs + y)

        def beside_place(q):
            return (q * cores + core, s)

        def line_place(q):
            return (h, q)

        def z_place(q):
            return (h, q * seqs + y)

        def x_place(r, c):
            return (r * cores + c, s)

        count = {}

        def take(name):
            number = count.get(name, 0)
            count[name] = number + 1
            return number

        z_order = [(1 - zh) * (zs - 1), near - zh, zh * zs + 1 - z]
        line_order = [q * seqs + b for q in z_order for b in range(seqs)] + [z * seqs + 1 - y]

        def over_z(src, dst):
            return Exchange(
                zs, z, z_place, src, dst, send.at[take("s")], zsem.at[take("z")], z_order
            )

        def over_line(src, dst):
            return Exchange(
                ss, s, line_place, src, dst, send.at[take("s")], lsem.at[take("l")], line_order
            )

        def over_plane(src, dst):
            return Exchange(ps, p, slab_place, src, dst, send.at[take("s")], psem.at[take("p")])

        def over_square(src, dst):
            return Exchange(ps, pf, ring_place, src, dst, send.at[take("s")], psem.at[take("p")])

        def over_half(src, dst):
            return Exchange(halves, zh, half_place, src, dst, send.at[take("s")], bsem.at[take("b")])

        def over_x(src, dst):
            return Exchange(xs, x_at, beside_place, src, dst, send.at[take("s")], bsem.at[take("b")])

        def gather(dst):
            return Gather(rs, seqs, r_at, core, chip_place, dst, send.at[take("s")], gsem.at[take("g")])

        def gather_square(dst):
            return Gather(us, seqs, u_at, core, square_place, dst, send.at[take("s")], gsem.at[take("g")])

        def add_rows(block):
            def add(a, b):
                extent = a.shape[0]

                def one(i):
                    at = aligned(i, block)
                    a[at, :] = (a[at, :].astype(f32) + b[at, :].astype(f32)).astype(bf16)

                loop(0, extent // block, one)

            return add

        def add_blocks(a, b):
            def one(i):
                a[i] = (a[i].astype(f32) + b[i].astype(f32)).astype(bf16)

            loop(0, a.shape[0], one)

        def reduce(stage, beside, landed, add):
            number = take("r")
            return Reduce(
                rs, seqs, r_at, core, chip_place, stage, beside, landed, ssem.at[number],
                rsem.at[number], add,
            )

        def reduce_square(stage, beside, landed, add):
            number = take("r")
            return Reduce(
                us, seqs, u_at, core, square_place, stage, beside, landed, ssem.at[number],
                rsem.at[number], add,
            )

        ex_small_z = over_z(lambda q: small, lambda q: small_z.at[q])
        ex_wq_z = over_z(lambda q: qkv_st.at[q], lambda q: wqg.at[p, q])
        ex_wo_z = over_z(lambda q: wout_ref, lambda q: wog.at[p, q])
        ex_x = over_line(lambda q: x_ref.at[lax.rem(q, seqs)], lambda q: xg.at[q])
        ex_x.order = [lax.rem(s + k, ss) for k in range(1, ss)]
        ga_small = gather(lambda q: small_g.at[q])
        ga_wq = gather(lambda q: wqg.at[q])
        ga_wo = gather(lambda q: wog.at[q])
        ex_wf_p = over_square(lambda q: fc_st.at[q], lambda q: wfg.at[t_at, q])
        ex_wf_1 = over_half(lambda q: wfg.at[t_at], lambda q: wfg.at[x_at * halves + q])
        ex_wf_2 = over_x(lambda q: wfg.at[t_at], lambda q: wfg.at[q * halves + zh])
        ex_wf_3 = over_x(lambda q: wfg.at[t_far], lambda q: wfg.at[q * halves + 1 - zh])
        ex_wp_1 = over_half(lambda q: wproj_ref, lambda q: wpg.at[x_at * halves + q])
        ex_wp_2 = over_x(lambda q: wproj_ref, lambda q: wpg.at[q * halves + zh])
        ex_wp_3 = over_x(lambda q: wpg.at[t_far], lambda q: wpg.at[q * halves + 1 - zh])
        ga_go = gather_square(lambda q: gog.at[q])
        ga_kv = [
            Gather(
                xs, 1, x_at, core, x_place,
                lambda q, i=i: kvg.at[q, :, :, i * query_block : (i + 1) * query_block],
                send.at[take("s")], ksem.at[i],
            )
            for i in range(halves)
        ]
        ex_o = over_line(lambda q: o_st.at[q], lambda q: og.at[lax.rem(q, seqs), q // seqs])
        ga_x2 = gather_square(lambda q: x2g.at[q])
        re_gs = reduce_square(
            lambda q: gs_st.at[q], lambda r: gs_in.at[r], lambda r: gs_red.at[r], add_rows(32),
        )
        re_fd = reduce_square(
            lambda q: fd_st.at[q], lambda r: fd_in.at[r], lambda r: fd_red.at[r], add_rows(32),
        )
        ex_do = over_line(
            lambda q: do_st.at[q // seqs, lax.rem(q, seqs)], lambda q: dog.at[q]
        )
        re_kv = [
            Reduce(
                xs, 1, x_at, core, x_place,
                lambda q, n=n: kv_st.at[n, q], lambda r, n=n: kv_in.at[n, r],
                lambda r, n=n: kv_red.at[n, r],
                ssem.at[take("r")], krsem.at[n], add_blocks,
            )
            for n in range(heads)
        ]
        ex_gf = over_line(lambda q: gf_st.at[q], lambda q: gfg.at[lax.rem(q, seqs), q // seqs])
        re_wo = reduce(
            lambda q: wog.at[q], lambda r: wo_in.at[r], lambda r: wo_red.at[r], add_blocks,
        )
        ex_go_z = over_z(lambda q: woz.at[q], lambda q: wozr.at[q])
        re_wq = reduce(
            lambda q: wqg.at[q], lambda r: wq_in.at[r], lambda r: wq_red.at[r], add_blocks,
        )
        ex_gq_z = over_z(lambda q: wqz.at[q], lambda q: wqzr.at[q])
        ex_gf_1 = over_x(lambda q: wfs.at[pl.ds(q * halves, halves)], lambda q: wfr)
        ex_gf_2 = over_half(lambda q: wfm.at[q], lambda q: wfq)
        ex_gf_3 = over_square(lambda q: wfz.at[q], lambda q: wfzr.at[q])
        ex_gp_1 = over_x(lambda q: wps.at[pl.ds(q * halves, halves)], lambda q: wpr)
        ex_gp_2 = over_half(lambda q: wpm.at[q], lambda q: wpq)
        ex_ar_p = over_plane(lambda q: arg.at[q], lambda q: ard.at[q])
        ex_ar_z = over_z(lambda q: ar_st.at[q], lambda q: arz.at[q])

        coming = [
            pltpu.make_async_copy(kept, held, in_sem.at[i])
            for i, (kept, held) in enumerate(
                (
                    (gain_hbm, gain_ref), (bias_hbm, bias_ref), (bfc_hbm, bfc_ref), (wqkv_hbm, wqkv_ref),
                    (wfc_hbm, wfc_ref), (x_hbm, x_ref), (wout_hbm, wout_ref), (wproj_hbm, wproj_ref),
                    (go_hbm, go_ref),
                )
            )
        ]
        for copy in coming:
            copy.start()
        leaving = [
            pltpu.make_async_copy(held, kept, home_sem.at[i])
            for i, (held, kept) in enumerate(
                (
                    (out_ref, out_hbm), (gin_ref, gin_hbm), (gqkv_ref, gqkv_hbm), (gout_ref, gout_hbm),
                    (gfc_ref, gfc_hbm), (gproj_ref, gproj_hbm), (owned_ref, owned_hbm),
                )
            )
        ]

        def leave(i):
            leaving[i].start()

        barrier = pltpu.get_barrier_semaphore()

        def greet(place, me, n):
            def one(k):
                pl.semaphore_signal(
                    barrier, inc=1, device_id=place(lax.rem(me + k, n)),
                    device_id_type=pl.DeviceIdType.MESH,
                )

            loop(1, n, one)

        greet(slab_place, p, ps)
        greet(line_place, s, ss)
        greet(ring_place, pf, ps)

        for copy in coming:
            copy.wait()
        small[...] = jnp.zeros_like(small)
        small[0:2, 0:rows] = gain_ref[...].astype(f32)
        small[2:8, 0:rows] = bias_ref[...].astype(f32)
        small[8:9, 0:ff_rows] = bfc_ref[...].astype(f32)
        for t in range(zs):
            for k in range(3):
                qkv_st[t, :, k * tw : (k + 1) * tw] = wqkv_ref[:, k * width + t * tw : k * width + (t + 1) * tw]
        for q in range(ps):
            for b in range(zs):
                at = ff_place(q, b) * ff_rows
                fc_st[q, :, b * ff_rows : (b + 1) * ff_rows] = wfc_ref[:, at : at + ff_rows]
        small_z[z] = small[...]
        wqg[p, z] = qkv_st[z]
        wog[p, z] = wout_ref[...]
        wfg[t_at, pf] = fc_st[pf]
        wpg[t_at] = wproj_ref[...]
        xg[s] = x_ref[y]
        ar_st[...] = jnp.zeros_like(ar_st)
        len_0 = len_ref[0]
        len_1 = len_ref[1]
        len_y = jnp.where(y == 0, len_0, len_1)
        home_row = lax.broadcasted_iota(jnp.int32, (home, 1), 0)
        home_place = s * group + h * sl + lax.rem(home_row, sl)
        keep = jnp.where(home_place < jnp.where(home_row < sl, len_0, len_1), 1.0, 0.0)
        gog[pf] = (go_ref[...].reshape(home, width).astype(f32) * keep).astype(bf16)

        def mask_block(q):
            column = lax.broadcasted_iota(jnp.int32, (8, qn), 1)
            place = (column // sl) * group + q * sl + lax.rem(column, sl)
            kneg[q] = jnp.where(place < len_y, 0.0, masked_score)

        loop(0, hs, mask_block)
        pl.semaphore_wait(barrier, 2 * (ps - 1) + ss - 1)

        ex_small_z.send()
        ex_wq_z.send()
        ex_x.send()

        ex_small_z.wait()
        small_g[p] = small_z[...]
        ga_small.send()
        ex_wq_z.wait()
        ga_wq.send()
        ex_wp_2.send()
        ex_wo_z.send()
        ex_wf_p.send()
        ga_small.relay()
        ga_wq.relay()

        def d_of(q, t):
            hq = q // cores // seqs * cores + q % cores
            return hq * ss + t * seqs + q // cores % seqs

        ga_small.wait()
        prm[...] = jnp.zeros_like(prm)
        for q in range(ps):
            for t in range(zs):
                d = d_of(q, t)
                prm[0:8, d * rows : (d + 1) * rows] = small_g[q, t, 0:8, 0:rows]
                at = (d * rows) % tw
                triple = (d * rows) // tw
                prm[8 + triple : 9 + triple, at : at + rows] = small_g[q, t, 3:4, 0:rows]
                prm[8 + triple : 9 + triple, 2 * tw + at : 2 * tw + at + rows] = small_g[q, t, 4:5, 0:rows]

        up_bias[...] = jnp.zeros_like(up_bias)
        for b in range(zs):
            q = ((b // halves) * seqs + y) * cores + core
            up_bias[0:1, b * ff_rows : (b + 1) * ff_rows] = small_g[q, (b % halves) * near + zl, 8:9, 0:ff_rows]

        def assemble(src, dst):
            def one(i):
                hq = i // zs
                xq = hq // cores
                cq = lax.rem(hq, cores)
                t = lax.rem(i, zs)
                dst[aligned(i, pair), :] = jnp.concatenate(
                    [src(xq, cq, 0, t).astype(f32), src(xq, cq, 1, t).astype(f32)], axis=0
                ).astype(bf16)

            loop(0, width // pair, one)

        ga_wq.wait()
        assemble(lambda a, c, b, t: wqg[(a * seqs + b) * cores + c, t], wq)

        def first_norm(i):
            xv = xg[pl.ds(2 * i, 2)].reshape(2 * sl, width).astype(f32)
            normed, inverse = norm_parts(xv)
            return normed, (normed * prm[0:1, :] + prm[2:3, :]).astype(bf16)

        for i in range(halves):
            for q in range(ss // halves * i, ss // halves * (i + 1)):
                @pl.when(s != q)
                def _(q=q):
                    ex_x.into(q).wait_recv()

            for j in range(zs // halves):
                _, first = first_norm(zs // halves * i + j)
                x2t[(zs // halves * i + j) * 2 * sl : (zs // halves * i + j + 1) * 2 * sl, 0:width] = first
            at = slice(i * query_block, (i + 1) * query_block)
            projected = nn(x2t[at, 0:width], wq[...]) + prm[pl.ds(8 + z, 1), 0 : 3 * tw]
            q_s[at, :] = (projected[:, 0:tw] * scale).astype(bf16)
            turned = projected[:, tw:].T.astype(bf16)
            kvg[h, 0, :, at] = turned[0:tw, :]
            kvg[h, 1, :, at] = turned[tw : 2 * tw, :]
            ga_kv[i].send()
        ex_wf_p.wait()
        ga_go.send()
        ex_wf_1.send()
        ex_wp_1.send()
        for i in range(halves):
            ga_kv[i].relay()
        ex_wo_z.wait()
        ga_wo.send()
        for i in range(halves):
            ga_kv[i].wait()

        lane_head = lax.broadcasted_iota(jnp.int32, (query_block, tw), 1) // HEAD_DIM

        def score(n, i):
            queries = q_s[i * query_block : (i + 1) * query_block, :]
            masked = jnp.where(lane_head == n, queries, jnp.zeros_like(queries))
            for b in range(hs):
                probs[n, i, :, b * qn : (b + 1) * qn] = nn(masked, kvg[b, 0])

        def soften(n, i, low_ref):
            for r in range(query_block // chunk):
                rat = slice(r * chunk, (r + 1) * chunk)
                sv = [probs[n, i, rat, b * qn : (b + 1) * qn] + kneg[b, 0:1, :] for b in range(hs)]
                top = jnp.max(functools.reduce(jnp.maximum, sv), axis=-1, keepdims=True)
                ev = [jnp.exp(v - top) for v in sv]
                inv = 1.0 / jnp.sum(functools.reduce(jnp.add, ev), axis=-1, keepdims=True)
                for b in range(hs):
                    value = ev[b] * inv
                    probs[n, i, rat, b * qn : (b + 1) * qn] = value
                    low_ref[rat, b * qn : (b + 1) * qn] = value.astype(bf16)

        def mix(n, i, low_ref):
            head_out = nt(low_ref[:, 0:qn], kvg[0, 1])
            for b in range(1, hs):
                head_out = head_out + nt(low_ref[:, b * qn : (b + 1) * qn], kvg[b, 1])
            at = slice(i * query_block, (i + 1) * query_block)
            o_s[at, :] = jnp.where(lane_head == n, head_out.astype(bf16), o_s[at, :])

        o_s[...] = jnp.zeros_like(o_s)
        score(0, 0)
        for n in range(heads):
            soften(n, 0, pb_scr)
            score(n, 1)
            if n:
                mix(n - 1, 1, ds_scr)
            soften(n, 1, ds_scr)
            if n < heads - 1:
                score(n + 1, 0)
            mix(n, 0, pb_scr)
            if n == 0:
                ex_wf_2.send()
            if n == 1:
                ex_wf_1.wait()
                ex_wf_3.send()
        mix(heads - 1, 1, ds_scr)

        def pack(ref, v):
            ref[0:sl, :], ref[sl:, :] = dense(v)

        def unpack(ref):
            return loose(ref[0:sl, :], ref[sl:, :])

        def lay_out(q):
            pack(o_st.at[q], o_s[aligned(q, sl), :])

        loop(0, ss, lay_out)
        ex_o.send()
        og[y, z] = o_st[s]
        ex_wp_1.wait()
        ex_wp_3.send()
        ga_wo.relay()
        ga_go.relay()

        ga_wo.wait()
        assemble(lambda a, c, b, t: wog[(a * seqs + b) * cores + c, t], wo)
        ex_o.wait()
        branch = jnp.broadcast_to(prm[5:6, :], (home, width))
        for t in range(zs):
            mixed = jnp.concatenate([unpack(og.at[a, t]) for a in range(seqs)], axis=0)
            mixed_s[t] = mixed
            branch = branch + nn(mixed, wo[t * tw : (t + 1) * tw, :])
        middle = x_ref[...].reshape(home, width).astype(f32) + branch
        normed, _ = norm_parts(middle)
        x2g[pf] = (normed * prm[1:2, :] + prm[6:7, :]).astype(bf16)
        ga_x2.send(us - 1)
        middle_s[...] = middle
        for ex in (ga_go, ex_wf_2, ex_wp_2, ex_wf_3, ex_wp_3):
            ex.wait()
        assemble(
            lambda a, c, b, t: wfg[a * halves + t // near, (lax.rem(t, near) * seqs + b) * cores + c], wf
        )

        def feed(k, running):
            r = ga_x2.peer(k)

            @pl.when(k > 0)
            def _():
                ga_x2.relay_from(k)

            ga_x2.wait_from(k)
            at = aligned(r, duo)
            chip = pl.ds(cores * r, cores)
            hid = nn(x2g[chip].reshape(duo, width), wf[...]) + up_bias[0:1, :]
            gate = 1.0 / (1.0 + jnp.exp(-quick_slope * hid))
            act[at, :] = (hid * gate).astype(bf16)
            flow = nt(gog[chip].reshape(duo, width), wpg[...].reshape(part, width))
            slope = gate + quick_slope * hid * gate * (1.0 - gate)
            back = (flow * slope).astype(bf16)
            gh[at, :] = back
            gs_st[chip] = nt(back, wf[...]).astype(bf16).reshape(cores, home, width)
            re_gs.aside(r).start()

            @pl.when(k == 0)
            def _():
                ga_x2.send_last()

            @pl.when(k > 1)
            def _():
                re_gs.combine_out(k - 1)

            return running + jnp.sum(back.astype(f32), axis=0, keepdims=True)

        grad_up = lax.fori_loop(0, us, feed, jnp.zeros((1, part), f32))

        def turn_act(q):
            at = aligned(q, home)
            x2t[0:part, at] = act[at, :].T

        loop(0, ps, turn_act)
        re_gs.combine_out(us - 1)
        re_gs.combine(u_at)

        def proj_grad(c):
            wps[pl.ds(2 * c, 2)] = nn(
                x2t[aligned(c, 2 * ff_rows), :], gog[...].reshape(slab, width)
            ).astype(bf16).reshape(2, ff_rows, width)

        loop(0, zs // 2, proj_grad)
        ex_gp_1.send()

        def feed_down(r):
            chip = pl.ds(cores * r, cores)
            fd_st[chip] = nn(act[aligned(r, duo), :], wpg[...].reshape(part, width)).astype(bf16).reshape(
                cores, home, width
            )
            re_fd.aside(r).start()

        loop(0, us, feed_down)

        def scatter_rows(c, val, put):
            for j in range(val.shape[0] // rows):
                d = c * (val.shape[0] // rows) + j
                hq = d // ss
                sd = lax.rem(d, ss)
                put(
                    hq // cores, lax.rem(hq, cores), lax.rem(sd, seqs), sd // seqs,
                    val[j * rows : (j + 1) * rows, :].astype(bf16),
                )

        def turn_in(q):
            x2t[:, aligned(q, home)] = x2g[q].T

        loop(0, ps, turn_in)

        def fc_grad(c):
            def put(a, c, b, t, value):
                wfs[a * halves + t // near, (lax.rem(t, near) * seqs + b) * cores + c] = value

            scatter_rows(c, nn(x2t[aligned(c, quad), :], gh[...]), put)

        loop(0, width // quad, fc_grad)
        ex_gf_1.send()

        for t in range(zs):
            x2t[t * tw : (t + 1) * tw, 0:home] = mixed_s[t].T
        grad_final = go_ref[...].reshape(home, width).astype(f32) * keep

        re_gs.wait()

        def landed_sum(re, own):
            total = own
            for k in range(1, us):
                total = total + re.landed(re.peer(k))[...].astype(f32)
            return total

        grad_second = landed_sum(re_gs, gs_st[pf].astype(f32))
        n2, r2 = norm_parts(middle_s[...])
        grad_middle = grad_final + norm_backward(grad_second * prm[1:2, :], n2, r2)
        grad_branch = grad_middle.astype(bf16)
        for t in range(zs):
            value = nt(grad_branch, wo[t * tw : (t + 1) * tw, :]).astype(bf16)
            for a in range(seqs):
                pack(do_st.at[t, a], value[a * sl : (a + 1) * sl, :])
        ex_do.send()
        dog[s] = do_st[z, y]
        gm_s[...] = grad_middle
        sums[...] = jnp.zeros_like(sums)
        arg[...] = jnp.zeros_like(arg)
        for q in range(ps):
            c, b, a = q % cores, q // cores % seqs, q // cores // seqs
            for i in range(zs):
                at = (a * halves + i // near) * ff_rows
                arg[q, 8 + i : 9 + i, 0:ff_rows] = jnp.where(
                    (core == c) & (y == b) & (zl == i % near), grad_up[:, at : at + ff_rows], 0.0
                )
        sums[1:2, :] = jnp.sum(grad_second * n2, axis=0, keepdims=True)
        sums[6:7, :] = jnp.sum(grad_second, axis=0, keepdims=True)
        sums[5:6, :] = jnp.sum(grad_branch.astype(f32), axis=0, keepdims=True)


        def out_grad(c):
            def put(a, c, b, t, value):
                wog[(a * seqs + b) * cores + c, t] = value

            scatter_rows(c, nn(x2t[aligned(c, quad), 0:home], gm_s[...].astype(bf16)), put)

        ga_wo.drain()
        loop(0, width // quad, out_grad)
        re_wo.send_aside()
        re_wo.send()

        ex_do.wait()
        ex_gp_1.wait()

        def proj_sum(q):
            wpm[q] = (wps[t_at - zh + q].astype(f32) + wpr[q].astype(f32)).astype(bf16)

        loop(0, halves, proj_sum)
        ex_gp_2.send()
        re_fd.send()

        def gather_do(i):
            at = aligned(i, 2 * sl)
            value = jnp.concatenate([unpack(dog.at[2 * i]), unpack(dog.at[2 * i + 1])], axis=0)
            o_s[at, :] = value
            dot_s[:, at] = value.T
            qt_s[:, at] = q_s[at, :].T

        loop(0, ss // 2, gather_do)
        dq_s[...] = jnp.zeros_like(dq_s)

        def slope_in(n, i, out_ref):
            outer = o_s[i * query_block : (i + 1) * query_block, :]
            masked = jnp.where(lane_head == n, outer, jnp.zeros_like(outer))
            for b in range(hs):
                out_ref[:, b * qn : (b + 1) * qn] = nn(masked, kvg[b, 1])

        def slopes(n, i, in_ref, slope_ref, low_ref):
            for r in range(query_block // chunk):
                rat = slice(r * chunk, (r + 1) * chunk)
                dp = [in_ref[rat, b * qn : (b + 1) * qn] for b in range(hs)]
                pv = [probs[n, i, rat, b * qn : (b + 1) * qn] for b in range(hs)]
                delta = jnp.sum(
                    functools.reduce(jnp.add, [a * c for a, c in zip(dp, pv)]), axis=-1, keepdims=True
                )
                for b in range(hs):
                    slope_ref[rat, b * qn : (b + 1) * qn] = (pv[b] * (dp[b] - delta)).astype(bf16)
                    low_ref[rat, b * qn : (b + 1) * qn] = pv[b].astype(bf16)

        def slope_out(n, i, slope_ref, low_ref):
            at = slice(i * query_block, (i + 1) * query_block)
            head_rows = slice(n * HEAD_DIM, (n + 1) * HEAD_DIM)
            head_dq = nt(slope_ref[:, 0:qn], kvg[0, 0])
            for b in range(1, hs):
                head_dq = head_dq + nt(slope_ref[:, b * qn : (b + 1) * qn], kvg[b, 0])
            dq_s[at, :] = jnp.where(
                lane_head == n, (head_dq.astype(bf16).astype(f32) * scale).astype(bf16), dq_s[at, :]
            )
            for b in range(hs):
                new_k = nn(qt_s[head_rows, at], slope_ref[:, b * qn : (b + 1) * qn])
                new_v = nn(dot_s[head_rows, at], low_ref[:, b * qn : (b + 1) * qn])
                if i == 0:
                    dkt[b] = new_k
                    dvt[b] = new_v
                else:
                    kv_st[n, b, 0] = (dkt[b] + new_k).astype(bf16)
                    kv_st[n, b, 1] = (dvt[b] + new_v).astype(bf16)

        def final_rows(re, own, landed, dst):
            def one(t):
                total = own[p, t].astype(f32)
                for k in range(1, rs):
                    total = total + landed[re.peer(k), t].astype(f32)
                dst[t] = total.astype(bf16)

            loop(0, zs, one)

        slope_in(0, 0, s_scr)
        for n in range(heads):
            slopes(n, 0, s_scr, ds_scr, pb_scr)
            slope_in(n, 1, t_scr)
            slope_out(n, 0, ds_scr, pb_scr)
            if n:
                re_kv[n - 1].send()
            slopes(n, 1, t_scr, ds_scr, pb_scr)
            if n < heads - 1:
                slope_in(n + 1, 0, s_scr)
            slope_out(n, 1, ds_scr, pb_scr)
            re_kv[n].send_aside()
            if n == heads - 1:
                re_wo.wait()
                final_rows(re_wo, wog, wo_red, woz)
                ex_go_z.send()
                wozr[z] = woz[z]
            if n == 0:
                ex_gf_1.wait()

                def fc_sum(i):
                    q, b = i // ps, lax.rem(i, ps)
                    wfm[q, b] = (wfs[t_at - zh + q, b].astype(f32) + wfr[q, b].astype(f32)).astype(bf16)

                loop(0, halves * ps, fc_sum)
                ex_gf_2.send()
        re_kv[heads - 1].send()

        gpt[0:tw, :] = dq_s[...].T

        def turn_first(i):
            _, first = first_norm(i)
            x2t[:, aligned(i, 2 * sl)] = first.T

        loop(0, zs, turn_first)

        for n in range(heads):
            re_kv[n].wait()
            for k in range(2):
                at = (1 + k) * tw + n * HEAD_DIM
                gpt[at : at + HEAD_DIM, :] = (
                    kv_st[n, h, k].astype(f32) + kv_red[n, re_kv[n].peer(1), k].astype(f32)
                ).astype(bf16)
        gp[...] = gpt[...].T

        gain_sum = jnp.zeros((1, width), f32)
        shift_sum = jnp.zeros((1, width), f32)
        block = ss // halves

        def first_grad(i):
            value = nt(gp[aligned(i, block * sl), :], wq[...])
            gf_st[pl.ds(block * i, block)] = value.astype(bf16).reshape(block, sl, width)

        first_grad(1 - zh)
        ex_gf.send(0, 1)

        def qkv_grad(c):
            def put(a, c, b, t, value):
                wqg[(a * seqs + b) * cores + c, t] = value

            scatter_rows(c, nn(x2t[aligned(c, quad), 0:qn], gp[...]), put)

        ga_wq.drain()
        loop(0, width // quad, qkv_grad)
        re_wq.send_aside()
        first_grad(zh)
        re_wq.send()
        ex_gf.send(1)
        gfg[y, z] = gf_st[s]
        ex_gf_2.wait()

        def fc_last(q):
            wfz[q] = (wfm[zh, q].astype(f32) + wfq[q].astype(f32)).astype(bf16)

        loop(0, ps, fc_last)
        ex_gf_3.send()
        wfzr[pf] = wfz[pf]
        for i in range(zs):
            value = gf_st[2 * i : 2 * i + 2].reshape(2 * sl, width).astype(f32)
            normed, _ = first_norm(i)
            gain_sum = gain_sum + jnp.sum(value * normed, axis=0, keepdims=True)
            shift_sum = shift_sum + jnp.sum(value, axis=0, keepdims=True)

        sums[0:1, :] = gain_sum
        sums[2:3, :] = shift_sum
        re_fd.wait()
        feed_out = landed_sum(re_fd, fd_st[pf].astype(f32)) + prm[7:8, :]
        final = middle_s[...] + feed_out
        out_ref[...] = (final * keep).astype(bf16).reshape(seqs, sl, width)
        leave(0)
        xv = x_ref[...].reshape(home, width).astype(f32)
        br = middle_s[...] - xv
        place = lax.broadcasted_iota(jnp.int32, (1, 128), 1)
        squares = jnp.zeros((1, 128), f32)
        for k, value in enumerate((xv, br, feed_out, final)):
            squares = squares + jnp.where(place == k, jnp.sum(keep * value * value), 0.0)
        for q in range(ps):
            arg[q, 12:13, :] = squares
        projected_sum = jnp.sum(gp[...].astype(f32), axis=0, keepdims=True)
        for i in range(zs):
            at = slice(i * tw, (i + 1) * tw)
            sums[3:4, at] = jnp.where(z == i, projected_sum[:, 0:tw], 0.0)
            sums[4:5, at] = jnp.where(z == i, projected_sum[:, 2 * tw :], 0.0)
        sums[7:8, :] = jnp.sum(gog[pf].astype(f32), axis=0, keepdims=True)

        for q in range(ps):
            for i in range(zs):
                at = d_of(q, i) * rows
                arg[q, 0:8, i * rows : (i + 1) * rows] = sums[0:8, at : at + rows]
        ex_ar_p.send()
        ard[p] = arg[p]

        ex_gp_2.wait()
        gproj_ref[...] = wpm[zh].astype(f32) + wpq[...].astype(f32)
        leave(5)

        re_wq.wait()
        final_rows(re_wq, wqg, wq_red, wqz)
        ex_gq_z.send()
        wqzr[z] = wqz[z]
        ex_ar_p.wait()
        total = functools.reduce(jnp.add, [ard[q] for q in range(ps)])
        for i in range(zs):
            ar_st[i, 0:8, 0:rows] = total[0:8, i * rows : (i + 1) * rows]
            ar_st[i, 8:9, :] = total[8 + i : 9 + i, :]
            ar_st[i, 9:10, :] = total[12:13, :]
        ex_ar_z.send()
        arz[z] = ar_st[z]
        ex_go_z.wait()
        gout_ref[...] = functools.reduce(jnp.add, [wozr[t].astype(f32) for t in range(zs)])
        leave(3)

        for ex in (
            ex_small_z, ex_wq_z, ex_wo_z, ex_x, ga_small, ex_wf_p, ex_wf_1, ex_wf_2, ex_wf_3,
            ex_wp_1, ex_wp_2, ex_wp_3,
            ga_go, *ga_kv, ex_o, re_gs, re_fd, ex_do, *re_kv, re_wo, ex_go_z, re_wq,
            ex_gf_1, ex_gf_2, ex_gf_3, ex_gp_1, ex_gp_2, ex_ar_p,
        ):
            ex.drain()
        ga_x2.drain(us - 1)

        ex_gf.wait()
        grad_first = functools.reduce(jnp.add, [gfg[:, t].astype(f32) for t in range(zs)]).reshape(home, width)
        n1, r1 = norm_parts(x_ref[...].reshape(home, width).astype(f32))
        grad_in = gm_s[...] + norm_backward(grad_first * prm[0:1, :], n1, r1)
        gin_ref[...] = grad_in.reshape(seqs, sl, width)
        leave(1)

        ex_gf_3.wait()
        for q in range(ps):
            for b in range(zs):
                at = ff_place(q, b) * ff_rows
                gfc_ref[:, at : at + ff_rows] = wfzr[q, :, b * ff_rows : (b + 1) * ff_rows].astype(f32)
        leave(4)
        ex_gq_z.wait()
        for i in range(zs):
            for k in range(3):
                at = k * width + i * tw
                gqkv_ref[:, at : at + tw] = wqzr[i, :, k * tw : (k + 1) * tw].astype(f32)
        leave(2)
        ex_ar_z.wait()
        owned = functools.reduce(jnp.add, [arz[t] for t in range(zs)])
        owned_ref[...] = owned
        leave(6)
        for ex in (ex_gf, ex_gq_z, ex_ar_z):
            ex.drain()
        for copy in leaving:
            copy.wait()

    vm = pltpu.VMEM
    scratch = [
        vm((seqs, sl, width), bf16),
        vm((seqs, sl, width), bf16),
        vm((rows, 3 * width), bf16),
        vm((rows, width), bf16),
        vm((rows, ps * part), bf16),
        vm((ff_rows, width), bf16),
        vm((1, ff_rows), bf16),
        vm((2, rows), bf16),
        vm((6, rows), bf16),
        pltpu.SemaphoreType.DMA((9,)),
        vm((seqs, sl, width), bf16),
        vm((seqs, sl, width), f32),
        vm((rows, 3 * width), f32),
        vm((rows, width), f32),
        vm((rows, ps * part), f32),
        vm((ff_rows, width), f32),
        vm((16, 128), f32),
        pltpu.SemaphoreType.DMA((7,)),
        vm((16, 128), f32),
        vm((zs, 16, 128), f32),
        vm((ps, zs, 16, 128), f32),
        vm((16, width), f32),
        vm((8, part), f32),
        vm((zs, rows, 3 * tw), bf16),
        vm((ps, rows, part), bf16),
        vm((ps, zs, rows, 3 * tw), bf16),
        vm((ps, zs, rows, width), bf16),
        vm((zs, ps, rows, part), bf16),
        vm((zs, ff_rows, width), bf16),
        vm((width, 3 * tw), bf16),
        vm((width, width), bf16),
        vm((width, part), bf16),
        vm((ss, sl, width), bf16),
        vm((qn, tw), bf16),
        vm((hs, 2, tw, qn), bf16),
        vm((hs, 8, qn), f32),
        vm((heads, blocks, query_block, hs * qn), f32),
        vm((query_block, hs * qn), f32),
        vm((query_block, hs * qn), f32),
        vm((query_block, hs * qn), bf16),
        vm((query_block, hs * qn), bf16),
        vm((qn, tw), bf16),
        vm((ss, sl * tw // lanes_per, lanes_per), bf16),
        vm((seqs, zs, sl * tw // lanes_per, lanes_per), bf16),
        vm((zs, home, tw), bf16),
        vm((home, width), f32),
        vm((home, width), f32),
        vm((ps, home, width), bf16),
        vm((ps, home, width), bf16),
        vm((slab, part), bf16),
        vm((slab, part), bf16),
        vm((width, slab), bf16),
        vm((ps, home, width), bf16),
        vm((rs, home, width), bf16),
        vm((rs, home, width), bf16),
        vm((ps, home, width), bf16),
        vm((rs, home, width), bf16),
        vm((rs, home, width), bf16),
        vm((zs, seqs, sl * tw // lanes_per, lanes_per), bf16),
        vm((ss, sl * tw // lanes_per, lanes_per), bf16),
        vm((tw, qn), bf16),
        vm((tw, qn), bf16),
        vm((qn, tw), bf16),
        vm((hs, HEAD_DIM, qn), f32),
        vm((hs, HEAD_DIM, qn), f32),
        vm((heads, hs, 2, HEAD_DIM, qn), bf16),
        vm((heads, xs, 2, HEAD_DIM, qn), bf16),
        vm((heads, xs, 2, HEAD_DIM, qn), bf16),
        vm((3 * tw, qn), bf16),
        vm((qn, 3 * tw), bf16),
        vm((ss, sl, width), bf16),
        vm((seqs, zs, sl, width), bf16),
        vm((rs, zs, rows, width), bf16),
        vm((rs, zs, rows, width), bf16),
        vm((zs, rows, width), bf16),
        vm((zs, rows, width), bf16),
        vm((rs, zs, rows, 3 * tw), bf16),
        vm((rs, zs, rows, 3 * tw), bf16),
        vm((zs, rows, 3 * tw), bf16),
        vm((zs, rows, 3 * tw), bf16),
        vm((zs, ps, rows, part), bf16),
        vm((halves, ps, rows, part), bf16),
        vm((halves, ps, rows, part), bf16),
        vm((ps, rows, part), bf16),
        vm((ps, rows, part), bf16),
        vm((ps, rows, part), bf16),
        vm((zs, ff_rows, width), bf16),
        vm((halves, ff_rows, width), bf16),
        vm((halves, ff_rows, width), bf16),
        vm((ff_rows, width), bf16),
        vm((ps, 16, 128), f32),
        vm((ps, 16, 128), f32),
        vm((8, width), f32),
        vm((zs, 16, 128), f32),
        vm((zs, 16, 128), f32),
        pltpu.SemaphoreType.DMA((33,)),
        pltpu.SemaphoreType.DMA((10, zs)),
        pltpu.SemaphoreType.DMA((4, ss)),
        pltpu.SemaphoreType.DMA((3, ps)),
        pltpu.SemaphoreType.DMA((10, 2)),
        pltpu.SemaphoreType.DMA((6, ps)),
        pltpu.SemaphoreType.DMA((7, 2, rs)),
        pltpu.SemaphoreType.DMA((zs, hs)),
        pltpu.SemaphoreType.DMA((heads, 2, xs)),
        pltpu.SemaphoreType.DMA((7, 2)),
    ]
    in_smem = pl.BlockSpec(memory_space=pltpu.SMEM)
    in_place = pl.BlockSpec(memory_space=pl.ANY)
    shapes = (
        jax.ShapeDtypeStruct((seqs, sl, width), bf16),
        jax.ShapeDtypeStruct((seqs, sl, width), f32),
        jax.ShapeDtypeStruct((rows, 3 * width), f32),
        jax.ShapeDtypeStruct((rows, width), f32),
        jax.ShapeDtypeStruct((rows, ps * part), f32),
        jax.ShapeDtypeStruct((ff_rows, width), f32),
        jax.ShapeDtypeStruct((1, ff_rows), f32),
        jax.ShapeDtypeStruct((2, rows), f32),
        jax.ShapeDtypeStruct((6, rows), f32),
        jax.ShapeDtypeStruct((1, 4), f32),
    )
    results = pl.pallas_call(
        kernel,
        out_shape=shapes[0:6] + (jax.ShapeDtypeStruct((16, 128), f32),),
        in_specs=[in_smem] + [in_place] * 9,
        out_specs=(in_place,) * 7,
        scratch_shapes=scratch,
        compiler_params=pltpu.CompilerParams(
            collective_id=0, has_side_effects=True, vmem_limit_bytes=63 * 1024 * 1024
        ),
        name="layer",
    )(
        lengths,
        layer_input.reshape(seqs, sl, width),
        grad_out.reshape(seqs, sl, width),
        w_qkv,
        w_out,
        w_fc,
        w_proj,
        b_fc.reshape(1, ff_rows),
        norm_gains,
        biases,
    )

    def finish(len_ref, *refs):
        given, kept, held, small_held = refs[0:7], refs[7:17], refs[17:24], refs[24:28]
        in_sem, out_sem = refs[28:]
        arrive = [pltpu.make_async_copy(given[i], held[i], in_sem.at[i]) for i in range(7)]
        leave = [
            pltpu.make_async_copy(ref, kept[i], out_sem.at[i])
            for i, ref in enumerate(held[0:6] + small_held)
        ]
        for i in (6, 1, 4, 5, 2, 0, 3):
            arrive[i].start()
        arrive[6].wait()
        owned = held[6]
        small_held[0][...] = owned[8:9, 0:ff_rows]
        small_held[1][...] = owned[0:2, 0:rows]
        small_held[2][...] = owned[2:8, 0:rows]
        valid = (len_ref[0] + len_ref[1]).astype(f32) * width
        small_held[3][...] = jnp.sqrt(owned[9:10, 0:4] / valid)
        for i in range(6, 10):
            leave[i].start()
        for i in (1, 4, 5, 2, 0, 3):
            arrive[i].wait()
            leave[i].start()
        for copy in leave:
            copy.wait()

    final = pl.pallas_call(
        finish,
        out_shape=shapes,
        in_specs=[in_smem] + [in_place] * 7,
        out_specs=(in_place,) * 10,
        scratch_shapes=[vm(s.shape, s.dtype) for s in shapes[0:6]]
        + [vm((16, 128), f32)]
        + [vm(s.shape, s.dtype) for s in shapes[6:]]
        + [pltpu.SemaphoreType.DMA((7,)), pltpu.SemaphoreType.DMA((10,))],
        name="finish",
    )(lengths, *results)
    return (
        final[0].reshape(layer_input.shape),
        final[1].reshape(layer_input.shape),
        *final[2:6],
        final[6].reshape(ff_rows),
        final[7],
        final[8],
        final[9].reshape(4),
    )


def fits(seqs, sl, width, hs, ss, qkv_rows):
    if seqs != 2 or ss % seqs or hs % cores:
        return False
    zs = ss // seqs
    if width % zs or (width // zs) % HEAD_DIM or zs != 4 or hs != zs or qkv_rows % 8:
        return False
    tw = width // zs
    keys = ss * sl * hs
    return tw <= 256 and keys * ss * sl * (tw // HEAD_DIM) * 4 <= 16 * 1024 * 1024


def on_device(layer_input, grad_out, lengths, w_qkv, w_out, w_fc, w_proj, b_fc, norm_gains, biases):
    seqs, _, sl, width = layer_input.shape
    hs, ss = lax.axis_size("head"), lax.axis_size("seq")
    chosen = fused_layer if fits(seqs, sl, width, hs, ss, w_qkv.shape[0]) else spread_layer
    return chosen(
        layer_input, grad_out, lengths, w_qkv, w_out, w_fc, w_proj, b_fc, norm_gains, biases
    )


def solution(mesh):
    return jax.shard_map(
        on_device,
        mesh=mesh,
        in_specs=(
            P(None, "seq", "head", None),
            P(None, "seq", "head", None),
            P(),
            P(("head", "seq"), None),
            P(("head", "seq"), None),
            P(("head", "seq"), None),
            P(("head", "seq"), None),
            P(("head", "seq")),
            P(None, ("head", "seq")),
            P(None, ("head", "seq")),
        ),
        out_specs=(
            P(None, "seq", "head", None),
            P(None, "seq", "head", None),
            P(("head", "seq"), None),
            P(("head", "seq"), None),
            P(("head", "seq"), None),
            P(("head", "seq"), None),
            P(("head", "seq")),
            P(None, ("head", "seq")),
            P(None, ("head", "seq")),
            P(),
        ),
        check_vma=False,
    )
```

```python
import functools

import jax
import jax.numpy as jnp
from jax import lax
from jax.sharding import PartitionSpec as P
from jax.experimental import pallas as pl
from jax.experimental.pallas import tpu as pltpu

HEAD_DIM = 64


masked_score = -1e30
block_keys = 512
quick_slope = 1.702
epsilon = 1e-05


def layer_norm_parts(inputs):
    centre = inputs - jnp.mean(inputs, axis=-1, keepdims=True)
    inverse = lax.rsqrt(jnp.mean(centre * centre, axis=-1, keepdims=True) + epsilon)
    return (centre * inverse, inverse)


def norm_backward(grad_normed, normed, inverse):
    return inverse * (
        grad_normed
        - jnp.mean(grad_normed, axis=-1, keepdims=True)
        - normed * jnp.mean(grad_normed * normed, axis=-1, keepdims=True)
    )


def split_heads(piece_block):
    return piece_block.reshape(
        piece_block.shape[0], piece_block.shape[1], piece_block.shape[2] // HEAD_DIM, HEAD_DIM
    )


def head_scores(left_side, right_side):
    return jnp.einsum("sqhd,skhd->shqk", left_side, right_side, preferred_element_type=jnp.float32)


def weighted(probabilities, right_side):
    return jnp.einsum(
        "shqk,skhd->sqhd", probabilities, right_side, preferred_element_type=jnp.float32
    )


def transposed(probabilities, right_side):
    return jnp.einsum(
        "shqk,sqhd->skhd", probabilities, right_side, preferred_element_type=jnp.float32
    )


def over_blocks(step_fn, running, pieces):
    extent = pieces[0].shape[1]
    number = extent // block_keys
    parted = tuple(
        (
            piece_part.reshape(
                (piece_part.shape[0], number, block_keys) + piece_part.shape[2:]
            ).swapaxes(0, 1)
            for piece_part in pieces
        )
    )

    def advance(inner_run, element):
        position, blocks = element
        return (step_fn(inner_run, blocks, position * block_keys), None)

    return lax.scan(advance, running, (jnp.arange(number, dtype=jnp.int32), parted))[0]


def spread_layer(layer_input, grad_out, lengths, w_qkv, w_out, w_fc, w_proj, b_fc, norm_gains, biases):
    sequences = layer_input.shape[0]
    slice_len = layer_input.shape[2]
    model_width = layer_input.shape[3]
    head_ways = lax.axis_size("head")
    group_len = slice_len * head_ways
    local_width = model_width // head_ways
    head_count = local_width // HEAD_DIM
    head_place = lax.axis_index("head")
    cycle_place = lax.axis_index("seq")
    flat_rows = sequences * slice_len
    full_qkv, full_out, full_fc, full_proj, full_bias_fc, full_gains, full_biases = (
        lax.all_gather(w_qkv, ("head", "seq"), axis=0, tiled=True),
        lax.all_gather(w_out, ("head", "seq"), axis=0, tiled=True),
        lax.all_gather(w_fc, ("head", "seq"), axis=0, tiled=True),
        lax.all_gather(w_proj, ("head", "seq"), axis=0, tiled=True),
        lax.all_gather(b_fc, ("head", "seq"), axis=0, tiled=True),
        lax.all_gather(norm_gains, ("head", "seq"), axis=1, tiled=True),
        lax.all_gather(biases, ("head", "seq"), axis=1, tiled=True),
    )
    gain_vals = full_gains.astype(jnp.float32)
    shift_vals = full_biases.astype(jnp.float32)
    bias_up = full_bias_fc.astype(jnp.float32)
    token_places = (
        cycle_place * group_len + head_place * slice_len + jnp.arange(slice_len, dtype=jnp.int32)
    )
    token_keep = (
        (token_places[None, :] < lengths[:, None]).astype(jnp.float32).reshape(flat_rows, 1)
    )
    own_places = cycle_place * group_len + jnp.arange(group_len, dtype=jnp.int32)
    own_allowed = (own_places[None, :] < lengths[:, None])[:, None, None, :]

    def allowed_at(offset, extent):
        places = offset + jnp.arange(extent, dtype=jnp.int32)
        return (places[None, :] < lengths[:, None])[:, None, None, :]

    inputs = layer_input.reshape(flat_rows, model_width).astype(jnp.float32)
    normed_one, inverse_one = layer_norm_parts(inputs)
    first_in = (normed_one * gain_vals[0] + shift_vals[0]).astype(jnp.bfloat16)
    projected = jnp.dot(first_in, full_qkv, preferred_element_type=jnp.float32)
    query_scale = HEAD_DIM ** (-0.5)
    queries = ((projected[:, :model_width] + shift_vals[1]) * query_scale).astype(jnp.bfloat16)
    keys_new = projected[:, model_width : 2 * model_width].astype(jnp.bfloat16)
    values_new = (projected[:, 2 * model_width :] + shift_vals[2]).astype(jnp.bfloat16)
    packed = jnp.stack([queries, keys_new, values_new], axis=1).reshape(
        sequences, slice_len, 3, head_ways, local_width
    )
    spread = lax.all_to_all(packed, "head", split_axis=3, concat_axis=1, tiled=True)
    query_block = spread[:, :, 0, 0]
    key_block = spread[:, :, 1, 0]
    value_block = spread[:, :, 2, 0]
    query_heads = split_heads(query_block)
    key_heads = split_heads(key_block)
    value_heads = split_heads(value_block)

    def maxima_step(running, pieces, offset):
        highest, denominator = running
        scores = head_scores(query_heads, split_heads(pieces[0]))
        allowed = allowed_at(offset, pieces[0].shape[1])
        scores = jnp.where(allowed, scores, masked_score)
        raised = jnp.maximum(highest, jnp.max(scores, axis=-1))
        weights = jnp.where(allowed, jnp.exp(scores - raised[..., None]), 0.0)
        denominator = denominator * jnp.exp(highest - raised) + jnp.sum(weights, axis=-1)
        return (raised, denominator)

    zero_rows = jnp.zeros((sequences, head_count, group_len), jnp.float32)
    highest, denominator = over_blocks(
        maxima_step,
        (zero_rows + masked_score, zero_rows),
        (lax.all_gather(key_block, "seq", axis=1, tiled=True),),
    )
    log_total = highest + jnp.log(denominator)

    def attention_weights(key_piece, offset):
        scores = head_scores(query_heads, key_piece)
        allowed = allowed_at(offset, key_piece.shape[1])
        return jnp.where(
            allowed, jnp.exp(jnp.where(allowed, scores, masked_score) - log_total[..., None]), 0.0
        )

    zero_heads = jnp.zeros((sequences, group_len, head_count, HEAD_DIM), jnp.float32)

    def output_step(running, pieces, offset):
        probabilities = attention_weights(split_heads(pieces[0]), offset)
        return running + weighted(probabilities.astype(jnp.bfloat16), split_heads(pieces[1]))

    attended = over_blocks(
        output_step,
        zero_heads,
        (
            lax.all_gather(key_block, "seq", axis=1, tiled=True),
            lax.all_gather(value_block, "seq", axis=1, tiled=True),
        ),
    )
    mixed_heads = attended.astype(jnp.bfloat16).reshape(
        sequences, head_ways, slice_len, local_width
    )
    gathered_out = lax.all_to_all(mixed_heads, "head", split_axis=1, concat_axis=3, tiled=True)
    mixed_rows = gathered_out.reshape(flat_rows, model_width)
    branch = jnp.dot(mixed_rows, full_out, preferred_element_type=jnp.float32) + shift_vals[3]
    middle = inputs + branch
    normed_two, inverse_two = layer_norm_parts(middle)
    second_in = (normed_two * gain_vals[1] + shift_vals[4]).astype(jnp.bfloat16)
    hidden = jnp.dot(second_in, full_fc, preferred_element_type=jnp.float32) + bias_up
    gate_sig = jax.nn.sigmoid(quick_slope * hidden)
    activated = (hidden * gate_sig).astype(jnp.bfloat16)
    feed_out = jnp.dot(activated, full_proj, preferred_element_type=jnp.float32) + shift_vals[5]
    final_rows = middle + feed_out
    result = (final_rows * token_keep).astype(jnp.bfloat16).reshape(layer_input.shape)
    local_squares = jnp.stack(
        [
            jnp.sum(token_keep * inputs * inputs),
            jnp.sum(token_keep * branch * branch),
            jnp.sum(token_keep * feed_out * feed_out),
            jnp.sum(token_keep * final_rows * final_rows),
        ]
    )
    squares = lax.psum(local_squares, ("head", "seq"))
    valid_count = jnp.sum(lengths).astype(jnp.float32) * model_width
    root_means = jnp.sqrt(squares / valid_count)
    grad_final = grad_out.reshape(flat_rows, model_width).astype(jnp.float32) * token_keep
    grad_feed = grad_final.astype(jnp.bfloat16)
    grad_proj = jnp.dot(activated.T, grad_feed, preferred_element_type=jnp.float32)
    grad_shift_proj = jnp.sum(grad_feed.astype(jnp.float32), axis=0)
    grad_act = jnp.dot(grad_feed, full_proj.T, preferred_element_type=jnp.float32)
    grad_hidden = (
        grad_act * (gate_sig + quick_slope * hidden * gate_sig * (1.0 - gate_sig))
    ).astype(jnp.bfloat16)
    grad_fc = jnp.dot(second_in.T, grad_hidden, preferred_element_type=jnp.float32)
    grad_bias_up = jnp.sum(grad_hidden.astype(jnp.float32), axis=0)
    grad_second = jnp.dot(grad_hidden, full_fc.T, preferred_element_type=jnp.float32)
    grad_gain_two = jnp.sum(grad_second * normed_two, axis=0)
    grad_shift_two = jnp.sum(grad_second, axis=0)
    grad_middle = grad_final + norm_backward(grad_second * gain_vals[1], normed_two, inverse_two)
    grad_branch = grad_middle.astype(jnp.bfloat16)
    grad_out_weight = jnp.dot(mixed_rows.T, grad_branch, preferred_element_type=jnp.float32)
    grad_shift_out = jnp.sum(grad_branch.astype(jnp.float32), axis=0)
    grad_mixed = jnp.dot(grad_branch, full_out.T, preferred_element_type=jnp.float32).astype(
        jnp.bfloat16
    )
    grad_spread = lax.all_to_all(
        grad_mixed.reshape(sequences, slice_len, head_ways, local_width),
        "head",
        split_axis=2,
        concat_axis=1,
        tiled=True,
    )
    grad_block = grad_spread[:, :, 0]
    grad_heads = split_heads(grad_block)

    def delta_step(running, pieces, offset):
        probabilities = attention_weights(split_heads(pieces[0]), offset)
        grad_probs = head_scores(grad_heads, split_heads(pieces[1]))
        return running + jnp.sum(probabilities * grad_probs, axis=-1)

    row_delta = over_blocks(
        delta_step,
        zero_rows,
        (
            lax.all_gather(key_block, "seq", axis=1, tiled=True),
            lax.all_gather(value_block, "seq", axis=1, tiled=True),
        ),
    )

    def query_step(running, pieces, offset):
        key_piece = split_heads(pieces[0])
        probabilities = attention_weights(key_piece, offset)
        grad_probs = head_scores(grad_heads, split_heads(pieces[1]))
        slopes = (probabilities * (grad_probs - row_delta[..., None])).astype(jnp.bfloat16)
        return running + weighted(slopes, key_piece)

    grad_query = over_blocks(
        query_step,
        zero_heads,
        (
            lax.all_gather(key_block, "seq", axis=1, tiled=True),
            lax.all_gather(value_block, "seq", axis=1, tiled=True),
        ),
    )
    all_logs, all_deltas = (
        lax.all_gather(log_total.transpose(0, 2, 1), "seq", axis=1, tiled=True),
        lax.all_gather(row_delta.transpose(0, 2, 1), "seq", axis=1, tiled=True),
    )

    def key_step(running, pieces, offset):
        query_piece = split_heads(pieces[0])
        grad_piece = split_heads(pieces[1])
        extent = pieces[0].shape[1]
        log_piece = lax.dynamic_slice_in_dim(all_logs, offset, extent, 1).transpose(0, 2, 1)
        delta_piece = lax.dynamic_slice_in_dim(all_deltas, offset, extent, 1).transpose(0, 2, 1)
        scores = head_scores(query_piece, key_heads)
        probabilities = jnp.where(
            own_allowed,
            jnp.exp(jnp.where(own_allowed, scores, masked_score) - log_piece[..., None]),
            0.0,
        )
        grad_value = running[1] + transposed(probabilities.astype(jnp.bfloat16), grad_piece)
        grad_probs = head_scores(grad_piece, value_heads)
        slopes = (probabilities * (grad_probs - delta_piece[..., None])).astype(jnp.bfloat16)
        grad_key = running[0] + transposed(slopes, query_piece)
        return (grad_key, grad_value)

    grad_key, grad_value = over_blocks(
        key_step,
        (zero_heads, zero_heads),
        (
            lax.all_gather(query_block, "seq", axis=1, tiled=True),
            lax.all_gather(grad_block, "seq", axis=1, tiled=True),
        ),
    )
    stacked = jnp.stack([grad_query, grad_key, grad_value], axis=2).astype(jnp.bfloat16)
    stacked = stacked.reshape(sequences, head_ways, slice_len, 3, local_width)
    returned = lax.all_to_all(stacked, "head", split_axis=1, concat_axis=4, tiled=True)
    column_scale = jnp.concatenate(
        [
            jnp.full((model_width,), query_scale, jnp.float32),
            jnp.ones((2 * model_width,), jnp.float32),
        ]
    )
    grad_projected = returned.reshape(flat_rows, 3 * model_width).astype(jnp.float32) * column_scale
    grad_shift_query = jnp.sum(grad_projected[:, :model_width], axis=0)
    grad_shift_value = jnp.sum(grad_projected[:, 2 * model_width :], axis=0)
    grad_projected_low = grad_projected.astype(jnp.bfloat16)
    grad_qkv = jnp.dot(first_in.T, grad_projected_low, preferred_element_type=jnp.float32)
    grad_first = jnp.dot(grad_projected_low, full_qkv.T, preferred_element_type=jnp.float32)
    grad_gain_one = jnp.sum(grad_first * normed_one, axis=0)
    grad_shift_one = jnp.sum(grad_first, axis=0)
    grad_inputs = grad_middle + norm_backward(grad_first * gain_vals[0], normed_one, inverse_one)
    grad_gain_rows = jnp.stack([grad_gain_one, grad_gain_two])
    grad_shift_rows = jnp.stack(
        [
            grad_shift_one,
            grad_shift_query,
            grad_shift_value,
            grad_shift_out,
            grad_shift_two,
            grad_shift_proj,
        ]
    )
    owned_grads = (
        lax.psum_scatter(grad_qkv, ("head", "seq"), scatter_dimension=0, tiled=True),
        lax.psum_scatter(grad_out_weight, ("head", "seq"), scatter_dimension=0, tiled=True),
        lax.psum_scatter(grad_fc, ("head", "seq"), scatter_dimension=0, tiled=True),
        lax.psum_scatter(grad_proj, ("head", "seq"), scatter_dimension=0, tiled=True),
        lax.psum_scatter(grad_bias_up, ("head", "seq"), scatter_dimension=0, tiled=True),
        lax.psum_scatter(grad_gain_rows, ("head", "seq"), scatter_dimension=1, tiled=True),
        lax.psum_scatter(grad_shift_rows, ("head", "seq"), scatter_dimension=1, tiled=True),
    )
    return (
        result,
        grad_inputs.reshape(layer_input.shape),
        owned_grads[0],
        owned_grads[1],
        owned_grads[2],
        owned_grads[3],
        owned_grads[4],
        owned_grads[5],
        owned_grads[6],
        root_means,
    )


f32 = jnp.float32
bf16 = jnp.bfloat16
cores = 2
halves = 2
lanes_per = 128


def nn(left, right):
    return lax.dot_general(left, right, (((1,), (0,)), ((), ())), preferred_element_type=f32)


def nt(left, right):
    return lax.dot_general(left, right, (((1,), (1,)), ((), ())), preferred_element_type=f32)


def loop(low, high, step_fn, unroll=1):
    def advance(index, carry):
        step_fn(index)
        return carry

    lax.fori_loop(low, high, advance, 0, unroll=unroll)


def aligned(index, extent):
    return pl.ds(pl.multiple_of(index * extent, extent), extent)


def norm_parts(v):
    centre = v - jnp.mean(v, axis=-1, keepdims=True)
    inverse = lax.rsqrt(jnp.mean(centre * centre, axis=-1, keepdims=True) + epsilon)
    return centre * inverse, inverse


def remote(src, dst, send_sem, recv_sem, place):
    return pltpu.make_async_remote_copy(
        src_ref=src,
        dst_ref=dst,
        send_sem=send_sem,
        recv_sem=recv_sem,
        device_id=place,
        device_id_type=pl.DeviceIdType.MESH,
    )


def dense(v):
    n = v.shape[0]
    low = v[:, 0:lanes_per]
    rest = v[:, lanes_per:]
    return low, jnp.concatenate([rest[0 : n // 2], rest[n // 2 :]], axis=1)


def loose(low, rest):
    wide = rest.shape[1] // 2
    return jnp.concatenate(
        [low, jnp.concatenate([rest[:, 0:wide], rest[:, wide:]], axis=0)], axis=1
    )


class Exchange:
    def __init__(self, n, me, place, src, dst, send_sem, recv_sem, order=None):
        self.n, self.me, self.place, self.src, self.dst = n, me, place, src, dst
        self.send_sem, self.recv_sem, self.order = send_sem, recv_sem, order

    def out(self, q):
        return remote(
            self.src(q), self.dst(self.me), self.send_sem, self.recv_sem.at[self.me], self.place(q)
        )

    def into(self, q):
        return remote(
            self.dst(q), self.dst(q), self.send_sem, self.recv_sem.at[q], self.place(q)
        )

    def peer(self, k):
        return lax.rem(self.me + k, self.n)

    def send(self, low=0, high=None):
        if self.order is None:
            loop(1, self.n, lambda k: self.out(self.peer(k)).start())
        else:
            for q in self.order[low:high]:
                self.out(q).start()

    def wait(self):
        loop(1, self.n, lambda k: self.into(self.peer(k)).wait_recv())

    def drain(self):
        loop(1, self.n, lambda k: self.out(self.peer(k)).wait_send())


def chip_peer(n, inner, me, k):
    outer = n // inner
    a = lax.rem(me // inner + lax.rem(k, outer), outer)
    b = lax.rem(lax.rem(me, inner) + k // outer, inner)
    return a * inner + b


class Gather:
    def __init__(self, n, inner, me, core, place, dst, send_sem, recv_sem):
        self.n, self.inner, self.me, self.core, self.place, self.dst = n, inner, me, core, place, dst
        self.send_sem, self.recv_sem = send_sem, recv_sem
        self.mine = me * cores + core

    def peer(self, k):
        return chip_peer(self.n, self.inner, self.me, k)

    def move(self, slot, place):
        return remote(
            self.dst(slot), self.dst(slot), self.send_sem, self.recv_sem.at[slot], place
        )

    def out(self, k):
        return self.move(self.mine, self.place(self.peer(k), self.core))

    def aside(self, k):
        return self.move(
            self.peer(k) * cores + self.core, self.place(self.me, 1 - self.core)
        )

    def send(self, last=None):
        loop(1, last or self.n, lambda k: self.out(k).start())
        self.aside(0).start()

    def send_last(self):
        loop(1, self.n - 1, lambda k: self.out(k).wait_send())
        self.out(self.n - 1).start()

    def relay_from(self, k):
        self.out_slot(k, self.core).wait_recv()
        self.aside(k).start()

    def out_slot(self, k, core):
        return self.move(self.peer(k) * cores + core, self.place(self.peer(k), core))

    def wait_from(self, k):
        self.out_slot(k, 1 - self.core).wait_recv()

    def relay(self):
        loop(1, self.n, self.relay_from)

    def wait(self):
        loop(0, self.n, self.wait_from)

    def drain(self, first=1):
        loop(first, self.n, lambda k: self.out(k).wait_send())
        loop(0, self.n, lambda k: self.aside(k).wait_send())


class Reduce:
    def __init__(self, n, inner, me, core, place, stage, beside, landed, sems, recv_sems, add):
        self.n, self.inner, self.me, self.core, self.place = n, inner, me, core, place
        self.stage, self.beside, self.landed = stage, beside, landed
        self.sems, self.recv_sems, self.add = sems, recv_sems, add

    def peer(self, k):
        return chip_peer(self.n, self.inner, self.me, k)

    def own(self, r):
        return self.stage(r * cores + self.core)

    def aside(self, r):
        return remote(
            self.stage(r * cores + 1 - self.core),
            self.beside(r),
            self.sems.at[0],
            self.recv_sems.at[0, r],
            self.place(self.me, 1 - self.core),
        )

    def out(self, r):
        return remote(
            self.own(r),
            self.landed(self.me),
            self.sems.at[1],
            self.recv_sems.at[1, self.me],
            self.place(r, self.core),
        )

    def combine(self, r):
        self.aside(r).wait_recv()
        self.add(self.own(r), self.beside(r))

    def combine_out(self, k):
        r = self.peer(k)
        self.combine(r)
        self.out(r).start()

    def send_aside(self):
        loop(1, self.n, lambda k: self.aside(self.peer(k)).start())
        self.aside(self.me).start()

    def send(self):
        loop(1, self.n, self.combine_out)
        self.combine(self.me)

    def wait(self):
        def one(k):
            r = self.peer(k)
            remote(
                self.landed(r), self.landed(r), self.sems.at[1], self.recv_sems.at[1, r],
                self.place(r, self.core),
            ).wait_recv()

        loop(1, self.n, one)

    def drain_aside(self):
        loop(0, self.n, lambda k: self.aside(self.peer(k)).wait_send())

    def drain(self):
        self.drain_aside()
        loop(1, self.n, lambda k: self.out(self.peer(k)).wait_send())


def fused_layer(layer_input, grad_out, lengths, w_qkv, w_out, w_fc, w_proj, b_fc, norm_gains, biases):
    seqs, _, sl, width = layer_input.shape
    hs = lax.axis_size("head")
    ss = lax.axis_size("seq")
    zs = ss // seqs
    ps = hs * seqs
    xs = hs // cores
    rs = xs * seqs
    group = sl * hs
    tw = width // zs
    heads = tw // HEAD_DIM
    rows = w_qkv.shape[0]
    ff_rows = w_proj.shape[0]
    part = ff_rows * zs
    home = seqs * sl
    qn = ss * sl
    slab = ps * home
    near = zs // halves
    us = near * seqs
    duo = cores * home
    query_block = 256
    blocks = qn // query_block
    chunk = 32
    pair = 2 * rows
    quad = 8 * rows
    scale = HEAD_DIM ** (-0.5)

    def ff_place(q, b):
        u, c = q // cores, q % cores
        head_of = (b // halves) * cores + c
        return head_of * ss + ((b % halves) * near + u // seqs) * seqs + u % seqs

    def kernel(
        len_ref, x_hbm, go_hbm, wqkv_hbm, wout_hbm, wfc_hbm, wproj_hbm, bfc_hbm, gain_hbm, bias_hbm,
        out_hbm, gin_hbm, gqkv_hbm, gout_hbm, gfc_hbm, gproj_hbm, owned_hbm,
        x_ref, go_ref, wqkv_ref, wout_ref, wfc_ref, wproj_ref, bfc_ref, gain_ref, bias_ref, in_sem,
        out_ref, gin_ref, gqkv_ref, gout_ref, gfc_ref, gproj_ref, owned_ref, home_sem,
        small, small_z, small_g, prm, up_bias,
        qkv_st, fc_st, wqg, wog, wfg, wpg, wq, wo, wf,
        xg, q_s, kvg, kneg, probs, s_scr, t_scr, pb_scr, ds_scr, o_s, o_st, og, mixed_s,
        middle_s, gm_s,
        x2g, gog, act, gh, x2t, gs_st, gs_in, gs_red, fd_st, fd_in, fd_red,
        do_st, dog, dot_s, qt_s, dq_s, dkt, dvt, kv_st, kv_in, kv_red, gpt, gp,
        gf_st, gfg, wo_in, wo_red, woz, wozr, wq_in, wq_red, wqz, wqzr,
        wfs, wfr, wfm, wfq, wfz, wfzr, wps, wpr, wpm, wpq, arg, ard, sums, ar_st, arz,
        send, zsem, lsem, psem, bsem, gsem, rsem, ksem, krsem, ssem,
    ):
        h = lax.axis_index("head")
        s = lax.axis_index("seq")
        z = s // seqs
        y = lax.rem(s, seqs)
        core = lax.rem(h, cores)
        r_at = (h // cores) * seqs + y
        x_at = h // cores
        p = r_at * cores + core
        zh = z // near
        zl = lax.rem(z, near)
        u_at = zl * seqs + y
        pf = u_at * cores + core
        t_at = x_at * halves + zh
        t_far = x_at * halves + 1 - zh

        def chip_place(r, c):
            return ((r // seqs) * cores + c, z * seqs + lax.rem(r, seqs))

        def slab_place(q):
            return chip_place(q // cores, lax.rem(q, cores))

        def square_place(u, c):
            return (x_at * cores + c, (zh * near + u // seqs) * seqs + lax.rem(u, seqs))

        def ring_place(q):
            return square_place(q // cores, lax.rem(q, cores))

        def half_place(q):
            return (h, (q * near + zl) * seqs + y)

        def beside_place(q):
            return (q * cores + core, s)

        def line_place(q):
            return (h, q)

        def z_place(q):
            return (h, q * seqs + y)

        def x_place(r, c):
            return (r * cores + c, s)

        count = {}

        def take(name):
            number = count.get(name, 0)
            count[name] = number + 1
            return number

        z_order = [(1 - zh) * (zs - 1), near - zh, zh * zs + 1 - z]
        line_order = [q * seqs + b for q in z_order for b in range(seqs)] + [z * seqs + 1 - y]

        def over_z(src, dst):
            return Exchange(
                zs, z, z_place, src, dst, send.at[take("s")], zsem.at[take("z")], z_order
            )

        def over_line(src, dst):
            return Exchange(
                ss, s, line_place, src, dst, send.at[take("s")], lsem.at[take("l")], line_order
            )

        def over_plane(src, dst):
            return Exchange(ps, p, slab_place, src, dst, send.at[take("s")], psem.at[take("p")])

        def over_square(src, dst):
            return Exchange(ps, pf, ring_place, src, dst, send.at[take("s")], psem.at[take("p")])

        def over_half(src, dst):
            return Exchange(halves, zh, half_place, src, dst, send.at[take("s")], bsem.at[take("b")])

        def over_x(src, dst):
            return Exchange(xs, x_at, beside_place, src, dst, send.at[take("s")], bsem.at[take("b")])

        def gather(dst):
            return Gather(rs, seqs, r_at, core, chip_place, dst, send.at[take("s")], gsem.at[take("g")])

        def gather_square(dst):
            return Gather(us, seqs, u_at, core, square_place, dst, send.at[take("s")], gsem.at[take("g")])

        def add_rows(block):
            def add(a, b):
                extent = a.shape[0]

                def one(i):
                    at = aligned(i, block)
                    a[at, :] = (a[at, :].astype(f32) + b[at, :].astype(f32)).astype(bf16)

                loop(0, extent // block, one)

            return add

        def add_blocks(a, b):
            def one(i):
                a[i] = (a[i].astype(f32) + b[i].astype(f32)).astype(bf16)

            loop(0, a.shape[0], one)

        def reduce(stage, beside, landed, add):
            number = take("r")
            return Reduce(
                rs, seqs, r_at, core, chip_place, stage, beside, landed, ssem.at[number],
                rsem.at[number], add,
            )

        def reduce_square(stage, beside, landed, add):
            number = take("r")
            return Reduce(
                us, seqs, u_at, core, square_place, stage, beside, landed, ssem.at[number],
                rsem.at[number], add,
            )

        ex_small_z = over_z(lambda q: small, lambda q: small_z.at[q])
        ex_wq_z = over_z(lambda q: qkv_st.at[q], lambda q: wqg.at[p, q])
        ex_wo_z = over_z(lambda q: wout_ref, lambda q: wog.at[p, q])
        ex_x = over_line(lambda q: x_ref.at[lax.rem(q, seqs)], lambda q: xg.at[q])
        ex_x.order = [lax.rem(s + k, ss) for k in range(1, ss)]
        ga_small = gather(lambda q: small_g.at[q])
        ga_wq = gather(lambda q: wqg.at[q])
        ga_wo = gather(lambda q: wog.at[q])
        ex_wf_p = over_square(lambda q: fc_st.at[q], lambda q: wfg.at[t_at, q])
        ex_wf_1 = over_half(lambda q: wfg.at[t_at], lambda q: wfg.at[x_at * halves + q])
        ex_wf_2 = over_x(lambda q: wfg.at[t_at], lambda q: wfg.at[q * halves + zh])
        ex_wf_3 = over_x(lambda q: wfg.at[t_far], lambda q: wfg.at[q * halves + 1 - zh])
        ex_wp_1 = over_half(lambda q: wproj_ref, lambda q: wpg.at[x_at * halves + q])
        ex_wp_2 = over_x(lambda q: wproj_ref, lambda q: wpg.at[q * halves + zh])
        ex_wp_3 = over_x(lambda q: wpg.at[t_far], lambda q: wpg.at[q * halves + 1 - zh])
        ga_go = gather_square(lambda q: gog.at[q])
        half_at = (1 - zh, zh)
        ga_kv = [
            Gather(
                xs, 1, x_at, core, x_place,
                lambda q, i=i: kvg.at[q, :, :, aligned(half_at[i], query_block)],
                send.at[take("s")], ksem.at[i],
            )
            for i in range(halves)
        ]
        ex_o = over_line(lambda q: o_st.at[q], lambda q: og.at[lax.rem(q, seqs), q // seqs])
        ga_x2 = gather_square(lambda q: x2g.at[q])
        re_gs = reduce_square(
            lambda q: gs_st.at[q], lambda r: gs_in.at[r], lambda r: gs_red.at[r], add_rows(32),
        )
        re_fd = reduce_square(
            lambda q: fd_st.at[q], lambda r: fd_in.at[r], lambda r: fd_red.at[r], add_rows(32),
        )
        ex_do = over_line(
            lambda q: do_st.at[q // seqs, lax.rem(q, seqs)], lambda q: dog.at[q]
        )
        re_kv = [
            Reduce(
                xs, 1, x_at, core, x_place,
                lambda q, n=n: kv_st.at[n, q], lambda r, n=n: kv_in.at[n, r],
                lambda r, n=n: kv_red.at[n, r],
                ssem.at[take("r")], krsem.at[n], add_blocks,
            )
            for n in range(heads)
        ]
        ex_gf = over_line(lambda q: gf_st.at[q], lambda q: gfg.at[lax.rem(q, seqs), q // seqs])
        re_wo = reduce(
            lambda q: wog.at[q], lambda r: wo_in.at[r], lambda r: wo_red.at[r], add_blocks,
        )
        ex_go_z = over_z(lambda q: woz.at[q], lambda q: wozr.at[q])
        re_wq = reduce(
            lambda q: wqg.at[q], lambda r: wq_in.at[r], lambda r: wq_red.at[r], add_blocks,
        )
        ex_gq_z = over_z(lambda q: wqz.at[q], lambda q: wqzr.at[q])
        ex_gf_1 = over_x(lambda q: wfs.at[pl.ds(q * halves, halves)], lambda q: wfr)
        ex_gf_2 = over_half(lambda q: wfm.at[q], lambda q: wfq)
        ex_gf_3 = over_square(lambda q: wfz.at[q], lambda q: wfzr.at[q])
        ex_gp_1 = over_x(lambda q: wps.at[pl.ds(q * halves, halves)], lambda q: wpr)
        ex_gp_2 = over_half(lambda q: wpm.at[q], lambda q: wpq)
        ex_ar_p = over_plane(lambda q: arg.at[q], lambda q: ard.at[q])
        ex_ar_z = over_z(lambda q: ar_st.at[q], lambda q: arz.at[q])

        coming = [
            pltpu.make_async_copy(kept, held, in_sem.at[i])
            for i, (kept, held) in enumerate(
                (
                    (gain_hbm, gain_ref), (bias_hbm, bias_ref), (bfc_hbm, bfc_ref), (wqkv_hbm, wqkv_ref),
                    (wfc_hbm, wfc_ref), (x_hbm, x_ref), (wout_hbm, wout_ref), (wproj_hbm, wproj_ref),
                    (go_hbm, go_ref),
                )
            )
        ]
        for copy in coming:
            copy.start()
        leaving = [
            pltpu.make_async_copy(held, kept, home_sem.at[i])
            for i, (held, kept) in enumerate(
                (
                    (out_ref, out_hbm), (gin_ref, gin_hbm), (gqkv_ref, gqkv_hbm), (gout_ref, gout_hbm),
                    (gfc_ref, gfc_hbm), (gproj_ref, gproj_hbm), (owned_ref, owned_hbm),
                )
            )
        ]

        def leave(i):
            leaving[i].start()

        barrier = pltpu.get_barrier_semaphore()

        def greet(place, me, n):
            def one(k):
                pl.semaphore_signal(
                    barrier, inc=1, device_id=place(lax.rem(me + k, n)),
                    device_id_type=pl.DeviceIdType.MESH,
                )

            loop(1, n, one)

        greet(slab_place, p, ps)
        greet(line_place, s, ss)
        greet(ring_place, pf, ps)

        for copy in coming:
            copy.wait()
        small[...] = jnp.zeros_like(small)
        small[0:2, 0:rows] = gain_ref[...].astype(f32)
        small[2:8, 0:rows] = bias_ref[...].astype(f32)
        small[8:9, 0:ff_rows] = bfc_ref[...].astype(f32)
        for t in range(zs):
            for k in range(3):
                qkv_st[t, :, k * tw : (k + 1) * tw] = wqkv_ref[:, k * width + t * tw : k * width + (t + 1) * tw]
        for q in range(ps):
            for b in range(zs):
                at = ff_place(q, b) * ff_rows
                fc_st[q, :, b * ff_rows : (b + 1) * ff_rows] = wfc_ref[:, at : at + ff_rows]
        small_z[z] = small[...]
        wqg[p, z] = qkv_st[z]
        wog[p, z] = wout_ref[...]
        wfg[t_at, pf] = fc_st[pf]
        wpg[t_at] = wproj_ref[...]
        xg[s] = x_ref[y]
        ar_st[...] = jnp.zeros_like(ar_st)
        len_0 = len_ref[0]
        len_1 = len_ref[1]
        len_y = jnp.where(y == 0, len_0, len_1)
        home_row = lax.broadcasted_iota(jnp.int32, (home, 1), 0)
        home_place = s * group + h * sl + lax.rem(home_row, sl)
        keep = jnp.where(home_place < jnp.where(home_row < sl, len_0, len_1), 1.0, 0.0)
        gog[pf] = (go_ref[...].reshape(home, width).astype(f32) * keep).astype(bf16)

        def mask_block(q):
            column = lax.broadcasted_iota(jnp.int32, (8, qn), 1)
            place = (column // sl) * group + q * sl + lax.rem(column, sl)
            kneg[q] = jnp.where(place < len_y, 0.0, masked_score)

        loop(0, hs, mask_block)
        pl.semaphore_wait(barrier, 2 * (ps - 1) + ss - 1)

        ex_small_z.send()
        ex_wq_z.send()
        ex_x.send()

        ex_small_z.wait()
        small_g[p] = small_z[...]
        ga_small.send()
        ex_wq_z.wait()
        ga_wq.send()
        ex_wp_2.send()
        ex_wo_z.send()
        ex_wf_p.send()
        ga_small.relay()
        ga_wq.relay()

        def d_of(q, t):
            hq = q // cores // seqs * cores + q % cores
            return hq * ss + t * seqs + q // cores % seqs

        ga_small.wait()
        prm[...] = jnp.zeros_like(prm)
        for q in range(ps):
            for t in range(zs):
                d = d_of(q, t)
                prm[0:8, d * rows : (d + 1) * rows] = small_g[q, t, 0:8, 0:rows]
                at = (d * rows) % tw
                triple = (d * rows) // tw
                prm[8 + triple : 9 + triple, at : at + rows] = small_g[q, t, 3:4, 0:rows]
                prm[8 + triple : 9 + triple, 2 * tw + at : 2 * tw + at + rows] = small_g[q, t, 4:5, 0:rows]

        up_bias[...] = jnp.zeros_like(up_bias)
        for b in range(zs):
            q = ((b // halves) * seqs + y) * cores + core
            up_bias[0:1, b * ff_rows : (b + 1) * ff_rows] = small_g[q, (b % halves) * near + zl, 8:9, 0:ff_rows]

        def assemble(src, dst):
            def one(i):
                hq = i // zs
                xq = hq // cores
                cq = lax.rem(hq, cores)
                t = lax.rem(i, zs)
                dst[aligned(i, pair), :] = jnp.concatenate(
                    [src(xq, cq, 0, t).astype(f32), src(xq, cq, 1, t).astype(f32)], axis=0
                ).astype(bf16)

            loop(0, width // pair, one)

        ga_wq.wait()
        assemble(lambda a, c, b, t: wqg[(a * seqs + b) * cores + c, t], wq)

        def first_norm(i):
            xv = xg[pl.ds(2 * i, 2)].reshape(2 * sl, width).astype(f32)
            normed, inverse = norm_parts(xv)
            return normed, (normed * prm[0:1, :] + prm[2:3, :]).astype(bf16)

        for i in range(halves):
            turn_at = half_at[i]
            for b in range(ss // halves):
                @pl.when(s != ss // halves * turn_at + b)
                def _(q=ss // halves * turn_at + b):
                    ex_x.into(q).wait_recv()

            for b in range(zs // halves):
                _, first = first_norm(zs // halves * turn_at + b)
                x2t[aligned(zs // halves * turn_at + b, 2 * sl), 0:width] = first
            at = aligned(turn_at, query_block)
            projected = nn(x2t[at, 0:width], wq[...]) + prm[pl.ds(8 + z, 1), 0 : 3 * tw]
            q_s[at, :] = (projected[:, 0:tw] * scale).astype(bf16)
            turned = projected[:, tw:].T.astype(bf16)
            kvg[h, 0, :, at] = turned[0:tw, :]
            kvg[h, 1, :, at] = turned[tw : 2 * tw, :]
            ga_kv[i].send()
        ex_wf_p.wait()
        ga_go.send()
        ex_wf_1.send()
        ex_wp_1.send()
        for i in range(halves):
            ga_kv[i].relay()
        ex_wo_z.wait()
        ga_wo.send()
        for i in range(halves):
            ga_kv[i].wait()

        lane_head = lax.broadcasted_iota(jnp.int32, (query_block, tw), 1) // HEAD_DIM

        def score(n, i):
            queries = q_s[i * query_block : (i + 1) * query_block, :]
            masked = jnp.where(lane_head == n, queries, jnp.zeros_like(queries))
            for b in range(hs):
                probs[n, i, :, b * qn : (b + 1) * qn] = nn(masked, kvg[b, 0])

        def soften(n, i, low_ref):
            for r in range(query_block // chunk):
                rat = slice(r * chunk, (r + 1) * chunk)
                sv = [probs[n, i, rat, b * qn : (b + 1) * qn] + kneg[b, 0:1, :] for b in range(hs)]
                top = jnp.max(functools.reduce(jnp.maximum, sv), axis=-1, keepdims=True)
                ev = [jnp.exp(v - top) for v in sv]
                inv = 1.0 / jnp.sum(functools.reduce(jnp.add, ev), axis=-1, keepdims=True)
                for b in range(hs):
                    value = ev[b] * inv
                    probs[n, i, rat, b * qn : (b + 1) * qn] = value
                    low_ref[rat, b * qn : (b + 1) * qn] = value.astype(bf16)

        def mix(n, i, low_ref):
            head_out = nt(low_ref[:, 0:qn], kvg[0, 1])
            for b in range(1, hs):
                head_out = head_out + nt(low_ref[:, b * qn : (b + 1) * qn], kvg[b, 1])
            at = slice(i * query_block, (i + 1) * query_block)
            o_s[at, :] = jnp.where(lane_head == n, head_out.astype(bf16), o_s[at, :])

        o_s[...] = jnp.zeros_like(o_s)
        score(0, 0)
        for n in range(heads):
            soften(n, 0, pb_scr)
            score(n, 1)
            if n:
                mix(n - 1, 1, ds_scr)
            soften(n, 1, ds_scr)
            if n < heads - 1:
                score(n + 1, 0)
            mix(n, 0, pb_scr)
            if n == 0:
                ex_wf_2.send()
            if n == 1:
                ex_wf_1.wait()
                ex_wf_3.send()
        mix(heads - 1, 1, ds_scr)

        def pack(ref, v):
            ref[0:sl, :], ref[sl:, :] = dense(v)

        def unpack(ref):
            return loose(ref[0:sl, :], ref[sl:, :])

        def lay_out(q):
            pack(o_st.at[q], o_s[aligned(q, sl), :])

        loop(0, ss, lay_out)
        ex_o.send()
        og[y, z] = o_st[s]
        ex_wp_1.wait()
        ex_wp_3.send()
        ga_wo.relay()
        ga_go.relay()

        ga_wo.wait()
        assemble(lambda a, c, b, t: wog[(a * seqs + b) * cores + c, t], wo)
        ex_o.wait()
        branch = jnp.broadcast_to(prm[5:6, :], (home, width))
        for t in range(zs):
            mixed = jnp.concatenate([unpack(og.at[a, t]) for a in range(seqs)], axis=0)
            mixed_s[t] = mixed
            branch = branch + nn(mixed, wo[t * tw : (t + 1) * tw, :])
        middle = x_ref[...].reshape(home, width).astype(f32) + branch
        normed, _ = norm_parts(middle)
        x2g[pf] = (normed * prm[1:2, :] + prm[6:7, :]).astype(bf16)
        ga_x2.send(us - 1)
        middle_s[...] = middle
        for ex in (ga_go, ex_wf_2, ex_wp_2, ex_wf_3, ex_wp_3):
            ex.wait()
        assemble(
            lambda a, c, b, t: wfg[a * halves + t // near, (lax.rem(t, near) * seqs + b) * cores + c], wf
        )

        def feed(k, running):
            r = ga_x2.peer(k)

            @pl.when(k > 0)
            def _():
                ga_x2.relay_from(k)

            ga_x2.wait_from(k)
            at = aligned(r, duo)
            chip = pl.ds(cores * r, cores)
            hid = nn(x2g[chip].reshape(duo, width), wf[...]) + up_bias[0:1, :]
            gate = 1.0 / (1.0 + jnp.exp(-quick_slope * hid))
            act[at, :] = (hid * gate).astype(bf16)
            flow = nt(gog[chip].reshape(duo, width), wpg[...].reshape(part, width))
            slope = gate + quick_slope * hid * gate * (1.0 - gate)
            back = (flow * slope).astype(bf16)
            gh[at, :] = back
            gs_st[chip] = nt(back, wf[...]).astype(bf16).reshape(cores, home, width)
            re_gs.aside(r).start()

            @pl.when(k == 0)
            def _():
                ga_x2.send_last()

            @pl.when(k > 1)
            def _():
                re_gs.combine_out(k - 1)

            return running + jnp.sum(back.astype(f32), axis=0, keepdims=True)

        grad_up = lax.fori_loop(0, us, feed, jnp.zeros((1, part), f32))

        def turn_act(q):
            at = aligned(q, home)
            x2t[0:part, at] = act[at, :].T

        loop(0, ps, turn_act)
        re_gs.combine_out(us - 1)
        re_gs.combine(u_at)

        def proj_grad(c):
            wps[pl.ds(2 * c, 2)] = nn(
                x2t[aligned(c, 2 * ff_rows), :], gog[...].reshape(slab, width)
            ).astype(bf16).reshape(2, ff_rows, width)

        loop(0, zs // 2, proj_grad)
        ex_gp_1.send()

        def feed_down(r):
            chip = pl.ds(cores * r, cores)
            fd_st[chip] = nn(act[aligned(r, duo), :], wpg[...].reshape(part, width)).astype(bf16).reshape(
                cores, home, width
            )
            re_fd.aside(r).start()

        loop(0, us, feed_down)

        def scatter_rows(c, val, put):
            for j in range(val.shape[0] // rows):
                d = c * (val.shape[0] // rows) + j
                hq = d // ss
                sd = lax.rem(d, ss)
                put(
                    hq // cores, lax.rem(hq, cores), lax.rem(sd, seqs), sd // seqs,
                    val[j * rows : (j + 1) * rows, :].astype(bf16),
                )

        def turn_in(q):
            x2t[:, aligned(q, home)] = x2g[q].T

        loop(0, ps, turn_in)

        def fc_grad(c):
            def put(a, c, b, t, value):
                wfs[a * halves + t // near, (lax.rem(t, near) * seqs + b) * cores + c] = value

            scatter_rows(c, nn(x2t[aligned(c, quad), :], gh[...]), put)

        loop(0, width // quad, fc_grad)
        ex_gf_1.send()

        for t in range(zs):
            x2t[t * tw : (t + 1) * tw, 0:home] = mixed_s[t].T
        grad_final = go_ref[...].reshape(home, width).astype(f32) * keep

        re_gs.wait()

        def landed_sum(re, own):
            total = own
            for k in range(1, us):
                total = total + re.landed(re.peer(k))[...].astype(f32)
            return total

        grad_second = landed_sum(re_gs, gs_st[pf].astype(f32))
        n2, r2 = norm_parts(middle_s[...])
        grad_middle = grad_final + norm_backward(grad_second * prm[1:2, :], n2, r2)
        grad_branch = grad_middle.astype(bf16)
        for t in range(zs):
            value = nt(grad_branch, wo[t * tw : (t + 1) * tw, :]).astype(bf16)
            for a in range(seqs):
                pack(do_st.at[t, a], value[a * sl : (a + 1) * sl, :])
        ex_do.send()
        dog[s] = do_st[z, y]
        gm_s[...] = grad_middle
        sums[...] = jnp.zeros_like(sums)
        arg[...] = jnp.zeros_like(arg)
        for q in range(ps):
            c, b, a = q % cores, q // cores % seqs, q // cores // seqs
            for i in range(zs):
                at = (a * halves + i // near) * ff_rows
                arg[q, 8 + i : 9 + i, 0:ff_rows] = jnp.where(
                    (core == c) & (y == b) & (zl == i % near), grad_up[:, at : at + ff_rows], 0.0
                )
        sums[1:2, :] = jnp.sum(grad_second * n2, axis=0, keepdims=True)
        sums[6:7, :] = jnp.sum(grad_second, axis=0, keepdims=True)
        sums[5:6, :] = jnp.sum(grad_branch.astype(f32), axis=0, keepdims=True)


        def out_grad(c):
            def put(a, c, b, t, value):
                wog[(a * seqs + b) * cores + c, t] = value

            scatter_rows(c, nn(x2t[aligned(c, quad), 0:home], gm_s[...].astype(bf16)), put)

        ga_wo.drain()
        loop(0, width // quad, out_grad)
        re_wo.send_aside()
        re_wo.send()

        ex_do.wait()
        ex_gp_1.wait()

        def proj_sum(q):
            wpm[q] = (wps[t_at - zh + q].astype(f32) + wpr[q].astype(f32)).astype(bf16)

        loop(0, halves, proj_sum)
        ex_gp_2.send()
        re_fd.send()

        def gather_do(i):
            at = aligned(i, 2 * sl)
            value = jnp.concatenate([unpack(dog.at[2 * i]), unpack(dog.at[2 * i + 1])], axis=0)
            o_s[at, :] = value
            dot_s[:, at] = value.T
            qt_s[:, at] = q_s[at, :].T

        loop(0, ss // 2, gather_do)
        dq_s[...] = jnp.zeros_like(dq_s)

        def slope_in(n, i, out_ref):
            outer = o_s[i * query_block : (i + 1) * query_block, :]
            masked = jnp.where(lane_head == n, outer, jnp.zeros_like(outer))
            for b in range(hs):
                out_ref[:, b * qn : (b + 1) * qn] = nn(masked, kvg[b, 1])

        def slopes(n, i, in_ref, slope_ref, low_ref):
            for r in range(query_block // chunk):
                rat = slice(r * chunk, (r + 1) * chunk)
                dp = [in_ref[rat, b * qn : (b + 1) * qn] for b in range(hs)]
                pv = [probs[n, i, rat, b * qn : (b + 1) * qn] for b in range(hs)]
                delta = jnp.sum(
                    functools.reduce(jnp.add, [a * c for a, c in zip(dp, pv)]), axis=-1, keepdims=True
                )
                for b in range(hs):
                    slope_ref[rat, b * qn : (b + 1) * qn] = (pv[b] * (dp[b] - delta)).astype(bf16)
                    low_ref[rat, b * qn : (b + 1) * qn] = pv[b].astype(bf16)

        def slope_out(n, i, slope_ref, low_ref):
            at = slice(i * query_block, (i + 1) * query_block)
            head_rows = slice(n * HEAD_DIM, (n + 1) * HEAD_DIM)
            head_dq = nt(slope_ref[:, 0:qn], kvg[0, 0])
            for b in range(1, hs):
                head_dq = head_dq + nt(slope_ref[:, b * qn : (b + 1) * qn], kvg[b, 0])
            dq_s[at, :] = jnp.where(
                lane_head == n, (head_dq.astype(bf16).astype(f32) * scale).astype(bf16), dq_s[at, :]
            )
            for b in range(hs):
                new_k = nn(qt_s[head_rows, at], slope_ref[:, b * qn : (b + 1) * qn])
                new_v = nn(dot_s[head_rows, at], low_ref[:, b * qn : (b + 1) * qn])
                if i == 0:
                    dkt[b] = new_k
                    dvt[b] = new_v
                else:
                    kv_st[n, b, 0] = (dkt[b] + new_k).astype(bf16)
                    kv_st[n, b, 1] = (dvt[b] + new_v).astype(bf16)

        def final_rows(re, own, landed, dst):
            def one(t):
                total = own[p, t].astype(f32)
                for k in range(1, rs):
                    total = total + landed[re.peer(k), t].astype(f32)
                dst[t] = total.astype(bf16)

            loop(0, zs, one)

        slope_in(0, 0, s_scr)
        for n in range(heads):
            slopes(n, 0, s_scr, ds_scr, pb_scr)
            slope_in(n, 1, t_scr)
            slope_out(n, 0, ds_scr, pb_scr)
            if n:
                re_kv[n - 1].send()
            slopes(n, 1, t_scr, ds_scr, pb_scr)
            if n < heads - 1:
                slope_in(n + 1, 0, s_scr)
            slope_out(n, 1, ds_scr, pb_scr)
            re_kv[n].send_aside()
            if n == heads - 1:
                re_wo.wait()
                final_rows(re_wo, wog, wo_red, woz)
                ex_go_z.send()
                wozr[z] = woz[z]
            if n == 0:
                ex_gf_1.wait()

                def fc_sum(i):
                    q, b = i // ps, lax.rem(i, ps)
                    wfm[q, b] = (wfs[t_at - zh + q, b].astype(f32) + wfr[q, b].astype(f32)).astype(bf16)

                loop(0, halves * ps, fc_sum)
                ex_gf_2.send()
        re_kv[heads - 1].send()

        gpt[0:tw, :] = dq_s[...].T

        def turn_first(i):
            _, first = first_norm(i)
            x2t[:, aligned(i, 2 * sl)] = first.T

        loop(0, zs, turn_first)

        for n in range(heads):
            re_kv[n].wait()
            for k in range(2):
                at = (1 + k) * tw + n * HEAD_DIM
                gpt[at : at + HEAD_DIM, :] = (
                    kv_st[n, h, k].astype(f32) + kv_red[n, re_kv[n].peer(1), k].astype(f32)
                ).astype(bf16)
        gp[...] = gpt[...].T

        gain_sum = jnp.zeros((1, width), f32)
        shift_sum = jnp.zeros((1, width), f32)
        block = ss // halves

        def first_grad(i):
            value = nt(gp[aligned(i, block * sl), :], wq[...])
            gf_st[pl.ds(block * i, block)] = value.astype(bf16).reshape(block, sl, width)

        first_grad(1 - zh)
        ex_gf.send(0, 1)

        def qkv_grad(c):
            def put(a, c, b, t, value):
                wqg[(a * seqs + b) * cores + c, t] = value

            scatter_rows(c, nn(x2t[aligned(c, quad), 0:qn], gp[...]), put)

        ga_wq.drain()
        loop(0, width // quad, qkv_grad)
        re_wq.send_aside()
        first_grad(zh)
        re_wq.send()
        ex_gf.send(1)
        gfg[y, z] = gf_st[s]
        ex_gf_2.wait()

        def fc_last(q):
            wfz[q] = (wfm[zh, q].astype(f32) + wfq[q].astype(f32)).astype(bf16)

        loop(0, ps, fc_last)
        ex_gf_3.send()
        wfzr[pf] = wfz[pf]
        for i in range(zs):
            value = gf_st[2 * i : 2 * i + 2].reshape(2 * sl, width).astype(f32)
            normed, _ = first_norm(i)
            gain_sum = gain_sum + jnp.sum(value * normed, axis=0, keepdims=True)
            shift_sum = shift_sum + jnp.sum(value, axis=0, keepdims=True)

        sums[0:1, :] = gain_sum
        sums[2:3, :] = shift_sum
        re_fd.wait()
        feed_out = landed_sum(re_fd, fd_st[pf].astype(f32)) + prm[7:8, :]
        final = middle_s[...] + feed_out
        out_ref[...] = (final * keep).astype(bf16).reshape(seqs, sl, width)
        leave(0)
        xv = x_ref[...].reshape(home, width).astype(f32)
        br = middle_s[...] - xv
        place = lax.broadcasted_iota(jnp.int32, (1, 128), 1)
        squares = jnp.zeros((1, 128), f32)
        for k, value in enumerate((xv, br, feed_out, final)):
            squares = squares + jnp.where(place == k, jnp.sum(keep * value * value), 0.0)
        for q in range(ps):
            arg[q, 12:13, :] = squares
        projected_sum = jnp.sum(gp[...].astype(f32), axis=0, keepdims=True)
        for i in range(zs):
            at = slice(i * tw, (i + 1) * tw)
            sums[3:4, at] = jnp.where(z == i, projected_sum[:, 0:tw], 0.0)
            sums[4:5, at] = jnp.where(z == i, projected_sum[:, 2 * tw :], 0.0)
        sums[7:8, :] = jnp.sum(gog[pf].astype(f32), axis=0, keepdims=True)

        for q in range(ps):
            for i in range(zs):
                at = d_of(q, i) * rows
                arg[q, 0:8, i * rows : (i + 1) * rows] = sums[0:8, at : at + rows]
        ex_ar_p.send()
        ard[p] = arg[p]

        ex_gp_2.wait()
        gproj_ref[...] = wpm[zh].astype(f32) + wpq[...].astype(f32)
        leave(5)

        re_wq.wait()
        final_rows(re_wq, wqg, wq_red, wqz)
        ex_gq_z.send()
        wqzr[z] = wqz[z]
        ex_ar_p.wait()
        total = functools.reduce(jnp.add, [ard[q] for q in range(ps)])
        for i in range(zs):
            ar_st[i, 0:8, 0:rows] = total[0:8, i * rows : (i + 1) * rows]
            ar_st[i, 8:9, :] = total[8 + i : 9 + i, :]
            ar_st[i, 9:10, :] = total[12:13, :]
        ex_ar_z.send()
        arz[z] = ar_st[z]
        ex_go_z.wait()
        gout_ref[...] = functools.reduce(jnp.add, [wozr[t].astype(f32) for t in range(zs)])
        leave(3)

        for ex in (
            ex_small_z, ex_wq_z, ex_wo_z, ex_x, ga_small, ex_wf_p, ex_wf_1, ex_wf_2, ex_wf_3,
            ex_wp_1, ex_wp_2, ex_wp_3,
            ga_go, *ga_kv, ex_o, re_gs, re_fd, ex_do, *re_kv, re_wo, ex_go_z, re_wq,
            ex_gf_1, ex_gf_2, ex_gf_3, ex_gp_1, ex_gp_2, ex_ar_p,
        ):
            ex.drain()
        ga_x2.drain(us - 1)

        ex_gf.wait()
        grad_first = functools.reduce(jnp.add, [gfg[:, t].astype(f32) for t in range(zs)]).reshape(home, width)
        n1, r1 = norm_parts(x_ref[...].reshape(home, width).astype(f32))
        grad_in = gm_s[...] + norm_backward(grad_first * prm[0:1, :], n1, r1)
        gin_ref[...] = grad_in.reshape(seqs, sl, width)
        leave(1)

        ex_gf_3.wait()
        for q in range(ps):
            for b in range(zs):
                at = ff_place(q, b) * ff_rows
                gfc_ref[:, at : at + ff_rows] = wfzr[q, :, b * ff_rows : (b + 1) * ff_rows].astype(f32)
        leave(4)
        ex_gq_z.wait()
        for i in range(zs):
            for k in range(3):
                at = k * width + i * tw
                gqkv_ref[:, at : at + tw] = wqzr[i, :, k * tw : (k + 1) * tw].astype(f32)
        leave(2)
        ex_ar_z.wait()
        owned = functools.reduce(jnp.add, [arz[t] for t in range(zs)])
        owned_ref[...] = owned
        leave(6)
        for ex in (ex_gf, ex_gq_z, ex_ar_z):
            ex.drain()
        for copy in leaving:
            copy.wait()

    vm = pltpu.VMEM
    scratch = [
        vm((seqs, sl, width), bf16),
        vm((seqs, sl, width), bf16),
        vm((rows, 3 * width), bf16),
        vm((rows, width), bf16),
        vm((rows, ps * part), bf16),
        vm((ff_rows, width), bf16),
        vm((1, ff_rows), bf16),
        vm((2, rows), bf16),
        vm((6, rows), bf16),
        pltpu.SemaphoreType.DMA((9,)),
        vm((seqs, sl, width), bf16),
        vm((seqs, sl, width), f32),
        vm((rows, 3 * width), f32),
        vm((rows, width), f32),
        vm((rows, ps * part), f32),
        vm((ff_rows, width), f32),
        vm((16, 128), f32),
        pltpu.SemaphoreType.DMA((7,)),
        vm((16, 128), f32),
        vm((zs, 16, 128), f32),
        vm((ps, zs, 16, 128), f32),
        vm((16, width), f32),
        vm((8, part), f32),
        vm((zs, rows, 3 * tw), bf16),
        vm((ps, rows, part), bf16),
        vm((ps, zs, rows, 3 * tw), bf16),
        vm((ps, zs, rows, width), bf16),
        vm((zs, ps, rows, part), bf16),
        vm((zs, ff_rows, width), bf16),
        vm((width, 3 * tw), bf16),
        vm((width, width), bf16),
        vm((width, part), bf16),
        vm((ss, sl, width), bf16),
        vm((qn, tw), bf16),
        vm((hs, 2, tw, qn), bf16),
        vm((hs, 8, qn), f32),
        vm((heads, blocks, query_block, hs * qn), f32),
        vm((query_block, hs * qn), f32),
        vm((query_block, hs * qn), f32),
        vm((query_block, hs * qn), bf16),
        vm((query_block, hs * qn), bf16),
        vm((qn, tw), bf16),
        vm((ss, sl * tw // lanes_per, lanes_per), bf16),
        vm((seqs, zs, sl * tw // lanes_per, lanes_per), bf16),
        vm((zs, home, tw), bf16),
        vm((home, width), f32),
        vm((home, width), f32),
        vm((ps, home, width), bf16),
        vm((ps, home, width), bf16),
        vm((slab, part), bf16),
        vm((slab, part), bf16),
        vm((width, slab), bf16),
        vm((ps, home, width), bf16),
        vm((rs, home, width), bf16),
        vm((rs, home, width), bf16),
        vm((ps, home, width), bf16),
        vm((rs, home, width), bf16),
        vm((rs, home, width), bf16),
        vm((zs, seqs, sl * tw // lanes_per, lanes_per), bf16),
        vm((ss, sl * tw // lanes_per, lanes_per), bf16),
        vm((tw, qn), bf16),
        vm((tw, qn), bf16),
        vm((qn, tw), bf16),
        vm((hs, HEAD_DIM, qn), f32),
        vm((hs, HEAD_DIM, qn), f32),
        vm((heads, hs, 2, HEAD_DIM, qn), bf16),
        vm((heads, xs, 2, HEAD_DIM, qn), bf16),
        vm((heads, xs, 2, HEAD_DIM, qn), bf16),
        vm((3 * tw, qn), bf16),
        vm((qn, 3 * tw), bf16),
        vm((ss, sl, width), bf16),
        vm((seqs, zs, sl, width), bf16),
        vm((rs, zs, rows, width), bf16),
        vm((rs, zs, rows, width), bf16),
        vm((zs, rows, width), bf16),
        vm((zs, rows, width), bf16),
        vm((rs, zs, rows, 3 * tw), bf16),
        vm((rs, zs, rows, 3 * tw), bf16),
        vm((zs, rows, 3 * tw), bf16),
        vm((zs, rows, 3 * tw), bf16),
        vm((zs, ps, rows, part), bf16),
        vm((halves, ps, rows, part), bf16),
        vm((halves, ps, rows, part), bf16),
        vm((ps, rows, part), bf16),
        vm((ps, rows, part), bf16),
        vm((ps, rows, part), bf16),
        vm((zs, ff_rows, width), bf16),
        vm((halves, ff_rows, width), bf16),
        vm((halves, ff_rows, width), bf16),
        vm((ff_rows, width), bf16),
        vm((ps, 16, 128), f32),
        vm((ps, 16, 128), f32),
        vm((8, width), f32),
        vm((zs, 16, 128), f32),
        vm((zs, 16, 128), f32),
        pltpu.SemaphoreType.DMA((33,)),
        pltpu.SemaphoreType.DMA((10, zs)),
        pltpu.SemaphoreType.DMA((4, ss)),
        pltpu.SemaphoreType.DMA((3, ps)),
        pltpu.SemaphoreType.DMA((10, 2)),
        pltpu.SemaphoreType.DMA((6, ps)),
        pltpu.SemaphoreType.DMA((7, 2, rs)),
        pltpu.SemaphoreType.DMA((zs, hs)),
        pltpu.SemaphoreType.DMA((heads, 2, xs)),
        pltpu.SemaphoreType.DMA((7, 2)),
    ]
    in_smem = pl.BlockSpec(memory_space=pltpu.SMEM)
    in_place = pl.BlockSpec(memory_space=pl.ANY)
    shapes = (
        jax.ShapeDtypeStruct((seqs, sl, width), bf16),
        jax.ShapeDtypeStruct((seqs, sl, width), f32),
        jax.ShapeDtypeStruct((rows, 3 * width), f32),
        jax.ShapeDtypeStruct((rows, width), f32),
        jax.ShapeDtypeStruct((rows, ps * part), f32),
        jax.ShapeDtypeStruct((ff_rows, width), f32),
        jax.ShapeDtypeStruct((1, ff_rows), f32),
        jax.ShapeDtypeStruct((2, rows), f32),
        jax.ShapeDtypeStruct((6, rows), f32),
        jax.ShapeDtypeStruct((1, 4), f32),
    )
    results = pl.pallas_call(
        kernel,
        out_shape=shapes[0:6] + (jax.ShapeDtypeStruct((16, 128), f32),),
        in_specs=[in_smem] + [in_place] * 9,
        out_specs=(in_place,) * 7,
        scratch_shapes=scratch,
        compiler_params=pltpu.CompilerParams(
            collective_id=0, has_side_effects=True, vmem_limit_bytes=63 * 1024 * 1024
        ),
        name="layer",
    )(
        lengths,
        layer_input.reshape(seqs, sl, width),
        grad_out.reshape(seqs, sl, width),
        w_qkv,
        w_out,
        w_fc,
        w_proj,
        b_fc.reshape(1, ff_rows),
        norm_gains,
        biases,
    )

    def finish(len_ref, *refs):
        given, kept, held, small_held = refs[0:7], refs[7:17], refs[17:24], refs[24:28]
        in_sem, out_sem = refs[28:]
        arrive = [pltpu.make_async_copy(given[i], held[i], in_sem.at[i]) for i in range(7)]
        leave = [
            pltpu.make_async_copy(ref, kept[i], out_sem.at[i])
            for i, ref in enumerate(held[0:6] + small_held)
        ]
        for i in (6, 1, 4, 5, 2, 0, 3):
            arrive[i].start()
        arrive[6].wait()
        owned = held[6]
        small_held[0][...] = owned[8:9, 0:ff_rows]
        small_held[1][...] = owned[0:2, 0:rows]
        small_held[2][...] = owned[2:8, 0:rows]
        valid = (len_ref[0] + len_ref[1]).astype(f32) * width
        small_held[3][...] = jnp.sqrt(owned[9:10, 0:4] / valid)
        for i in range(6, 10):
            leave[i].start()
        for i in (1, 4, 5, 2, 0, 3):
            arrive[i].wait()
            leave[i].start()
        for copy in leave:
            copy.wait()

    final = pl.pallas_call(
        finish,
        out_shape=shapes,
        in_specs=[in_smem] + [in_place] * 7,
        out_specs=(in_place,) * 10,
        scratch_shapes=[vm(s.shape, s.dtype) for s in shapes[0:6]]
        + [vm((16, 128), f32)]
        + [vm(s.shape, s.dtype) for s in shapes[6:]]
        + [pltpu.SemaphoreType.DMA((7,)), pltpu.SemaphoreType.DMA((10,))],
        name="finish",
    )(lengths, *results)
    return (
        final[0].reshape(layer_input.shape),
        final[1].reshape(layer_input.shape),
        *final[2:6],
        final[6].reshape(ff_rows),
        final[7],
        final[8],
        final[9].reshape(4),
    )


def fits(seqs, sl, width, hs, ss, qkv_rows):
    if seqs != 2 or ss % seqs or hs % cores:
        return False
    zs = ss // seqs
    if width % zs or (width // zs) % HEAD_DIM or zs != 4 or hs != zs or qkv_rows % 8:
        return False
    tw = width // zs
    keys = ss * sl * hs
    return tw <= 256 and keys * ss * sl * (tw // HEAD_DIM) * 4 <= 16 * 1024 * 1024


def on_device(layer_input, grad_out, lengths, w_qkv, w_out, w_fc, w_proj, b_fc, norm_gains, biases):
    seqs, _, sl, width = layer_input.shape
    hs, ss = lax.axis_size("head"), lax.axis_size("seq")
    chosen = fused_layer if fits(seqs, sl, width, hs, ss, w_qkv.shape[0]) else spread_layer
    return chosen(
        layer_input, grad_out, lengths, w_qkv, w_out, w_fc, w_proj, b_fc, norm_gains, biases
    )


def solution(mesh):
    return jax.shard_map(
        on_device,
        mesh=mesh,
        in_specs=(
            P(None, "seq", "head", None),
            P(None, "seq", "head", None),
            P(),
            P(("head", "seq"), None),
            P(("head", "seq"), None),
            P(("head", "seq"), None),
            P(("head", "seq"), None),
            P(("head", "seq")),
            P(None, ("head", "seq")),
            P(None, ("head", "seq")),
        ),
        out_specs=(
            P(None, "seq", "head", None),
            P(None, "seq", "head", None),
            P(("head", "seq"), None),
            P(("head", "seq"), None),
            P(("head", "seq"), None),
            P(("head", "seq"), None),
            P(("head", "seq")),
            P(None, ("head", "seq")),
            P(None, ("head", "seq")),
            P(),
        ),
        check_vma=False,
    )
```

```python
import functools

import jax
import jax.numpy as jnp
from jax import lax
from jax.sharding import PartitionSpec as P
from jax.experimental import pallas as pl
from jax.experimental.pallas import tpu as pltpu

HEAD_DIM = 64


masked_score = -1e30
block_keys = 512
quick_slope = 1.702
epsilon = 1e-05


def layer_norm_parts(inputs):
    centre = inputs - jnp.mean(inputs, axis=-1, keepdims=True)
    inverse = lax.rsqrt(jnp.mean(centre * centre, axis=-1, keepdims=True) + epsilon)
    return (centre * inverse, inverse)


def norm_backward(grad_normed, normed, inverse):
    return inverse * (
        grad_normed
        - jnp.mean(grad_normed, axis=-1, keepdims=True)
        - normed * jnp.mean(grad_normed * normed, axis=-1, keepdims=True)
    )


def split_heads(piece_block):
    return piece_block.reshape(
        piece_block.shape[0], piece_block.shape[1], piece_block.shape[2] // HEAD_DIM, HEAD_DIM
    )


def head_scores(left_side, right_side):
    return jnp.einsum("sqhd,skhd->shqk", left_side, right_side, preferred_element_type=jnp.float32)


def weighted(probabilities, right_side):
    return jnp.einsum(
        "shqk,skhd->sqhd", probabilities, right_side, preferred_element_type=jnp.float32
    )


def transposed(probabilities, right_side):
    return jnp.einsum(
        "shqk,sqhd->skhd", probabilities, right_side, preferred_element_type=jnp.float32
    )


def over_blocks(step_fn, running, pieces):
    extent = pieces[0].shape[1]
    number = extent // block_keys
    parted = tuple(
        (
            piece_part.reshape(
                (piece_part.shape[0], number, block_keys) + piece_part.shape[2:]
            ).swapaxes(0, 1)
            for piece_part in pieces
        )
    )

    def advance(inner_run, element):
        position, blocks = element
        return (step_fn(inner_run, blocks, position * block_keys), None)

    return lax.scan(advance, running, (jnp.arange(number, dtype=jnp.int32), parted))[0]


def spread_layer(layer_input, grad_out, lengths, w_qkv, w_out, w_fc, w_proj, b_fc, norm_gains, biases):
    sequences = layer_input.shape[0]
    slice_len = layer_input.shape[2]
    model_width = layer_input.shape[3]
    head_ways = lax.axis_size("head")
    group_len = slice_len * head_ways
    local_width = model_width // head_ways
    head_count = local_width // HEAD_DIM
    head_place = lax.axis_index("head")
    cycle_place = lax.axis_index("seq")
    flat_rows = sequences * slice_len
    full_qkv, full_out, full_fc, full_proj, full_bias_fc, full_gains, full_biases = (
        lax.all_gather(w_qkv, ("head", "seq"), axis=0, tiled=True),
        lax.all_gather(w_out, ("head", "seq"), axis=0, tiled=True),
        lax.all_gather(w_fc, ("head", "seq"), axis=0, tiled=True),
        lax.all_gather(w_proj, ("head", "seq"), axis=0, tiled=True),
        lax.all_gather(b_fc, ("head", "seq"), axis=0, tiled=True),
        lax.all_gather(norm_gains, ("head", "seq"), axis=1, tiled=True),
        lax.all_gather(biases, ("head", "seq"), axis=1, tiled=True),
    )
    gain_vals = full_gains.astype(jnp.float32)
    shift_vals = full_biases.astype(jnp.float32)
    bias_up = full_bias_fc.astype(jnp.float32)
    token_places = (
        cycle_place * group_len + head_place * slice_len + jnp.arange(slice_len, dtype=jnp.int32)
    )
    token_keep = (
        (token_places[None, :] < lengths[:, None]).astype(jnp.float32).reshape(flat_rows, 1)
    )
    own_places = cycle_place * group_len + jnp.arange(group_len, dtype=jnp.int32)
    own_allowed = (own_places[None, :] < lengths[:, None])[:, None, None, :]

    def allowed_at(offset, extent):
        places = offset + jnp.arange(extent, dtype=jnp.int32)
        return (places[None, :] < lengths[:, None])[:, None, None, :]

    inputs = layer_input.reshape(flat_rows, model_width).astype(jnp.float32)
    normed_one, inverse_one = layer_norm_parts(inputs)
    first_in = (normed_one * gain_vals[0] + shift_vals[0]).astype(jnp.bfloat16)
    projected = jnp.dot(first_in, full_qkv, preferred_element_type=jnp.float32)
    query_scale = HEAD_DIM ** (-0.5)
    queries = ((projected[:, :model_width] + shift_vals[1]) * query_scale).astype(jnp.bfloat16)
    keys_new = projected[:, model_width : 2 * model_width].astype(jnp.bfloat16)
    values_new = (projected[:, 2 * model_width :] + shift_vals[2]).astype(jnp.bfloat16)
    packed = jnp.stack([queries, keys_new, values_new], axis=1).reshape(
        sequences, slice_len, 3, head_ways, local_width
    )
    spread = lax.all_to_all(packed, "head", split_axis=3, concat_axis=1, tiled=True)
    query_block = spread[:, :, 0, 0]
    key_block = spread[:, :, 1, 0]
    value_block = spread[:, :, 2, 0]
    query_heads = split_heads(query_block)
    key_heads = split_heads(key_block)
    value_heads = split_heads(value_block)

    def maxima_step(running, pieces, offset):
        highest, denominator = running
        scores = head_scores(query_heads, split_heads(pieces[0]))
        allowed = allowed_at(offset, pieces[0].shape[1])
        scores = jnp.where(allowed, scores, masked_score)
        raised = jnp.maximum(highest, jnp.max(scores, axis=-1))
        weights = jnp.where(allowed, jnp.exp(scores - raised[..., None]), 0.0)
        denominator = denominator * jnp.exp(highest - raised) + jnp.sum(weights, axis=-1)
        return (raised, denominator)

    zero_rows = jnp.zeros((sequences, head_count, group_len), jnp.float32)
    highest, denominator = over_blocks(
        maxima_step,
        (zero_rows + masked_score, zero_rows),
        (lax.all_gather(key_block, "seq", axis=1, tiled=True),),
    )
    log_total = highest + jnp.log(denominator)

    def attention_weights(key_piece, offset):
        scores = head_scores(query_heads, key_piece)
        allowed = allowed_at(offset, key_piece.shape[1])
        return jnp.where(
            allowed, jnp.exp(jnp.where(allowed, scores, masked_score) - log_total[..., None]), 0.0
        )

    zero_heads = jnp.zeros((sequences, group_len, head_count, HEAD_DIM), jnp.float32)

    def output_step(running, pieces, offset):
        probabilities = attention_weights(split_heads(pieces[0]), offset)
        return running + weighted(probabilities.astype(jnp.bfloat16), split_heads(pieces[1]))

    attended = over_blocks(
        output_step,
        zero_heads,
        (
            lax.all_gather(key_block, "seq", axis=1, tiled=True),
            lax.all_gather(value_block, "seq", axis=1, tiled=True),
        ),
    )
    mixed_heads = attended.astype(jnp.bfloat16).reshape(
        sequences, head_ways, slice_len, local_width
    )
    gathered_out = lax.all_to_all(mixed_heads, "head", split_axis=1, concat_axis=3, tiled=True)
    mixed_rows = gathered_out.reshape(flat_rows, model_width)
    branch = jnp.dot(mixed_rows, full_out, preferred_element_type=jnp.float32) + shift_vals[3]
    middle = inputs + branch
    normed_two, inverse_two = layer_norm_parts(middle)
    second_in = (normed_two * gain_vals[1] + shift_vals[4]).astype(jnp.bfloat16)
    hidden = jnp.dot(second_in, full_fc, preferred_element_type=jnp.float32) + bias_up
    gate_sig = jax.nn.sigmoid(quick_slope * hidden)
    activated = (hidden * gate_sig).astype(jnp.bfloat16)
    feed_out = jnp.dot(activated, full_proj, preferred_element_type=jnp.float32) + shift_vals[5]
    final_rows = middle + feed_out
    result = (final_rows * token_keep).astype(jnp.bfloat16).reshape(layer_input.shape)
    local_squares = jnp.stack(
        [
            jnp.sum(token_keep * inputs * inputs),
            jnp.sum(token_keep * branch * branch),
            jnp.sum(token_keep * feed_out * feed_out),
            jnp.sum(token_keep * final_rows * final_rows),
        ]
    )
    squares = lax.psum(local_squares, ("head", "seq"))
    valid_count = jnp.sum(lengths).astype(jnp.float32) * model_width
    root_means = jnp.sqrt(squares / valid_count)
    grad_final = grad_out.reshape(flat_rows, model_width).astype(jnp.float32) * token_keep
    grad_feed = grad_final.astype(jnp.bfloat16)
    grad_proj = jnp.dot(activated.T, grad_feed, preferred_element_type=jnp.float32)
    grad_shift_proj = jnp.sum(grad_feed.astype(jnp.float32), axis=0)
    grad_act = jnp.dot(grad_feed, full_proj.T, preferred_element_type=jnp.float32)
    grad_hidden = (
        grad_act * (gate_sig + quick_slope * hidden * gate_sig * (1.0 - gate_sig))
    ).astype(jnp.bfloat16)
    grad_fc = jnp.dot(second_in.T, grad_hidden, preferred_element_type=jnp.float32)
    grad_bias_up = jnp.sum(grad_hidden.astype(jnp.float32), axis=0)
    grad_second = jnp.dot(grad_hidden, full_fc.T, preferred_element_type=jnp.float32)
    grad_gain_two = jnp.sum(grad_second * normed_two, axis=0)
    grad_shift_two = jnp.sum(grad_second, axis=0)
    grad_middle = grad_final + norm_backward(grad_second * gain_vals[1], normed_two, inverse_two)
    grad_branch = grad_middle.astype(jnp.bfloat16)
    grad_out_weight = jnp.dot(mixed_rows.T, grad_branch, preferred_element_type=jnp.float32)
    grad_shift_out = jnp.sum(grad_branch.astype(jnp.float32), axis=0)
    grad_mixed = jnp.dot(grad_branch, full_out.T, preferred_element_type=jnp.float32).astype(
        jnp.bfloat16
    )
    grad_spread = lax.all_to_all(
        grad_mixed.reshape(sequences, slice_len, head_ways, local_width),
        "head",
        split_axis=2,
        concat_axis=1,
        tiled=True,
    )
    grad_block = grad_spread[:, :, 0]
    grad_heads = split_heads(grad_block)

    def delta_step(running, pieces, offset):
        probabilities = attention_weights(split_heads(pieces[0]), offset)
        grad_probs = head_scores(grad_heads, split_heads(pieces[1]))
        return running + jnp.sum(probabilities * grad_probs, axis=-1)

    row_delta = over_blocks(
        delta_step,
        zero_rows,
        (
            lax.all_gather(key_block, "seq", axis=1, tiled=True),
            lax.all_gather(value_block, "seq", axis=1, tiled=True),
        ),
    )

    def query_step(running, pieces, offset):
        key_piece = split_heads(pieces[0])
        probabilities = attention_weights(key_piece, offset)
        grad_probs = head_scores(grad_heads, split_heads(pieces[1]))
        slopes = (probabilities * (grad_probs - row_delta[..., None])).astype(jnp.bfloat16)
        return running + weighted(slopes, key_piece)

    grad_query = over_blocks(
        query_step,
        zero_heads,
        (
            lax.all_gather(key_block, "seq", axis=1, tiled=True),
            lax.all_gather(value_block, "seq", axis=1, tiled=True),
        ),
    )
    all_logs, all_deltas = (
        lax.all_gather(log_total.transpose(0, 2, 1), "seq", axis=1, tiled=True),
        lax.all_gather(row_delta.transpose(0, 2, 1), "seq", axis=1, tiled=True),
    )

    def key_step(running, pieces, offset):
        query_piece = split_heads(pieces[0])
        grad_piece = split_heads(pieces[1])
        extent = pieces[0].shape[1]
        log_piece = lax.dynamic_slice_in_dim(all_logs, offset, extent, 1).transpose(0, 2, 1)
        delta_piece = lax.dynamic_slice_in_dim(all_deltas, offset, extent, 1).transpose(0, 2, 1)
        scores = head_scores(query_piece, key_heads)
        probabilities = jnp.where(
            own_allowed,
            jnp.exp(jnp.where(own_allowed, scores, masked_score) - log_piece[..., None]),
            0.0,
        )
        grad_value = running[1] + transposed(probabilities.astype(jnp.bfloat16), grad_piece)
        grad_probs = head_scores(grad_piece, value_heads)
        slopes = (probabilities * (grad_probs - delta_piece[..., None])).astype(jnp.bfloat16)
        grad_key = running[0] + transposed(slopes, query_piece)
        return (grad_key, grad_value)

    grad_key, grad_value = over_blocks(
        key_step,
        (zero_heads, zero_heads),
        (
            lax.all_gather(query_block, "seq", axis=1, tiled=True),
            lax.all_gather(grad_block, "seq", axis=1, tiled=True),
        ),
    )
    stacked = jnp.stack([grad_query, grad_key, grad_value], axis=2).astype(jnp.bfloat16)
    stacked = stacked.reshape(sequences, head_ways, slice_len, 3, local_width)
    returned = lax.all_to_all(stacked, "head", split_axis=1, concat_axis=4, tiled=True)
    column_scale = jnp.concatenate(
        [
            jnp.full((model_width,), query_scale, jnp.float32),
            jnp.ones((2 * model_width,), jnp.float32),
        ]
    )
    grad_projected = returned.reshape(flat_rows, 3 * model_width).astype(jnp.float32) * column_scale
    grad_shift_query = jnp.sum(grad_projected[:, :model_width], axis=0)
    grad_shift_value = jnp.sum(grad_projected[:, 2 * model_width :], axis=0)
    grad_projected_low = grad_projected.astype(jnp.bfloat16)
    grad_qkv = jnp.dot(first_in.T, grad_projected_low, preferred_element_type=jnp.float32)
    grad_first = jnp.dot(grad_projected_low, full_qkv.T, preferred_element_type=jnp.float32)
    grad_gain_one = jnp.sum(grad_first * normed_one, axis=0)
    grad_shift_one = jnp.sum(grad_first, axis=0)
    grad_inputs = grad_middle + norm_backward(grad_first * gain_vals[0], normed_one, inverse_one)
    grad_gain_rows = jnp.stack([grad_gain_one, grad_gain_two])
    grad_shift_rows = jnp.stack(
        [
            grad_shift_one,
            grad_shift_query,
            grad_shift_value,
            grad_shift_out,
            grad_shift_two,
            grad_shift_proj,
        ]
    )
    owned_grads = (
        lax.psum_scatter(grad_qkv, ("head", "seq"), scatter_dimension=0, tiled=True),
        lax.psum_scatter(grad_out_weight, ("head", "seq"), scatter_dimension=0, tiled=True),
        lax.psum_scatter(grad_fc, ("head", "seq"), scatter_dimension=0, tiled=True),
        lax.psum_scatter(grad_proj, ("head", "seq"), scatter_dimension=0, tiled=True),
        lax.psum_scatter(grad_bias_up, ("head", "seq"), scatter_dimension=0, tiled=True),
        lax.psum_scatter(grad_gain_rows, ("head", "seq"), scatter_dimension=1, tiled=True),
        lax.psum_scatter(grad_shift_rows, ("head", "seq"), scatter_dimension=1, tiled=True),
    )
    return (
        result,
        grad_inputs.reshape(layer_input.shape),
        owned_grads[0],
        owned_grads[1],
        owned_grads[2],
        owned_grads[3],
        owned_grads[4],
        owned_grads[5],
        owned_grads[6],
        root_means,
    )


f32 = jnp.float32
bf16 = jnp.bfloat16
cores = 2
halves = 2
lanes_per = 128


def nn(left, right):
    return lax.dot_general(left, right, (((1,), (0,)), ((), ())), preferred_element_type=f32)


def nt(left, right):
    return lax.dot_general(left, right, (((1,), (1,)), ((), ())), preferred_element_type=f32)


def loop(low, high, step_fn, unroll=1):
    def advance(index, carry):
        step_fn(index)
        return carry

    lax.fori_loop(low, high, advance, 0, unroll=unroll)


def aligned(index, extent):
    return pl.ds(pl.multiple_of(index * extent, extent), extent)


def norm_parts(v):
    centre = v - jnp.mean(v, axis=-1, keepdims=True)
    inverse = lax.rsqrt(jnp.mean(centre * centre, axis=-1, keepdims=True) + epsilon)
    return centre * inverse, inverse


def remote(src, dst, send_sem, recv_sem, place):
    return pltpu.make_async_remote_copy(
        src_ref=src,
        dst_ref=dst,
        send_sem=send_sem,
        recv_sem=recv_sem,
        device_id=place,
        device_id_type=pl.DeviceIdType.MESH,
    )


def dense(v):
    n = v.shape[0]
    low = v[:, 0:lanes_per]
    rest = v[:, lanes_per:]
    return low, jnp.concatenate([rest[0 : n // 2], rest[n // 2 :]], axis=1)


def loose(low, rest):
    wide = rest.shape[1] // 2
    return jnp.concatenate(
        [low, jnp.concatenate([rest[:, 0:wide], rest[:, wide:]], axis=0)], axis=1
    )


class Exchange:
    def __init__(self, n, me, place, src, dst, send_sem, recv_sem, order=None):
        self.n, self.me, self.place, self.src, self.dst = n, me, place, src, dst
        self.send_sem, self.recv_sem, self.order = send_sem, recv_sem, order

    def out(self, q):
        return remote(
            self.src(q), self.dst(self.me), self.send_sem, self.recv_sem.at[self.me], self.place(q)
        )

    def into(self, q):
        return remote(
            self.dst(q), self.dst(q), self.send_sem, self.recv_sem.at[q], self.place(q)
        )

    def peer(self, k):
        return lax.rem(self.me + k, self.n)

    def send(self, low=0, high=None):
        if self.order is None:
            loop(1, self.n, lambda k: self.out(self.peer(k)).start())
        else:
            for q in self.order[low:high]:
                self.out(q).start()

    def wait(self):
        loop(1, self.n, lambda k: self.into(self.peer(k)).wait_recv())

    def drain(self):
        loop(1, self.n, lambda k: self.out(self.peer(k)).wait_send())


def chip_peer(n, inner, me, k):
    outer = n // inner
    a = lax.rem(me // inner + lax.rem(k, outer), outer)
    b = lax.rem(lax.rem(me, inner) + k // outer, inner)
    return a * inner + b


class Gather:
    def __init__(self, n, inner, me, core, place, dst, send_sem, recv_sem):
        self.n, self.inner, self.me, self.core, self.place, self.dst = n, inner, me, core, place, dst
        self.send_sem, self.recv_sem = send_sem, recv_sem
        self.mine = me * cores + core

    def peer(self, k):
        return chip_peer(self.n, self.inner, self.me, k)

    def move(self, slot, place):
        return remote(
            self.dst(slot), self.dst(slot), self.send_sem, self.recv_sem.at[slot], place
        )

    def out(self, k):
        return self.move(self.mine, self.place(self.peer(k), self.core))

    def aside(self, k):
        return self.move(
            self.peer(k) * cores + self.core, self.place(self.me, 1 - self.core)
        )

    def send(self, last=None):
        loop(1, last or self.n, lambda k: self.out(k).start())
        self.aside(0).start()

    def send_last(self):
        loop(1, self.n - 1, lambda k: self.out(k).wait_send())
        self.out(self.n - 1).start()

    def relay_from(self, k):
        self.out_slot(k, self.core).wait_recv()
        self.aside(k).start()

    def out_slot(self, k, core):
        return self.move(self.peer(k) * cores + core, self.place(self.peer(k), core))

    def wait_from(self, k):
        self.out_slot(k, 1 - self.core).wait_recv()

    def relay(self):
        loop(1, self.n, self.relay_from)

    def wait(self):
        loop(0, self.n, self.wait_from)

    def drain(self, first=1):
        loop(first, self.n, lambda k: self.out(k).wait_send())
        loop(0, self.n, lambda k: self.aside(k).wait_send())


class Reduce:
    def __init__(self, n, inner, me, core, place, stage, beside, landed, sems, recv_sems, add):
        self.n, self.inner, self.me, self.core, self.place = n, inner, me, core, place
        self.stage, self.beside, self.landed = stage, beside, landed
        self.sems, self.recv_sems, self.add = sems, recv_sems, add

    def peer(self, k):
        return chip_peer(self.n, self.inner, self.me, k)

    def own(self, r):
        return self.stage(r * cores + self.core)

    def aside(self, r):
        return remote(
            self.stage(r * cores + 1 - self.core),
            self.beside(r),
            self.sems.at[0],
            self.recv_sems.at[0, r],
            self.place(self.me, 1 - self.core),
        )

    def out(self, r):
        return remote(
            self.own(r),
            self.landed(self.me),
            self.sems.at[1],
            self.recv_sems.at[1, self.me],
            self.place(r, self.core),
        )

    def combine(self, r):
        self.aside(r).wait_recv()
        self.add(self.own(r), self.beside(r))

    def combine_out(self, k):
        r = self.peer(k)
        self.combine(r)
        self.out(r).start()

    def send_aside(self):
        loop(1, self.n, lambda k: self.aside(self.peer(k)).start())
        self.aside(self.me).start()

    def send(self):
        loop(1, self.n, self.combine_out)
        self.combine(self.me)

    def wait(self):
        def one(k):
            r = self.peer(k)
            remote(
                self.landed(r), self.landed(r), self.sems.at[1], self.recv_sems.at[1, r],
                self.place(r, self.core),
            ).wait_recv()

        loop(1, self.n, one)

    def drain_aside(self):
        loop(0, self.n, lambda k: self.aside(self.peer(k)).wait_send())

    def drain(self):
        self.drain_aside()
        loop(1, self.n, lambda k: self.out(self.peer(k)).wait_send())


def fused_layer(layer_input, grad_out, lengths, w_qkv, w_out, w_fc, w_proj, b_fc, norm_gains, biases):
    seqs, _, sl, width = layer_input.shape
    hs = lax.axis_size("head")
    ss = lax.axis_size("seq")
    zs = ss // seqs
    ps = hs * seqs
    xs = hs // cores
    rs = xs * seqs
    group = sl * hs
    tw = width // zs
    heads = tw // HEAD_DIM
    rows = w_qkv.shape[0]
    ff_rows = w_proj.shape[0]
    part = ff_rows * zs
    home = seqs * sl
    qn = ss * sl
    slab = ps * home
    near = zs // halves
    us = near * seqs
    duo = cores * home
    query_block = 256
    blocks = qn // query_block
    chunk = 32
    pair = 2 * rows
    quad = 8 * rows
    scale = HEAD_DIM ** (-0.5)

    def ff_place(q, b):
        u, c = q // cores, q % cores
        head_of = (b // halves) * cores + c
        return head_of * ss + ((b % halves) * near + u // seqs) * seqs + u % seqs

    def kernel(
        len_ref, x_hbm, go_hbm, wqkv_hbm, wout_hbm, wfc_hbm, wproj_hbm, bfc_hbm, gain_hbm, bias_hbm,
        out_hbm, gin_hbm, gqkv_hbm, gout_hbm, gfc_hbm, gproj_hbm, owned_hbm,
        x_ref, go_ref, wqkv_ref, wout_ref, wfc_ref, wproj_ref, bfc_ref, gain_ref, bias_ref, in_sem,
        out_ref, gin_ref, gqkv_ref, gout_ref, gfc_ref, gproj_ref, owned_ref, home_sem,
        small, small_z, small_g, prm, up_bias,
        qkv_st, fc_st, wqg, wog, wfg, wpg, wq, wo, wf,
        xg, q_s, kvg, kneg, probs, s_scr, t_scr, pb_scr, ds_scr, o_s, o_st, og, mixed_s,
        middle_s, gm_s,
        x2g, gog, act, gh, x2t, gs_st, gs_in, gs_red, fd_st, fd_in, fd_red,
        do_st, dog, dot_s, qt_s, dq_s, dkt, dvt, kv_st, kv_in, kv_red, gpt, gp,
        gf_st, gfg, wo_in, wo_red, woz, wozr, wq_in, wq_red, wqz, wqzr,
        wfs, wfr, wfm, wfq, wfz, wfzr, wps, wpr, wpm, wpq, arg, ard, sums, ar_st, arz,
        send, zsem, lsem, psem, bsem, gsem, rsem, ksem, krsem, ssem,
    ):
        h = lax.axis_index("head")
        s = lax.axis_index("seq")
        z = s // seqs
        y = lax.rem(s, seqs)
        core = lax.rem(h, cores)
        r_at = (h // cores) * seqs + y
        x_at = h // cores
        p = r_at * cores + core
        zh = z // near
        zl = lax.rem(z, near)
        u_at = zl * seqs + y
        pf = u_at * cores + core
        t_at = x_at * halves + zh
        t_far = x_at * halves + 1 - zh

        def chip_place(r, c):
            return ((r // seqs) * cores + c, z * seqs + lax.rem(r, seqs))

        def slab_place(q):
            return chip_place(q // cores, lax.rem(q, cores))

        def square_place(u, c):
            return (x_at * cores + c, (zh * near + u // seqs) * seqs + lax.rem(u, seqs))

        def ring_place(q):
            return square_place(q // cores, lax.rem(q, cores))

        def half_place(q):
            return (h, (q * near + zl) * seqs + y)

        def beside_place(q):
            return (q * cores + core, s)

        def line_place(q):
            return (h, q)

        def z_place(q):
            return (h, q * seqs + y)

        def x_place(r, c):
            return (r * cores + c, s)

        count = {}

        def take(name):
            number = count.get(name, 0)
            count[name] = number + 1
            return number

        z_order = [(1 - zh) * (zs - 1), near - zh, zh * zs + 1 - z]
        line_order = [q * seqs + b for q in z_order for b in range(seqs)] + [z * seqs + 1 - y]

        def over_z(src, dst):
            return Exchange(
                zs, z, z_place, src, dst, send.at[take("s")], zsem.at[take("z")], z_order
            )

        def over_line(src, dst):
            return Exchange(
                ss, s, line_place, src, dst, send.at[take("s")], lsem.at[take("l")], line_order
            )

        def over_plane(src, dst):
            return Exchange(ps, p, slab_place, src, dst, send.at[take("s")], psem.at[take("p")])

        def over_square(src, dst):
            return Exchange(ps, pf, ring_place, src, dst, send.at[take("s")], psem.at[take("p")])

        def over_half(src, dst):
            return Exchange(halves, zh, half_place, src, dst, send.at[take("s")], bsem.at[take("b")])

        def over_x(src, dst):
            return Exchange(xs, x_at, beside_place, src, dst, send.at[take("s")], bsem.at[take("b")])

        def gather(dst):
            return Gather(rs, seqs, r_at, core, chip_place, dst, send.at[take("s")], gsem.at[take("g")])

        def gather_square(dst):
            return Gather(us, seqs, u_at, core, square_place, dst, send.at[take("s")], gsem.at[take("g")])

        def add_rows(block):
            def add(a, b):
                extent = a.shape[0]

                def one(i):
                    at = aligned(i, block)
                    a[at, :] = (a[at, :].astype(f32) + b[at, :].astype(f32)).astype(bf16)

                loop(0, extent // block, one)

            return add

        def add_blocks(a, b):
            def one(i):
                a[i] = (a[i].astype(f32) + b[i].astype(f32)).astype(bf16)

            loop(0, a.shape[0], one)

        def reduce(stage, beside, landed, add):
            number = take("r")
            return Reduce(
                rs, seqs, r_at, core, chip_place, stage, beside, landed, ssem.at[number],
                rsem.at[number], add,
            )

        def reduce_square(stage, beside, landed, add):
            number = take("r")
            return Reduce(
                us, seqs, u_at, core, square_place, stage, beside, landed, ssem.at[number],
                rsem.at[number], add,
            )

        ex_small_z = over_z(lambda q: small, lambda q: small_z.at[q])
        ex_wq_z = over_z(lambda q: qkv_st.at[q], lambda q: wqg.at[p, q])
        ex_wo_z = over_z(lambda q: wout_ref, lambda q: wog.at[p, q])
        ex_x = over_line(lambda q: x_ref.at[lax.rem(q, seqs)], lambda q: xg.at[q])
        ex_x.order = [lax.rem(s + k, ss) for k in range(1, ss)]
        ga_small = gather(lambda q: small_g.at[q])
        ga_wq = gather(lambda q: wqg.at[q])
        ga_wo = gather(lambda q: wog.at[q])
        ex_wf_p = over_square(lambda q: fc_st.at[q], lambda q: wfg.at[t_at, q])
        ex_wf_1 = over_half(lambda q: wfg.at[t_at], lambda q: wfg.at[x_at * halves + q])
        ex_wf_2 = over_x(lambda q: wfg.at[t_at], lambda q: wfg.at[q * halves + zh])
        ex_wf_3 = over_x(lambda q: wfg.at[t_far], lambda q: wfg.at[q * halves + 1 - zh])
        ex_wp_1 = over_half(lambda q: wproj_ref, lambda q: wpg.at[x_at * halves + q])
        ex_wp_2 = over_x(lambda q: wproj_ref, lambda q: wpg.at[q * halves + zh])
        ex_wp_3 = over_x(lambda q: wpg.at[t_far], lambda q: wpg.at[q * halves + 1 - zh])
        ga_go = gather_square(lambda q: gog.at[q])
        half_at = (1 - zh, zh)
        ga_kv = [
            Gather(
                xs, 1, x_at, core, x_place,
                lambda q, i=i: kvg.at[q, :, :, aligned(half_at[i], query_block)],
                send.at[take("s")], ksem.at[i],
            )
            for i in range(halves)
        ]
        ex_o = over_line(lambda q: o_st.at[q], lambda q: og.at[lax.rem(q, seqs), q // seqs])
        ga_x2 = gather_square(lambda q: x2g.at[q])
        re_gs = reduce_square(
            lambda q: gs_st.at[q], lambda r: gs_in.at[r], lambda r: gs_red.at[r], add_rows(32),
        )
        re_fd = reduce_square(
            lambda q: fd_st.at[q], lambda r: fd_in.at[r], lambda r: fd_red.at[r], add_rows(32),
        )
        ex_do = over_line(
            lambda q: do_st.at[q // seqs, lax.rem(q, seqs)], lambda q: dog.at[q]
        )
        re_kv = [
            Reduce(
                xs, 1, x_at, core, x_place,
                lambda q, n=n: kv_st.at[n, q], lambda r, n=n: kv_in.at[n, r],
                lambda r, n=n: kv_red.at[n, r],
                ssem.at[take("r")], krsem.at[n], add_blocks,
            )
            for n in range(heads)
        ]
        ex_gf = over_line(lambda q: gf_st.at[q], lambda q: gfg.at[lax.rem(q, seqs), q // seqs])
        re_wo = reduce(
            lambda q: wog.at[q], lambda r: wo_in.at[r], lambda r: wo_red.at[r], add_blocks,
        )
        ex_go_z = over_z(lambda q: woz.at[q], lambda q: wozr.at[q])
        re_wq = reduce(
            lambda q: wqg.at[q], lambda r: wq_in.at[r], lambda r: wq_red.at[r], add_blocks,
        )
        ex_gq_z = over_z(lambda q: wqz.at[q], lambda q: wqzr.at[q])
        ex_gf_1 = over_x(lambda q: wfs.at[pl.ds(q * halves, halves)], lambda q: wfr)
        ex_gf_2 = over_half(lambda q: wfm.at[q], lambda q: wfq)
        ex_gf_3 = over_square(lambda q: wfz.at[q], lambda q: wfzr.at[q])
        ex_gp_1 = over_x(lambda q: wps.at[pl.ds(q * halves, halves)], lambda q: wpr)
        ex_gp_2 = over_half(lambda q: wpm.at[q], lambda q: wpq)
        ex_ar_p = over_plane(lambda q: arg.at[q], lambda q: ard.at[q])
        ex_ar_z = over_z(lambda q: ar_st.at[q], lambda q: arz.at[q])

        coming = [
            pltpu.make_async_copy(kept, held, in_sem.at[i])
            for i, (kept, held) in enumerate(
                (
                    (gain_hbm, gain_ref), (bias_hbm, bias_ref), (bfc_hbm, bfc_ref), (wqkv_hbm, wqkv_ref),
                    (wfc_hbm, wfc_ref), (x_hbm, x_ref), (wout_hbm, wout_ref), (wproj_hbm, wproj_ref),
                    (go_hbm, go_ref),
                )
            )
        ]
        for copy in coming:
            copy.start()
        leaving = [
            pltpu.make_async_copy(held, kept, home_sem.at[i])
            for i, (held, kept) in enumerate(
                (
                    (out_ref, out_hbm), (gin_ref, gin_hbm), (gqkv_ref, gqkv_hbm), (gout_ref, gout_hbm),
                    (gfc_ref, gfc_hbm), (gproj_ref, gproj_hbm), (owned_ref, owned_hbm),
                )
            )
        ]

        def leave(i):
            leaving[i].start()

        barrier = pltpu.get_barrier_semaphore()

        def greet(place, me, n):
            def one(k):
                pl.semaphore_signal(
                    barrier, inc=1, device_id=place(lax.rem(me + k, n)),
                    device_id_type=pl.DeviceIdType.MESH,
                )

            loop(1, n, one)

        greet(slab_place, p, ps)
        greet(line_place, s, ss)
        greet(ring_place, pf, ps)

        for copy in coming:
            copy.wait()
        small[...] = jnp.zeros_like(small)
        small[0:2, 0:rows] = gain_ref[...].astype(f32)
        small[2:8, 0:rows] = bias_ref[...].astype(f32)
        small[8:9, 0:ff_rows] = bfc_ref[...].astype(f32)
        for t in range(zs):
            for k in range(3):
                qkv_st[t, :, k * tw : (k + 1) * tw] = wqkv_ref[:, k * width + t * tw : k * width + (t + 1) * tw]
        for q in range(ps):
            for b in range(zs):
                at = ff_place(q, b) * ff_rows
                fc_st[q, :, b * ff_rows : (b + 1) * ff_rows] = wfc_ref[:, at : at + ff_rows]
        small_z[z] = small[...]
        wqg[p, z] = qkv_st[z]
        wog[p, z] = wout_ref[...]
        wfg[t_at, pf] = fc_st[pf]
        wpg[t_at] = wproj_ref[...]
        xg[s] = x_ref[y]
        ar_st[...] = jnp.zeros_like(ar_st)
        len_0 = len_ref[0]
        len_1 = len_ref[1]
        len_y = jnp.where(y == 0, len_0, len_1)
        home_row = lax.broadcasted_iota(jnp.int32, (home, 1), 0)
        home_place = s * group + h * sl + lax.rem(home_row, sl)
        keep = jnp.where(home_place < jnp.where(home_row < sl, len_0, len_1), 1.0, 0.0)
        gog[pf] = (go_ref[...].reshape(home, width).astype(f32) * keep).astype(bf16)

        def mask_block(q):
            column = lax.broadcasted_iota(jnp.int32, (8, qn), 1)
            place = (column // sl) * group + q * sl + lax.rem(column, sl)
            kneg[q] = jnp.where(place < len_y, 0.0, masked_score)

        loop(0, hs, mask_block)
        pl.semaphore_wait(barrier, 2 * (ps - 1) + ss - 1)

        ex_small_z.send()
        ex_wq_z.send()
        ex_x.send()

        ex_small_z.wait()
        small_g[p] = small_z[...]
        ga_small.send()
        ex_wq_z.wait()
        ga_wq.send()
        ex_wp_2.send()
        ex_wo_z.send()
        ex_wf_p.send()
        ga_small.relay()
        ga_wq.relay()

        def d_of(q, t):
            hq = q // cores // seqs * cores + q % cores
            return hq * ss + t * seqs + q // cores % seqs

        ga_small.wait()
        prm[...] = jnp.zeros_like(prm)
        for q in range(ps):
            for t in range(zs):
                d = d_of(q, t)
                prm[0:8, d * rows : (d + 1) * rows] = small_g[q, t, 0:8, 0:rows]
                at = (d * rows) % tw
                triple = (d * rows) // tw
                prm[8 + triple : 9 + triple, at : at + rows] = small_g[q, t, 3:4, 0:rows]
                prm[8 + triple : 9 + triple, 2 * tw + at : 2 * tw + at + rows] = small_g[q, t, 4:5, 0:rows]

        up_bias[...] = jnp.zeros_like(up_bias)
        for b in range(zs):
            q = ((b // halves) * seqs + y) * cores + core
            up_bias[0:1, b * ff_rows : (b + 1) * ff_rows] = small_g[q, (b % halves) * near + zl, 8:9, 0:ff_rows]

        def assemble(src, dst):
            def one(i):
                hq = i // zs
                xq = hq // cores
                cq = lax.rem(hq, cores)
                t = lax.rem(i, zs)
                dst[aligned(i, pair), :] = jnp.concatenate(
                    [src(xq, cq, 0, t).astype(f32), src(xq, cq, 1, t).astype(f32)], axis=0
                ).astype(bf16)

            loop(0, width // pair, one)

        ga_wq.wait()
        assemble(lambda a, c, b, t: wqg[(a * seqs + b) * cores + c, t], wq)

        def first_norm(i):
            xv = xg[pl.ds(2 * i, 2)].reshape(2 * sl, width).astype(f32)
            normed, inverse = norm_parts(xv)
            return normed, (normed * prm[0:1, :] + prm[2:3, :]).astype(bf16)

        for i in range(halves):
            turn_at = half_at[i]
            for b in range(ss // halves):
                @pl.when(s != ss // halves * turn_at + b)
                def _(q=ss // halves * turn_at + b):
                    ex_x.into(q).wait_recv()

            for b in range(zs // halves):
                _, first = first_norm(zs // halves * turn_at + b)
                x2t[aligned(zs // halves * turn_at + b, 2 * sl), 0:width] = first
            at = aligned(turn_at, query_block)
            projected = nn(x2t[at, 0:width], wq[...]) + prm[pl.ds(8 + z, 1), 0 : 3 * tw]
            q_s[at, :] = (projected[:, 0:tw] * scale).astype(bf16)
            turned = projected[:, tw:].T.astype(bf16)
            kvg[h, 0, :, at] = turned[0:tw, :]
            kvg[h, 1, :, at] = turned[tw : 2 * tw, :]
            ga_kv[i].send()
        ex_wf_p.wait()
        ga_go.send()
        ex_wf_1.send()
        ex_wp_1.send()
        for i in range(halves):
            ga_kv[i].relay()
        ex_wo_z.wait()
        ga_wo.send()
        for i in range(halves):
            ga_kv[i].wait()

        lane_head = lax.broadcasted_iota(jnp.int32, (query_block, tw), 1) // HEAD_DIM

        def score(n, i):
            queries = q_s[i * query_block : (i + 1) * query_block, :]
            masked = jnp.where(lane_head == n, queries, jnp.zeros_like(queries))
            for b in range(hs):
                probs[n, i, :, b * qn : (b + 1) * qn] = nn(masked, kvg[b, 0])

        def soften(n, i, low_ref):
            for r in range(query_block // chunk):
                rat = slice(r * chunk, (r + 1) * chunk)
                sv = [probs[n, i, rat, b * qn : (b + 1) * qn] + kneg[b, 0:1, :] for b in range(hs)]
                top = jnp.max(functools.reduce(jnp.maximum, sv), axis=-1, keepdims=True)
                ev = [jnp.exp(v - top) for v in sv]
                inv = 1.0 / jnp.sum(functools.reduce(jnp.add, ev), axis=-1, keepdims=True)
                for b in range(hs):
                    value = ev[b] * inv
                    probs[n, i, rat, b * qn : (b + 1) * qn] = value
                    low_ref[rat, b * qn : (b + 1) * qn] = value.astype(bf16)

        def mix(n, i, low_ref):
            head_out = nt(low_ref[:, 0:qn], kvg[0, 1])
            for b in range(1, hs):
                head_out = head_out + nt(low_ref[:, b * qn : (b + 1) * qn], kvg[b, 1])
            at = slice(i * query_block, (i + 1) * query_block)
            o_s[at, :] = jnp.where(lane_head == n, head_out.astype(bf16), o_s[at, :])

        o_s[...] = jnp.zeros_like(o_s)
        score(0, 0)
        for n in range(heads):
            soften(n, 0, pb_scr)
            score(n, 1)
            if n:
                mix(n - 1, 1, ds_scr)
            soften(n, 1, ds_scr)
            if n < heads - 1:
                score(n + 1, 0)
            mix(n, 0, pb_scr)
            if n == 0:
                ex_wf_2.send()
            if n == 1:
                ex_wf_1.wait()
                ex_wf_3.send()
        mix(heads - 1, 1, ds_scr)

        def pack(ref, v):
            ref[0:sl, :], ref[sl:, :] = dense(v)

        def unpack(ref):
            return loose(ref[0:sl, :], ref[sl:, :])

        for q in line_order:
            pack(o_st.at[q], o_s[aligned(q, sl), :])
            ex_o.out(q).start()
        pack(o_st.at[s], o_s[aligned(s, sl), :])
        og[y, z] = o_st[s]
        ex_wp_1.wait()
        ex_wp_3.send()
        ga_wo.relay()
        ga_go.relay()

        ga_wo.wait()
        assemble(lambda a, c, b, t: wog[(a * seqs + b) * cores + c, t], wo)
        ex_o.wait()
        branch = jnp.broadcast_to(prm[5:6, :], (home, width))
        for t in range(zs):
            mixed = jnp.concatenate([unpack(og.at[a, t]) for a in range(seqs)], axis=0)
            mixed_s[t] = mixed
            branch = branch + nn(mixed, wo[t * tw : (t + 1) * tw, :])
        middle = x_ref[...].reshape(home, width).astype(f32) + branch
        normed, _ = norm_parts(middle)
        x2g[pf] = (normed * prm[1:2, :] + prm[6:7, :]).astype(bf16)
        ga_x2.send(us - 1)
        middle_s[...] = middle
        for ex in (ga_go, ex_wf_2, ex_wp_2, ex_wf_3, ex_wp_3):
            ex.wait()
        assemble(
            lambda a, c, b, t: wfg[a * halves + t // near, (lax.rem(t, near) * seqs + b) * cores + c], wf
        )

        def feed(k, running):
            r = ga_x2.peer(k)

            @pl.when(k > 0)
            def _():
                ga_x2.relay_from(k)

            ga_x2.wait_from(k)
            at = aligned(r, duo)
            chip = pl.ds(cores * r, cores)
            hid = nn(x2g[chip].reshape(duo, width), wf[...]) + up_bias[0:1, :]
            gate = 1.0 / (1.0 + jnp.exp(-quick_slope * hid))
            act[at, :] = (hid * gate).astype(bf16)
            flow = nt(gog[chip].reshape(duo, width), wpg[...].reshape(part, width))
            slope = gate + quick_slope * hid * gate * (1.0 - gate)
            back = (flow * slope).astype(bf16)
            gh[at, :] = back
            gs_st[chip] = nt(back, wf[...]).astype(bf16).reshape(cores, home, width)
            re_gs.aside(r).start()

            @pl.when(k == 0)
            def _():
                ga_x2.send_last()

            @pl.when(k > 1)
            def _():
                re_gs.combine_out(k - 1)

            return running + jnp.sum(back.astype(f32), axis=0, keepdims=True)

        grad_up = lax.fori_loop(0, us, feed, jnp.zeros((1, part), f32))

        def turn_act(q):
            at = aligned(q, home)
            x2t[0:part, at] = act[at, :].T

        loop(0, ps, turn_act)
        re_gs.combine_out(us - 1)
        re_gs.combine(u_at)

        def proj_grad(c):
            wps[pl.ds(2 * c, 2)] = nn(
                x2t[aligned(c, 2 * ff_rows), :], gog[...].reshape(slab, width)
            ).astype(bf16).reshape(2, ff_rows, width)

        loop(0, zs // 2, proj_grad)
        ex_gp_1.send()

        def feed_down(r):
            chip = pl.ds(cores * r, cores)
            fd_st[chip] = nn(act[aligned(r, duo), :], wpg[...].reshape(part, width)).astype(bf16).reshape(
                cores, home, width
            )
            re_fd.aside(r).start()

        loop(0, us, feed_down)

        def scatter_rows(c, val, put):
            for j in range(val.shape[0] // rows):
                d = c * (val.shape[0] // rows) + j
                hq = d // ss
                sd = lax.rem(d, ss)
                put(
                    hq // cores, lax.rem(hq, cores), lax.rem(sd, seqs), sd // seqs,
                    val[j * rows : (j + 1) * rows, :].astype(bf16),
                )

        def turn_in(q):
            x2t[:, aligned(q, home)] = x2g[q].T

        loop(0, ps, turn_in)

        def fc_grad(c):
            def put(a, c, b, t, value):
                wfs[a * halves + t // near, (lax.rem(t, near) * seqs + b) * cores + c] = value

            scatter_rows(c, nn(x2t[aligned(c, quad), :], gh[...]), put)

        loop(0, width // quad, fc_grad)
        ex_gf_1.send()

        for t in range(zs):
            x2t[t * tw : (t + 1) * tw, 0:home] = mixed_s[t].T
        grad_final = go_ref[...].reshape(home, width).astype(f32) * keep

        re_gs.wait()

        def landed_sum(re, own):
            total = own
            for k in range(1, us):
                total = total + re.landed(re.peer(k))[...].astype(f32)
            return total

        grad_second = landed_sum(re_gs, gs_st[pf].astype(f32))
        n2, r2 = norm_parts(middle_s[...])
        grad_middle = grad_final + norm_backward(grad_second * prm[1:2, :], n2, r2)
        grad_branch = grad_middle.astype(bf16)
        for t in z_order + [z]:
            value = nt(grad_branch, wo[aligned(t, tw), :]).astype(bf16)
            for a in range(seqs):
                pack(do_st.at[t, a], value[a * sl : (a + 1) * sl, :])
            if t is not z:
                for a in range(seqs):
                    ex_do.out(t * seqs + a).start()
        ex_do.out(z * seqs + 1 - y).start()
        dog[s] = do_st[z, y]
        gm_s[...] = grad_middle
        sums[...] = jnp.zeros_like(sums)
        arg[...] = jnp.zeros_like(arg)
        for q in range(ps):
            c, b, a = q % cores, q // cores % seqs, q // cores // seqs
            for i in range(zs):
                at = (a * halves + i // near) * ff_rows
                arg[q, 8 + i : 9 + i, 0:ff_rows] = jnp.where(
                    (core == c) & (y == b) & (zl == i % near), grad_up[:, at : at + ff_rows], 0.0
                )
        sums[1:2, :] = jnp.sum(grad_second * n2, axis=0, keepdims=True)
        sums[6:7, :] = jnp.sum(grad_second, axis=0, keepdims=True)
        sums[5:6, :] = jnp.sum(grad_branch.astype(f32), axis=0, keepdims=True)


        def out_grad(c):
            def put(a, c, b, t, value):
                wog[(a * seqs + b) * cores + c, t] = value

            scatter_rows(c, nn(x2t[aligned(c, quad), 0:home], gm_s[...].astype(bf16)), put)

        ga_wo.drain()
        loop(0, width // quad, out_grad)
        re_wo.send_aside()
        re_wo.send()

        ex_do.wait()
        ex_gp_1.wait()

        def proj_sum(q):
            wpm[q] = (wps[t_at - zh + q].astype(f32) + wpr[q].astype(f32)).astype(bf16)

        loop(0, halves, proj_sum)
        ex_gp_2.send()
        re_fd.send()

        def gather_do(i):
            at = aligned(i, 2 * sl)
            value = jnp.concatenate([unpack(dog.at[2 * i]), unpack(dog.at[2 * i + 1])], axis=0)
            o_s[at, :] = value
            dot_s[:, at] = value.T
            qt_s[:, at] = q_s[at, :].T

        loop(0, ss // 2, gather_do)
        dq_s[...] = jnp.zeros_like(dq_s)

        def slope_in(n, i, out_ref):
            outer = o_s[i * query_block : (i + 1) * query_block, :]
            masked = jnp.where(lane_head == n, outer, jnp.zeros_like(outer))
            for b in range(hs):
                out_ref[:, b * qn : (b + 1) * qn] = nn(masked, kvg[b, 1])

        def slopes(n, i, in_ref, slope_ref, low_ref):
            for r in range(query_block // chunk):
                rat = slice(r * chunk, (r + 1) * chunk)
                dp = [in_ref[rat, b * qn : (b + 1) * qn] for b in range(hs)]
                pv = [probs[n, i, rat, b * qn : (b + 1) * qn] for b in range(hs)]
                delta = jnp.sum(
                    functools.reduce(jnp.add, [a * c for a, c in zip(dp, pv)]), axis=-1, keepdims=True
                )
                for b in range(hs):
                    slope_ref[rat, b * qn : (b + 1) * qn] = (pv[b] * (dp[b] - delta)).astype(bf16)
                    low_ref[rat, b * qn : (b + 1) * qn] = pv[b].astype(bf16)

        def slope_out(n, i, slope_ref, low_ref):
            at = slice(i * query_block, (i + 1) * query_block)
            head_rows = slice(n * HEAD_DIM, (n + 1) * HEAD_DIM)
            head_dq = nt(slope_ref[:, 0:qn], kvg[0, 0])
            for b in range(1, hs):
                head_dq = head_dq + nt(slope_ref[:, b * qn : (b + 1) * qn], kvg[b, 0])
            dq_s[at, :] = jnp.where(
                lane_head == n, (head_dq.astype(bf16).astype(f32) * scale).astype(bf16), dq_s[at, :]
            )
            for b in range(hs):
                new_k = nn(qt_s[head_rows, at], slope_ref[:, b * qn : (b + 1) * qn])
                new_v = nn(dot_s[head_rows, at], low_ref[:, b * qn : (b + 1) * qn])
                if i == 0:
                    dkt[b] = new_k
                    dvt[b] = new_v
                else:
                    kv_st[n, b, 0] = (dkt[b] + new_k).astype(bf16)
                    kv_st[n, b, 1] = (dvt[b] + new_v).astype(bf16)

        def final_rows(re, own, landed, dst):
            def one(t):
                total = own[p, t].astype(f32)
                for k in range(1, rs):
                    total = total + landed[re.peer(k), t].astype(f32)
                dst[t] = total.astype(bf16)

            loop(0, zs, one)

        slope_in(0, 0, s_scr)
        for n in range(heads):
            slopes(n, 0, s_scr, ds_scr, pb_scr)
            slope_in(n, 1, t_scr)
            slope_out(n, 0, ds_scr, pb_scr)
            if n:
                re_kv[n - 1].send()
            slopes(n, 1, t_scr, ds_scr, pb_scr)
            if n < heads - 1:
                slope_in(n + 1, 0, s_scr)
            slope_out(n, 1, ds_scr, pb_scr)
            re_kv[n].send_aside()
            if n == heads - 1:
                re_wo.wait()
                final_rows(re_wo, wog, wo_red, woz)
                ex_go_z.send()
                wozr[z] = woz[z]
            if n == 0:
                ex_gf_1.wait()

                def fc_sum(i):
                    q, b = i // ps, lax.rem(i, ps)
                    wfm[q, b] = (wfs[t_at - zh + q, b].astype(f32) + wfr[q, b].astype(f32)).astype(bf16)

                loop(0, halves * ps, fc_sum)
                ex_gf_2.send()
        re_kv[heads - 1].send()

        gpt[0:tw, :] = dq_s[...].T

        def turn_first(i):
            _, first = first_norm(i)
            x2t[:, aligned(i, 2 * sl)] = first.T

        loop(0, zs, turn_first)

        for n in range(heads):
            re_kv[n].wait()
            for k in range(2):
                at = (1 + k) * tw + n * HEAD_DIM
                gpt[at : at + HEAD_DIM, :] = (
                    kv_st[n, h, k].astype(f32) + kv_red[n, re_kv[n].peer(1), k].astype(f32)
                ).astype(bf16)
        gp[...] = gpt[...].T

        gain_sum = jnp.zeros((1, width), f32)
        shift_sum = jnp.zeros((1, width), f32)
        block = ss // halves

        def first_grad(i):
            value = nt(gp[aligned(i, block * sl), :], wq[...])
            gf_st[pl.ds(block * i, block)] = value.astype(bf16).reshape(block, sl, width)

        first_grad(1 - zh)
        ex_gf.send(0, 1)

        def qkv_grad(c):
            def put(a, c, b, t, value):
                wqg[(a * seqs + b) * cores + c, t] = value

            scatter_rows(c, nn(x2t[aligned(c, quad), 0:qn], gp[...]), put)

        ga_wq.drain()
        loop(0, width // quad, qkv_grad)
        re_wq.send_aside()
        first_grad(zh)
        re_wq.send()
        ex_gf.send(1)
        gfg[y, z] = gf_st[s]
        ex_gf_2.wait()

        def fc_last(q):
            wfz[q] = (wfm[zh, q].astype(f32) + wfq[q].astype(f32)).astype(bf16)

        loop(0, ps, fc_last)
        ex_gf_3.send()
        wfzr[pf] = wfz[pf]
        for i in range(zs):
            value = gf_st[2 * i : 2 * i + 2].reshape(2 * sl, width).astype(f32)
            normed, _ = first_norm(i)
            gain_sum = gain_sum + jnp.sum(value * normed, axis=0, keepdims=True)
            shift_sum = shift_sum + jnp.sum(value, axis=0, keepdims=True)

        sums[0:1, :] = gain_sum
        sums[2:3, :] = shift_sum
        re_fd.wait()
        feed_out = landed_sum(re_fd, fd_st[pf].astype(f32)) + prm[7:8, :]
        final = middle_s[...] + feed_out
        out_ref[...] = (final * keep).astype(bf16).reshape(seqs, sl, width)
        leave(0)
        xv = x_ref[...].reshape(home, width).astype(f32)
        br = middle_s[...] - xv
        place = lax.broadcasted_iota(jnp.int32, (1, 128), 1)
        squares = jnp.zeros((1, 128), f32)
        for k, value in enumerate((xv, br, feed_out, final)):
            squares = squares + jnp.where(place == k, jnp.sum(keep * value * value), 0.0)
        for q in range(ps):
            arg[q, 12:13, :] = squares
        projected_sum = jnp.sum(gp[...].astype(f32), axis=0, keepdims=True)
        for i in range(zs):
            at = slice(i * tw, (i + 1) * tw)
            sums[3:4, at] = jnp.where(z == i, projected_sum[:, 0:tw], 0.0)
            sums[4:5, at] = jnp.where(z == i, projected_sum[:, 2 * tw :], 0.0)
        sums[7:8, :] = jnp.sum(gog[pf].astype(f32), axis=0, keepdims=True)

        for q in range(ps):
            for i in range(zs):
                at = d_of(q, i) * rows
                arg[q, 0:8, i * rows : (i + 1) * rows] = sums[0:8, at : at + rows]
        ex_ar_p.send()
        ard[p] = arg[p]

        ex_gp_2.wait()
        gproj_ref[...] = wpm[zh].astype(f32) + wpq[...].astype(f32)
        leave(5)

        re_wq.wait()
        final_rows(re_wq, wqg, wq_red, wqz)
        ex_gq_z.send()
        wqzr[z] = wqz[z]
        ex_ar_p.wait()
        total = functools.reduce(jnp.add, [ard[q] for q in range(ps)])
        for i in range(zs):
            ar_st[i, 0:8, 0:rows] = total[0:8, i * rows : (i + 1) * rows]
            ar_st[i, 8:9, :] = total[8 + i : 9 + i, :]
            ar_st[i, 9:10, :] = total[12:13, :]
        ex_ar_z.send()
        arz[z] = ar_st[z]
        ex_go_z.wait()
        gout_ref[...] = functools.reduce(jnp.add, [wozr[t].astype(f32) for t in range(zs)])
        leave(3)

        for ex in (
            ex_small_z, ex_wq_z, ex_wo_z, ex_x, ga_small, ex_wf_p, ex_wf_1, ex_wf_2, ex_wf_3,
            ex_wp_1, ex_wp_2, ex_wp_3,
            ga_go, *ga_kv, ex_o, re_gs, re_fd, ex_do, *re_kv, re_wo, ex_go_z, re_wq,
            ex_gf_1, ex_gf_2, ex_gf_3, ex_gp_1, ex_gp_2, ex_ar_p,
        ):
            ex.drain()
        ga_x2.drain(us - 1)

        ex_gf.wait()
        grad_first = functools.reduce(jnp.add, [gfg[:, t].astype(f32) for t in range(zs)]).reshape(home, width)
        n1, r1 = norm_parts(x_ref[...].reshape(home, width).astype(f32))
        grad_in = gm_s[...] + norm_backward(grad_first * prm[0:1, :], n1, r1)
        gin_ref[...] = grad_in.reshape(seqs, sl, width)
        leave(1)

        ex_gf_3.wait()
        for q in range(ps):
            for b in range(zs):
                at = ff_place(q, b) * ff_rows
                gfc_ref[:, at : at + ff_rows] = wfzr[q, :, b * ff_rows : (b + 1) * ff_rows].astype(f32)
        leave(4)
        ex_gq_z.wait()
        for i in range(zs):
            for k in range(3):
                at = k * width + i * tw
                gqkv_ref[:, at : at + tw] = wqzr[i, :, k * tw : (k + 1) * tw].astype(f32)
        leave(2)
        ex_ar_z.wait()
        owned = functools.reduce(jnp.add, [arz[t] for t in range(zs)])
        owned_ref[...] = owned
        leave(6)
        for ex in (ex_gf, ex_gq_z, ex_ar_z):
            ex.drain()
        for copy in leaving:
            copy.wait()

    vm = pltpu.VMEM
    scratch = [
        vm((seqs, sl, width), bf16),
        vm((seqs, sl, width), bf16),
        vm((rows, 3 * width), bf16),
        vm((rows, width), bf16),
        vm((rows, ps * part), bf16),
        vm((ff_rows, width), bf16),
        vm((1, ff_rows), bf16),
        vm((2, rows), bf16),
        vm((6, rows), bf16),
        pltpu.SemaphoreType.DMA((9,)),
        vm((seqs, sl, width), bf16),
        vm((seqs, sl, width), f32),
        vm((rows, 3 * width), f32),
        vm((rows, width), f32),
        vm((rows, ps * part), f32),
        vm((ff_rows, width), f32),
        vm((16, 128), f32),
        pltpu.SemaphoreType.DMA((7,)),
        vm((16, 128), f32),
        vm((zs, 16, 128), f32),
        vm((ps, zs, 16, 128), f32),
        vm((16, width), f32),
        vm((8, part), f32),
        vm((zs, rows, 3 * tw), bf16),
        vm((ps, rows, part), bf16),
        vm((ps, zs, rows, 3 * tw), bf16),
        vm((ps, zs, rows, width), bf16),
        vm((zs, ps, rows, part), bf16),
        vm((zs, ff_rows, width), bf16),
        vm((width, 3 * tw), bf16),
        vm((width, width), bf16),
        vm((width, part), bf16),
        vm((ss, sl, width), bf16),
        vm((qn, tw), bf16),
        vm((hs, 2, tw, qn), bf16),
        vm((hs, 8, qn), f32),
        vm((heads, blocks, query_block, hs * qn), f32),
        vm((query_block, hs * qn), f32),
        vm((query_block, hs * qn), f32),
        vm((query_block, hs * qn), bf16),
        vm((query_block, hs * qn), bf16),
        vm((qn, tw), bf16),
        vm((ss, sl * tw // lanes_per, lanes_per), bf16),
        vm((seqs, zs, sl * tw // lanes_per, lanes_per), bf16),
        vm((zs, home, tw), bf16),
        vm((home, width), f32),
        vm((home, width), f32),
        vm((ps, home, width), bf16),
        vm((ps, home, width), bf16),
        vm((slab, part), bf16),
        vm((slab, part), bf16),
        vm((width, slab), bf16),
        vm((ps, home, width), bf16),
        vm((rs, home, width), bf16),
        vm((rs, home, width), bf16),
        vm((ps, home, width), bf16),
        vm((rs, home, width), bf16),
        vm((rs, home, width), bf16),
        vm((zs, seqs, sl * tw // lanes_per, lanes_per), bf16),
        vm((ss, sl * tw // lanes_per, lanes_per), bf16),
        vm((tw, qn), bf16),
        vm((tw, qn), bf16),
        vm((qn, tw), bf16),
        vm((hs, HEAD_DIM, qn), f32),
        vm((hs, HEAD_DIM, qn), f32),
        vm((heads, hs, 2, HEAD_DIM, qn), bf16),
        vm((heads, xs, 2, HEAD_DIM, qn), bf16),
        vm((heads, xs, 2, HEAD_DIM, qn), bf16),
        vm((3 * tw, qn), bf16),
        vm((qn, 3 * tw), bf16),
        vm((ss, sl, width), bf16),
        vm((seqs, zs, sl, width), bf16),
        vm((rs, zs, rows, width), bf16),
        vm((rs, zs, rows, width), bf16),
        vm((zs, rows, width), bf16),
        vm((zs, rows, width), bf16),
        vm((rs, zs, rows, 3 * tw), bf16),
        vm((rs, zs, rows, 3 * tw), bf16),
        vm((zs, rows, 3 * tw), bf16),
        vm((zs, rows, 3 * tw), bf16),
        vm((zs, ps, rows, part), bf16),
        vm((halves, ps, rows, part), bf16),
        vm((halves, ps, rows, part), bf16),
        vm((ps, rows, part), bf16),
        vm((ps, rows, part), bf16),
        vm((ps, rows, part), bf16),
        vm((zs, ff_rows, width), bf16),
        vm((halves, ff_rows, width), bf16),
        vm((halves, ff_rows, width), bf16),
        vm((ff_rows, width), bf16),
        vm((ps, 16, 128), f32),
        vm((ps, 16, 128), f32),
        vm((8, width), f32),
        vm((zs, 16, 128), f32),
        vm((zs, 16, 128), f32),
        pltpu.SemaphoreType.DMA((33,)),
        pltpu.SemaphoreType.DMA((10, zs)),
        pltpu.SemaphoreType.DMA((4, ss)),
        pltpu.SemaphoreType.DMA((3, ps)),
        pltpu.SemaphoreType.DMA((10, 2)),
        pltpu.SemaphoreType.DMA((6, ps)),
        pltpu.SemaphoreType.DMA((7, 2, rs)),
        pltpu.SemaphoreType.DMA((zs, hs)),
        pltpu.SemaphoreType.DMA((heads, 2, xs)),
        pltpu.SemaphoreType.DMA((7, 2)),
    ]
    in_smem = pl.BlockSpec(memory_space=pltpu.SMEM)
    in_place = pl.BlockSpec(memory_space=pl.ANY)
    shapes = (
        jax.ShapeDtypeStruct((seqs, sl, width), bf16),
        jax.ShapeDtypeStruct((seqs, sl, width), f32),
        jax.ShapeDtypeStruct((rows, 3 * width), f32),
        jax.ShapeDtypeStruct((rows, width), f32),
        jax.ShapeDtypeStruct((rows, ps * part), f32),
        jax.ShapeDtypeStruct((ff_rows, width), f32),
        jax.ShapeDtypeStruct((1, ff_rows), f32),
        jax.ShapeDtypeStruct((2, rows), f32),
        jax.ShapeDtypeStruct((6, rows), f32),
        jax.ShapeDtypeStruct((1, 4), f32),
    )
    results = pl.pallas_call(
        kernel,
        out_shape=shapes[0:6] + (jax.ShapeDtypeStruct((16, 128), f32),),
        in_specs=[in_smem] + [in_place] * 9,
        out_specs=(in_place,) * 7,
        scratch_shapes=scratch,
        compiler_params=pltpu.CompilerParams(
            collective_id=0, has_side_effects=True, vmem_limit_bytes=63 * 1024 * 1024
        ),
        name="layer",
    )(
        lengths,
        layer_input.reshape(seqs, sl, width),
        grad_out.reshape(seqs, sl, width),
        w_qkv,
        w_out,
        w_fc,
        w_proj,
        b_fc.reshape(1, ff_rows),
        norm_gains,
        biases,
    )

    def finish(len_ref, *refs):
        given, kept, held, small_held = refs[0:7], refs[7:17], refs[17:24], refs[24:28]
        in_sem, out_sem = refs[28:]
        arrive = [pltpu.make_async_copy(given[i], held[i], in_sem.at[i]) for i in range(7)]
        leave = [
            pltpu.make_async_copy(ref, kept[i], out_sem.at[i])
            for i, ref in enumerate(held[0:6] + small_held)
        ]
        for i in (6, 1, 4, 5, 2, 0, 3):
            arrive[i].start()
        arrive[6].wait()
        owned = held[6]
        small_held[0][...] = owned[8:9, 0:ff_rows]
        small_held[1][...] = owned[0:2, 0:rows]
        small_held[2][...] = owned[2:8, 0:rows]
        valid = (len_ref[0] + len_ref[1]).astype(f32) * width
        small_held[3][...] = jnp.sqrt(owned[9:10, 0:4] / valid)
        for i in range(6, 10):
            leave[i].start()
        for i in (1, 4, 5, 2, 0, 3):
            arrive[i].wait()
            leave[i].start()
        for copy in leave:
            copy.wait()

    final = pl.pallas_call(
        finish,
        out_shape=shapes,
        in_specs=[in_smem] + [in_place] * 7,
        out_specs=(in_place,) * 10,
        scratch_shapes=[vm(s.shape, s.dtype) for s in shapes[0:6]]
        + [vm((16, 128), f32)]
        + [vm(s.shape, s.dtype) for s in shapes[6:]]
        + [pltpu.SemaphoreType.DMA((7,)), pltpu.SemaphoreType.DMA((10,))],
        name="finish",
    )(lengths, *results)
    return (
        final[0].reshape(layer_input.shape),
        final[1].reshape(layer_input.shape),
        *final[2:6],
        final[6].reshape(ff_rows),
        final[7],
        final[8],
        final[9].reshape(4),
    )


def fits(seqs, sl, width, hs, ss, qkv_rows):
    if seqs != 2 or ss % seqs or hs % cores:
        return False
    zs = ss // seqs
    if width % zs or (width // zs) % HEAD_DIM or zs != 4 or hs != zs or qkv_rows % 8:
        return False
    tw = width // zs
    keys = ss * sl * hs
    return tw <= 256 and keys * ss * sl * (tw // HEAD_DIM) * 4 <= 16 * 1024 * 1024


def on_device(layer_input, grad_out, lengths, w_qkv, w_out, w_fc, w_proj, b_fc, norm_gains, biases):
    seqs, _, sl, width = layer_input.shape
    hs, ss = lax.axis_size("head"), lax.axis_size("seq")
    chosen = fused_layer if fits(seqs, sl, width, hs, ss, w_qkv.shape[0]) else spread_layer
    return chosen(
        layer_input, grad_out, lengths, w_qkv, w_out, w_fc, w_proj, b_fc, norm_gains, biases
    )


def solution(mesh):
    return jax.shard_map(
        on_device,
        mesh=mesh,
        in_specs=(
            P(None, "seq", "head", None),
            P(None, "seq", "head", None),
            P(),
            P(("head", "seq"), None),
            P(("head", "seq"), None),
            P(("head", "seq"), None),
            P(("head", "seq"), None),
            P(("head", "seq")),
            P(None, ("head", "seq")),
            P(None, ("head", "seq")),
        ),
        out_specs=(
            P(None, "seq", "head", None),
            P(None, "seq", "head", None),
            P(("head", "seq"), None),
            P(("head", "seq"), None),
            P(("head", "seq"), None),
            P(("head", "seq"), None),
            P(("head", "seq")),
            P(None, ("head", "seq")),
            P(None, ("head", "seq")),
            P(),
        ),
        check_vma=False,
    )
```
